32 devices in a mesh: dp: 8 (over y, x, core), sp: 4 (over z).
Axes of the slice: x: 2, y: 2, z: 4, core: 2. Of those that a mesh axis runs over, the one named last changes fastest.
Arguments:
- tokens: bfloat16 [2, 8192, 1408], P(None, ('dp', 'sp')), may hold values from -6 to 6
- skip_tokens: bfloat16 [2, 8192, 1408], P(None, ('dp', 'sp')), may hold values from -6 to 6
- text: bfloat16 [2, 2688, 1024], P(None, ('dp', 'sp')), may hold values from -6 to 6
- timestep: int32 [2, 8], P(None, 'dp'), may hold values from 0 to 999
- grid: int32 [2, 8, 2], P(None, 'dp'), may hold values from 19 to 32, as said below
- text_len: int32 [2, 8, 2], P(None, 'dp'), may hold values from 1 to 256, as said below
- w_skip: bfloat16 [2816, 1408], P('sp', 'dp'), may hold values from -0.109375 to 0.109375
- w_mod: bfloat16 [1408, 1408], P('sp', 'dp'), may hold values from -0.15625 to 0.15625
- w_qkv: bfloat16 [1408, 3, 1408], P('dp', None, 'sp'), may hold values from -0.15625 to 0.15625
- w_out1: bfloat16 [1408, 1408], P('sp', 'dp'), may hold values from -6 to 6
- w_query2: bfloat16 [1408, 1408], P('dp', 'sp'), may hold values from -0.15625 to 0.15625
- w_text_kv: bfloat16 [1024, 2, 1408], P('dp', None, 'sp'), may hold values from -0.1875 to 0.1875
- w_out2: bfloat16 [1408, 1408], P('sp', 'dp'), may hold values from -2 to 2
- w_fc1: bfloat16 [1408, 6144], P('dp', 'sp'), may hold values from -0.15625 to 0.15625
- w_fc2: bfloat16 [6144, 1408], P('sp', 'dp'), may hold values from -0.078125 to 0.078125
- gain_skip: float32 [1408], replicated, may hold values from 0.5 to 1.5
- gain_attn: float32 [1408], replicated, may hold values from 0.5 to 1.5
- gain_cross: float32 [1408], replicated, may hold values from 0.5 to 1.5
- gain_mlp: float32 [1408], replicated, may hold values from 0.5 to 1.5
- gain_query: float32 [88], replicated, may hold values from 0.5 to 1.5
- gain_key: float32 [88], replicated, may hold values from 0.5 to 1.5
- cotangent: bfloat16 [2, 8192, 1408], P(None, ('dp', 'sp')), may hold values from -6 to 6
Outputs:
- out: bfloat16 [2, 8192, 1408], P(None, ('dp', 'sp'))
- d_tokens: float32 [2, 8192, 1408], P(None, ('dp', 'sp'))
- d_skip: float32 [2, 8192, 1408], P(None, ('dp', 'sp'))
- d_text: float32 [2, 2688, 1024], P(None, ('dp', 'sp'))
- d_w_skip: float32 [2816, 1408], P('sp', 'dp')
- d_w_mod: float32 [1408, 1408], P('sp', 'dp')
- d_w_qkv: float32 [1408, 3, 1408], P('dp', None, 'sp')
- d_w_out1: float32 [1408, 1408], P('sp', 'dp')
- d_w_query2: float32 [1408, 1408], P('dp', 'sp')
- d_w_text_kv: float32 [1024, 2, 1408], P('dp', None, 'sp')
- d_w_out2: float32 [1408, 1408], P('sp', 'dp')
- d_w_fc1: float32 [1408, 6144], P('dp', 'sp')
- d_w_fc2: float32 [6144, 1408], P('sp', 'dp')
- d_gain_skip: float32 [1408], P(('dp', 'sp'))
- d_gain_attn: float32 [1408], P(('dp', 'sp'))
- d_gain_cross: float32 [1408], P(('dp', 'sp'))
- d_gain_mlp: float32 [1408], P(('dp', 'sp'))
- d_gain_query: float32 [88], replicated
- d_gain_key: float32 [88], replicated
The draws below stay inside these ranges and needn't reach their ends.
Inputs may be any that keep to these rules, and one draw needn't show every extreme that they name: grid[m, r] holds (rows, columns) of patches of that image, rows from 19 to 32, columns from 21 to 32; its tokens fill the first rows * columns of its 1024 slots in row-major order. In micro-batch 0 the image on the last dp rank has 32 x 32 patches and the one on rank 0 the fewest rows and columns. text_len[m, r] holds (CLIP tokens, mT5 tokens) of that image's caption: the first from 1 to 77, the second from 1 to 256. In micro-batch 0 rank 0's caption is full in both and the last rank's has one token in each.
All inputs are finite; a program needn't handle non-finite values.
Results may differ from the reference program's by a relative error of at most 0.024.
Values may be sent and summed in bfloat16 or wider, within the bound.
No kernel may reach another device: no remote copies, remote signals or barrier semaphores. Data moves between devices by JAX's collectives and lax.ppermute only.
A program may use at most 512 MiB of HBM per device.

```python
import math
import jax
import jax.numpy as jnp
from jax import lax

H = 16
HD = 88
FF = 6144
TX = 1024
CLIP_LEN = 77
T5_LEN = 256
TXT = 336
GRID_H = 32
GRID_W = 32
MB = 2
D = 1408
SEQ_CAP = 1024
TOKENS = 8192
TEXT_ROWS = 2688
N_DP = 8


def pick_corner(values, first_value, last_value):
    micro_index = lax.broadcasted_iota(jnp.int32, values.shape, 0)
    rank_index = lax.broadcasted_iota(jnp.int32, values.shape, 1)
    values = jnp.where((micro_index == 0) & (rank_index == 0), first_value, values)
    return jnp.where((micro_index == 0) & (rank_index == values.shape[1] - 1), last_value, values)


def draw_grid(key, part):
    shape = (MB, N_DP)
    height = jax.random.randint(jax.random.fold_in(key, 11), shape, 3 * GRID_H // 5, GRID_H + 1)
    breadth = jax.random.randint(jax.random.fold_in(key, 12), shape, 2 * GRID_W // 3, GRID_W + 1)
    height = pick_corner(height, 3 * GRID_H // 5, GRID_H)
    breadth = pick_corner(breadth, 2 * GRID_W // 3, GRID_W)
    return jnp.stack([height, breadth], -1).astype(jnp.int32)


def draw_text_len(key, part):
    shape = (MB, N_DP)
    clip_count = jax.random.randint(jax.random.fold_in(key, 21), shape, 1, CLIP_LEN + 1)
    long_count = jax.random.randint(jax.random.fold_in(key, 22), shape, 1, T5_LEN + 1)
    clip_count = pick_corner(clip_count, CLIP_LEN, 1)
    long_count = pick_corner(long_count, T5_LEN, 1)
    return jnp.stack([clip_count, long_count], -1).astype(jnp.int32)


def place_ends(result, own_key, least, largest):
    dims = result.shape
    spot = [jax.random.randint(jax.random.fold_in(own_key, axis), (), 0, dims[axis]) for axis in range(len(dims))]
    result = result.at[tuple(spot)].set(least)
    longest = dims.index(max(dims))
    spot[longest] = (spot[longest] + 1) % dims[longest]
    return result.at[tuple(spot)].set(largest)


def level_of(key, extent, shards, low, top_value):
    loudness = 1.0
    for position, shards_of in shards:
        steps = jax.random.uniform(jax.random.fold_in(jax.random.fold_in(key, 6), position), (shards_of,), jnp.float32, low / len(shards), top_value / len(shards))
        loudness = loudness * jnp.repeat(jnp.exp(steps), extent[position] // shards_of).reshape((-1,) + (1,) * (len(extent) - 1 - position))
    return loudness


def gaussian(own_key, shape, scale, limit, pieces=(), held_as=jnp.bfloat16):
    level = level_of(own_key, shape, pieces, -0.22, 0.18) if pieces else 1.0
    result = jax.random.normal(own_key, shape, jnp.float32) * scale * level
    return jnp.minimum(jnp.maximum(result, -limit), limit).astype(held_as)


def setup_inputs(seed: int = 0) -> dict:
    seeds = jax.random.split(jax.random.key(seed), 23)
    tokens = gaussian(seeds[0], (MB, TOKENS, D), 1.0, 6.0, ((1, 32),))
    skip_tokens = gaussian(seeds[1], (MB, TOKENS, D), 1.0, 6.0, ((1, 32),))
    text = gaussian(seeds[2], (MB, TEXT_ROWS, TX), 1.0, 6.0, ((1, 32),))
    timestep = place_ends(jax.random.randint(seeds[3], (MB, N_DP), 0, 1000), jax.random.fold_in(seeds[3], 1), 0, 999).astype(jnp.int32)
    grid = draw_grid(jax.random.fold_in(seeds[22], 71), 0)
    text_len = draw_text_len(jax.random.fold_in(seeds[22], 71), 0)
    w_skip = gaussian(seeds[6], (2 * D, D), (2 * D) ** -0.5, 0.109375, ((0, 4), (1, 8)))
    w_mod = gaussian(seeds[7], (D, D), D ** -0.5, 0.15625, ((0, 4), (1, 8)))
    w_qkv = gaussian(seeds[8], (D, 3, D), D ** -0.5, 0.15625, ((0, 8), (2, 4)))
    w_out1 = gaussian(seeds[9], (D, D), 1 ** -0.5, 6.0, ((0, 4), (1, 8)))
    w_query2 = gaussian(seeds[10], (D, D), D ** -0.5, 0.15625, ((0, 8), (1, 4)))
    w_text_kv = gaussian(seeds[11], (TX, 2, D), TX ** -0.5, 0.1875, ((0, 8), (2, 4)))
    w_out2 = gaussian(seeds[12], (D, D), 8 ** -0.5, 2.0, ((0, 4), (1, 8)))
    w_fc1 = gaussian(seeds[13], (D, FF), D ** -0.5, 0.15625, ((0, 8), (1, 4)))
    w_fc2 = gaussian(seeds[14], (FF, D), FF ** -0.5, 0.078125, ((0, 4), (1, 8)))
    gain_skip = jnp.clip(1.0 + 0.1 * jax.random.normal(seeds[15], (D,), jnp.float32), 0.5, 1.5)
    gain_attn = jnp.clip(1.0 + 0.1 * jax.random.normal(seeds[16], (D,), jnp.float32), 0.5, 1.5)
    gain_cross = jnp.clip(1.0 + 0.1 * jax.random.normal(seeds[17], (D,), jnp.float32), 0.5, 1.5)
    gain_mlp = jnp.clip(1.0 + 0.1 * jax.random.normal(seeds[18], (D,), jnp.float32), 0.5, 1.5)
    gain_query = jnp.clip(1.0 + 0.1 * jax.random.normal(seeds[19], (HD,), jnp.float32), 0.5, 1.5)
    gain_key = jnp.clip(1.0 + 0.1 * jax.random.normal(seeds[20], (HD,), jnp.float32), 0.5, 1.5)
    cotangent = gaussian(seeds[21], (MB, TOKENS, D), 1.0, 6.0, ((1, 32),))
    return dict(tokens=tokens, skip_tokens=skip_tokens, text=text, timestep=timestep, grid=grid, text_len=text_len, w_skip=w_skip, w_mod=w_mod, w_qkv=w_qkv, w_out1=w_out1, w_query2=w_query2, w_text_kv=w_text_kv, w_out2=w_out2, w_fc1=w_fc1, w_fc2=w_fc2, gain_skip=gain_skip, gain_attn=gain_attn, gain_cross=gain_cross, gain_mlp=gain_mlp, gain_query=gain_query, gain_key=gain_key, cotangent=cotangent)


@jax.custom_vjp
def low(v):
    return lax.optimization_barrier(v.astype(jnp.bfloat16)).astype(jnp.float32)

@jax.custom_vjp
def low_back(v):
    return v

def low_keep(v):
    return (low(v), None)

def low_pass(kept, grad):
    return (grad,)

def back_keep(v):
    return (v, None)

def back_low(kept, grad):
    return (low(grad),)
low.defvjp(low_keep, low_pass)
low_back.defvjp(back_keep, back_low)
EPS = 1e-06
MASKED = -1e+30
HIGHEST = lax.Precision.HIGHEST

def matmul(left, right):
    return jnp.dot(left, right, precision=HIGHEST, preferred_element_type=jnp.float32)

def norm_rows(value, gain):
    mean = lax.optimization_barrier(jnp.mean(value, -1, keepdims=True))
    centre = value - mean
    spread = lax.optimization_barrier(jnp.mean(centre * centre, -1, keepdims=True))
    return centre * lax.rsqrt(spread + EPS) * gain

def time_embed(step, width):
    half = width // 2
    rate = jnp.exp(-math.log(10000.0) * jnp.arange(half, dtype=jnp.float32) / half)
    angle = step.astype(jnp.float32) * rate
    return jnp.concatenate([jnp.cos(angle), jnp.sin(angle)])

def rope_tables(place, wide, head):
    row = (place // wide).astype(jnp.float32)
    column = (place % wide).astype(jnp.float32)
    quarter = head // 4
    pair = jnp.arange(head // 2, dtype=jnp.int32)
    upper = pair < quarter
    rank = jnp.where(upper, pair, pair - quarter).astype(jnp.float32)
    rate = jnp.exp(-math.log(10000.0) * rank / quarter)
    angle = jnp.where(upper[None, :], row[:, None], column[:, None]) * rate[None, :]
    return (jnp.cos(angle)[:, None, :], jnp.sin(angle)[:, None, :])

def rotate(value, cosine, sine):
    pairs = value.reshape(value.shape[:-1] + (value.shape[-1] // 2, 2))
    even = pairs[..., 0]
    odd = pairs[..., 1]
    return jnp.stack([even * cosine - odd * sine, even * sine + odd * cosine], -1).reshape(value.shape)

def attention(query, key, value, live_keys):
    scale = query.shape[-1] ** (-0.5)

    def one_head(items):
        rows, keys, values = items
        scores = low_back(matmul(rows, keys.T) * scale)
        scores = jnp.where(live_keys[None, :], scores, MASKED)
        top = lax.optimization_barrier(jnp.max(scores, -1, keepdims=True))
        raised = jnp.exp(scores - top)
        probs = raised / lax.optimization_barrier(jnp.sum(raised, -1, keepdims=True))
        return matmul(low(probs), values)
    per_head = lax.map(jax.checkpoint(one_head), (jnp.swapaxes(query, 0, 1), jnp.swapaxes(key, 0, 1), jnp.swapaxes(value, 0, 1)))
    return jnp.swapaxes(per_head, 0, 1)

def block(image, skips, words, weights, gains, step, high, wide, clip_count, long_count):
    w_skip, w_mod, w_qkv, w_out1, w_query2, w_text_kv, w_out2, w_fc1, w_fc2 = weights
    gain_skip, gain_attn, gain_cross, gain_mlp, gain_query, gain_key = gains
    rows = image.shape[0]
    width = image.shape[1]
    place = jnp.arange(rows, dtype=jnp.int32)
    live_mask = place < high * wide
    base = low_back(matmul(jnp.concatenate([image, skips], 1), w_skip))
    stream = norm_rows(base, gain_skip)
    shift = matmul(low(jax.nn.silu(time_embed(step, width)))[None, :], w_mod)
    pre_attn = low(norm_rows(stream, gain_attn) + shift)
    projected = low_back(matmul(pre_attn, w_qkv.reshape(width, 3 * width))).reshape(rows, 3, H, HD)
    cosine, sine = rope_tables(place, wide, HD)
    query = low_back(low(rotate(norm_rows(projected[:, 0], gain_query), cosine, sine)))
    key = low_back(low(rotate(norm_rows(projected[:, 1], gain_key), cosine, sine)))
    value = low_back(low(projected[:, 2]))
    attended = low_back(low(attention(query, key, value, live_mask))).reshape(rows, width)
    stream1 = stream + low_back(matmul(attended, w_out1))
    pre_cross = low(norm_rows(stream1, gain_cross))
    query2 = low_back(low(matmul(pre_cross, w_query2))).reshape(rows, H, HD)
    text_kv = low_back(low(matmul(words, w_text_kv.reshape(words.shape[1], 2 * width))))
    text_slots = words.shape[0]
    text_place = jnp.arange(text_slots, dtype=jnp.int32)
    text_live = (text_place < clip_count) | (text_place >= CLIP_LEN) & (text_place < CLIP_LEN + long_count)
    key2 = text_kv[:, :width].reshape(text_slots, H, HD)
    value2 = text_kv[:, width:].reshape(text_slots, H, HD)
    crossed = low_back(low(attention(query2, key2, value2, text_live))).reshape(rows, width)
    stream2 = stream1 + low_back(matmul(crossed, w_out2))
    pre_mlp = low(norm_rows(stream2, gain_mlp))
    hidden = low_back(matmul(pre_mlp, w_fc1))
    stream3 = stream2 + low_back(matmul(low(jax.nn.gelu(hidden, approximate=True)), w_fc2))
    return stream3 * live_mask.astype(jnp.float32)[:, None]

def reference(tokens, skip_tokens, text, timestep, grid, text_len, w_skip, w_mod, w_qkv, w_out1, w_query2, w_text_kv, w_out2, w_fc1, w_fc2, gain_skip, gain_attn, gain_cross, gain_mlp, gain_query, gain_key, cotangent):
    images = MB * N_DP
    weights = tuple((weight.astype(jnp.float32) for weight in (w_skip, w_mod, w_qkv, w_out1, w_query2, w_text_kv, w_out2, w_fc1, w_fc2)))
    gains = tuple((gain.astype(jnp.float32) for gain in (gain_skip, gain_attn, gain_cross, gain_mlp, gain_query, gain_key)))
    items = (tokens.reshape(images, SEQ_CAP, -1), skip_tokens.reshape(images, SEQ_CAP, -1), text.reshape(images, TXT, -1), cotangent.reshape(images, SEQ_CAP, -1), timestep.reshape(images), grid.reshape(images, 2), text_len.reshape(images, 2))

    def one_image(totals, item):
        image, skips, words, incoming, step, shape, lengths = item

        def forward(image_f, skips_f, words_f, weights_f, gains_f):
            return block(image_f, skips_f, words_f, weights_f, gains_f, step, shape[0], shape[1], lengths[0], lengths[1])
        primal, pull = jax.vjp(forward, image.astype(jnp.float32), skips.astype(jnp.float32), words.astype(jnp.float32), weights, gains)
        d_image, d_skips, d_words, d_weights, d_gains = pull(incoming.astype(jnp.float32))
        totals = jax.tree.map(jnp.add, totals, (d_weights, d_gains))
        return (totals, (primal.astype(jnp.bfloat16), d_image, d_skips, d_words))
    start_totals = jax.tree.map(jnp.zeros_like, (weights, gains))
    (d_weights, d_gains), (results, d_images, d_skips, d_words) = lax.scan(one_image, start_totals, items)
    return (results.reshape(tokens.shape), d_images.reshape(tokens.shape), d_skips.reshape(tokens.shape), d_words.reshape(text.shape), d_weights[0], d_weights[1], d_weights[2], d_weights[3], d_weights[4], d_weights[5], d_weights[6], d_weights[7], d_weights[8], d_gains[0], d_gains[1], d_gains[2], d_gains[3], d_gains[4], d_gains[5])
```

```python
import math

import jax
import jax.numpy as jnp
from jax import lax
from jax.experimental import pallas as pl
from jax.experimental.pallas import tpu as pltpu
from jax.sharding import PartitionSpec as P

H = 16
HD = 88
HP = 96
CLIP_LEN = 77
ROWS = 256

EPS = 1e-06
MASKED = -1e30
LOG2E = 1.4426950408889634
BF = jnp.bfloat16
F32 = jnp.float32


def norm_parts(value):
    mean = jnp.mean(value, -1, keepdims=True)
    centre = value - mean
    scale = lax.rsqrt(jnp.mean(centre * centre, -1, keepdims=True) + EPS)
    return centre * scale, scale


def norm_rows(value, gain):
    return norm_parts(value)[0] * gain


def norm_back(value, gain, incoming):
    unit, scale = norm_parts(value)
    leading = incoming * gain
    inner = jnp.mean(leading * unit, -1, keepdims=True)
    back = scale * (leading - jnp.mean(leading, -1, keepdims=True) - unit * inner)
    return back, jnp.sum(incoming * unit, 0)


def time_embed(step, width):
    half = width // 2
    rate = jnp.exp(-math.log(10000.0) * jnp.arange(half, dtype=F32) / half)
    angle = step.astype(F32)[..., None] * rate
    return jnp.concatenate([jnp.cos(angle), jnp.sin(angle)], -1)


def mix(spec, left, right):
    return jnp.einsum(spec, left, right, preferred_element_type=F32)


def rope_tables(sequence, wide, local):
    place = jnp.arange(sequence, dtype=jnp.int32)[None, :, None]
    wide = wide[:, None, None]
    lane = jnp.arange(local * HP, dtype=jnp.int32)[None, None, :] % HP
    pair = lane // 2
    quarter = HD // 4
    upper = pair < quarter
    rank = jnp.where(upper, pair, pair - quarter).astype(F32)
    rate = jnp.exp(-math.log(10000.0) * rank / quarter)
    angle = jnp.where(upper, place // wide, place % wide).astype(F32) * rate
    sine = jnp.sin(angle)
    return jnp.cos(angle), jnp.where(lane % 2 == 0, -sine, sine)


def pad_heads(packed):
    rows, lanes = packed.shape
    groups = packed.reshape(rows, lanes // HD, HD)
    return jnp.pad(groups, ((0, 0), (0, 0), (0, HP - HD))).reshape(rows, -1)


def cut_heads(padded):
    rows, lanes = padded.shape
    return padded.reshape(rows, lanes // HP, HP)[:, :, :HD].reshape(rows, -1)


def head_masks(shape, local):
    lane = lax.broadcasted_iota(jnp.int32, shape, len(shape) - 1)
    inside = lane % HP < HD
    return [((lane // HP == h) & inside).astype(F32) for h in range(local)]


def head_mean(value, masks):
    total = None
    for mask in masks:
        term = (jnp.sum(value * mask, -1, keepdims=True) * (1.0 / HD)) * mask
        total = term if total is None else total + term
    return total


def head_unit(value, masks):
    centre = value - head_mean(value, masks)
    spread = None
    square = centre * centre
    for mask in masks:
        mean = jnp.sum(square * mask, -1, keepdims=True) * (1.0 / HD)
        term = lax.rsqrt(mean + EPS) * mask
        spread = term if spread is None else spread + term
    return centre * spread, spread


def turn_pairs(value):
    lanes = value.shape[-1]
    after = pltpu.roll(value, lanes - 1, 1)
    before = pltpu.roll(value, 1, 1)
    lane = lax.broadcasted_iota(jnp.int32, value.shape, 1)
    return jnp.where(lane % 2 == 0, after, before)


def dot_nt(left, right):
    return lax.dot_general(left, right, (((1,), (1,)), ((), ())), preferred_element_type=F32)


def dot_nn(left, right):
    return lax.dot_general(left, right, (((1,), (0,)), ((), ())), preferred_element_type=F32)


def dot_tn(left, right):
    return lax.dot_general(left, right, (((0,), (0,)), ((), ())), preferred_element_type=F32)


def self_forward(raw, counts, cosine, sine, gain_q, gain_k):
    parts, micros, slots, packed = raw.shape
    lanes = packed // 3
    local = lanes // HP
    sequence = parts * slots
    factor = HD ** (-0.5) * LOG2E

    def kernel(count_ref, raw_ref, cos_ref, sin_ref, gq_ref, gk_ref, out_ref, q_ref, k_ref, lse_ref):
        count = count_ref[pl.program_id(0)]
        blocks = (count + slots - 1) // slots
        out_ref[...] = jnp.zeros_like(out_ref)
        masks = head_masks((1, lanes), local)

        def prepare(part, carry):
            spot = pl.ds(pl.multiple_of(part * slots, slots), slots)
            cosine, sine = cos_ref[0, spot, :], sin_ref[0, spot, :]
            for index, gain_ref, dest in ((0, gq_ref, q_ref), (1, gk_ref, k_ref)):
                value = raw_ref[part, 0, :, index * lanes : (index + 1) * lanes].astype(F32)
                scaled = head_unit(value, masks)[0] * gain_ref[...]
                dest[0, spot, :] = (scaled * cosine + turn_pairs(scaled) * sine).astype(BF)
            return carry

        lax.fori_loop(0, parts, prepare, 0)
        column = lax.broadcasted_iota(jnp.int32, (1, sequence), 1)
        bias = jnp.where(column < count, 0.0, MASKED)
        for h in range(local):
            cut = slice(h * HP, (h + 1) * HP)
            keys = k_ref[0, :, cut]
            values = raw_ref[:, 0, :, 2 * lanes + h * HP : 2 * lanes + (h + 1) * HP].reshape(sequence, HP)

            def one_block(part, carry):
                spot = pl.ds(pl.multiple_of(part * slots, slots), slots)
                scores = dot_nt(q_ref[0, spot, cut], keys) + bias
                top = jnp.max(scores, -1, keepdims=True)
                raised = jnp.exp2((scores - top) * factor)
                total = jnp.sum(raised, -1, keepdims=True)
                result = dot_nn(raised.astype(BF), values) / total
                out_ref[part, 0, :, cut] = result.astype(BF)
                norm = jnp.broadcast_to(top * factor + jnp.log2(total), (slots, 128))
                lse_ref[0, h : h + 1, spot] = jnp.transpose(norm)[0:1, :]
                return carry

            lax.fori_loop(0, blocks, one_block, 0)

    whole = lambda m, c: (0, m, 0, 0)
    table = lambda m, c: (m, 0, 0)
    fixed = lambda m, c: (0, 0)
    return pl.pallas_call(
        kernel,
        name="self_forward",
        grid_spec=pltpu.PrefetchScalarGridSpec(
            num_scalar_prefetch=1,
            grid=(micros,),
            in_specs=[
                pl.BlockSpec((parts, 1, slots, packed), whole),
                pl.BlockSpec((1, sequence, lanes), table),
                pl.BlockSpec((1, sequence, lanes), table),
                pl.BlockSpec((1, lanes), fixed),
                pl.BlockSpec((1, lanes), fixed),
            ],
            out_specs=[
                pl.BlockSpec((parts, 1, slots, lanes), whole),
                pl.BlockSpec((1, sequence, lanes), table),
                pl.BlockSpec((1, sequence, lanes), table),
                pl.BlockSpec((1, local, sequence), table),
            ],
        ),
        out_shape=[
            jax.ShapeDtypeStruct((parts, micros, slots, lanes), BF),
            jax.ShapeDtypeStruct((micros, sequence, lanes), BF),
            jax.ShapeDtypeStruct((micros, sequence, lanes), BF),
            jax.ShapeDtypeStruct((micros, local, sequence), F32),
        ],
        compiler_params=pltpu.CompilerParams(vmem_limit_bytes=48 << 20),
        cost_estimate=pl.CostEstimate(
            flops=4 * micros * local * sequence * sequence * HP,
            bytes_accessed=2 * micros * sequence * lanes * 10,
            transcendentals=micros * local * sequence * sequence,
        ),
    )(counts, raw, cosine, sine, gain_q, gain_k)


def self_backward(raw, counts, cosine, sine, gain_q, gain_k, turned_q, turned_k, norms, incoming):
    parts, micros, slots, packed = raw.shape
    lanes = packed // 3
    local = lanes // HP
    sequence = parts * slots
    scale = HD ** (-0.5)
    factor = scale * LOG2E

    def kernel(
        count_ref,
        raw_ref,
        cos_ref,
        sin_ref,
        gq_ref,
        gk_ref,
        q_ref,
        k_ref,
        lse_ref,
        in_ref,
        out_ref,
        dgq_ref,
        dgk_ref,
        dq_s,
        dk_s,
        dv_s,
    ):
        count = count_ref[pl.program_id(0)]
        blocks = (count + slots - 1) // slots
        dq_s[...] = jnp.zeros_like(dq_s)
        dk_s[...] = jnp.zeros_like(dk_s)
        dv_s[...] = jnp.zeros_like(dv_s)
        row = lax.broadcasted_iota(jnp.int32, (sequence, 1), 0)
        bias = jnp.where(row < count, 0.0, MASKED)
        for h in range(local):
            cut = slice(h * HP, (h + 1) * HP)
            keys = k_ref[0, :, cut]
            values = raw_ref[:, 0, :, 2 * lanes + h * HP : 2 * lanes + (h + 1) * HP].reshape(sequence, HP)

            def one_block(part, carry):
                spot = pl.ds(pl.multiple_of(part * slots, slots), slots)
                rows = q_ref[0, spot, cut]
                grads = in_ref[part, 0, :, cut]
                norm = lse_ref[0, h : h + 1, spot]
                probs = jnp.exp2(dot_nt(keys, rows) * factor + bias - norm)
                d_probs = dot_nt(values, grads)
                inner = jnp.sum(probs * d_probs, 0, keepdims=True)
                d_scores = (probs * (d_probs - inner)).astype(BF)
                dv_s[:, cut] += dot_nn(probs.astype(BF), grads)
                dk_s[:, cut] += dot_nn(d_scores, rows)
                dq_s[spot, cut] = dot_tn(d_scores, keys)
                return carry

            lax.fori_loop(0, blocks, one_block, 0)
        masks = head_masks((1, lanes), local)

        def finish(part, carry):
            spot = pl.ds(pl.multiple_of(part * slots, slots), slots)
            cosine, sine = cos_ref[0, spot, :], sin_ref[0, spot, :]
            sums = []
            for index, gain_ref, source in ((0, gq_ref, dq_s), (1, gk_ref, dk_s)):
                grad = source[spot, :] * scale
                grad = grad * cosine - turn_pairs(grad) * sine
                value = raw_ref[part, 0, :, index * lanes : (index + 1) * lanes].astype(F32)
                unit, spread = head_unit(value, masks)
                leading = grad * gain_ref[...]
                back = leading - head_mean(leading, masks) - unit * head_mean(leading * unit, masks)
                out_ref[part, 0, :, index * lanes : (index + 1) * lanes] = (spread * back).astype(BF)
                sums.append(carry[index] + jnp.sum(grad * unit, 0, keepdims=True))
            out_ref[part, 0, :, 2 * lanes : 3 * lanes] = dv_s[spot, :].astype(BF)
            return tuple(sums)

        zero = jnp.zeros((1, lanes), F32)
        d_gains = lax.fori_loop(0, parts, finish, (zero, zero))
        dgq_ref[0] = d_gains[0]
        dgk_ref[0] = d_gains[1]

    whole = lambda m, c: (0, m, 0, 0)
    table = lambda m, c: (m, 0, 0)
    fixed = lambda m, c: (0, 0)
    return pl.pallas_call(
        kernel,
        name="self_backward",
        grid_spec=pltpu.PrefetchScalarGridSpec(
            num_scalar_prefetch=1,
            grid=(micros,),
            in_specs=[
                pl.BlockSpec((parts, 1, slots, packed), whole),
                pl.BlockSpec((1, sequence, lanes), table),
                pl.BlockSpec((1, sequence, lanes), table),
                pl.BlockSpec((1, lanes), fixed),
                pl.BlockSpec((1, lanes), fixed),
                pl.BlockSpec((1, sequence, lanes), table),
                pl.BlockSpec((1, sequence, lanes), table),
                pl.BlockSpec((1, local, sequence), table),
                pl.BlockSpec((parts, 1, slots, lanes), whole),
            ],
            out_specs=[
                pl.BlockSpec((parts, 1, slots, packed), whole),
                pl.BlockSpec((1, 1, lanes), table),
                pl.BlockSpec((1, 1, lanes), table),
            ],
            scratch_shapes=[pltpu.VMEM((sequence, lanes), F32) for index in range(3)],
        ),
        out_shape=[
            jax.ShapeDtypeStruct((parts, micros, slots, packed), BF),
            jax.ShapeDtypeStruct((micros, 1, lanes), F32),
            jax.ShapeDtypeStruct((micros, 1, lanes), F32),
        ],
        compiler_params=pltpu.CompilerParams(vmem_limit_bytes=48 << 20),
        cost_estimate=pl.CostEstimate(
            flops=10 * micros * local * sequence * sequence * HP,
            bytes_accessed=2 * micros * sequence * lanes * 14,
            transcendentals=micros * local * sequence * sequence,
        ),
    )(counts, raw, cosine, sine, gain_q, gain_k, turned_q, turned_k, norms, incoming)


def text_bias(lengths_ref, micro, words, axis):
    place = lax.broadcasted_iota(jnp.int32, (1, words) if axis else (words, 1), axis)
    live = (place < lengths_ref[micro, 0]) | (
        (place >= CLIP_LEN) & (place < CLIP_LEN + lengths_ref[micro, 1])
    )
    return jnp.where(live, 0.0, MASKED)


def cross_forward(query, text_kv, lengths):
    parts, micros, slots, lanes = query.shape
    words = text_kv.shape[2]
    local = lanes // HP
    factor = HD ** (-0.5) * LOG2E

    def kernel(len_ref, q_ref, kv_ref, out_ref):
        bias = text_bias(len_ref, pl.program_id(1), words, 1)
        for h in range(local):
            cut = slice(h * HP, (h + 1) * HP)
            scores = dot_nt(q_ref[0, 0, :, cut], kv_ref[0, 0, :, cut]) + bias
            top = jnp.max(scores, -1, keepdims=True)
            raised = jnp.exp2((scores - top) * factor)
            total = jnp.sum(raised, -1, keepdims=True)
            values = kv_ref[0, 0, :, lanes + h * HP : lanes + (h + 1) * HP]
            out_ref[0, 0, :, cut] = (dot_nn(raised.astype(BF), values) / total).astype(BF)

    spot = lambda p, m, c: (p, m, 0, 0)
    return pl.pallas_call(
        kernel,
        name="cross_forward",
        grid_spec=pltpu.PrefetchScalarGridSpec(
            num_scalar_prefetch=1,
            grid=(parts, micros),
            in_specs=[
                pl.BlockSpec((1, 1, slots, lanes), spot),
                pl.BlockSpec((1, 1, words, 2 * lanes), spot),
            ],
            out_specs=pl.BlockSpec((1, 1, slots, lanes), spot),
        ),
        out_shape=jax.ShapeDtypeStruct(query.shape, BF),
        compiler_params=pltpu.CompilerParams(vmem_limit_bytes=32 << 20),
        cost_estimate=pl.CostEstimate(
            flops=4 * parts * micros * slots * words * lanes,
            bytes_accessed=4 * parts * micros * (slots + words) * lanes,
            transcendentals=parts * micros * local * slots * words,
        ),
    )(lengths, query, text_kv)


def cross_backward(query, text_kv, lengths, incoming):
    parts, micros, slots, lanes = query.shape
    words = text_kv.shape[2]
    local = lanes // HP
    scale = HD ** (-0.5)
    factor = scale * LOG2E

    def kernel(len_ref, q_ref, kv_ref, in_ref, dq_ref, dkv_ref):
        bias = text_bias(len_ref, pl.program_id(1), words, 0)
        for h in range(local):
            cut = slice(h * HP, (h + 1) * HP)
            far = slice(lanes + h * HP, lanes + (h + 1) * HP)
            rows = q_ref[0, 0, :, cut]
            keys = kv_ref[0, 0, :, cut]
            grads = in_ref[0, 0, :, cut]
            scores = dot_nt(keys, rows) + bias
            top = jnp.max(scores, 0, keepdims=True)
            raised = jnp.exp2((scores - top) * factor)
            probs = raised * (1.0 / jnp.sum(raised, 0, keepdims=True))
            d_probs = dot_nt(kv_ref[0, 0, :, far], grads)
            inner = jnp.sum(probs * d_probs, 0, keepdims=True)
            d_scores = (probs * (d_probs - inner)).astype(BF)
            dkv_ref[0, 0, :, far] = dot_nn(probs.astype(BF), grads).astype(BF)
            dkv_ref[0, 0, :, cut] = (dot_nn(d_scores, rows) * scale).astype(BF)
            dq_ref[0, 0, :, cut] = (dot_tn(d_scores, keys) * scale).astype(BF)

    spot = lambda p, m, c: (p, m, 0, 0)
    return pl.pallas_call(
        kernel,
        name="cross_backward",
        grid_spec=pltpu.PrefetchScalarGridSpec(
            num_scalar_prefetch=1,
            grid=(parts, micros),
            in_specs=[
                pl.BlockSpec((1, 1, slots, lanes), spot),
                pl.BlockSpec((1, 1, words, 2 * lanes), spot),
                pl.BlockSpec((1, 1, slots, lanes), spot),
            ],
            out_specs=[
                pl.BlockSpec((1, 1, slots, lanes), spot),
                pl.BlockSpec((1, 1, words, 2 * lanes), spot),
            ],
        ),
        out_shape=[
            jax.ShapeDtypeStruct(query.shape, BF),
            jax.ShapeDtypeStruct(text_kv.shape, BF),
        ],
        compiler_params=pltpu.CompilerParams(vmem_limit_bytes=32 << 20),
        cost_estimate=pl.CostEstimate(
            flops=10 * parts * micros * slots * words * lanes,
            bytes_accessed=8 * parts * micros * (slots + words) * lanes,
            transcendentals=parts * micros * local * slots * words,
        ),
    )(lengths, query, text_kv, incoming)


class Cube:
    def __init__(self):
        self.size = lax.axis_size("dp")
        self.bits = self.size.bit_length() - 1
        self.rank = lax.axis_index("dp")

    def swap(self, value, bit):
        pairs = [(i, i ^ (1 << bit)) for i in range(self.size)]
        return lax.ppermute(value, "dp", pairs)

    def order(self, flip):
        outer = list(range(1, self.bits))
        return outer[::-1] if flip else outer

    def position(self):
        places = []
        for place in range(self.size):
            mask = 0
            for bit in range(self.bits):
                weight = self.bits - 1 if bit == 0 else bit - 1
                mask |= ((place >> weight) & 1) << bit
            places.append(mask)
        return places

    def owners(self):
        return self.rank ^ jnp.array(self.position(), jnp.int32)

    def gather(self, shard, flip):
        held = [(0, shard)]
        for bit in self.order(flip):
            held = held + [(mask | (1 << bit), self.swap(piece, bit)) for mask, piece in held]
        held = sorted(held, key=lambda item: self.position().index(item[0]))
        near = jnp.concatenate([piece for mask, piece in held], 1)
        return jnp.concatenate([near, self.swap(near, 0)], 1)

    def scatter(self, near, far, flip):
        held = (near + self.swap(far, 0).astype(F32)).astype(BF)
        parts, rows, lanes = held.shape
        outer = self.bits - 1
        held = held.reshape((parts,) + (2,) * outer + (rows >> outer, lanes))
        axes = list(range(outer, 0, -1))
        for bit in self.order(flip)[::-1]:
            axis = 1 + axes.index(bit)
            keep = lax.index_in_dim(held, 0, axis, keepdims=False)
            send = lax.index_in_dim(held, 1, axis, keepdims=False)
            held = (keep.astype(F32) + self.swap(send, bit).astype(F32)).astype(BF)
            axes.remove(bit)
        return held


def on_device(
    tokens,
    skip_tokens,
    text,
    timestep,
    grid,
    text_len,
    w_skip,
    w_mod,
    w_qkv,
    w_out1,
    w_query2,
    w_text_kv,
    w_out2,
    w_fc1,
    w_fc2,
    gain_skip,
    gain_attn,
    gain_cross,
    gain_mlp,
    gain_query,
    gain_key,
    cotangent,
):
    micros, slots, width = tokens.shape
    parts = lax.axis_size("sp")
    zone = lax.axis_index("sp")
    cube = Cube()
    ranks = cube.size
    owners = cube.owners()
    rows = micros * slots
    sequence = slots * parts
    local = H // parts
    lanes = local * HP
    text_slots = text.shape[1]
    words = text_slots * parts
    features = text.shape[2]
    strip = width // ranks

    def spread(shard):
        return lax.all_gather(shard, "sp", axis=0, tiled=False)

    def weight(shard, flip):
        return cube.gather(spread(shard), flip)

    half = w_skip.shape[0]
    skip_w = weight(w_skip.T, 0)
    qkv_w = weight(pad_heads(w_qkv.reshape(strip, -1)), 1)
    out1_w = weight(pad_heads(w_out1.T), 0)
    query2_w = weight(pad_heads(w_query2), 1)
    text_w = weight(pad_heads(w_text_kv.reshape(w_text_kv.shape[0], -1)), 0)
    out2_w = weight(pad_heads(w_out2.T), 1)
    fc1_w = weight(w_fc1, 0)
    fc2_w = weight(w_fc2.T, 1)

    def own_order(vector):
        return vector.reshape(ranks, -1)[owners].reshape(-1)

    def shuffle(count):
        block = count // ranks
        place = jnp.arange(count, dtype=jnp.int32)
        source = owners[place // block] * block + place % block
        return (place[:, None] == source[None, :]).astype(BF)

    turn = shuffle(width)
    text_turn = shuffle(features)
    g_skip, g_attn, g_cross, g_mlp = (
        own_order(gain) for gain in (gain_skip, gain_attn, gain_cross, gain_mlp)
    )

    wide = grid[:, 0, 1]
    counts = grid[:, 0, 0] * wide
    lengths = text_len[:, 0, :]
    place = zone * slots + jnp.arange(slots, dtype=jnp.int32)
    live = (place[None, :] < counts[:, None]).astype(F32).reshape(rows, 1)
    cosine, sine = rope_tables(sequence, wide, local)
    gain_q = pad_heads(jnp.tile(gain_query, local)[None, :])
    gain_k = pad_heads(jnp.tile(gain_key, local)[None, :])

    steps = lax.all_gather(timestep[:, 0], "dp", axis=0, tiled=False)
    time_act = jax.nn.silu(time_embed(steps, width)).astype(BF).reshape(ranks * micros, parts, -1)
    time_part = lax.dynamic_index_in_dim(time_act, zone, 1, keepdims=False)
    shift_part = jnp.dot(time_part, w_mod, preferred_element_type=F32)
    shift_own = lax.all_to_all(
        shift_part.reshape(ranks, micros, strip), "dp", split_axis=0, concat_axis=0, tiled=True
    )
    shift_own = lax.psum(shift_own, "sp")
    shift = jnp.transpose(shift_own[owners], (1, 0, 2)).reshape(micros, width)

    text_own = jnp.dot(text.reshape(-1, features), text_turn, preferred_element_type=F32).astype(BF)
    text_all = lax.all_gather(text_own.reshape(micros, text_slots, features), "sp", axis=1, tiled=True)
    text_all = text_all.reshape(micros * words, features)

    joined = jnp.stack([tokens, skip_tokens]).reshape(2, rows, parts // 2, half)
    joined = jnp.transpose(joined, (0, 2, 1, 3)).reshape(parts, rows, half)
    base = mix("pmk,pnk->mn", joined, skip_w)
    stream = norm_rows(base, g_skip)
    pre_attn = norm_rows(stream, g_attn).reshape(micros, slots, width) + shift[:, None, :]
    pre_attn = pre_attn.reshape(rows, width).astype(BF)
    projected = mix("mk,pkn->pmn", pre_attn, qkv_w).astype(BF)

    def exchange(value):
        return lax.all_to_all(value, "sp", split_axis=0, concat_axis=0, tiled=True)

    raw = exchange(projected.reshape(parts, micros, slots, 3 * lanes))
    attended, turned_q, turned_k, norms = self_forward(raw, counts, cosine, sine, gain_q, gain_k)
    attended = exchange(attended).reshape(parts, rows, lanes)
    stream1 = stream + mix("pmk,pnk->mn", attended, out1_w)
    pre_cross = norm_rows(stream1, g_cross).astype(BF)
    query2 = mix("mk,pkn->pmn", pre_cross, query2_w).astype(BF)
    query2 = query2.reshape(parts, micros, slots, lanes)
    text_kv = mix("mk,pkn->pmn", text_all, text_w).astype(BF)
    text_kv = text_kv.reshape(parts, micros, words, 2 * lanes)
    crossed = cross_forward(query2, text_kv, lengths).reshape(parts, rows, lanes)
    stream2 = stream1 + mix("pmk,pnk->mn", crossed, out2_w)
    pre_mlp = norm_rows(stream2, g_mlp).astype(BF)
    hidden = mix("mk,pkn->pmn", pre_mlp, fc1_w)
    activ = jax.nn.gelu(hidden, approximate=True).astype(BF)
    stream3 = stream2 + mix("pmk,pnk->mn", activ, fc2_w)
    result = jnp.dot((stream3 * live).astype(BF), turn.T, preferred_element_type=F32).astype(BF)

    def term(left, right, flip):
        cut = left.shape[1] // 2
        near = mix("md,pmn->pdn", left[:, :cut], right)
        far = mix("md,pmn->pdn", left[:, cut:], right).astype(BF)
        held = cube.scatter(near, far, flip)
        return lax.psum_scatter(held, "sp", scatter_dimension=0, tiled=False).astype(F32)

    grad3 = jnp.dot(cotangent.reshape(rows, width), turn, preferred_element_type=F32) * live
    d_mlp = grad3.astype(BF)
    term_fc2 = term(d_mlp, activ, 1)
    d_activ = mix("mn,pnk->pmk", d_mlp, fc2_w)
    unused, gelu_pull = jax.vjp(lambda value: jax.nn.gelu(value, approximate=True), hidden)
    d_hidden = gelu_pull(d_activ)[0].astype(BF)
    term_fc1 = term(pre_mlp, d_hidden, 0)
    d_stream2, d_gain_mlp = norm_back(stream2, g_mlp, mix("pmn,pkn->mk", d_hidden, fc1_w))
    grad2 = grad3 + d_stream2
    d_cross = grad2.astype(BF)
    term_out2 = term(d_cross, crossed, 1)
    d_crossed = mix("mn,pnk->pmk", d_cross, out2_w).astype(BF)
    d_query2, d_text_kv = cross_backward(
        query2, text_kv, lengths, d_crossed.reshape(parts, micros, slots, lanes)
    )
    d_query2 = d_query2.reshape(parts, rows, lanes)
    d_text_kv = d_text_kv.reshape(parts, micros * words, 2 * lanes)
    term_text = term(text_all, d_text_kv, 0)
    d_words = mix("pmn,pkn->mk", d_text_kv, text_w).astype(BF)
    d_words = lax.psum_scatter(
        d_words.reshape(micros, words, features), "sp", scatter_dimension=1, tiled=True
    )
    d_words = jnp.dot(d_words.reshape(-1, features), text_turn.T, preferred_element_type=F32)
    term_query2 = term(pre_cross, d_query2, 1)
    d_stream1, d_gain_cross = norm_back(stream1, g_cross, mix("pmn,pkn->mk", d_query2, query2_w))
    grad1 = grad2 + d_stream1
    d_attn = grad1.astype(BF)
    term_out1 = term(d_attn, attended, 0)
    d_attended = mix("mn,pnk->pmk", d_attn, out1_w).astype(BF)
    d_heads = exchange(d_attended.reshape(parts, micros, slots, lanes))
    d_raw, d_gain_q, d_gain_k = self_backward(
        raw, counts, cosine, sine, gain_q, gain_k, turned_q, turned_k, norms, d_heads
    )
    d_projected = exchange(d_raw).reshape(parts, rows, 3 * lanes)
    term_qkv = term(pre_attn, d_projected, 1)
    d_pre = mix("pmn,pkn->mk", d_projected, qkv_w)
    d_shift = jnp.sum(d_pre.reshape(micros, slots, width), 1)
    d_stream0, d_gain_attn = norm_back(stream, g_attn, d_pre)
    d_base, d_gain_skip = norm_back(base, g_skip, grad1 + d_stream0)
    d_base = d_base.astype(BF)
    term_skip = term(d_base, joined, 0)
    d_joined = mix("mn,pnk->pmk", d_base, skip_w).reshape(2, parts // 2, rows, half)
    d_joined = jnp.transpose(d_joined, (0, 2, 1, 3)).reshape(2, micros, slots, width)

    back = jnp.argsort(owners)
    d_shift = jnp.transpose(d_shift.reshape(micros, ranks, strip), (1, 0, 2))[back]
    d_shift = lax.all_to_all(d_shift, "dp", split_axis=0, concat_axis=0, tiled=True)
    d_shift = lax.psum(d_shift, "sp").reshape(ranks * micros, strip)
    term_mod = lax.dot_general(
        time_part.astype(F32), d_shift, (((0,), (0,)), ((), ())), precision=lax.Precision.HIGHEST
    )

    gains = jnp.stack([d_gain_skip, d_gain_attn, d_gain_cross, d_gain_mlp])
    gains = gains.reshape(4, ranks, strip)[:, back].reshape(4, width)
    heads = jnp.stack([jnp.sum(d_gain_q, (0, 1)), jnp.sum(d_gain_k, (0, 1))])
    heads = jnp.sum(heads.reshape(2, local, HP)[:, :, :HD], 1)
    packed = jnp.concatenate([gains.reshape(-1), heads.reshape(-1)])
    packed = lax.psum(packed, ("dp", "sp"))
    gains = packed[: 4 * width].reshape(4, ranks * parts, -1)
    gains = lax.dynamic_index_in_dim(gains, cube.rank * parts + zone, 1, keepdims=False)
    heads = packed[4 * width :].reshape(2, HD)

    def whole(term, groups):
        return cut_heads(term).reshape(term.shape[0], groups, -1)

    return (
        result.reshape(tokens.shape),
        d_joined[0],
        d_joined[1],
        d_words.reshape(text.shape),
        term_skip.T,
        term_mod,
        whole(term_qkv, 3),
        cut_heads(term_out1).T,
        cut_heads(term_query2),
        whole(term_text, 2),
        cut_heads(term_out2).T,
        term_fc1,
        term_fc2.T,
        gains[0],
        gains[1],
        gains[2],
        gains[3],
        heads[0],
        heads[1],
    )


def solution(mesh):
    rows = P(None, ("dp", "sp"), None)
    column = P("sp", "dp")
    row = P("dp", "sp")
    grouped = P("dp", None, "sp")
    in_specs = (
        (rows, rows, rows, P(None, "dp"), P(None, "dp", None), P(None, "dp", None))
        + (column, column, grouped, column, row, grouped, column, row, column)
        + (P(),) * 6
        + (rows,)
    )
    out_specs = (
        (rows, rows, rows, rows)
        + (column, column, grouped, column, row, grouped, column, row, column)
        + (P(("dp", "sp")),) * 4
        + (P(), P())
    )
    return jax.shard_map(
        on_device, mesh=mesh, in_specs=in_specs, out_specs=out_specs, check_vma=False
    )
```

```python
import math

import jax
import jax.numpy as jnp
from jax import lax
from jax.experimental import pallas as pl
from jax.experimental.pallas import tpu as pltpu
from jax.sharding import PartitionSpec as P

H = 16
HD = 88
HP = 96
CLIP_LEN = 77
ROWS = 256

EPS = 1e-06
MASKED = -1e30
LOG2E = 1.4426950408889634
BF = jnp.bfloat16
F32 = jnp.float32


def norm_parts(value):
    mean = jnp.mean(value, -1, keepdims=True)
    centre = value - mean
    scale = lax.rsqrt(jnp.mean(centre * centre, -1, keepdims=True) + EPS)
    return centre * scale, scale


def norm_rows(value, gain):
    return norm_parts(value)[0] * gain


def norm_back(value, gain, incoming):
    unit, scale = norm_parts(value)
    leading = incoming * gain
    inner = jnp.mean(leading * unit, -1, keepdims=True)
    back = scale * (leading - jnp.mean(leading, -1, keepdims=True) - unit * inner)
    return back, jnp.sum(incoming * unit, 0)


def time_embed(step, width):
    half = width // 2
    rate = jnp.exp(-math.log(10000.0) * jnp.arange(half, dtype=F32) / half)
    angle = step.astype(F32)[..., None] * rate
    return jnp.concatenate([jnp.cos(angle), jnp.sin(angle)], -1)


def mix(spec, left, right):
    return jnp.einsum(spec, left, right, preferred_element_type=F32)


def rope_tables(sequence, wide, local):
    place = jnp.arange(sequence, dtype=jnp.int32)[None, :, None]
    wide = wide[:, None, None]
    lane = jnp.arange(local * HP, dtype=jnp.int32)[None, None, :] % HP
    pair = lane // 2
    quarter = HD // 4
    upper = pair < quarter
    rank = jnp.where(upper, pair, pair - quarter).astype(F32)
    rate = jnp.exp(-math.log(10000.0) * rank / quarter)
    angle = jnp.where(upper, place // wide, place % wide).astype(F32) * rate
    sine = jnp.sin(angle)
    return jnp.cos(angle), jnp.where(lane % 2 == 0, -sine, sine)


def pad_heads(packed):
    rows, lanes = packed.shape
    groups = packed.reshape(rows, lanes // HD, HD)
    return jnp.pad(groups, ((0, 0), (0, 0), (0, HP - HD))).reshape(rows, -1)


def cut_heads(padded):
    rows, lanes = padded.shape
    return padded.reshape(rows, lanes // HP, HP)[:, :, :HD].reshape(rows, -1)


def head_masks(shape, local):
    lane = lax.broadcasted_iota(jnp.int32, shape, len(shape) - 1)
    inside = lane % HP < HD
    return [((lane // HP == h) & inside).astype(F32) for h in range(local)]


def head_mean(value, masks):
    total = None
    for mask in masks:
        term = (jnp.sum(value * mask, -1, keepdims=True) * (1.0 / HD)) * mask
        total = term if total is None else total + term
    return total


def head_unit(value, masks):
    centre = value - head_mean(value, masks)
    spread = None
    square = centre * centre
    for mask in masks:
        mean = jnp.sum(square * mask, -1, keepdims=True) * (1.0 / HD)
        term = lax.rsqrt(mean + EPS) * mask
        spread = term if spread is None else spread + term
    return centre * spread, spread


def turn_pairs(value):
    lanes = value.shape[-1]
    after = pltpu.roll(value, lanes - 1, 1)
    before = pltpu.roll(value, 1, 1)
    lane = lax.broadcasted_iota(jnp.int32, value.shape, 1)
    return jnp.where(lane % 2 == 0, after, before)


def dot_nt(left, right):
    return lax.dot_general(left, right, (((1,), (1,)), ((), ())), preferred_element_type=F32)


def dot_nn(left, right):
    return lax.dot_general(left, right, (((1,), (0,)), ((), ())), preferred_element_type=F32)


def dot_tn(left, right):
    return lax.dot_general(left, right, (((0,), (0,)), ((), ())), preferred_element_type=F32)


def self_forward(raw, counts, cosine, sine, gain_q, gain_k):
    parts, micros, slots, packed = raw.shape
    lanes = packed // 3
    local = lanes // HP
    sequence = parts * slots
    factor = HD ** (-0.5) * LOG2E

    def kernel(count_ref, raw_ref, cos_ref, sin_ref, gq_ref, gk_ref, out_ref, q_ref, k_ref, lse_ref):
        count = count_ref[pl.program_id(0)]
        blocks = (count + slots - 1) // slots
        out_ref[...] = jnp.zeros_like(out_ref)
        masks = head_masks((1, lanes), local)

        def prepare(part, carry):
            spot = pl.ds(pl.multiple_of(part * slots, slots), slots)
            cosine, sine = cos_ref[0, spot, :], sin_ref[0, spot, :]
            for index, gain_ref, dest in ((0, gq_ref, q_ref), (1, gk_ref, k_ref)):
                value = raw_ref[part, 0, :, index * lanes : (index + 1) * lanes].astype(F32)
                scaled = head_unit(value, masks)[0] * gain_ref[...]
                dest[0, spot, :] = (scaled * cosine + turn_pairs(scaled) * sine).astype(BF)
            return carry

        lax.fori_loop(0, parts, prepare, 0)
        column = lax.broadcasted_iota(jnp.int32, (1, sequence), 1)
        bias = jnp.where(column < count, 0.0, MASKED)
        for h in range(local):
            cut = slice(h * HP, (h + 1) * HP)
            keys = k_ref[0, :, cut]
            values = raw_ref[:, 0, :, 2 * lanes + h * HP : 2 * lanes + (h + 1) * HP].reshape(sequence, HP)

            def one_block(part, carry):
                spot = pl.ds(pl.multiple_of(part * slots, slots), slots)
                scores = dot_nt(q_ref[0, spot, cut], keys) + bias
                top = jnp.max(scores, -1, keepdims=True)
                raised = jnp.exp2((scores - top) * factor)
                total = jnp.sum(raised, -1, keepdims=True)
                result = dot_nn(raised.astype(BF), values) / total
                out_ref[part, 0, :, cut] = result.astype(BF)
                norm = jnp.broadcast_to(top * factor + jnp.log2(total), (slots, 128))
                lse_ref[0, h : h + 1, spot] = jnp.transpose(norm)[0:1, :]
                return carry

            lax.fori_loop(0, blocks, one_block, 0)

    whole = lambda m, c: (0, m, 0, 0)
    table = lambda m, c: (m, 0, 0)
    fixed = lambda m, c: (0, 0)
    return pl.pallas_call(
        kernel,
        name="self_forward",
        grid_spec=pltpu.PrefetchScalarGridSpec(
            num_scalar_prefetch=1,
            grid=(micros,),
            in_specs=[
                pl.BlockSpec((parts, 1, slots, packed), whole),
                pl.BlockSpec((1, sequence, lanes), table),
                pl.BlockSpec((1, sequence, lanes), table),
                pl.BlockSpec((1, lanes), fixed),
                pl.BlockSpec((1, lanes), fixed),
            ],
            out_specs=[
                pl.BlockSpec((parts, 1, slots, lanes), whole),
                pl.BlockSpec((1, sequence, lanes), table),
                pl.BlockSpec((1, sequence, lanes), table),
                pl.BlockSpec((1, local, sequence), table),
            ],
        ),
        out_shape=[
            jax.ShapeDtypeStruct((parts, micros, slots, lanes), BF),
            jax.ShapeDtypeStruct((micros, sequence, lanes), BF),
            jax.ShapeDtypeStruct((micros, sequence, lanes), BF),
            jax.ShapeDtypeStruct((micros, local, sequence), F32),
        ],
        compiler_params=pltpu.CompilerParams(vmem_limit_bytes=48 << 20),
        cost_estimate=pl.CostEstimate(
            flops=4 * micros * local * sequence * sequence * HP,
            bytes_accessed=2 * micros * sequence * lanes * 10,
            transcendentals=micros * local * sequence * sequence,
        ),
    )(counts, raw, cosine, sine, gain_q, gain_k)


def self_backward(raw, counts, cosine, sine, gain_q, gain_k, turned_q, turned_k, norms, incoming):
    parts, micros, slots, packed = raw.shape
    lanes = packed // 3
    local = lanes // HP
    sequence = parts * slots
    scale = HD ** (-0.5)
    factor = scale * LOG2E

    def kernel(
        count_ref,
        raw_ref,
        cos_ref,
        sin_ref,
        gq_ref,
        gk_ref,
        q_ref,
        k_ref,
        lse_ref,
        in_ref,
        out_ref,
        dgq_ref,
        dgk_ref,
        dq_s,
        dk_s,
        dv_s,
    ):
        count = count_ref[pl.program_id(0)]
        blocks = (count + slots - 1) // slots
        dq_s[...] = jnp.zeros_like(dq_s)
        dk_s[...] = jnp.zeros_like(dk_s)
        dv_s[...] = jnp.zeros_like(dv_s)
        row = lax.broadcasted_iota(jnp.int32, (sequence, 1), 0)
        bias = jnp.where(row < count, 0.0, MASKED)
        for h in range(local):
            cut = slice(h * HP, (h + 1) * HP)
            keys = k_ref[0, :, cut]
            values = raw_ref[:, 0, :, 2 * lanes + h * HP : 2 * lanes + (h + 1) * HP].reshape(sequence, HP)

            def one_block(part, carry):
                spot = pl.ds(pl.multiple_of(part * slots, slots), slots)
                rows = q_ref[0, spot, cut]
                grads = in_ref[part, 0, :, cut]
                norm = lse_ref[0, h : h + 1, spot]
                probs = jnp.exp2(dot_nt(keys, rows) * factor + bias - norm)
                d_probs = dot_nt(values, grads)
                inner = jnp.sum(probs * d_probs, 0, keepdims=True)
                d_scores = (probs * (d_probs - inner)).astype(BF)
                dv_s[:, cut] += dot_nn(probs.astype(BF), grads)
                dk_s[:, cut] += dot_nn(d_scores, rows)
                dq_s[spot, cut] = dot_tn(d_scores, keys)
                return carry

            lax.fori_loop(0, blocks, one_block, 0)
        masks = head_masks((1, lanes), local)

        def finish(part, carry):
            spot = pl.ds(pl.multiple_of(part * slots, slots), slots)
            cosine, sine = cos_ref[0, spot, :], sin_ref[0, spot, :]
            sums = []
            for index, gain_ref, source in ((0, gq_ref, dq_s), (1, gk_ref, dk_s)):
                grad = source[spot, :] * scale
                grad = grad * cosine - turn_pairs(grad) * sine
                value = raw_ref[part, 0, :, index * lanes : (index + 1) * lanes].astype(F32)
                unit, spread = head_unit(value, masks)
                leading = grad * gain_ref[...]
                back = leading - head_mean(leading, masks) - unit * head_mean(leading * unit, masks)
                out_ref[part, 0, :, index * lanes : (index + 1) * lanes] = (spread * back).astype(BF)
                sums.append(carry[index] + jnp.sum(grad * unit, 0, keepdims=True))
            out_ref[part, 0, :, 2 * lanes : 3 * lanes] = dv_s[spot, :].astype(BF)
            return tuple(sums)

        zero = jnp.zeros((1, lanes), F32)
        d_gains = lax.fori_loop(0, parts, finish, (zero, zero))
        dgq_ref[0] = d_gains[0]
        dgk_ref[0] = d_gains[1]

    whole = lambda m, c: (0, m, 0, 0)
    table = lambda m, c: (m, 0, 0)
    fixed = lambda m, c: (0, 0)
    return pl.pallas_call(
        kernel,
        name="self_backward",
        grid_spec=pltpu.PrefetchScalarGridSpec(
            num_scalar_prefetch=1,
            grid=(micros,),
            in_specs=[
                pl.BlockSpec((parts, 1, slots, packed), whole),
                pl.BlockSpec((1, sequence, lanes), table),
                pl.BlockSpec((1, sequence, lanes), table),
                pl.BlockSpec((1, lanes), fixed),
                pl.BlockSpec((1, lanes), fixed),
                pl.BlockSpec((1, sequence, lanes), table),
                pl.BlockSpec((1, sequence, lanes), table),
                pl.BlockSpec((1, local, sequence), table),
                pl.BlockSpec((parts, 1, slots, lanes), whole),
            ],
            out_specs=[
                pl.BlockSpec((parts, 1, slots, packed), whole),
                pl.BlockSpec((1, 1, lanes), table),
                pl.BlockSpec((1, 1, lanes), table),
            ],
            scratch_shapes=[pltpu.VMEM((sequence, lanes), F32) for index in range(3)],
        ),
        out_shape=[
            jax.ShapeDtypeStruct((parts, micros, slots, packed), BF),
            jax.ShapeDtypeStruct((micros, 1, lanes), F32),
            jax.ShapeDtypeStruct((micros, 1, lanes), F32),
        ],
        compiler_params=pltpu.CompilerParams(vmem_limit_bytes=48 << 20),
        cost_estimate=pl.CostEstimate(
            flops=10 * micros * local * sequence * sequence * HP,
            bytes_accessed=2 * micros * sequence * lanes * 14,
            transcendentals=micros * local * sequence * sequence,
        ),
    )(counts, raw, cosine, sine, gain_q, gain_k, turned_q, turned_k, norms, incoming)


def text_bias(lengths_ref, micro, words, axis):
    place = lax.broadcasted_iota(jnp.int32, (1, words) if axis else (words, 1), axis)
    live = (place < lengths_ref[micro, 0]) | (
        (place >= CLIP_LEN) & (place < CLIP_LEN + lengths_ref[micro, 1])
    )
    return jnp.where(live, 0.0, MASKED)


def cross_forward(query, text_kv, lengths):
    parts, micros, slots, lanes = query.shape
    words = text_kv.shape[2]
    local = lanes // HP
    factor = HD ** (-0.5) * LOG2E

    def kernel(len_ref, q_ref, kv_ref, out_ref):
        bias = text_bias(len_ref, pl.program_id(1), words, 1)
        for h in range(local):
            cut = slice(h * HP, (h + 1) * HP)
            scores = dot_nt(q_ref[0, 0, :, cut], kv_ref[0, 0, :, cut]) + bias
            top = jnp.max(scores, -1, keepdims=True)
            raised = jnp.exp2((scores - top) * factor)
            total = jnp.sum(raised, -1, keepdims=True)
            values = kv_ref[0, 0, :, lanes + h * HP : lanes + (h + 1) * HP]
            out_ref[0, 0, :, cut] = (dot_nn(raised.astype(BF), values) / total).astype(BF)

    spot = lambda p, m, c: (p, m, 0, 0)
    return pl.pallas_call(
        kernel,
        name="cross_forward",
        grid_spec=pltpu.PrefetchScalarGridSpec(
            num_scalar_prefetch=1,
            grid=(parts, micros),
            in_specs=[
                pl.BlockSpec((1, 1, slots, lanes), spot),
                pl.BlockSpec((1, 1, words, 2 * lanes), spot),
            ],
            out_specs=pl.BlockSpec((1, 1, slots, lanes), spot),
        ),
        out_shape=jax.ShapeDtypeStruct(query.shape, BF),
        compiler_params=pltpu.CompilerParams(vmem_limit_bytes=32 << 20),
        cost_estimate=pl.CostEstimate(
            flops=4 * parts * micros * slots * words * lanes,
            bytes_accessed=4 * parts * micros * (slots + words) * lanes,
            transcendentals=parts * micros * local * slots * words,
        ),
    )(lengths, query, text_kv)


def cross_backward(query, text_kv, lengths, incoming):
    parts, micros, slots, lanes = query.shape
    words = text_kv.shape[2]
    local = lanes // HP
    scale = HD ** (-0.5)
    factor = scale * LOG2E

    def kernel(len_ref, q_ref, kv_ref, in_ref, dq_ref, dkv_ref):
        bias = text_bias(len_ref, pl.program_id(1), words, 0)
        for h in range(local):
            cut = slice(h * HP, (h + 1) * HP)
            far = slice(lanes + h * HP, lanes + (h + 1) * HP)
            rows = q_ref[0, 0, :, cut]
            keys = kv_ref[0, 0, :, cut]
            grads = in_ref[0, 0, :, cut]
            scores = dot_nt(keys, rows) + bias
            top = jnp.max(scores, 0, keepdims=True)
            raised = jnp.exp2((scores - top) * factor)
            probs = raised * (1.0 / jnp.sum(raised, 0, keepdims=True))
            d_probs = dot_nt(kv_ref[0, 0, :, far], grads)
            inner = jnp.sum(probs * d_probs, 0, keepdims=True)
            d_scores = (probs * (d_probs - inner)).astype(BF)
            dkv_ref[0, 0, :, far] = dot_nn(probs.astype(BF), grads).astype(BF)
            dkv_ref[0, 0, :, cut] = (dot_nn(d_scores, rows) * scale).astype(BF)
            dq_ref[0, 0, :, cut] = (dot_tn(d_scores, keys) * scale).astype(BF)

    spot = lambda p, m, c: (p, m, 0, 0)
    return pl.pallas_call(
        kernel,
        name="cross_backward",
        grid_spec=pltpu.PrefetchScalarGridSpec(
            num_scalar_prefetch=1,
            grid=(parts, micros),
            in_specs=[
                pl.BlockSpec((1, 1, slots, lanes), spot),
                pl.BlockSpec((1, 1, words, 2 * lanes), spot),
                pl.BlockSpec((1, 1, slots, lanes), spot),
            ],
            out_specs=[
                pl.BlockSpec((1, 1, slots, lanes), spot),
                pl.BlockSpec((1, 1, words, 2 * lanes), spot),
            ],
        ),
        out_shape=[
            jax.ShapeDtypeStruct(query.shape, BF),
            jax.ShapeDtypeStruct(text_kv.shape, BF),
        ],
        compiler_params=pltpu.CompilerParams(vmem_limit_bytes=32 << 20),
        cost_estimate=pl.CostEstimate(
            flops=10 * parts * micros * slots * words * lanes,
            bytes_accessed=8 * parts * micros * (slots + words) * lanes,
            transcendentals=parts * micros * local * slots * words,
        ),
    )(lengths, query, text_kv, incoming)


def mlp_forward(rows_in, near1, far1, near2, far2):
    rows, width = rows_in.shape
    parts, half, ff = near1.shape
    step = 512 if ff % 512 == 0 else ff
    steps = ff // step

    def kernel(x_ref, n1_ref, f1_ref, n2_ref, f2_ref, hid_ref, act_ref, out_ref, xa, xb, ya, yb):
        first = (pl.program_id(0) == 0) & (pl.program_id(1) == 0)
        last = (pl.program_id(0) == parts - 1) & (pl.program_id(1) == steps - 1)

        @pl.when(first)
        def _():
            xa[...] = x_ref[:, :half]
            xb[...] = x_ref[:, half:]
            ya[...] = jnp.zeros_like(ya)
            yb[...] = jnp.zeros_like(yb)

        hidden = dot_nn(xa[...], n1_ref[0]) + dot_nn(xb[...], f1_ref[0])
        hid_ref[0] = hidden
        activ = jax.nn.gelu(hidden, approximate=True).astype(BF)
        act_ref[0] = activ
        ya[...] += dot_nt(activ, n2_ref[0])
        yb[...] += dot_nt(activ, f2_ref[0])

        @pl.when(last)
        def _():
            out_ref[:, :half] = ya[...]
            out_ref[:, half:] = yb[...]

    weight = pl.BlockSpec((1, half, step), lambda p, n: (p, 0, n))
    unit = pl.BlockSpec((1, rows, step), lambda p, n: (p, 0, n))
    whole = pl.BlockSpec((rows, width), lambda p, n: (0, 0))
    return pl.pallas_call(
        kernel,
        name="mlp_forward",
        grid=(parts, steps),
        in_specs=[whole, weight, weight, weight, weight],
        out_specs=[unit, unit, whole],
        out_shape=[
            jax.ShapeDtypeStruct((parts, rows, ff), F32),
            jax.ShapeDtypeStruct((parts, rows, ff), BF),
            jax.ShapeDtypeStruct((rows, width), F32),
        ],
        scratch_shapes=[
            pltpu.VMEM((rows, half), BF),
            pltpu.VMEM((rows, half), BF),
            pltpu.VMEM((rows, half), F32),
            pltpu.VMEM((rows, half), F32),
        ],
        compiler_params=pltpu.CompilerParams(vmem_limit_bytes=48 << 20),
        cost_estimate=pl.CostEstimate(
            flops=4 * rows * width * parts * ff,
            bytes_accessed=parts * ff * (4 * width + 6 * rows),
            transcendentals=rows * parts * ff,
        ),
    )(rows_in, near1, far1, near2, far2)


def gelu_slope(value):
    root = math.sqrt(2.0 / math.pi)
    square = value * value
    curve = jnp.tanh(root * value * (1.0 + 0.044715 * square))
    return 0.5 * (1.0 + curve) + 0.5 * value * (1.0 - curve * curve) * root * (
        1.0 + 3.0 * 0.044715 * square
    )


def mlp_backward(grads, rows_in, hidden, activ, near1, far1, near2, far2):
    rows, width = rows_in.shape
    parts, half, ff = near1.shape
    step = 512 if ff % 512 == 0 else ff
    steps = ff // step

    def kernel(
        g_ref, x_ref, hid_ref, act_ref, n1_ref, f1_ref, n2_ref, f2_ref,
        dn1_ref, df1_ref, dn2_ref, df2_ref, out_ref,
        ga, gb, gta, gtb, xta, xtb, ya, yb,
    ):
        first = (pl.program_id(0) == 0) & (pl.program_id(1) == 0)
        last = (pl.program_id(0) == parts - 1) & (pl.program_id(1) == steps - 1)

        @pl.when(first)
        def _():
            ga[...] = g_ref[:, :half]
            gb[...] = g_ref[:, half:]
            gta[...] = jnp.transpose(g_ref[:, :half])
            gtb[...] = jnp.transpose(g_ref[:, half:])
            xta[...] = jnp.transpose(x_ref[:, :half])
            xtb[...] = jnp.transpose(x_ref[:, half:])
            ya[...] = jnp.zeros_like(ya)
            yb[...] = jnp.zeros_like(yb)

        d_activ = dot_nn(ga[...], n2_ref[0]) + dot_nn(gb[...], f2_ref[0])
        activ = act_ref[0]
        dn2_ref[0] = dot_nn(gta[...], activ).astype(BF)
        df2_ref[0] = dot_nn(gtb[...], activ).astype(BF)
        d_hidden = (d_activ * gelu_slope(hid_ref[0])).astype(BF)
        dn1_ref[0] = dot_nn(xta[...], d_hidden).astype(BF)
        df1_ref[0] = dot_nn(xtb[...], d_hidden).astype(BF)
        ya[...] += dot_nt(d_hidden, n1_ref[0])
        yb[...] += dot_nt(d_hidden, f1_ref[0])

        @pl.when(last)
        def _():
            out_ref[:, :half] = ya[...]
            out_ref[:, half:] = yb[...]

    weight = pl.BlockSpec((1, half, step), lambda p, n: (p, 0, n))
    unit = pl.BlockSpec((1, rows, step), lambda p, n: (p, 0, n))
    whole = pl.BlockSpec((rows, width), lambda p, n: (0, 0))
    grad = jax.ShapeDtypeStruct((parts, half, ff), BF)
    return pl.pallas_call(
        kernel,
        name="mlp_backward",
        grid=(parts, steps),
        in_specs=[whole, whole, unit, unit, weight, weight, weight, weight],
        out_specs=[weight, weight, weight, weight, whole],
        out_shape=[grad, grad, grad, grad, jax.ShapeDtypeStruct((rows, width), F32)],
        scratch_shapes=[
            pltpu.VMEM((rows, half), BF),
            pltpu.VMEM((rows, half), BF),
            pltpu.VMEM((half, rows), BF),
            pltpu.VMEM((half, rows), BF),
            pltpu.VMEM((half, rows), BF),
            pltpu.VMEM((half, rows), BF),
            pltpu.VMEM((rows, half), F32),
            pltpu.VMEM((rows, half), F32),
        ],
        compiler_params=pltpu.CompilerParams(vmem_limit_bytes=56 << 20),
        cost_estimate=pl.CostEstimate(
            flops=8 * rows * width * parts * ff,
            bytes_accessed=parts * ff * (8 * width + 6 * rows),
            transcendentals=rows * parts * ff,
        ),
    )(grads, rows_in, hidden, activ, near1, far1, near2, far2)


def tie(*values):
    return lax.optimization_barrier(values)


class Cube:
    def __init__(self):
        self.size = lax.axis_size("dp")
        self.bits = self.size.bit_length() - 1
        self.outer = list(range(1, self.bits))
        self.rank = lax.axis_index("dp")
        self.masks = []
        for place in range(self.size):
            mask = place >> (self.bits - 1)
            for bit in self.outer:
                mask |= ((place >> (bit - 1)) & 1) << bit
            self.masks.append(mask)
        self.owners = self.rank ^ jnp.array(self.masks, jnp.int32)

    def swap(self, value, bit, axis="dp"):
        pairs = [(i, i ^ (1 << bit)) for i in range(lax.axis_size(axis))]
        return lax.ppermute(value, axis, pairs)

    def gather(self, shard, flip):
        held = [(0, shard)]
        for bit in self.outer[::-1] if flip else self.outer:
            held = held + [(mask | (1 << bit), self.swap(piece, bit)) for mask, piece in held]
        held = sorted(held, key=lambda item: self.masks.index(item[0]))
        near = jnp.concatenate([piece for mask, piece in held], 1)
        return near, self.swap(near, 0)

    def scatter(self, near, far, flip):
        rows = near.shape[1] // (self.size // 2)
        order = self.outer if flip else self.outer[::-1]
        other = self.swap(far, 0)
        yield other
        terms = {}
        for place in range(self.size // 2):
            cut = slice(place * rows, (place + 1) * rows)
            terms[self.masks[place]] = [near[:, cut], other[:, cut]]

        def total(mask):
            value = terms[mask][0].astype(F32)
            for term in terms[mask][1:]:
                value = value + term.astype(F32)
            return value.astype(BF)

        for bit in order:
            send = [mask for mask in terms if mask >> bit & 1]
            keep = [mask for mask in terms if not mask >> bit & 1]
            got = self.swap(jnp.concatenate([total(mask) for mask in send], 1), bit)
            yield got
            for place, mask in enumerate(send):
                terms[mask ^ (1 << bit)].append(got[:, place * rows : (place + 1) * rows])
            terms = {mask: terms[mask] for mask in keep}
        yield total(0)

    def trade(self, value):
        blocks = {mask: value[mask] for mask in range(self.size)}
        for bit in range(self.bits):
            send = sorted(mask for mask in blocks if mask >> bit & 1)
            got = self.swap(jnp.stack([blocks[mask] for mask in send]), bit)
            for place, mask in enumerate(send):
                blocks[mask] = got[place]
        return jnp.stack([blocks[mask] for mask in range(self.size)])

    def spread(self, value):
        held = value[None]
        for bit in range(self.bits):
            held = jnp.concatenate([held, self.swap(held, bit)])
        return held

    def add(self, value, axis):
        for bit in range(lax.axis_size(axis).bit_length() - 1):
            value = value + self.swap(value, bit, axis)
        return value


def on_device(
    tokens,
    skip_tokens,
    text,
    timestep,
    grid,
    text_len,
    w_skip,
    w_mod,
    w_qkv,
    w_out1,
    w_query2,
    w_text_kv,
    w_out2,
    w_fc1,
    w_fc2,
    gain_skip,
    gain_attn,
    gain_cross,
    gain_mlp,
    gain_query,
    gain_key,
    cotangent,
):
    micros, slots, width = tokens.shape
    parts = lax.axis_size("sp")
    zone = lax.axis_index("sp")
    cube = Cube()
    ranks = cube.size
    rows = micros * slots
    sequence = slots * parts
    local = H // parts
    lanes = local * HP
    text_slots = text.shape[1]
    words = text_slots * parts
    features = text.shape[2]
    strip = width // ranks
    half = w_skip.shape[0]
    middle = width // 2

    skip_pad = -(-half // 256) * 256 - half
    text_rows = w_text_kv.shape[0]
    shards = [
        jnp.pad(w_skip.T, ((0, 0), (0, skip_pad))),
        pad_heads(w_qkv.reshape(strip, -1)),
        jnp.concatenate([pad_heads(w_out1.T), pad_heads(w_query2), pad_heads(w_out2.T)], 1),
        jnp.pad(pad_heads(w_text_kv.reshape(text_rows, -1)), ((0, max(0, strip - text_rows)), (0, 0))),
        w_fc1,
        w_fc2.T,
    ]
    spread = []
    for shard in shards:
        if spread:
            shard, spread[-1] = tie(shard, spread[-1])
        spread.append(lax.all_gather(shard, "sp", axis=0, tiled=False))
    skip_z, qkv_z, cross_z, text_z, fc1_z, fc2_z = spread

    def join(near, far):
        return jnp.concatenate([near, far], 1)

    def split_weight(value, cut):
        left = join(*cube.gather(value[:, :, :cut], 0))
        right = join(*cube.gather(value[:, :, cut:], 1))
        return jnp.concatenate([left, right], 2)

    skip_w = split_weight(skip_z, (half + skip_pad) // 2)
    qkv_w = split_weight(qkv_z, (3 * lanes) // 256 * 128 + 128)
    out1_w = join(*cube.gather(cross_z[:, :, :lanes], 0))
    query2_w = join(*cube.gather(cross_z[:, :, lanes : 2 * lanes], 1))
    out2_w = join(*cube.gather(cross_z[:, :, 2 * lanes :], 0))
    text_w = join(*cube.gather(text_z[:, :text_rows], 1))
    fc1_n, fc1_f = cube.gather(fc1_z, 0)
    fc2_n, fc2_f = cube.gather(fc2_z, 1)

    gains = jnp.stack([gain_skip, gain_attn, gain_cross, gain_mlp])
    gains = gains.reshape(4, ranks, strip)[:, cube.owners].reshape(4, width)
    g_skip, g_attn, g_cross, g_mlp = gains

    def shuffle(count):
        block = count // ranks
        place = jnp.arange(count, dtype=jnp.int32)
        source = cube.owners[place // block] * block + place % block
        return (place[:, None] == source[None, :]).astype(BF)

    turn = shuffle(width)
    text_turn = shuffle(features)

    wide = grid[:, 0, 1]
    counts = grid[:, 0, 0] * wide
    lengths = text_len[:, 0, :]
    place = zone * slots + jnp.arange(slots, dtype=jnp.int32)
    live = (place[None, :] < counts[:, None]).astype(F32).reshape(rows, 1)
    cosine, sine = rope_tables(sequence, wide, local)
    gain_q = pad_heads(jnp.tile(gain_query, local)[None, :])
    gain_k = pad_heads(jnp.tile(gain_key, local)[None, :])

    steps = cube.spread(timestep[:, 0])
    time_act = jax.nn.silu(time_embed(steps, width)).astype(BF).reshape(ranks * micros, parts, -1)
    time_part = lax.dynamic_index_in_dim(time_act, zone, 1, keepdims=False)
    shift = jnp.dot(time_part, w_mod, preferred_element_type=F32)
    shift = cube.trade(cube.add(shift, "sp").reshape(ranks, micros, strip))
    shift = jnp.stack([shift[mask] for mask in cube.masks], 1).reshape(micros, width)

    text_own = jnp.dot(text.reshape(-1, features), text_turn, preferred_element_type=F32).astype(BF)
    text_all = lax.all_gather(text_own, "sp", axis=0, tiled=False)
    text_all = jnp.transpose(text_all.reshape(parts, micros, text_slots, features), (1, 0, 2, 3))
    text_all = text_all.reshape(micros * words, features)

    grad3 = jnp.dot(cotangent.reshape(rows, width), turn, preferred_element_type=F32) * live
    d_mlp = grad3.astype(BF)

    joined = jnp.stack([tokens, skip_tokens]).reshape(2, rows, parts // 2, half)
    joined = jnp.transpose(joined, (0, 2, 1, 3)).reshape(parts, rows, half)
    joined = jnp.pad(joined, ((0, 0), (0, 0), (0, skip_pad)))
    base = mix("pmk,pnk->mn", joined, skip_w)
    stream = norm_rows(base, g_skip)
    pre_attn = norm_rows(stream, g_attn).reshape(micros, slots, width) + shift[:, None, :]
    pre_attn = pre_attn.reshape(rows, width).astype(BF)
    projected = mix("mk,pkn->pmn", pre_attn, qkv_w).astype(BF)

    def exchange(value):
        return lax.all_to_all(value, "sp", split_axis=0, concat_axis=0, tiled=True)

    raw = exchange(projected.reshape(parts, micros, slots, 3 * lanes))
    text_kv = mix("mk,pkn->pmn", text_all, text_w).astype(BF)
    text_kv = text_kv.reshape(parts, micros, words, 2 * lanes)
    attended, turned_q, turned_k, norms = self_forward(raw, counts, cosine, sine, gain_q, gain_k)
    attended = exchange(attended).reshape(parts, rows, lanes)
    stream1 = stream + mix("pmk,pnk->mn", attended, out1_w)
    pre_cross = norm_rows(stream1, g_cross).astype(BF)
    query2 = mix("mk,pkn->pmn", pre_cross, query2_w).astype(BF)
    query2 = query2.reshape(parts, micros, slots, lanes)
    crossed = cross_forward(query2, text_kv, lengths).reshape(parts, rows, lanes)
    stream2 = stream1 + mix("pmk,pnk->mn", crossed, out2_w)
    pre_mlp = norm_rows(stream2, g_mlp).astype(BF)
    hidden, activ, mlp_out = mlp_forward(pre_mlp, fc1_n, fc1_f, fc2_n, fc2_f)
    result = ((stream2 + mlp_out) * live).astype(BF)

    def halves(left, right):
        near = mix("md,pmn->pdn", left[:, : left.shape[1] // 2], right)
        far = mix("md,pmn->pdn", left[:, left.shape[1] // 2 :], right).astype(BF)
        return near, far

    def settle(value):
        return lax.psum_scatter(value, "sp", scatter_dimension=0, tiled=False)

    d_fc1_n, d_fc1_f, d_fc2_n, d_fc2_f, d_pre_mlp = mlp_backward(
        d_mlp, pre_mlp, hidden, activ, fc1_n, fc1_f, fc2_n, fc2_f
    )
    sum_fc2 = cube.scatter(d_fc2_n, d_fc2_f, 1)
    sum_fc1 = cube.scatter(d_fc1_n, d_fc1_f, 0)
    fc2_1, fc1_1 = next(sum_fc2), next(sum_fc1)
    d_stream2, d_gain_mlp = norm_back(stream2, g_mlp, d_pre_mlp)
    grad2 = grad3 + d_stream2
    d_cross = grad2.astype(BF)
    out2_n, out2_f = halves(d_cross, crossed)
    d_crossed = mix("mn,pnk->pmk", d_cross, out2_w).astype(BF)
    d_query2, d_text_kv = cross_backward(
        query2, text_kv, lengths, d_crossed.reshape(parts, micros, slots, lanes)
    )
    d_query2 = d_query2.reshape(parts, rows, lanes)
    d_text_kv = d_text_kv.reshape(parts, micros * words, 2 * lanes)
    fc2_2, fc1_2 = next(sum_fc2), next(sum_fc1)
    sum_out2 = cube.scatter(out2_n, out2_f, 1)
    out2_1 = next(sum_out2)
    query2_n, query2_f = halves(pre_cross, d_query2)
    sum_query2 = cube.scatter(query2_n, query2_f, 0)
    query2_1 = next(sum_query2)
    d_stream1, d_gain_cross = norm_back(stream1, g_cross, mix("pmn,pkn->mk", d_query2, query2_w))
    grad1 = grad2 + d_stream1
    d_attn = grad1.astype(BF)
    d_attended = mix("mn,pnk->pmk", d_attn, out1_w).astype(BF)
    d_heads = exchange(d_attended.reshape(parts, micros, slots, lanes))
    text_n, text_f = halves(text_all, d_text_kv)
    sum_text = cube.scatter(text_n, text_f, 1)
    text_1 = next(sum_text)
    out1_n, out1_f = halves(d_attn, attended)
    sum_out1 = cube.scatter(out1_n, out1_f, 0)
    out1_1 = next(sum_out1)
    d_words = mix("pmn,pkn->mk", d_text_kv, text_w).astype(BF).reshape(micros, parts, text_slots, features)
    d_words = jnp.transpose(d_words, (1, 0, 2, 3)).reshape(parts, micros * text_slots, features)
    d_words = settle(d_words)
    d_raw, d_gain_q, d_gain_k = self_backward(
        raw, counts, cosine, sine, gain_q, gain_k, turned_q, turned_k, norms, d_heads
    )
    d_projected = exchange(d_raw).reshape(parts, rows, 3 * lanes)
    fc2_3, fc1_3 = next(sum_fc2), next(sum_fc1)
    fc2_4, fc1_4 = next(sum_fc2), next(sum_fc1)
    term_fc2, term_fc1 = settle(fc2_4), settle(fc1_4)
    for stage in range(len(cube.outer)):
        out2_1, query2_1, text_1, out1_1 = (
            next(value) for value in (sum_out2, sum_query2, sum_text, sum_out1)
        )
    cross_1 = [next(value) for value in (sum_out1, sum_query2, sum_out2)]
    term_cross = settle(jnp.concatenate(cross_1, 2))
    term_text = settle(next(sum_text))
    d_words = jnp.dot(d_words, text_turn.T, preferred_element_type=F32)

    d_pre = mix("pmn,pkn->mk", d_projected, qkv_w)
    d_shift = jnp.sum(d_pre.reshape(micros, slots, width), 1)
    d_stream0, d_gain_attn = norm_back(stream, g_attn, d_pre)
    d_base, d_gain_skip = norm_back(base, g_skip, grad1 + d_stream0)
    d_base = d_base.astype(BF)

    def split_term(left, right, cut):
        for part, flip in ((right[:, :, :cut], 0), (right[:, :, cut:], 1)):
            yield cube.scatter(*halves(left, part), flip)

    def finish(sums):
        values = [list(value)[-1] for value in sums]
        return settle(jnp.concatenate(values, 2))

    term_qkv = finish(split_term(pre_attn, d_projected, (3 * lanes) // 256 * 128 + 128))
    term_skip = finish(split_term(d_base, joined, (half + skip_pad) // 2))
    d_joined = mix("mn,pnk->pmk", d_base, skip_w)[:, :, :half].reshape(2, parts // 2, rows, half)
    d_joined = jnp.transpose(d_joined, (0, 2, 1, 3)).reshape(2, micros, slots, width)
    result = jnp.dot(result, turn.T, preferred_element_type=F32).astype(BF)

    d_shift = d_shift.reshape(micros, ranks, strip)
    d_shift = jnp.stack([d_shift[:, cube.masks.index(mask)] for mask in range(ranks)])
    d_shift = cube.add(cube.trade(d_shift), "sp").reshape(ranks * micros, strip)
    term_mod = lax.dot_general(
        time_part.astype(F32), d_shift, (((0,), (0,)), ((), ())), precision=lax.Precision.HIGHEST
    )

    places = jnp.array([cube.masks.index(mask) for mask in range(ranks)], jnp.int32)
    places = places[jnp.arange(ranks, dtype=jnp.int32) ^ cube.rank]
    gains = jnp.stack([d_gain_skip, d_gain_attn, d_gain_cross, d_gain_mlp])
    gains = gains.reshape(4, ranks, strip)[:, places].reshape(-1)
    heads = jnp.stack([jnp.sum(d_gain_q, (0, 1)), jnp.sum(d_gain_k, (0, 1))])
    heads = jnp.sum(heads.reshape(2, local, HP)[:, :, :HD], 1)
    packed = jnp.concatenate([gains, heads.reshape(-1)])
    packed = cube.add(cube.add(packed, "sp"), "dp")
    gains = packed[: 4 * width].reshape(4, ranks * parts, -1)
    gains = lax.dynamic_index_in_dim(gains, cube.rank * parts + zone, 1, keepdims=False)
    heads = packed[4 * width :].reshape(2, HD)

    def whole(term, groups):
        return cut_heads(term.astype(F32)).reshape(term.shape[0], groups, -1)

    return (
        result.reshape(tokens.shape),
        d_joined[0],
        d_joined[1],
        d_words.reshape(text.shape),
        term_skip.astype(F32)[:, :half].T,
        term_mod,
        whole(term_qkv, 3),
        cut_heads(term_cross[:, :lanes].astype(F32)).T,
        cut_heads(term_cross[:, lanes : 2 * lanes].astype(F32)),
        whole(term_text, 2),
        cut_heads(term_cross[:, 2 * lanes :].astype(F32)).T,
        term_fc1.astype(F32),
        term_fc2.astype(F32).T,
        gains[0],
        gains[1],
        gains[2],
        gains[3],
        heads[0],
        heads[1],
    )


def solution(mesh):
    rows = P(None, ("dp", "sp"), None)
    column = P("sp", "dp")
    row = P("dp", "sp")
    grouped = P("dp", None, "sp")
    in_specs = (
        (rows, rows, rows, P(None, "dp"), P(None, "dp", None), P(None, "dp", None))
        + (column, column, grouped, column, row, grouped, column, row, column)
        + (P(),) * 6
        + (rows,)
    )
    out_specs = (
        (rows, rows, rows, rows)
        + (column, column, grouped, column, row, grouped, column, row, column)
        + (P(("dp", "sp")),) * 4
        + (P(), P())
    )
    return jax.shard_map(
        on_device, mesh=mesh, in_specs=in_specs, out_specs=out_specs, check_vma=False
    )
```

```python
import math

import jax
import jax.numpy as jnp
from jax import lax
from jax.experimental import pallas as pl
from jax.experimental.pallas import tpu as pltpu
from jax.sharding import PartitionSpec as P

H = 16
HD = 88
HP = 96
CLIP_LEN = 77
ROWS = 256

EPS = 1e-06
MASKED = -1e30
LOG2E = 1.4426950408889634
BF = jnp.bfloat16
F32 = jnp.float32


def norm_parts(value):
    mean = jnp.mean(value, -1, keepdims=True)
    centre = value - mean
    scale = lax.rsqrt(jnp.mean(centre * centre, -1, keepdims=True) + EPS)
    return centre * scale, scale


def norm_rows(value, gain):
    return norm_parts(value)[0] * gain


def norm_back(value, gain, incoming):
    unit, scale = norm_parts(value)
    leading = incoming * gain
    inner = jnp.mean(leading * unit, -1, keepdims=True)
    back = scale * (leading - jnp.mean(leading, -1, keepdims=True) - unit * inner)
    return back, jnp.sum(incoming * unit, 0)


def time_embed(step, width):
    half = width // 2
    rate = jnp.exp(-math.log(10000.0) * jnp.arange(half, dtype=F32) / half)
    angle = step.astype(F32)[..., None] * rate
    return jnp.concatenate([jnp.cos(angle), jnp.sin(angle)], -1)


def mix(spec, left, right):
    return jnp.einsum(spec, left, right, preferred_element_type=F32)


def rope_tables(sequence, wide, local):
    place = jnp.arange(sequence, dtype=jnp.int32)[None, :, None]
    wide = wide[:, None, None]
    lane = jnp.arange(local * HP, dtype=jnp.int32)[None, None, :] % HP
    pair = lane // 2
    quarter = HD // 4
    upper = pair < quarter
    rank = jnp.where(upper, pair, pair - quarter).astype(F32)
    rate = jnp.exp(-math.log(10000.0) * rank / quarter)
    angle = jnp.where(upper, place // wide, place % wide).astype(F32) * rate
    sine = jnp.sin(angle)
    return jnp.cos(angle), jnp.where(lane % 2 == 0, -sine, sine)


def pad_heads(packed):
    rows, lanes = packed.shape
    groups = packed.reshape(rows, lanes // HD, HD)
    return jnp.pad(groups, ((0, 0), (0, 0), (0, HP - HD))).reshape(rows, -1)


def cut_heads(padded):
    rows, lanes = padded.shape
    return padded.reshape(rows, lanes // HP, HP)[:, :, :HD].reshape(rows, -1)


def head_masks(shape, local):
    lane = lax.broadcasted_iota(jnp.int32, shape, len(shape) - 1)
    inside = lane % HP < HD
    return [((lane // HP == h) & inside).astype(F32) for h in range(local)]


def head_mean(value, masks):
    total = None
    for mask in masks:
        term = (jnp.sum(value * mask, -1, keepdims=True) * (1.0 / HD)) * mask
        total = term if total is None else total + term
    return total


def head_unit(value, masks):
    centre = value - head_mean(value, masks)
    spread = None
    square = centre * centre
    for mask in masks:
        mean = jnp.sum(square * mask, -1, keepdims=True) * (1.0 / HD)
        term = lax.rsqrt(mean + EPS) * mask
        spread = term if spread is None else spread + term
    return centre * spread, spread


def turn_pairs(value):
    lanes = value.shape[-1]
    after = pltpu.roll(value, lanes - 1, 1)
    before = pltpu.roll(value, 1, 1)
    lane = lax.broadcasted_iota(jnp.int32, value.shape, 1)
    return jnp.where(lane % 2 == 0, after, before)


def dot_nt(left, right):
    return lax.dot_general(left, right, (((1,), (1,)), ((), ())), preferred_element_type=F32)


def dot_nn(left, right):
    return lax.dot_general(left, right, (((1,), (0,)), ((), ())), preferred_element_type=F32)


def dot_tn(left, right):
    return lax.dot_general(left, right, (((0,), (0,)), ((), ())), preferred_element_type=F32)


def self_forward(raw, counts, cosine, sine, gain_q, gain_k):
    parts, micros, slots, packed = raw.shape
    lanes = packed // 3
    local = lanes // HP
    sequence = parts * slots
    factor = HD ** (-0.5) * LOG2E

    def kernel(count_ref, raw_ref, cos_ref, sin_ref, gq_ref, gk_ref, out_ref, q_ref, k_ref, lse_ref):
        count = count_ref[pl.program_id(0)]
        blocks = (count + slots - 1) // slots
        out_ref[...] = jnp.zeros_like(out_ref)
        masks = head_masks((1, lanes), local)

        def prepare(part, carry):
            spot = pl.ds(pl.multiple_of(part * slots, slots), slots)
            cosine, sine = cos_ref[0, spot, :], sin_ref[0, spot, :]
            for index, gain_ref, dest in ((0, gq_ref, q_ref), (1, gk_ref, k_ref)):
                value = raw_ref[part, 0, :, index * lanes : (index + 1) * lanes].astype(F32)
                scaled = head_unit(value, masks)[0] * gain_ref[...]
                dest[0, spot, :] = (scaled * cosine + turn_pairs(scaled) * sine).astype(BF)
            return carry

        lax.fori_loop(0, parts, prepare, 0)
        column = lax.broadcasted_iota(jnp.int32, (1, sequence), 1)
        bias = jnp.where(column < count, 0.0, MASKED)
        for h in range(local):
            cut = slice(h * HP, (h + 1) * HP)
            keys = k_ref[0, :, cut]
            values = raw_ref[:, 0, :, 2 * lanes + h * HP : 2 * lanes + (h + 1) * HP].reshape(sequence, HP)

            def one_block(part, carry):
                spot = pl.ds(pl.multiple_of(part * slots, slots), slots)
                scores = dot_nt(q_ref[0, spot, cut], keys) + bias
                top = jnp.max(scores, -1, keepdims=True)
                raised = jnp.exp2((scores - top) * factor)
                total = jnp.sum(raised, -1, keepdims=True)
                result = dot_nn(raised.astype(BF), values) / total
                out_ref[part, 0, :, cut] = result.astype(BF)
                norm = jnp.broadcast_to(top * factor + jnp.log2(total), (slots, 128))
                lse_ref[0, h : h + 1, spot] = jnp.transpose(norm)[0:1, :]
                return carry

            lax.fori_loop(0, blocks, one_block, 0)

    whole = lambda m, c: (0, m, 0, 0)
    table = lambda m, c: (m, 0, 0)
    fixed = lambda m, c: (0, 0)
    return pl.pallas_call(
        kernel,
        name="self_forward",
        grid_spec=pltpu.PrefetchScalarGridSpec(
            num_scalar_prefetch=1,
            grid=(micros,),
            in_specs=[
                pl.BlockSpec((parts, 1, slots, packed), whole),
                pl.BlockSpec((1, sequence, lanes), table),
                pl.BlockSpec((1, sequence, lanes), table),
                pl.BlockSpec((1, lanes), fixed),
                pl.BlockSpec((1, lanes), fixed),
            ],
            out_specs=[
                pl.BlockSpec((parts, 1, slots, lanes), whole),
                pl.BlockSpec((1, sequence, lanes), table),
                pl.BlockSpec((1, sequence, lanes), table),
                pl.BlockSpec((1, local, sequence), table),
            ],
        ),
        out_shape=[
            jax.ShapeDtypeStruct((parts, micros, slots, lanes), BF),
            jax.ShapeDtypeStruct((micros, sequence, lanes), BF),
            jax.ShapeDtypeStruct((micros, sequence, lanes), BF),
            jax.ShapeDtypeStruct((micros, local, sequence), F32),
        ],
        compiler_params=pltpu.CompilerParams(vmem_limit_bytes=48 << 20),
        cost_estimate=pl.CostEstimate(
            flops=4 * micros * local * sequence * sequence * HP,
            bytes_accessed=2 * micros * sequence * lanes * 10,
            transcendentals=micros * local * sequence * sequence,
        ),
    )(counts, raw, cosine, sine, gain_q, gain_k)


def self_backward(raw, counts, cosine, sine, gain_q, gain_k, turned_q, turned_k, norms, incoming):
    parts, micros, slots, packed = raw.shape
    lanes = packed // 3
    local = lanes // HP
    sequence = parts * slots
    scale = HD ** (-0.5)
    factor = scale * LOG2E

    def kernel(
        count_ref,
        raw_ref,
        cos_ref,
        sin_ref,
        gq_ref,
        gk_ref,
        q_ref,
        k_ref,
        lse_ref,
        in_ref,
        out_ref,
        dgq_ref,
        dgk_ref,
        dq_s,
        dk_s,
        dv_s,
    ):
        count = count_ref[pl.program_id(0)]
        blocks = (count + slots - 1) // slots
        dq_s[...] = jnp.zeros_like(dq_s)
        dk_s[...] = jnp.zeros_like(dk_s)
        dv_s[...] = jnp.zeros_like(dv_s)
        row = lax.broadcasted_iota(jnp.int32, (sequence, 1), 0)
        bias = jnp.where(row < count, 0.0, MASKED)
        for h in range(local):
            cut = slice(h * HP, (h + 1) * HP)
            keys = k_ref[0, :, cut]
            values = raw_ref[:, 0, :, 2 * lanes + h * HP : 2 * lanes + (h + 1) * HP].reshape(sequence, HP)

            def one_block(part, carry):
                spot = pl.ds(pl.multiple_of(part * slots, slots), slots)
                rows = q_ref[0, spot, cut]
                grads = in_ref[part, 0, :, cut]
                norm = lse_ref[0, h : h + 1, spot]
                probs = jnp.exp2(dot_nt(keys, rows) * factor + bias - norm)
                d_probs = dot_nt(values, grads)
                inner = jnp.sum(probs * d_probs, 0, keepdims=True)
                d_scores = (probs * (d_probs - inner)).astype(BF)
                dv_s[:, cut] += dot_nn(probs.astype(BF), grads)
                dk_s[:, cut] += dot_nn(d_scores, rows)
                dq_s[spot, cut] = dot_tn(d_scores, keys)
                return carry

            lax.fori_loop(0, blocks, one_block, 0)
        masks = head_masks((1, lanes), local)

        def finish(part, carry):
            spot = pl.ds(pl.multiple_of(part * slots, slots), slots)
            cosine, sine = cos_ref[0, spot, :], sin_ref[0, spot, :]
            sums = []
            for index, gain_ref, source in ((0, gq_ref, dq_s), (1, gk_ref, dk_s)):
                grad = source[spot, :] * scale
                grad = grad * cosine - turn_pairs(grad) * sine
                value = raw_ref[part, 0, :, index * lanes : (index + 1) * lanes].astype(F32)
                unit, spread = head_unit(value, masks)
                leading = grad * gain_ref[...]
                back = leading - head_mean(leading, masks) - unit * head_mean(leading * unit, masks)
                out_ref[part, 0, :, index * lanes : (index + 1) * lanes] = (spread * back).astype(BF)
                sums.append(carry[index] + jnp.sum(grad * unit, 0, keepdims=True))
            out_ref[part, 0, :, 2 * lanes : 3 * lanes] = dv_s[spot, :].astype(BF)
            return tuple(sums)

        zero = jnp.zeros((1, lanes), F32)
        d_gains = lax.fori_loop(0, parts, finish, (zero, zero))
        dgq_ref[0] = d_gains[0]
        dgk_ref[0] = d_gains[1]

    whole = lambda m, c: (0, m, 0, 0)
    table = lambda m, c: (m, 0, 0)
    fixed = lambda m, c: (0, 0)
    return pl.pallas_call(
        kernel,
        name="self_backward",
        grid_spec=pltpu.PrefetchScalarGridSpec(
            num_scalar_prefetch=1,
            grid=(micros,),
            in_specs=[
                pl.BlockSpec((parts, 1, slots, packed), whole),
                pl.BlockSpec((1, sequence, lanes), table),
                pl.BlockSpec((1, sequence, lanes), table),
                pl.BlockSpec((1, lanes), fixed),
                pl.BlockSpec((1, lanes), fixed),
                pl.BlockSpec((1, sequence, lanes), table),
                pl.BlockSpec((1, sequence, lanes), table),
                pl.BlockSpec((1, local, sequence), table),
                pl.BlockSpec((parts, 1, slots, lanes), whole),
            ],
            out_specs=[
                pl.BlockSpec((parts, 1, slots, packed), whole),
                pl.BlockSpec((1, 1, lanes), table),
                pl.BlockSpec((1, 1, lanes), table),
            ],
            scratch_shapes=[pltpu.VMEM((sequence, lanes), F32) for index in range(3)],
        ),
        out_shape=[
            jax.ShapeDtypeStruct((parts, micros, slots, packed), BF),
            jax.ShapeDtypeStruct((micros, 1, lanes), F32),
            jax.ShapeDtypeStruct((micros, 1, lanes), F32),
        ],
        compiler_params=pltpu.CompilerParams(vmem_limit_bytes=48 << 20),
        cost_estimate=pl.CostEstimate(
            flops=10 * micros * local * sequence * sequence * HP,
            bytes_accessed=2 * micros * sequence * lanes * 14,
            transcendentals=micros * local * sequence * sequence,
        ),
    )(counts, raw, cosine, sine, gain_q, gain_k, turned_q, turned_k, norms, incoming)


def text_bias(lengths_ref, micro, words, axis):
    place = lax.broadcasted_iota(jnp.int32, (1, words) if axis else (words, 1), axis)
    live = (place < lengths_ref[micro, 0]) | (
        (place >= CLIP_LEN) & (place < CLIP_LEN + lengths_ref[micro, 1])
    )
    return jnp.where(live, 0.0, MASKED)


def cross_forward(query, text_kv, lengths):
    parts, micros, slots, lanes = query.shape
    words = text_kv.shape[2]
    local = lanes // HP
    factor = HD ** (-0.5) * LOG2E

    def kernel(len_ref, q_ref, kv_ref, out_ref):
        bias = text_bias(len_ref, pl.program_id(1), words, 1)
        for h in range(local):
            cut = slice(h * HP, (h + 1) * HP)
            scores = dot_nt(q_ref[0, 0, :, cut], kv_ref[0, 0, :, cut]) + bias
            top = jnp.max(scores, -1, keepdims=True)
            raised = jnp.exp2((scores - top) * factor)
            total = jnp.sum(raised, -1, keepdims=True)
            values = kv_ref[0, 0, :, lanes + h * HP : lanes + (h + 1) * HP]
            out_ref[0, 0, :, cut] = (dot_nn(raised.astype(BF), values) / total).astype(BF)

    spot = lambda p, m, c: (p, m, 0, 0)
    return pl.pallas_call(
        kernel,
        name="cross_forward",
        grid_spec=pltpu.PrefetchScalarGridSpec(
            num_scalar_prefetch=1,
            grid=(parts, micros),
            in_specs=[
                pl.BlockSpec((1, 1, slots, lanes), spot),
                pl.BlockSpec((1, 1, words, 2 * lanes), spot),
            ],
            out_specs=pl.BlockSpec((1, 1, slots, lanes), spot),
        ),
        out_shape=jax.ShapeDtypeStruct(query.shape, BF),
        compiler_params=pltpu.CompilerParams(vmem_limit_bytes=32 << 20),
        cost_estimate=pl.CostEstimate(
            flops=4 * parts * micros * slots * words * lanes,
            bytes_accessed=4 * parts * micros * (slots + words) * lanes,
            transcendentals=parts * micros * local * slots * words,
        ),
    )(lengths, query, text_kv)


def cross_backward(query, text_kv, lengths, incoming):
    parts, micros, slots, lanes = query.shape
    words = text_kv.shape[2]
    local = lanes // HP
    scale = HD ** (-0.5)
    factor = scale * LOG2E

    def kernel(len_ref, q_ref, kv_ref, in_ref, dq_ref, dkv_ref):
        bias = text_bias(len_ref, pl.program_id(1), words, 0)
        for h in range(local):
            cut = slice(h * HP, (h + 1) * HP)
            far = slice(lanes + h * HP, lanes + (h + 1) * HP)
            rows = q_ref[0, 0, :, cut]
            keys = kv_ref[0, 0, :, cut]
            grads = in_ref[0, 0, :, cut]
            scores = dot_nt(keys, rows) + bias
            top = jnp.max(scores, 0, keepdims=True)
            raised = jnp.exp2((scores - top) * factor)
            probs = raised * (1.0 / jnp.sum(raised, 0, keepdims=True))
            d_probs = dot_nt(kv_ref[0, 0, :, far], grads)
            inner = jnp.sum(probs * d_probs, 0, keepdims=True)
            d_scores = (probs * (d_probs - inner)).astype(BF)
            dkv_ref[0, 0, :, far] = dot_nn(probs.astype(BF), grads).astype(BF)
            dkv_ref[0, 0, :, cut] = (dot_nn(d_scores, rows) * scale).astype(BF)
            dq_ref[0, 0, :, cut] = (dot_tn(d_scores, keys) * scale).astype(BF)

    spot = lambda p, m, c: (p, m, 0, 0)
    return pl.pallas_call(
        kernel,
        name="cross_backward",
        grid_spec=pltpu.PrefetchScalarGridSpec(
            num_scalar_prefetch=1,
            grid=(parts, micros),
            in_specs=[
                pl.BlockSpec((1, 1, slots, lanes), spot),
                pl.BlockSpec((1, 1, words, 2 * lanes), spot),
                pl.BlockSpec((1, 1, slots, lanes), spot),
            ],
            out_specs=[
                pl.BlockSpec((1, 1, slots, lanes), spot),
                pl.BlockSpec((1, 1, words, 2 * lanes), spot),
            ],
        ),
        out_shape=[
            jax.ShapeDtypeStruct(query.shape, BF),
            jax.ShapeDtypeStruct(text_kv.shape, BF),
        ],
        compiler_params=pltpu.CompilerParams(vmem_limit_bytes=32 << 20),
        cost_estimate=pl.CostEstimate(
            flops=10 * parts * micros * slots * words * lanes,
            bytes_accessed=8 * parts * micros * (slots + words) * lanes,
            transcendentals=parts * micros * local * slots * words,
        ),
    )(lengths, query, text_kv, incoming)


def mlp_forward(rows_in, grads, near1, far1, near2, far2):
    rows, width = rows_in.shape
    parts, half, ff = near1.shape
    step = 384 if ff % 384 == 0 else ff
    steps = ff // step

    def kernel(
        x_ref, g_ref, n1_ref, f1_ref, n2_ref, f2_ref,
        hid_ref, act_ref, out_ref, dn2_ref, df2_ref,
        xa, xb, gta, gtb, ya, yb,
    ):
        first = (pl.program_id(0) == 0) & (pl.program_id(1) == 0)
        last = (pl.program_id(0) == parts - 1) & (pl.program_id(1) == steps - 1)

        @pl.when(first)
        def _():
            xa[...] = x_ref[:, :half]
            xb[...] = x_ref[:, half:]
            gta[...] = jnp.transpose(g_ref[:, :half])
            gtb[...] = jnp.transpose(g_ref[:, half:])
            ya[...] = jnp.zeros_like(ya)
            yb[...] = jnp.zeros_like(yb)

        hidden = dot_nn(xa[...], n1_ref[0]) + dot_nn(xb[...], f1_ref[0])
        hid_ref[0] = hidden
        activ = jax.nn.gelu(hidden, approximate=True).astype(BF)
        act_ref[0] = activ
        ya[...] += dot_nt(activ, n2_ref[0])
        yb[...] += dot_nt(activ, f2_ref[0])
        dn2_ref[0] = dot_nn(gta[...], activ).astype(BF)
        df2_ref[0] = dot_nn(gtb[...], activ).astype(BF)

        @pl.when(last)
        def _():
            out_ref[:, :half] = ya[...]
            out_ref[:, half:] = yb[...]

    weight = pl.BlockSpec((1, half, step), lambda p, n: (p, 0, n))
    unit = pl.BlockSpec((1, rows, step), lambda p, n: (p, 0, n))
    whole = pl.BlockSpec((rows, width), lambda p, n: (0, 0))
    grad = jax.ShapeDtypeStruct((parts, half, ff), BF)
    return pl.pallas_call(
        kernel,
        name="mlp_forward",
        grid=(parts, steps),
        in_specs=[whole, whole, weight, weight, weight, weight],
        out_specs=[unit, unit, whole, weight, weight],
        out_shape=[
            jax.ShapeDtypeStruct((parts, rows, ff), F32),
            jax.ShapeDtypeStruct((parts, rows, ff), BF),
            jax.ShapeDtypeStruct((rows, width), F32),
            grad,
            grad,
        ],
        scratch_shapes=[
            pltpu.VMEM((rows, half), BF),
            pltpu.VMEM((rows, half), BF),
            pltpu.VMEM((half, rows), BF),
            pltpu.VMEM((half, rows), BF),
            pltpu.VMEM((rows, half), F32),
            pltpu.VMEM((rows, half), F32),
        ],
        compiler_params=pltpu.CompilerParams(vmem_limit_bytes=48 << 20),
        cost_estimate=pl.CostEstimate(
            flops=6 * rows * width * parts * ff,
            bytes_accessed=parts * ff * (6 * width + 6 * rows),
            transcendentals=rows * parts * ff,
        ),
    )(rows_in, grads, near1, far1, near2, far2)


def gelu_slope(value):
    root = math.sqrt(2.0 / math.pi)
    square = value * value
    curve = jnp.tanh(root * value * (1.0 + 0.044715 * square))
    return 0.5 * (1.0 + curve) + 0.5 * value * (1.0 - curve * curve) * root * (
        1.0 + 3.0 * 0.044715 * square
    )


def mlp_backward(grads, rows_in, hidden, near1, far1, near2, far2):
    rows, width = rows_in.shape
    parts, half, ff = near1.shape
    step = 384 if ff % 384 == 0 else ff
    steps = ff // step

    def kernel(
        g_ref, x_ref, hid_ref, n1_ref, f1_ref, n2_ref, f2_ref,
        dn1_ref, df1_ref, out_ref,
        ga, gb, xta, xtb, ya, yb,
    ):
        first = (pl.program_id(0) == 0) & (pl.program_id(1) == 0)
        last = (pl.program_id(0) == parts - 1) & (pl.program_id(1) == steps - 1)

        @pl.when(first)
        def _():
            ga[...] = g_ref[:, :half]
            gb[...] = g_ref[:, half:]
            xta[...] = jnp.transpose(x_ref[:, :half])
            xtb[...] = jnp.transpose(x_ref[:, half:])
            ya[...] = jnp.zeros_like(ya)
            yb[...] = jnp.zeros_like(yb)

        d_activ = dot_nn(ga[...], n2_ref[0]) + dot_nn(gb[...], f2_ref[0])
        d_hidden = (d_activ * gelu_slope(hid_ref[0])).astype(BF)
        dn1_ref[0] = dot_nn(xta[...], d_hidden).astype(BF)
        df1_ref[0] = dot_nn(xtb[...], d_hidden).astype(BF)
        ya[...] += dot_nt(d_hidden, n1_ref[0])
        yb[...] += dot_nt(d_hidden, f1_ref[0])

        @pl.when(last)
        def _():
            out_ref[:, :half] = ya[...]
            out_ref[:, half:] = yb[...]

    weight = pl.BlockSpec((1, half, step), lambda p, n: (p, 0, n))
    unit = pl.BlockSpec((1, rows, step), lambda p, n: (p, 0, n))
    whole = pl.BlockSpec((rows, width), lambda p, n: (0, 0))
    grad = jax.ShapeDtypeStruct((parts, half, ff), BF)
    return pl.pallas_call(
        kernel,
        name="mlp_backward",
        grid=(parts, steps),
        in_specs=[whole, whole, unit, weight, weight, weight, weight],
        out_specs=[weight, weight, whole],
        out_shape=[grad, grad, jax.ShapeDtypeStruct((rows, width), F32)],
        scratch_shapes=[
            pltpu.VMEM((rows, half), BF),
            pltpu.VMEM((rows, half), BF),
            pltpu.VMEM((half, rows), BF),
            pltpu.VMEM((half, rows), BF),
            pltpu.VMEM((rows, half), F32),
            pltpu.VMEM((rows, half), F32),
        ],
        compiler_params=pltpu.CompilerParams(vmem_limit_bytes=48 << 20),
        cost_estimate=pl.CostEstimate(
            flops=6 * rows * width * parts * ff,
            bytes_accessed=parts * ff * (6 * width + 4 * rows),
            transcendentals=rows * parts * ff,
        ),
    )(grads, rows_in, hidden, near1, far1, near2, far2)


def tie(*values):
    return lax.optimization_barrier(values)


class Cube:
    def __init__(self):
        self.size = lax.axis_size("dp")
        self.bits = self.size.bit_length() - 1
        self.outer = list(range(1, self.bits))
        self.rank = lax.axis_index("dp")
        self.masks = []
        for place in range(self.size):
            mask = place >> (self.bits - 1)
            for bit in self.outer:
                mask |= ((place >> (bit - 1)) & 1) << bit
            self.masks.append(mask)
        self.owners = self.rank ^ jnp.array(self.masks, jnp.int32)

    def swap(self, value, bit, axis="dp"):
        pairs = [(i, i ^ (1 << bit)) for i in range(lax.axis_size(axis))]
        return lax.ppermute(value, axis, pairs)

    def trade(self, value):
        blocks = {mask: value[mask] for mask in range(self.size)}
        for bit in range(self.bits):
            send = sorted(mask for mask in blocks if mask >> bit & 1)
            got = self.swap(jnp.stack([blocks[mask] for mask in send]), bit)
            for place, mask in enumerate(send):
                blocks[mask] = got[place]
        return jnp.stack([blocks[mask] for mask in range(self.size)])

    def spread(self, value):
        held = value[None]
        for bit in range(self.bits):
            held = jnp.concatenate([held, self.swap(held, bit)])
        return held

    def add(self, value, axis):
        for bit in range(lax.axis_size(axis).bit_length() - 1):
            value = value + self.swap(value, bit, axis)
        return value


class Gather:
    def __init__(self, cube, shard, flip):
        self.cube = cube
        self.masks = [0]
        self.pieces = [shard]
        self.todo = cube.outer[::-1] if flip else list(cube.outer)

    def move(self):
        bit = self.todo.pop(0)
        self.masks = self.masks + [mask | (1 << bit) for mask in self.masks]
        self.pieces = self.pieces + [self.cube.swap(piece, bit) for piece in self.pieces]

    def join(self):
        while self.todo:
            self.move()
        order = sorted(range(len(self.masks)), key=lambda i: self.cube.masks.index(self.masks[i]))
        return jnp.concatenate([self.pieces[i] for i in order], 1)


class Scatter:
    def __init__(self, cube, near, far, flip):
        self.cube = cube
        self.todo = list(cube.outer) if flip else cube.outer[::-1]
        self.near = near
        self.rows = near.shape[1] // (cube.size // 2)
        self.pieces = [cube.swap(far, 0)]
        self.terms = None
        self.packet = None

    def absorb(self):
        got = self.pieces[0]
        if self.terms is None:
            self.terms = {}
            for place in range(self.cube.size // 2):
                cut = slice(place * self.rows, (place + 1) * self.rows)
                self.terms[self.cube.masks[place]] = [self.near[:, cut], got[:, cut]]
            return
        for place, mask in enumerate(self.sent):
            self.terms[mask ^ self.bit].append(got[:, place * self.rows : (place + 1) * self.rows])
            del self.terms[mask]

    def total(self, mask):
        value = self.terms[mask][0].astype(F32)
        for term in self.terms[mask][1:]:
            value = value + term.astype(F32)
        return value.astype(BF)

    def pack(self):
        self.absorb()
        self.bit = 1 << self.todo.pop(0)
        self.sent = [mask for mask in self.terms if mask & self.bit]
        self.pieces = [jnp.concatenate([self.total(mask) for mask in self.sent], 1)]
        self.packet = True

    def move(self):
        if not self.packet:
            self.pack()
        self.pieces = [self.cube.swap(self.pieces[0], self.bit.bit_length() - 1)]
        self.packet = None

    def result(self):
        while self.todo or self.packet:
            self.move()
        self.absorb()
        return self.total(0)


def bind(value, *movers):
    flat = [piece for mover in movers for piece in mover.pieces]
    held = tie(value, *flat)
    spot = 1
    for mover in movers:
        count = len(mover.pieces)
        mover.pieces = list(held[spot : spot + count])
        spot += count
    return held[0]


def on_device(
    tokens,
    skip_tokens,
    text,
    timestep,
    grid,
    text_len,
    w_skip,
    w_mod,
    w_qkv,
    w_out1,
    w_query2,
    w_text_kv,
    w_out2,
    w_fc1,
    w_fc2,
    gain_skip,
    gain_attn,
    gain_cross,
    gain_mlp,
    gain_query,
    gain_key,
    cotangent,
):
    micros, slots, width = tokens.shape
    parts = lax.axis_size("sp")
    zone = lax.axis_index("sp")
    cube = Cube()
    ranks = cube.size
    rows = micros * slots
    sequence = slots * parts
    local = H // parts
    lanes = local * HP
    text_slots = text.shape[1]
    words = text_slots * parts
    features = text.shape[2]
    strip = width // ranks
    half = w_skip.shape[0]
    middle = width // 2

    skip_pad = -(-half // 256) * 256 - half
    skip_cut = (half + skip_pad) // 2
    qkv_cut = (3 * lanes) // 256 * 128 + 128
    text_rows = w_text_kv.shape[0]
    hidden_cut = w_fc1.shape[1] // 2

    def spread(shard, before=None):
        if before is not None:
            shard, before = tie(shard, before)
        return lax.all_gather(shard, "sp", axis=0, tiled=False)

    def fetch(value, cut):
        return Gather(cube, value[:, :, :cut], 0), Gather(cube, value[:, :, cut:], 1)

    def rows_of(mover):
        near = mover.join()
        return jnp.concatenate([near, cube.swap(near, 0)], 1)

    skip_z = spread(jnp.pad(w_skip.T, ((0, 0), (0, skip_pad))))
    skip_m = fetch(skip_z, skip_cut)
    for mover in skip_m:
        mover.move()
    qkv_z = spread(pad_heads(w_qkv.reshape(strip, -1)), skip_z)
    fc1_z = spread(w_fc1, qkv_z)
    fc2_z = spread(w_fc2.T, fc1_z)
    qkv_m = fetch(qkv_z, qkv_cut)
    skip_w = jnp.concatenate([rows_of(mover) for mover in skip_m], 2)
    for mover in qkv_m:
        mover.move()

    gains = jnp.stack([gain_skip, gain_attn, gain_cross, gain_mlp])
    gains = gains.reshape(4, ranks, strip)[:, cube.owners].reshape(4, width)
    g_skip, g_attn, g_cross, g_mlp = gains

    def shuffle(count):
        block = count // ranks
        place = jnp.arange(count, dtype=jnp.int32)
        source = cube.owners[place // block] * block + place % block
        return (place[:, None] == source[None, :]).astype(BF)

    turn = shuffle(width)
    text_turn = shuffle(features)

    wide = grid[:, 0, 1]
    counts = grid[:, 0, 0] * wide
    lengths = text_len[:, 0, :]
    place = zone * slots + jnp.arange(slots, dtype=jnp.int32)
    live = (place[None, :] < counts[:, None]).astype(F32).reshape(rows, 1)
    cosine, sine = rope_tables(sequence, wide, local)
    gain_q = pad_heads(jnp.tile(gain_query, local)[None, :])
    gain_k = pad_heads(jnp.tile(gain_key, local)[None, :])

    steps = cube.spread(timestep[:, 0])
    time_act = jax.nn.silu(time_embed(steps, width)).astype(BF).reshape(ranks * micros, parts, -1)
    time_part = lax.dynamic_index_in_dim(time_act, zone, 1, keepdims=False)
    shift = jnp.dot(time_part, w_mod, preferred_element_type=F32)
    shift = cube.trade(cube.add(shift, "sp").reshape(ranks, micros, strip))
    shift = jnp.stack([shift[mask] for mask in cube.masks], 1).reshape(micros, width)

    grad3 = jnp.dot(cotangent.reshape(rows, width), turn, preferred_element_type=F32) * live
    d_mlp = grad3.astype(BF)

    joined = jnp.stack([tokens, skip_tokens]).reshape(2, rows, parts // 2, half)
    joined = jnp.transpose(joined, (0, 2, 1, 3)).reshape(parts, rows, half)
    joined = jnp.pad(joined, ((0, 0), (0, 0), (0, skip_pad)))
    base = mix("pmk,pnk->mn", joined, skip_w)
    stream = norm_rows(base, g_skip)
    pre_attn = norm_rows(stream, g_attn).reshape(micros, slots, width) + shift[:, None, :]
    pre_attn = pre_attn.reshape(rows, width).astype(BF)
    pre_attn = bind(pre_attn, *qkv_m)
    qkv_w = jnp.concatenate([rows_of(mover) for mover in qkv_m], 2)
    fc_m = fetch(fc1_z, hidden_cut) + fetch(fc2_z, hidden_cut)[::-1]
    projected = mix("mk,pkn->pmn", pre_attn, qkv_w).astype(BF)
    projected = bind(projected, *fc_m)
    for mover in fc_m:
        mover.move()

    def exchange(value):
        return lax.all_to_all(value, "sp", split_axis=0, concat_axis=0, tiled=True)

    raw = exchange(projected.reshape(parts, micros, slots, 3 * lanes))
    raw = bind(raw, *fc_m)
    cross_z = jnp.concatenate([pad_heads(w_out1.T), pad_heads(w_query2), pad_heads(w_out2.T)], 1)
    cross_z = spread(cross_z, raw)
    text_z = jnp.pad(pad_heads(w_text_kv.reshape(text_rows, -1)), ((0, max(0, strip - text_rows)), (0, 0)))
    text_z = spread(text_z, cross_z)
    text_own = jnp.dot(text.reshape(-1, features), text_turn, preferred_element_type=F32).astype(BF)
    text_all = spread(text_own, text_z)
    text_all = jnp.transpose(text_all.reshape(parts, micros, text_slots, features), (1, 0, 2, 3))
    text_all = text_all.reshape(micros * words, features)
    while fc_m[0].todo:
        for mover in fc_m:
            mover.move()
    attended, turned_q, turned_k, norms = self_forward(raw, counts, cosine, sine, gain_q, gain_k)
    attended = bind(attended, *fc_m)
    attended = exchange(attended).reshape(parts, rows, lanes)
    fc1_n, fc2_n = [mover.join() for mover in fc_m[:2]], [mover.join() for mover in fc_m[:1:-1]]
    fc1_f, fc2_f = ([cube.swap(near, 0) for near in value] for value in (fc1_n, fc2_n))
    out1_w = rows_of(Gather(cube, cross_z[:, :, :lanes], 0))
    query2_w = rows_of(Gather(cube, cross_z[:, :, lanes : 2 * lanes], 1))
    out2_w = rows_of(Gather(cube, cross_z[:, :, 2 * lanes :], 0))
    text_w = rows_of(Gather(cube, text_z[:, :text_rows], 1))
    stream1 = stream + mix("pmk,pnk->mn", attended, out1_w)
    pre_cross = norm_rows(stream1, g_cross).astype(BF)
    query2 = mix("mk,pkn->pmn", pre_cross, query2_w).astype(BF)
    query2 = query2.reshape(parts, micros, slots, lanes)
    text_kv = mix("mk,pkn->pmn", text_all, text_w).astype(BF)
    text_kv = text_kv.reshape(parts, micros, words, 2 * lanes)
    crossed = cross_forward(query2, text_kv, lengths).reshape(parts, rows, lanes)
    stream2 = stream1 + mix("pmk,pnk->mn", crossed, out2_w)
    pre_mlp = norm_rows(stream2, g_mlp).astype(BF)
    forward = [
        mlp_forward(pre_mlp, d_mlp, n1, f1, n2, f2)
        for n1, f1, n2, f2 in zip(fc1_n, fc1_f, fc2_n, fc2_f)
    ]
    result = ((stream2 + forward[0][2] + forward[1][2]) * live).astype(BF)
    fc2_s = [Scatter(cube, item[3], item[4], flip) for flip, item in enumerate(forward)]

    def halves(left, right):
        near = mix("md,pmn->pdn", left[:, : left.shape[1] // 2], right)
        far = mix("md,pmn->pdn", left[:, left.shape[1] // 2 :], right).astype(BF)
        return near, far

    def settle(values, before=None):
        value = values[0] if len(values) == 1 else jnp.concatenate(values, 2)
        if before is not None:
            value, before = tie(value, before)
        return lax.psum_scatter(value, "sp", scatter_dimension=0, tiled=False)

    backward = []
    for index in range(2):
        item = mlp_backward(
            d_mlp, pre_mlp, forward[index][0], fc1_n[index], fc1_f[index], fc2_n[index], fc2_f[index]
        )
        backward.append(item)
    fc1_s = [Scatter(cube, item[0], item[1], flip) for flip, item in enumerate(backward)]
    d_pre_mlp = bind(backward[0][2] + backward[1][2], *fc2_s)
    for mover in fc2_s:
        mover.pack()
    d_pre_mlp = bind(d_pre_mlp, *fc2_s)
    for mover in fc2_s:
        mover.move()
    d_stream2, d_gain_mlp = norm_back(stream2, g_mlp, d_pre_mlp)
    grad2 = grad3 + d_stream2
    d_cross = grad2.astype(BF)
    d_crossed = mix("mn,pnk->pmk", d_cross, out2_w).astype(BF)
    d_query2, d_text_kv = cross_backward(
        query2, text_kv, lengths, d_crossed.reshape(parts, micros, slots, lanes)
    )
    d_query2 = bind(d_query2, *fc1_s, *fc2_s)
    for mover in fc1_s + fc2_s:
        mover.pack()
    d_query2 = bind(d_query2, *fc1_s, *fc2_s)
    for mover in fc2_s + fc1_s:
        mover.move()
    d_query2 = d_query2.reshape(parts, rows, lanes)
    d_text_kv = d_text_kv.reshape(parts, micros * words, 2 * lanes)
    d_stream1, d_gain_cross = norm_back(stream1, g_cross, mix("pmn,pkn->mk", d_query2, query2_w))
    grad1 = grad2 + d_stream1
    d_attn = grad1.astype(BF)
    d_attended = mix("mn,pnk->pmk", d_attn, out1_w).astype(BF)
    d_heads = exchange(d_attended.reshape(parts, micros, slots, lanes))
    d_words = mix("pmn,pkn->mk", d_text_kv, text_w).astype(BF).reshape(micros, parts, text_slots, features)
    d_words = jnp.transpose(d_words, (1, 0, 2, 3)).reshape(parts, micros * text_slots, features)
    out2_s = Scatter(cube, *halves(d_cross, crossed), 1)
    query2_s = Scatter(cube, *halves(pre_cross, d_query2), 0)
    text_s = Scatter(cube, *halves(text_all, d_text_kv), 1)
    out1_s = Scatter(cube, *halves(d_attn, attended), 0)
    cross_s = [out2_s, query2_s, text_s, out1_s]
    d_heads = bind(d_heads, *fc2_s, *cross_s)
    total_fc2 = [mover.result() for mover in fc2_s]
    term_fc2 = settle(total_fc2)
    d_raw, d_gain_q, d_gain_k = self_backward(
        raw, counts, cosine, sine, gain_q, gain_k, turned_q, turned_k, norms, d_heads
    )
    d_words = settle([d_words])
    d_raw = bind(d_raw, *fc1_s)
    d_projected = exchange(d_raw).reshape(parts, rows, 3 * lanes)
    for mover in fc1_s:
        mover.pack()
    for mover in cross_s:
        mover.pack()
    for mover in fc1_s + cross_s:
        mover.move()
    d_projected = bind(d_projected, *fc1_s, *cross_s)
    total_fc1 = [mover.result() for mover in fc1_s]
    term_fc1 = settle(total_fc1)
    d_words = jnp.dot(d_words.reshape(-1, features), text_turn.T, preferred_element_type=F32)

    def split_term(left, right, cut):
        return [
            Scatter(cube, *halves(left, part), flip)
            for part, flip in ((right[:, :, :cut], 0), (right[:, :, cut:], 1))
        ]

    qkv_s = split_term(pre_attn, d_projected, qkv_cut)
    d_pre = mix("pmn,pkn->mk", d_projected, qkv_w)
    d_pre = bind(d_pre, *qkv_s)
    for mover in qkv_s:
        mover.pack()
    d_pre = bind(d_pre, *qkv_s)
    for mover in qkv_s:
        mover.move()
    d_shift = jnp.sum(d_pre.reshape(micros, slots, width), 1)
    d_stream0, d_gain_attn = norm_back(stream, g_attn, d_pre)
    d_base, d_gain_skip = norm_back(base, g_skip, grad1 + d_stream0)
    d_base = d_base.astype(BF)
    skip_s = split_term(d_base, joined, skip_cut)
    for mover in skip_s:
        mover.move()
    term_cross = settle([out1_s.result(), query2_s.result(), out2_s.result()])
    term_text = settle([text_s.result()])
    term_qkv = settle([mover.result() for mover in qkv_s])
    term_skip = settle([mover.result() for mover in skip_s])
    d_joined = mix("mn,pnk->pmk", d_base, skip_w)[:, :, :half].reshape(2, parts // 2, rows, half)
    d_joined = jnp.transpose(d_joined, (0, 2, 1, 3)).reshape(2, micros, slots, width)
    result = jnp.dot(result, turn.T, preferred_element_type=F32).astype(BF)

    d_shift = d_shift.reshape(micros, ranks, strip)
    d_shift = jnp.stack([d_shift[:, cube.masks.index(mask)] for mask in range(ranks)])
    d_shift = cube.add(cube.trade(d_shift), "sp").reshape(ranks * micros, strip)
    term_mod = lax.dot_general(
        time_part.astype(F32), d_shift, (((0,), (0,)), ((), ())), precision=lax.Precision.HIGHEST
    )

    places = jnp.array([cube.masks.index(mask) for mask in range(ranks)], jnp.int32)
    places = places[jnp.arange(ranks, dtype=jnp.int32) ^ cube.rank]
    gains = jnp.stack([d_gain_skip, d_gain_attn, d_gain_cross, d_gain_mlp])
    gains = gains.reshape(4, ranks, strip)[:, places].reshape(-1)
    heads = jnp.stack([jnp.sum(d_gain_q, (0, 1)), jnp.sum(d_gain_k, (0, 1))])
    heads = jnp.sum(heads.reshape(2, local, HP)[:, :, :HD], 1)
    packed = jnp.concatenate([gains, heads.reshape(-1)])
    packed = cube.add(cube.add(packed, "sp"), "dp")
    gains = packed[: 4 * width].reshape(4, ranks * parts, -1)
    gains = lax.dynamic_index_in_dim(gains, cube.rank * parts + zone, 1, keepdims=False)
    heads = packed[4 * width :].reshape(2, HD)

    def whole(term, groups):
        return cut_heads(term.astype(F32)).reshape(term.shape[0], groups, -1)

    return (
        result.reshape(tokens.shape),
        d_joined[0],
        d_joined[1],
        d_words.reshape(text.shape),
        term_skip.astype(F32)[:, :half].T,
        term_mod,
        whole(term_qkv, 3),
        cut_heads(term_cross[:, :lanes].astype(F32)).T,
        cut_heads(term_cross[:, lanes : 2 * lanes].astype(F32)),
        whole(term_text, 2),
        cut_heads(term_cross[:, 2 * lanes :].astype(F32)).T,
        term_fc1.astype(F32),
        term_fc2.astype(F32).T,
        gains[0],
        gains[1],
        gains[2],
        gains[3],
        heads[0],
        heads[1],
    )


def solution(mesh):
    rows = P(None, ("dp", "sp"), None)
    column = P("sp", "dp")
    row = P("dp", "sp")
    grouped = P("dp", None, "sp")
    in_specs = (
        (rows, rows, rows, P(None, "dp"), P(None, "dp", None), P(None, "dp", None))
        + (column, column, grouped, column, row, grouped, column, row, column)
        + (P(),) * 6
        + (rows,)
    )
    out_specs = (
        (rows, rows, rows, rows)
        + (column, column, grouped, column, row, grouped, column, row, column)
        + (P(("dp", "sp")),) * 4
        + (P(), P())
    )
    return jax.shard_map(
        on_device, mesh=mesh, in_specs=in_specs, out_specs=out_specs, check_vma=False
    )
```

```python
import math

import jax
import jax.numpy as jnp
from jax import lax
from jax.experimental import pallas as pl
from jax.experimental.pallas import tpu as pltpu
from jax.sharding import PartitionSpec as P

H = 16
HD = 88
HP = 96
CLIP_LEN = 77
ROWS = 256

EPS = 1e-06
MASKED = -1e30
LOG2E = 1.4426950408889634
BF = jnp.bfloat16
F32 = jnp.float32


def time_embed(step, width):
    half = width // 2
    rate = jnp.exp(-math.log(10000.0) * jnp.arange(half, dtype=F32) / half)
    angle = step.astype(F32)[..., None] * rate
    return jnp.concatenate([jnp.cos(angle), jnp.sin(angle)], -1)


def rope_tables(sequence, wide, lanes):
    place = jnp.arange(sequence, dtype=jnp.int32)[None, :, None]
    wide = wide[:, None, None]
    lane = jnp.arange(lanes, dtype=jnp.int32)[None, None, :] % HP
    pair = lane // 2
    quarter = HD // 4
    upper = pair < quarter
    rank = jnp.where(upper, pair, pair - quarter).astype(F32)
    rate = jnp.exp(-math.log(10000.0) * rank / quarter)
    angle = jnp.where(upper, place // wide, place % wide).astype(F32) * rate
    sine = jnp.sin(angle)
    return jnp.cos(angle), jnp.where(lane % 2 == 0, -sine, sine)


def pad_heads(packed, local):
    rows, lanes = packed.shape
    groups = packed.reshape(rows, lanes // (local * HD), local, HD)
    groups = jnp.pad(groups, ((0, 0), (0, 0), (0, 0), (0, HP - HD)))
    groups = groups.reshape(rows, -1, local * HP)
    return jnp.pad(groups, ((0, 0), (0, 0), (0, -local * HP % 128))).reshape(rows, -1)


def cut_heads(padded, local):
    rows = padded.shape[0]
    groups = padded.reshape(rows, -1, local * HP + -local * HP % 128)[:, :, : local * HP]
    return groups.reshape(rows, -1, local, HP)[..., :HD].reshape(rows, -1)


def head_masks(shape, local):
    lane = lax.broadcasted_iota(jnp.int32, shape, len(shape) - 1)
    inside = lane % HP < HD
    return [((lane // HP == h) & inside).astype(F32) for h in range(local)]


def head_mean(value, masks):
    total = None
    for mask in masks:
        term = (jnp.sum(value * mask, -1, keepdims=True) * (1.0 / HD)) * mask
        total = term if total is None else total + term
    return total


def head_unit(value, masks):
    centre = value - head_mean(value, masks)
    spread = None
    square = centre * centre
    for mask in masks:
        mean = jnp.sum(square * mask, -1, keepdims=True) * (1.0 / HD)
        term = lax.rsqrt(mean + EPS) * mask
        spread = term if spread is None else spread + term
    return centre * spread, spread


def turn_pairs(value):
    lanes = value.shape[-1]
    after = pltpu.roll(value, lanes - 1, 1)
    before = pltpu.roll(value, 1, 1)
    lane = lax.broadcasted_iota(jnp.int32, value.shape, 1)
    return jnp.where(lane % 2 == 0, after, before)


def dot_nt(left, right):
    return lax.dot_general(left, right, (((1,), (1,)), ((), ())), preferred_element_type=F32)


def dot_nn(left, right):
    return lax.dot_general(left, right, (((1,), (0,)), ((), ())), preferred_element_type=F32)


def dot_tn(left, right):
    return lax.dot_general(left, right, (((0,), (0,)), ((), ())), preferred_element_type=F32)


def self_forward(raw, counts, cosine, sine, gain_q, gain_k):
    parts, micros, slots, packed = raw.shape
    lanes = packed // 3
    local = lanes // HP
    sequence = parts * slots
    factor = HD ** (-0.5) * LOG2E

    def kernel(count_ref, raw_ref, cos_ref, sin_ref, gq_ref, gk_ref, out_ref, q_ref, k_ref, lse_ref):
        count = count_ref[pl.program_id(0)]
        blocks = (count + slots - 1) // slots
        out_ref[...] = jnp.zeros_like(out_ref)
        masks = head_masks((1, lanes), local)

        def prepare(part, carry):
            spot = pl.ds(pl.multiple_of(part * slots, slots), slots)
            cosine, sine = cos_ref[0, spot, :], sin_ref[0, spot, :]
            for index, gain_ref, dest in ((0, gq_ref, q_ref), (1, gk_ref, k_ref)):
                value = raw_ref[part, 0, :, index * lanes : (index + 1) * lanes].astype(F32)
                scaled = head_unit(value, masks)[0] * gain_ref[...]
                dest[0, spot, :] = (scaled * cosine + turn_pairs(scaled) * sine).astype(BF)
            return carry

        lax.fori_loop(0, parts, prepare, 0)
        column = lax.broadcasted_iota(jnp.int32, (1, sequence), 1)
        bias = jnp.where(column < count, 0.0, MASKED)
        for h in range(local):
            cut = slice(h * HP, (h + 1) * HP)
            keys = k_ref[0, :, cut]
            values = raw_ref[:, 0, :, 2 * lanes + h * HP : 2 * lanes + (h + 1) * HP].reshape(sequence, HP)

            def one_block(part, carry):
                spot = pl.ds(pl.multiple_of(part * slots, slots), slots)
                scores = dot_nt(q_ref[0, spot, cut], keys) + bias
                top = jnp.max(scores, -1, keepdims=True)
                raised = jnp.exp2((scores - top) * factor)
                total = jnp.sum(raised, -1, keepdims=True)
                result = dot_nn(raised.astype(BF), values) / total
                out_ref[part, 0, :, cut] = result.astype(BF)
                norm = jnp.broadcast_to(top * factor + jnp.log2(total), (slots, 128))
                lse_ref[0, h : h + 1, spot] = jnp.transpose(norm)[0:1, :]
                return carry

            lax.fori_loop(0, blocks, one_block, 0)

    whole = lambda m, c: (0, m, 0, 0)
    table = lambda m, c: (m, 0, 0)
    fixed = lambda m, c: (0, 0)
    return pl.pallas_call(
        kernel,
        name="self_forward",
        grid_spec=pltpu.PrefetchScalarGridSpec(
            num_scalar_prefetch=1,
            grid=(micros,),
            in_specs=[
                pl.BlockSpec((parts, 1, slots, packed), whole),
                pl.BlockSpec((1, sequence, lanes), table),
                pl.BlockSpec((1, sequence, lanes), table),
                pl.BlockSpec((1, lanes), fixed),
                pl.BlockSpec((1, lanes), fixed),
            ],
            out_specs=[
                pl.BlockSpec((parts, 1, slots, lanes), whole),
                pl.BlockSpec((1, sequence, lanes), table),
                pl.BlockSpec((1, sequence, lanes), table),
                pl.BlockSpec((1, local, sequence), table),
            ],
        ),
        out_shape=[
            jax.ShapeDtypeStruct((parts, micros, slots, lanes), BF),
            jax.ShapeDtypeStruct((micros, sequence, lanes), BF),
            jax.ShapeDtypeStruct((micros, sequence, lanes), BF),
            jax.ShapeDtypeStruct((micros, local, sequence), F32),
        ],
        compiler_params=pltpu.CompilerParams(vmem_limit_bytes=48 << 20),
        cost_estimate=cost(4 * micros * local * sequence * sequence * HP),
    )(counts, raw, cosine, sine, gain_q, gain_k)


def self_backward(raw, counts, cosine, sine, gain_q, gain_k, turned_q, turned_k, norms, incoming):
    parts, micros, slots, packed = raw.shape
    lanes = packed // 3
    local = lanes // HP
    sequence = parts * slots
    scale = HD ** (-0.5)
    factor = scale * LOG2E

    def kernel(
        count_ref,
        raw_ref,
        cos_ref,
        sin_ref,
        gq_ref,
        gk_ref,
        q_ref,
        k_ref,
        lse_ref,
        in_ref,
        out_ref,
        dgq_ref,
        dgk_ref,
        dq_s,
        dk_s,
        dv_s,
    ):
        count = count_ref[pl.program_id(0)]
        blocks = (count + slots - 1) // slots
        dq_s[...] = jnp.zeros_like(dq_s)
        dk_s[...] = jnp.zeros_like(dk_s)
        dv_s[...] = jnp.zeros_like(dv_s)
        row = lax.broadcasted_iota(jnp.int32, (sequence, 1), 0)
        bias = jnp.where(row < count, 0.0, MASKED)
        for h in range(local):
            cut = slice(h * HP, (h + 1) * HP)
            keys = k_ref[0, :, cut]
            values = raw_ref[:, 0, :, 2 * lanes + h * HP : 2 * lanes + (h + 1) * HP].reshape(sequence, HP)

            def one_block(part, carry):
                spot = pl.ds(pl.multiple_of(part * slots, slots), slots)
                rows = q_ref[0, spot, cut]
                grads = in_ref[part, 0, :, cut]
                norm = lse_ref[0, h : h + 1, spot]
                probs = jnp.exp2(dot_nt(keys, rows) * factor + bias - norm)
                d_probs = dot_nt(values, grads)
                inner = jnp.sum(probs * d_probs, 0, keepdims=True)
                d_scores = (probs * (d_probs - inner)).astype(BF)
                dv_s[:, cut] += dot_nn(probs.astype(BF), grads)
                dk_s[:, cut] += dot_nn(d_scores, rows)
                dq_s[spot, cut] = dot_tn(d_scores, keys)
                return carry

            lax.fori_loop(0, blocks, one_block, 0)
        masks = head_masks((1, lanes), local)

        def finish(part, carry):
            spot = pl.ds(pl.multiple_of(part * slots, slots), slots)
            cosine, sine = cos_ref[0, spot, :], sin_ref[0, spot, :]
            sums = []
            for index, gain_ref, source in ((0, gq_ref, dq_s), (1, gk_ref, dk_s)):
                grad = source[spot, :] * scale
                grad = grad * cosine - turn_pairs(grad) * sine
                value = raw_ref[part, 0, :, index * lanes : (index + 1) * lanes].astype(F32)
                unit, spread = head_unit(value, masks)
                leading = grad * gain_ref[...]
                back = leading - head_mean(leading, masks) - unit * head_mean(leading * unit, masks)
                out_ref[part, 0, :, index * lanes : (index + 1) * lanes] = (spread * back).astype(BF)
                sums.append(carry[index] + jnp.sum(grad * unit, 0, keepdims=True))
            out_ref[part, 0, :, 2 * lanes : 3 * lanes] = dv_s[spot, :].astype(BF)
            return tuple(sums)

        zero = jnp.zeros((1, lanes), F32)
        d_gains = lax.fori_loop(0, parts, finish, (zero, zero))
        dgq_ref[0] = d_gains[0]
        dgk_ref[0] = d_gains[1]

    whole = lambda m, c: (0, m, 0, 0)
    table = lambda m, c: (m, 0, 0)
    fixed = lambda m, c: (0, 0)
    return pl.pallas_call(
        kernel,
        name="self_backward",
        grid_spec=pltpu.PrefetchScalarGridSpec(
            num_scalar_prefetch=1,
            grid=(micros,),
            in_specs=[
                pl.BlockSpec((parts, 1, slots, packed), whole),
                pl.BlockSpec((1, sequence, lanes), table),
                pl.BlockSpec((1, sequence, lanes), table),
                pl.BlockSpec((1, lanes), fixed),
                pl.BlockSpec((1, lanes), fixed),
                pl.BlockSpec((1, sequence, lanes), table),
                pl.BlockSpec((1, sequence, lanes), table),
                pl.BlockSpec((1, local, sequence), table),
                pl.BlockSpec((parts, 1, slots, lanes), whole),
            ],
            out_specs=[
                pl.BlockSpec((parts, 1, slots, packed), whole),
                pl.BlockSpec((1, 1, lanes), table),
                pl.BlockSpec((1, 1, lanes), table),
            ],
            scratch_shapes=[pltpu.VMEM((sequence, lanes), F32) for index in range(3)],
        ),
        out_shape=[
            jax.ShapeDtypeStruct((parts, micros, slots, packed), BF),
            jax.ShapeDtypeStruct((micros, 1, lanes), F32),
            jax.ShapeDtypeStruct((micros, 1, lanes), F32),
        ],
        compiler_params=pltpu.CompilerParams(vmem_limit_bytes=48 << 20),
        cost_estimate=cost(10 * micros * local * sequence * sequence * HP),
    )(counts, raw, cosine, sine, gain_q, gain_k, turned_q, turned_k, norms, incoming)


def cost(flops):
    return pl.CostEstimate(flops=flops, bytes_accessed=flops // 1000, transcendentals=0)


def full(shape):
    return pl.BlockSpec(shape, lambda *index: (0,) * len(shape))


def params(megabytes=48):
    return pltpu.CompilerParams(vmem_limit_bytes=megabytes << 20)


class Lanes:
    def __init__(self, near, far, block=None, index=0):
        self.near, self.far = near, far
        self.block = block or near.shape[2]
        self.index = index

    def spec(self):
        index = self.index
        return pl.BlockSpec((1, self.near.shape[1], self.block), lambda p, *rest: (p, 0, index))


def to_lanes(value, weights, dtype=BF, name="to_lanes"):
    rows = value.shape[1]
    parts, half, _ = weights[0].near.shape
    total = sum(weight.block for weight in weights)

    def kernel(x_ref, *refs):
        out_ref = refs[-1]
        at = 0
        for index, weight in enumerate(weights):
            result = dot_nn(x_ref[0], refs[2 * index][0]) + dot_nn(x_ref[1], refs[2 * index + 1][0])
            out_ref[0, :, at : at + weight.block] = result.astype(dtype)
            at += weight.block

    return pl.pallas_call(
        kernel,
        name=name,
        grid=(parts,),
        in_specs=[full(value.shape)] + [weight.spec() for weight in weights for side in range(2)],
        out_specs=pl.BlockSpec((1, rows, total), lambda p: (p, 0, 0)),
        out_shape=jax.ShapeDtypeStruct((parts, rows, total), dtype),
        compiler_params=params(),
        cost_estimate=cost(4 * rows * half * parts * total),
    )(value, *[side for weight in weights for side in (weight.near, weight.far)])


def to_inputs(value, weights, kept):
    rows = value.shape[1]
    parts, half, _ = weights[0].near.shape
    sides = parts // 2

    def kernel(x_ref, *refs):
        out_ref = refs[-1]
        for side in range(sides):

            @pl.when(pl.program_id(0) % sides == side)
            def _():
                at = 0
                for index, weight in enumerate(weights):
                    result = dot_nn(x_ref[0], refs[2 * index][0]) + dot_nn(
                        x_ref[1], refs[2 * index + 1][0]
                    )
                    take = min(weight.block, kept - at)
                    start = side * kept + at
                    out_ref[0, :, start : start + take] = result[:, :take]
                    at += take

    return pl.pallas_call(
        kernel,
        name="to_inputs",
        grid=(parts,),
        in_specs=[full(value.shape)] + [weight.spec() for weight in weights for side in range(2)],
        out_specs=pl.BlockSpec((1, rows, sides * kept), lambda p: (p // sides, 0, 0)),
        out_shape=jax.ShapeDtypeStruct((2, rows, sides * kept), F32),
        compiler_params=params(),
        cost_estimate=cost(4 * rows * half * parts * kept),
    )(value, *[side for weight in weights for side in (weight.near, weight.far)])


def to_features(value, weights, extras, outs, finish, name="to_features"):
    parts, rows, total = value.shape
    half = weights[0].near.shape[1]
    count = 2 * len(weights)

    def kernel(*refs):
        y_ref, weight_refs = refs[0], refs[1 : 1 + count]
        extra_refs = refs[1 + count : 1 + count + len(extras)]
        out_refs = refs[1 + count + len(extras) : -1]
        sums = refs[-1]

        @pl.when(pl.program_id(0) == 0)
        def _():
            sums[...] = jnp.zeros_like(sums)

        at = 0
        for index, weight in enumerate(weights):
            left = y_ref[0, :, at : at + weight.block]
            for side in range(2):
                sums[side] += dot_nt(left, weight_refs[2 * index + side][0])
            at += weight.block

        @pl.when(pl.program_id(0) == parts - 1)
        def _():
            finish([sums[0], sums[1]], extra_refs, out_refs)

    return pl.pallas_call(
        kernel,
        name=name,
        grid=(parts,),
        in_specs=[pl.BlockSpec((1, rows, total), lambda p: (p, 0, 0))]
        + [weight.spec() for weight in weights for side in range(2)]
        + [full(extra.shape) for extra in extras],
        out_specs=[full(out.shape) for out in outs],
        out_shape=outs,
        scratch_shapes=[pltpu.VMEM((2, rows, half), F32)],
        compiler_params=params(56),
        cost_estimate=cost(4 * rows * half * parts * total),
    )(value, *[side for weight in weights for side in (weight.near, weight.far)], *extras)


def terms_of(pairs, name="terms_of"):
    half = pairs[0][0].shape[2]
    parts = pairs[0][1].shape[0]
    total = sum(pair[2] for pair in pairs)
    rows = [pair[0].shape[1] for pair in pairs]

    def kernel(*refs):
        count = len(pairs)
        lefts, rights = refs[:count], refs[count : 2 * count]
        near_ref, far_ref = refs[2 * count : 2 * count + 2]
        turned = refs[2 * count + 2 :]

        @pl.when(pl.program_id(0) == 0)
        def _():
            for left, flat in zip(lefts, turned):
                for side in range(2):
                    flat[side] = jnp.transpose(left[side])

        at = 0
        for pair, right, flat in zip(pairs, rights, turned):
            lanes = pair[2]
            near_ref[0, :, at : at + lanes] = dot_nn(flat[0], right[0]).astype(BF)
            far_ref[0, :, at : at + lanes] = dot_nn(flat[1], right[0]).astype(BF)
            at += lanes

    def right_spec(pair):
        return pl.BlockSpec((1, pair[1].shape[1], pair[2]), lambda p: (p, 0, pair[3]))

    out = jax.ShapeDtypeStruct((parts, half, total), BF)
    return pl.pallas_call(
        kernel,
        name=name,
        grid=(parts,),
        in_specs=[full(pair[0].shape) for pair in pairs] + [right_spec(pair) for pair in pairs],
        out_specs=[pl.BlockSpec((1, half, total), lambda p: (p, 0, 0))] * 2,
        out_shape=[out, out],
        scratch_shapes=[pltpu.VMEM((2, half, count), BF) for count in rows],
        compiler_params=params(),
        cost_estimate=cost(sum(4 * half * parts * pair[2] * count for pair, count in zip(pairs, rows))),
    )(*[pair[0] for pair in pairs], *[pair[1] for pair in pairs])


def norm_unit(halves):
    width = 2 * halves[0].shape[-1]
    mean = sum(jnp.sum(half, -1, keepdims=True) for half in halves) / width
    centre = [half - mean for half in halves]
    spread = sum(jnp.sum(half * half, -1, keepdims=True) for half in centre) / width
    scale = lax.rsqrt(spread + EPS)
    return [half * scale for half in centre], scale


def norm_back(halves, gain_ref, incoming):
    width = 2 * halves[0].shape[-1]
    unit, scale = norm_unit(halves)
    leading = [incoming[side] * gain_ref[side] for side in range(2)]
    mean = sum(jnp.sum(half, -1, keepdims=True) for half in leading) / width
    inner = sum(jnp.sum(leading[side] * unit[side], -1, keepdims=True) for side in range(2)) / width
    back = [scale * (leading[side] - mean - unit[side] * inner) for side in range(2)]
    gains = [jnp.sum(incoming[side] * unit[side], 0, keepdims=True) for side in range(2)]
    return back, gains


def join_rows(pieces, name="join_rows"):
    parts, rows, lanes = pieces[0].shape
    count = len(pieces)
    if rows % 16:
        return jnp.concatenate(pieces, 1)

    def kernel(*refs):
        for index in range(count):

            @pl.when(pl.program_id(1) == index)
            def _():
                refs[-1][...] = refs[index][...]

    return pl.pallas_call(
        kernel,
        name=name,
        grid=(parts, count),
        in_specs=[pl.BlockSpec((1, rows, lanes), lambda p, i: (p, 0, 0))] * count,
        out_specs=pl.BlockSpec((1, rows, lanes), lambda p, i: (p, i, 0)),
        out_shape=jax.ShapeDtypeStruct((parts, count * rows, lanes), BF),
        compiler_params=params(24),
        cost_estimate=cost(parts * count * rows * lanes),
    )(*pieces)


def sum_rows(terms, rows, count, name="sum_rows"):
    parts, _, lanes = terms[0][0].shape
    if rows % 16:
        value = 0.0
        for array, first, step in terms:
            blocks = array.reshape(parts, -1, rows, lanes)[:, first :: step][:, :count]
            value = value + blocks.astype(F32)
        return value.astype(BF).reshape(parts, count * rows, lanes)

    def kernel(*refs):
        value = refs[0][...].astype(F32)
        for ref in refs[1:-1]:
            value = value + ref[...].astype(F32)
        refs[-1][...] = value.astype(BF)

    def spec(first, step):
        return pl.BlockSpec((1, rows, lanes), lambda p, i: (p, first + step * i, 0))

    return pl.pallas_call(
        kernel,
        name=name,
        grid=(parts, count),
        in_specs=[spec(first, step) for _, first, step in terms],
        out_specs=spec(0, 1),
        out_shape=jax.ShapeDtypeStruct((parts, count * rows, lanes), BF),
        compiler_params=params(24),
        cost_estimate=cost(parts * count * rows * lanes),
    )(*[term[0] for term in terms])


def side_by_side(left, right, kept, lanes):
    rows, width = left.shape
    count = width // kept

    def kernel(left_ref, right_ref, out_ref):
        for index, ref in enumerate((left_ref, right_ref)):
            for side in range(count):
                spot = count * index + side
                out_ref[spot, :, :kept] = ref[:, side * kept : (side + 1) * kept]
                if lanes > kept:
                    out_ref[spot, :, kept:] = jnp.zeros((rows, lanes - kept), BF)

    return pl.pallas_call(
        kernel,
        name="side_by_side",
        out_shape=jax.ShapeDtypeStruct((2 * count, rows, lanes), BF),
        compiler_params=params(24),
        cost_estimate=cost(4 * rows * lanes),
    )(left, right)


def mlp_forward(rows_in, grads, start, weight1, weight2, part, live=None):
    _, rows, half = rows_in.shape
    parts, _, lanes = weight1.near.shape
    ff = lanes // 2
    step = 384 if ff % 384 == 0 else ff
    steps = ff // step
    extras = [] if live is None else [live]

    def kernel(x_ref, g_ref, s_ref, n1_ref, f1_ref, n2_ref, f2_ref, *refs):
        hid_ref, act_ref, out_ref, dn2_ref, df2_ref, turned, sums = refs[len(extras) :]
        first = (pl.program_id(0) == 0) & (pl.program_id(1) == 0)
        last = (pl.program_id(0) == parts - 1) & (pl.program_id(1) == steps - 1)

        @pl.when(first)
        def _():
            for side in range(2):
                turned[side] = jnp.transpose(g_ref[side])
            sums[...] = s_ref[...]

        hidden = dot_nn(x_ref[0], n1_ref[0]) + dot_nn(x_ref[1], f1_ref[0])
        hid_ref[0] = hidden
        activ = jax.nn.gelu(hidden, approximate=True).astype(BF)
        act_ref[0] = activ
        sums[0] += dot_nt(activ, n2_ref[0])
        sums[1] += dot_nt(activ, f2_ref[0])
        dn2_ref[0] = dot_nn(turned[0], activ).astype(BF)
        df2_ref[0] = dot_nn(turned[1], activ).astype(BF)

        @pl.when(last)
        def _():
            if live is None:
                out_ref[...] = sums[...]
            else:
                out_ref[...] = (sums[...] * refs[0][...]).astype(BF)

    weight = pl.BlockSpec((1, half, step), lambda p, n: (p, 0, part * steps + n))
    grad = pl.BlockSpec((1, half, step), lambda p, n: (p, 0, n))
    unit = pl.BlockSpec((1, rows, step), lambda p, n: (p, 0, n))
    whole = full((2, rows, half))
    grad_shape = jax.ShapeDtypeStruct((parts, half, ff), BF)
    return pl.pallas_call(
        kernel,
        name="mlp_forward",
        grid=(parts, steps),
        in_specs=[whole, whole, whole, weight, weight, weight, weight] + [full(extra.shape) for extra in extras],
        out_specs=[unit, unit, whole, grad, grad],
        out_shape=[
            jax.ShapeDtypeStruct((parts, rows, ff), F32),
            jax.ShapeDtypeStruct((parts, rows, ff), BF),
            jax.ShapeDtypeStruct((2, rows, half), F32 if live is None else BF),
            grad_shape,
            grad_shape,
        ],
        scratch_shapes=[pltpu.VMEM((2, half, rows), BF), pltpu.VMEM((2, rows, half), F32)],
        compiler_params=params(),
        cost_estimate=cost(12 * rows * half * parts * ff),
    )(rows_in, grads, start, weight1.near, weight1.far, weight2.near, weight2.far, *extras)


def gelu_slope(value):
    root = math.sqrt(2.0 / math.pi)
    square = value * value
    curve = jnp.tanh(root * value * (1.0 + 0.044715 * square))
    return 0.5 * (1.0 + curve) + 0.5 * value * (1.0 - curve * curve) * root * (
        1.0 + 3.0 * 0.044715 * square
    )


def mlp_backward(grads, rows_in, hidden, weight1, weight2, part, start, finish=None):
    _, rows, half = rows_in.shape
    parts, _, lanes = weight1.near.shape
    ff = lanes // 2
    step = 384 if ff % 384 == 0 else ff
    steps = ff // step
    extras = list(finish or []) + ([] if start is None else [start])

    def kernel(g_ref, x_ref, hid_ref, n1_ref, f1_ref, n2_ref, f2_ref, *refs):
        extra_refs, refs = refs[: len(extras)], refs[len(extras) :]
        dn1_ref, df1_ref = refs[:2]
        out_refs = refs[2:-2]
        turned, sums = refs[-2:]
        first = (pl.program_id(0) == 0) & (pl.program_id(1) == 0)
        last = (pl.program_id(0) == parts - 1) & (pl.program_id(1) == steps - 1)

        @pl.when(first)
        def _():
            for side in range(2):
                turned[side] = jnp.transpose(x_ref[side])
            sums[...] = jnp.zeros_like(sums) if start is None else extra_refs[-1][...]

        d_activ = dot_nn(g_ref[0], n2_ref[0]) + dot_nn(g_ref[1], f2_ref[0])
        d_hidden = (d_activ * gelu_slope(hid_ref[0])).astype(BF)
        dn1_ref[0] = dot_nn(turned[0], d_hidden).astype(BF)
        df1_ref[0] = dot_nn(turned[1], d_hidden).astype(BF)
        sums[0] += dot_nt(d_hidden, n1_ref[0])
        sums[1] += dot_nt(d_hidden, f1_ref[0])

        @pl.when(last)
        def _():
            if finish is None:
                out_refs[0][...] = sums[...]
            else:
                value_ref, gain_ref, add_ref = extra_refs[:3]
                add_norm_back([sums[0], sums[1]], value_ref, gain_ref, add_ref, *out_refs)

    weight = pl.BlockSpec((1, half, step), lambda p, n: (p, 0, part * steps + n))
    grad = pl.BlockSpec((1, half, step), lambda p, n: (p, 0, n))
    unit = pl.BlockSpec((1, rows, step), lambda p, n: (p, 0, n))
    whole = full((2, rows, half))
    grad_shape = jax.ShapeDtypeStruct((parts, half, ff), BF)
    wide = jax.ShapeDtypeStruct((2, rows, half), F32)
    outs = [wide] if finish is None else [wide, *back_shapes(rows, half)]
    return pl.pallas_call(
        kernel,
        name="mlp_backward",
        grid=(parts, steps),
        in_specs=[whole, whole, unit, weight, weight, weight, weight] + [full(extra.shape) for extra in extras],
        out_specs=[grad, grad] + [full(out.shape) for out in outs],
        out_shape=[grad_shape, grad_shape] + outs,
        scratch_shapes=[pltpu.VMEM((2, half, rows), BF), pltpu.VMEM((2, rows, half), F32)],
        compiler_params=params(56),
        cost_estimate=cost(12 * rows * half * parts * ff),
    )(grads, rows_in, hidden, weight1.near, weight1.far, weight2.near, weight2.far, *extras)


def back_shapes(rows, half):
    return [jax.ShapeDtypeStruct((2, rows, half), BF), jax.ShapeDtypeStruct((2, 1, half), F32)]


def add_norm_back(incoming, value_ref, gain_ref, add_ref, out_ref, low_ref, d_gain_ref):
    back, gains = norm_back([value_ref[0], value_ref[1]], gain_ref, incoming)
    for side in range(2):
        total = add_ref[side] + back[side]
        out_ref[side] = total
        low_ref[side] = total.astype(BF)
        d_gain_ref[side] = gains[side]


def text_bias(lengths_ref, micro, words, strip, text_slots, axis):
    spot = lax.broadcasted_iota(jnp.int32, (1, words) if axis else (words, 1), axis)
    inner = spot % strip
    place = spot // strip * text_slots + inner
    live = (place < lengths_ref[micro, 0]) | (
        (place >= CLIP_LEN) & (place < CLIP_LEN + lengths_ref[micro, 1])
    )
    return jnp.where(live & (inner < text_slots), 0.0, MASKED)


def cross_forward(query, text_kv, lengths, text_slots):
    parts, micros, slots, lanes = query.shape
    zones, strip = text_kv.shape[1], text_kv.shape[3]
    words = zones * strip
    local = lanes // HP
    factor = HD ** (-0.5) * LOG2E

    def kernel(len_ref, q_ref, kv_ref, out_ref):
        bias = text_bias(len_ref, pl.program_id(1), words, strip, text_slots, 1)
        for h in range(local):
            cut = slice(h * HP, (h + 1) * HP)
            keys = kv_ref[0, :, 0, :, cut].reshape(words, HP)
            scores = dot_nt(q_ref[0, 0, :, cut], keys) + bias
            top = jnp.max(scores, -1, keepdims=True)
            raised = jnp.exp2((scores - top) * factor)
            total = jnp.sum(raised, -1, keepdims=True)
            values = kv_ref[0, :, 0, :, lanes + h * HP : lanes + (h + 1) * HP].reshape(words, HP)
            out_ref[0, 0, :, cut] = (dot_nn(raised.astype(BF), values) / total).astype(BF)

    spot = lambda p, m, c: (p, m, 0, 0)
    far = lambda p, m, c: (p, 0, m, 0, 0)
    return pl.pallas_call(
        kernel,
        name="cross_forward",
        grid_spec=pltpu.PrefetchScalarGridSpec(
            num_scalar_prefetch=1,
            grid=(parts, micros),
            in_specs=[
                pl.BlockSpec((1, 1, slots, lanes), spot),
                pl.BlockSpec((1, zones, 1, strip, 2 * lanes), far),
            ],
            out_specs=pl.BlockSpec((1, 1, slots, lanes), spot),
        ),
        out_shape=jax.ShapeDtypeStruct(query.shape, BF),
        compiler_params=pltpu.CompilerParams(vmem_limit_bytes=32 << 20),
        cost_estimate=cost(4 * parts * micros * slots * words * lanes),
    )(lengths, query, text_kv)


def cross_backward(query, text_kv, lengths, incoming, text_slots):
    parts, micros, slots, lanes = query.shape
    zones, strip = text_kv.shape[1], text_kv.shape[3]
    words = zones * strip
    local = lanes // HP
    scale = HD ** (-0.5)
    factor = scale * LOG2E

    def kernel(len_ref, q_ref, kv_ref, in_ref, dq_ref, dkv_ref):
        bias = text_bias(len_ref, pl.program_id(1), words, strip, text_slots, 0)
        for h in range(local):
            cut = slice(h * HP, (h + 1) * HP)
            far = slice(lanes + h * HP, lanes + (h + 1) * HP)
            rows = q_ref[0, 0, :, cut]
            keys = kv_ref[0, :, 0, :, cut].reshape(words, HP)
            values = kv_ref[0, :, 0, :, far].reshape(words, HP)
            grads = in_ref[0, 0, :, cut]
            scores = dot_nt(keys, rows) + bias
            top = jnp.max(scores, 0, keepdims=True)
            raised = jnp.exp2((scores - top) * factor)
            probs = raised * (1.0 / jnp.sum(raised, 0, keepdims=True))
            d_probs = dot_nt(values, grads)
            inner = jnp.sum(probs * d_probs, 0, keepdims=True)
            d_scores = (probs * (d_probs - inner)).astype(BF)
            shape = (zones, strip, HP)
            dkv_ref[0, :, 0, :, far] = dot_nn(probs.astype(BF), grads).astype(BF).reshape(shape)
            dkv_ref[0, :, 0, :, cut] = (dot_nn(d_scores, rows) * scale).astype(BF).reshape(shape)
            dq_ref[0, 0, :, cut] = (dot_tn(d_scores, keys) * scale).astype(BF)

    spot = lambda p, m, c: (p, m, 0, 0)
    far = lambda p, m, c: (p, 0, m, 0, 0)
    return pl.pallas_call(
        kernel,
        name="cross_backward",
        grid_spec=pltpu.PrefetchScalarGridSpec(
            num_scalar_prefetch=1,
            grid=(parts, micros),
            in_specs=[
                pl.BlockSpec((1, 1, slots, lanes), spot),
                pl.BlockSpec((1, zones, 1, strip, 2 * lanes), far),
                pl.BlockSpec((1, 1, slots, lanes), spot),
            ],
            out_specs=[
                pl.BlockSpec((1, 1, slots, lanes), spot),
                pl.BlockSpec((1, zones, 1, strip, 2 * lanes), far),
            ],
        ),
        out_shape=[
            jax.ShapeDtypeStruct(query.shape, BF),
            jax.ShapeDtypeStruct(text_kv.shape, BF),
        ],
        compiler_params=pltpu.CompilerParams(vmem_limit_bytes=32 << 20),
        cost_estimate=cost(10 * parts * micros * slots * words * lanes),
    )(lengths, query, text_kv, incoming)


def tie(*values):
    return lax.optimization_barrier(values)


class Cube:
    def __init__(self):
        self.size = lax.axis_size("dp")
        self.bits = self.size.bit_length() - 1
        self.outer = list(range(1, self.bits))
        self.rank = lax.axis_index("dp")
        self.masks = []
        for place in range(self.size):
            mask = place >> (self.bits - 1)
            for bit in self.outer:
                mask |= ((place >> (bit - 1)) & 1) << bit
            self.masks.append(mask)
        self.owners = self.rank ^ jnp.array(self.masks, jnp.int32)

    def swap(self, value, bit, axis="dp"):
        pairs = [(i, i ^ (1 << bit)) for i in range(lax.axis_size(axis))]
        return lax.ppermute(value, axis, pairs)

    def trade(self, value):
        blocks = {mask: value[mask] for mask in range(self.size)}
        for bit in range(self.bits):
            send = sorted(mask for mask in blocks if mask >> bit & 1)
            got = self.swap(jnp.stack([blocks[mask] for mask in send]), bit)
            for place, mask in enumerate(send):
                blocks[mask] = got[place]
        return jnp.stack([blocks[mask] for mask in range(self.size)])

    def spread(self, value):
        held = value[None]
        for bit in range(self.bits):
            held = jnp.concatenate([held, self.swap(held, bit)])
        return held

    def add(self, value, axis):
        for bit in range(lax.axis_size(axis).bit_length() - 1):
            value = value + self.swap(value, bit, axis)
        return value


class Gather:
    def __init__(self, cube, shard, flip):
        self.cube = cube
        self.masks = [0]
        self.pieces = [shard]
        self.todo = cube.outer[::-1] if flip else list(cube.outer)

    def move(self):
        bit = self.todo.pop(0)
        self.masks = self.masks + [mask | (1 << bit) for mask in self.masks]
        self.pieces = self.pieces + [self.cube.swap(piece, bit) for piece in self.pieces]

    def join(self):
        while self.todo:
            self.move()
        order = sorted(range(len(self.masks)), key=lambda i: self.cube.masks.index(self.masks[i]))
        self.pieces = [join_rows([self.pieces[i] for i in order])]

    def weight(self):
        near = self.pieces[0]
        return Lanes(near, self.cube.swap(near, 0))


class Scatter:
    def __init__(self, cube, near, far, flip):
        self.cube = cube
        self.todo = list(cube.outer) if flip else cube.outer[::-1]
        self.rows = near.shape[1] // (cube.size // 2)
        self.places = list(range(cube.size // 2))
        self.near = near
        self.got = []
        self.pieces = [cube.swap(far, 0)]
        self.arriving = self.places
        self.packed = False

    def total(self, places):
        first = places[0]
        step = places[1] - first if len(places) > 1 else 1
        terms = [(self.near, first, step)]
        for value, held in self.got:
            spots = [held.index(place) for place in places]
            terms.append((value, spots[0], spots[1] - spots[0] if len(spots) > 1 else 1))
        return sum_rows(terms, self.rows, len(places))

    def absorb(self):
        self.got.append((self.pieces[0], self.arriving))

    def pack(self):
        self.absorb()
        self.bit = self.todo.pop(0)
        weight = 1 << (self.bit - 1)
        sent = [place for place in self.places if place & weight]
        self.places = [place for place in self.places if not place & weight]
        self.arriving = [place ^ weight for place in sent]
        self.pieces = [self.total(sent)]
        self.packed = True

    def move(self):
        if not self.packed:
            self.pack()
        self.pieces = [self.cube.swap(self.pieces[0], self.bit)]
        self.packed = False

    def result(self):
        while self.todo or self.packed:
            self.move()
        self.absorb()
        return self.total([0])


def bind(value, *movers):
    flat = [piece for mover in movers for piece in mover.pieces]
    held = tie(value, *flat)
    spot = 1
    for mover in movers:
        count = len(mover.pieces)
        mover.pieces = list(held[spot : spot + count])
        spot += count
    return held[0]


def on_device(
    tokens,
    skip_tokens,
    text,
    timestep,
    grid,
    text_len,
    w_skip,
    w_mod,
    w_qkv,
    w_out1,
    w_query2,
    w_text_kv,
    w_out2,
    w_fc1,
    w_fc2,
    gain_skip,
    gain_attn,
    gain_cross,
    gain_mlp,
    gain_query,
    gain_key,
    cotangent,
):
    micros, slots, width = tokens.shape
    parts = lax.axis_size("sp")
    zone = lax.axis_index("sp")
    cube = Cube()
    ranks = cube.size
    rows = micros * slots
    sequence = slots * parts
    local = H // parts
    lanes = local * HP + -local * HP % 128
    text_slots = text.shape[1]
    text_strip = -(-text_slots // 16) * 16
    features = text.shape[2]
    strip = width // ranks
    middle = width // 2
    kept = w_skip.shape[0]
    skip_lanes = -(-kept // 256) * 256
    skip_cut = skip_lanes // 2
    qkv_cut = (3 * lanes) // 256 * 128 + 128
    text_rows = w_text_kv.shape[0]

    def spread(shard, before=None):
        if before is not None:
            shard, before = tie(shard, before)
        return lax.all_gather(shard, "sp", axis=0, tiled=False)

    def fetch(value, cut):
        return [Gather(cube, value[:, :, :cut], 0), Gather(cube, value[:, :, cut:], 1)]

    def advance(movers):
        for mover in movers:
            mover.move()

    def join(movers):
        for mover in movers:
            mover.join()

    def exchange(value):
        return lax.all_to_all(value, "sp", split_axis=0, concat_axis=0, tiled=True)

    skip_z = spread(jnp.pad(w_skip.T, ((0, 0), (0, skip_lanes - kept))))
    skip_m = fetch(skip_z, skip_cut)
    qkv_z = spread(pad_heads(w_qkv.reshape(strip, -1), local), skip_z)
    while skip_m[0].todo:
        advance(skip_m)
    qkv_z = bind(qkv_z, *skip_m)
    fc1_z = spread(w_fc1, qkv_z)
    fc2_z = spread(w_fc2.T, fc1_z)
    join(skip_m)
    skip_w = [mover.weight() for mover in skip_m]
    qkv_m = fetch(qkv_z, qkv_cut)
    advance(qkv_m)

    def shuffle(count):
        block = count // ranks
        place = jnp.arange(count, dtype=jnp.int32)
        source = cube.owners[place // block] * block + place % block
        return (place[:, None] == source[None, :]).astype(BF)

    turn = shuffle(width)
    text_turn = shuffle(features)
    gains = jnp.stack([gain_skip, gain_attn, gain_cross, gain_mlp])
    gains = gains.reshape(4, ranks, strip)[:, cube.owners].reshape(4, 2, 1, middle)
    g_skip, g_attn, g_cross, g_mlp = gains

    wide = grid[:, 0, 1]
    counts = grid[:, 0, 0] * wide
    lengths = text_len[:, 0, :]
    place = zone * slots + jnp.arange(slots, dtype=jnp.int32)
    live = (place[None, :] < counts[:, None]).astype(F32).reshape(rows, 1)
    cosine, sine = rope_tables(sequence, wide, lanes)
    gain_q = pad_heads(jnp.tile(gain_query, local)[None, :], local)
    gain_k = pad_heads(jnp.tile(gain_key, local)[None, :], local)

    steps = cube.spread(timestep[:, 0])
    time_act = jax.nn.silu(time_embed(steps, width)).astype(BF).reshape(ranks * micros, parts, -1)
    time_part = lax.dynamic_index_in_dim(time_act, zone, 1, keepdims=False)
    shift = jnp.dot(time_part, w_mod, preferred_element_type=F32)
    shift = cube.trade(cube.add(shift, "sp").reshape(ranks, micros, strip))
    shift = jnp.stack([shift[mask] for mask in cube.masks]).reshape(2, ranks // 2, micros, strip)
    shift = jnp.transpose(shift, (0, 2, 1, 3)).reshape(2, micros, middle)

    grad3 = jnp.stack(
        [
            jnp.dot(cotangent.reshape(rows, width), side, preferred_element_type=F32) * live
            for side in (turn[:, :middle], turn[:, middle:])
        ]
    )
    d_mlp = grad3.astype(BF)

    wide_shape = jax.ShapeDtypeStruct((2, rows, middle), F32)
    low_shape = jax.ShapeDtypeStruct((2, rows, middle), BF)
    gain_shape = jax.ShapeDtypeStruct((2, 1, middle), F32)
    joined = side_by_side(tokens.reshape(rows, width), skip_tokens.reshape(rows, width), kept, skip_lanes)

    def first_norms(sums, extra, out):
        g0_ref, g1_ref, shift_ref = extra
        base_ref, stream_ref, pre_ref = out
        unit, _ = norm_unit(sums)
        stream = [unit[side] * g0_ref[side] for side in range(2)]
        unit, _ = norm_unit(stream)
        for side in range(2):
            base_ref[side] = sums[side]
            stream_ref[side] = stream[side]
            for micro in range(micros):
                cut = slice(micro * slots, (micro + 1) * slots)
                pre = unit[side][cut] * g1_ref[side] + shift_ref[side, micro : micro + 1]
                pre_ref[side, cut] = pre.astype(BF)

    def next_norm(sums, extra, out):
        before_ref, gain_ref = extra
        after_ref, pre_ref = out
        stream = [before_ref[side] + sums[side] for side in range(2)]
        unit, _ = norm_unit(stream)
        for side in range(2):
            after_ref[side] = stream[side]
            pre_ref[side] = (unit[side] * gain_ref[side]).astype(BF)

    base, stream, pre_attn = to_features(
        joined, skip_w, [g_skip, g_attn, shift], [wide_shape, wide_shape, low_shape], first_norms
    )
    while qkv_m[0].todo:
        advance(qkv_m)
    pre_attn = bind(pre_attn, *qkv_m)
    join(qkv_m)
    qkv_w = [mover.weight() for mover in qkv_m]
    fc_m = [Gather(cube, fc1_z, 0), Gather(cube, fc2_z, 1)]
    projected = to_lanes(pre_attn, qkv_w)
    projected = bind(projected, fc_m[0])
    advance(fc_m)
    raw = exchange(projected.reshape(parts, micros, slots, 3 * lanes))
    raw = bind(raw, *fc_m)
    cross_z = jnp.concatenate([pad_heads(side, local) for side in (w_out1.T, w_query2, w_out2.T)], 1)
    cross_z = spread(cross_z, raw)
    text_z = jnp.pad(pad_heads(w_text_kv.reshape(text_rows, -1), local), ((0, max(0, strip - text_rows)), (0, 0)))
    text_z = spread(text_z, cross_z)
    text_own = jnp.dot(text.reshape(-1, features), text_turn, preferred_element_type=F32).astype(BF)
    text_own = jnp.pad(
        text_own.reshape(micros, text_slots, features), ((0, 0), (0, text_strip - text_slots), (0, 0))
    ).reshape(micros * text_strip, features)
    text_all = spread(text_own, text_z).reshape(-1, features)
    text_all = jnp.stack([text_all[:, : features // 2], text_all[:, features // 2 :]])
    while fc_m[0].todo:
        advance(fc_m)
    attended, turned_q, turned_k, norms = self_forward(raw, counts, cosine, sine, gain_q, gain_k)
    attended = bind(attended, *fc_m)
    attended = exchange(attended).reshape(parts, rows, lanes)
    cross_m = fetch(cross_z, 2 * lanes)
    text_m = Gather(cube, text_z[:, :text_rows], 1)
    join(cross_m)
    first_w, out2_w = [mover.weight() for mover in cross_m]
    out1_w, query2_w = (Lanes(first_w.near, first_w.far, lanes, index) for index in range(2))
    join(fc_m)
    fc1_w, fc2_w = [mover.weight() for mover in fc_m]
    text_m.join()
    text_w = text_m.weight()
    stream1, pre_cross = to_features(
        attended, [out1_w], [stream, g_cross], [wide_shape, low_shape], next_norm
    )
    query2 = to_lanes(pre_cross, [query2_w]).reshape(parts, micros, slots, lanes)
    text_kv = to_lanes(text_all, [text_w]).reshape(parts, parts, micros, text_strip, 2 * lanes)
    crossed = cross_forward(query2, text_kv, lengths, text_slots).reshape(parts, rows, lanes)
    stream2, pre_mlp = to_features(
        crossed, [out2_w], [stream1, g_mlp], [wide_shape, low_shape], next_norm
    )
    hidden0, activ0, partial, fc2_n0, fc2_f0 = mlp_forward(pre_mlp, d_mlp, stream2, fc1_w, fc2_w, 0)
    hidden1, activ1, result, fc2_n1, fc2_f1 = mlp_forward(pre_mlp, d_mlp, partial, fc1_w, fc2_w, 1, live)
    fc2_s = [Scatter(cube, fc2_n0, fc2_f0, 0), Scatter(cube, fc2_n1, fc2_f1, 1)]

    def pack(movers):
        for mover in movers:
            mover.pack()

    def settle(values, before=None):
        value = values[0] if len(values) == 1 else jnp.concatenate(values, 2)
        if before is not None:
            value, before = tie(value, before)
        return lax.psum_scatter(value, "sp", scatter_dimension=0, tiled=False)

    fc1_n0, fc1_f0, partial = mlp_backward(d_mlp, pre_mlp, hidden0, fc1_w, fc2_w, 0, None)
    partial = bind(partial, *fc2_s)
    pack(fc2_s)
    partial = bind(partial, *fc2_s)
    advance(fc2_s)
    fc1_n1, fc1_f1, grad2, d_cross, d_gain_mlp = mlp_backward(
        d_mlp, pre_mlp, hidden1, fc1_w, fc2_w, 1, partial, [stream2, g_mlp, grad3]
    )
    fc1_s = [Scatter(cube, fc1_n0, fc1_f0, 0), Scatter(cube, fc1_n1, fc1_f1, 1)]
    d_crossed = to_lanes(d_cross, [out2_w])
    d_crossed = bind(d_crossed, *fc2_s)
    pack(fc2_s)
    d_crossed = bind(d_crossed, *fc2_s)
    advance(fc2_s)
    d_query2, d_text_kv = cross_backward(
        query2, text_kv, lengths, d_crossed.reshape(parts, micros, slots, lanes), text_slots
    )
    d_query2 = bind(d_query2, *fc1_s)
    pack(fc1_s)
    d_query2 = bind(d_query2, *fc1_s)
    advance(fc1_s)
    d_query2 = d_query2.reshape(parts, rows, lanes)
    d_text_kv = d_text_kv.reshape(parts, -1, 2 * lanes)

    def go_back(sums, extra, out):
        add_norm_back(sums, *extra, *out)

    grad1, d_attn, d_gain_cross = to_features(
        d_query2, [query2_w], [stream1, g_cross, grad2], [wide_shape, low_shape, gain_shape], go_back
    )
    d_attended = to_lanes(d_attn, [out1_w])
    d_heads = exchange(d_attended.reshape(parts, micros, slots, lanes))

    def words_back(sums, extra, out):
        size = micros * text_strip
        for zone in range(parts):
            for side in range(2):
                out[0][zone, side] = sums[side][zone * size : (zone + 1) * size].astype(BF)

    words_shape = jax.ShapeDtypeStruct((parts, 2, micros * text_strip, features // 2), BF)
    d_words = to_features(d_text_kv, [text_w], [], [words_shape], words_back)[0]
    d_words = settle([d_words])
    text_s = Scatter(cube, *terms_of([(text_all, d_text_kv, 2 * lanes, 0)]), 1)
    cross_s = Scatter(
        cube,
        *terms_of([(d_attn, attended, lanes, 0), (pre_cross, d_query2, lanes, 0), (d_cross, crossed, lanes, 0)]),
        0,
    )
    total_fc2 = [mover.result() for mover in fc2_s]
    term_fc2 = settle(total_fc2)
    d_heads = bind(d_heads, text_s, cross_s)
    d_raw, d_gain_q, d_gain_k = self_backward(
        raw, counts, cosine, sine, gain_q, gain_k, turned_q, turned_k, norms, d_heads
    )
    d_raw = bind(d_raw, *fc1_s)
    d_projected = exchange(d_raw).reshape(parts, rows, 3 * lanes)
    pack(fc1_s)
    advance(fc1_s)
    pack([cross_s, text_s])
    advance([cross_s, text_s])
    total_fc1 = [mover.result() for mover in fc1_s]

    def last_norms(sums, extra, out):
        stream_ref, g1_ref, base_ref, g0_ref, add_ref = extra
        low_ref, d_shift_ref, d_g1_ref, d_g0_ref = out
        back, gains1 = norm_back([stream_ref[0], stream_ref[1]], g1_ref, sums)
        total = [add_ref[side] + back[side] for side in range(2)]
        back, gains0 = norm_back([base_ref[0], base_ref[1]], g0_ref, total)
        for side in range(2):
            low_ref[side] = back[side].astype(BF)
            d_g1_ref[side] = gains1[side]
            d_g0_ref[side] = gains0[side]
            for micro in range(micros):
                part = sums[side][micro * slots : (micro + 1) * slots]
                d_shift_ref[side, micro : micro + 1] = jnp.sum(part, 0, keepdims=True)

    qkv_t = [terms_of([(pre_attn, d_projected, 3 * lanes, 0)])]
    qkv_s = [Scatter(cube, *qkv_t[0], 0)]
    shift_shape = jax.ShapeDtypeStruct((2, micros, middle), F32)
    d_base, d_shift, d_gain_attn, d_gain_skip = to_features(
        d_projected,
        qkv_w,
        [stream, g_attn, base, g_skip, grad1],
        [low_shape, shift_shape, gain_shape, gain_shape],
        last_norms,
    )
    d_base = bind(d_base, *qkv_s)
    pack(qkv_s)
    d_base = bind(d_base, *qkv_s)
    advance(qkv_s)
    skip_s = [Scatter(cube, *terms_of([(d_base, joined, skip_lanes, 0)]), 1)]
    term_fc1 = settle(total_fc1, d_base)
    pack(skip_s)
    advance(skip_s)
    term_cross = settle([cross_s.result()])
    term_text = settle([text_s.result()])
    term_qkv = settle([mover.result() for mover in qkv_s])
    term_skip = settle([mover.result() for mover in skip_s])
    d_joined = to_inputs(d_base, skip_w, kept)
    result = (
        jnp.dot(result[0], turn[:, :middle].T, preferred_element_type=F32)
        + jnp.dot(result[1], turn[:, middle:].T, preferred_element_type=F32)
    ).astype(BF)
    d_words = d_words.reshape(2, micros * text_strip, features // 2)
    d_words = jnp.dot(
        d_words[0], text_turn[:, : features // 2].T, preferred_element_type=F32
    ) + jnp.dot(d_words[1], text_turn[:, features // 2 :].T, preferred_element_type=F32)
    d_words = d_words.reshape(micros, text_strip, features)[:, :text_slots]

    d_shift = jnp.transpose(d_shift.reshape(2, micros, ranks // 2, strip), (0, 2, 1, 3))
    d_shift = d_shift.reshape(ranks, micros, strip)
    d_shift = jnp.stack([d_shift[cube.masks.index(mask)] for mask in range(ranks)])
    d_shift = cube.add(cube.trade(d_shift), "sp").reshape(ranks * micros, strip)
    term_mod = lax.dot_general(
        time_part.astype(F32), d_shift, (((0,), (0,)), ((), ())), precision=lax.Precision.HIGHEST
    )

    places = jnp.array([cube.masks.index(mask) for mask in range(ranks)], jnp.int32)
    places = places[jnp.arange(ranks, dtype=jnp.int32) ^ cube.rank]
    gains = jnp.stack([d_gain_skip, d_gain_attn, d_gain_cross, d_gain_mlp])
    gains = gains.reshape(4, ranks, strip)[:, places].reshape(-1)
    heads = jnp.stack([jnp.sum(d_gain_q, (0, 1)), jnp.sum(d_gain_k, (0, 1))])
    heads = jnp.sum(heads[:, : local * HP].reshape(2, local, HP)[:, :, :HD], 1)
    packed = jnp.concatenate([gains, heads.reshape(-1)])
    packed = cube.add(cube.add(packed, "sp"), "dp")
    gains = packed[: 4 * width].reshape(4, ranks * parts, -1)
    gains = lax.dynamic_index_in_dim(gains, cube.rank * parts + zone, 1, keepdims=False)
    heads = packed[4 * width :].reshape(2, HD)

    def whole(term, groups):
        return cut_heads(term.astype(F32), local).reshape(term.shape[0], groups, -1)

    return (
        result.reshape(tokens.shape),
        d_joined[0].reshape(tokens.shape),
        d_joined[1].reshape(tokens.shape),
        d_words.reshape(text.shape),
        term_skip.astype(F32)[:, :kept].T,
        term_mod,
        whole(term_qkv, 3),
        cut_heads(term_cross[:, :lanes].astype(F32), local).T,
        cut_heads(term_cross[:, lanes : 2 * lanes].astype(F32), local),
        whole(term_text, 2),
        cut_heads(term_cross[:, 2 * lanes :].astype(F32), local).T,
        term_fc1.astype(F32),
        term_fc2.astype(F32).T,
        gains[0],
        gains[1],
        gains[2],
        gains[3],
        heads[0],
        heads[1],
    )


def solution(mesh):
    rows = P(None, ("dp", "sp"), None)
    column = P("sp", "dp")
    row = P("dp", "sp")
    grouped = P("dp", None, "sp")
    in_specs = (
        (rows, rows, rows, P(None, "dp"), P(None, "dp", None), P(None, "dp", None))
        + (column, column, grouped, column, row, grouped, column, row, column)
        + (P(),) * 6
        + (rows,)
    )
    out_specs = (
        (rows, rows, rows, rows)
        + (column, column, grouped, column, row, grouped, column, row, column)
        + (P(("dp", "sp")),) * 4
        + (P(), P())
    )
    return jax.shard_map(
        on_device, mesh=mesh, in_specs=in_specs, out_specs=out_specs, check_vma=False
    )
```

```python
import math

import jax
import jax.numpy as jnp
from jax import lax
from jax.experimental import pallas as pl
from jax.experimental.pallas import tpu as pltpu
from jax.sharding import PartitionSpec as P

H = 16
HD = 88
HP = 96
CLIP_LEN = 77
ROWS = 256

EPS = 1e-06
MASKED = -1e30
LOG2E = 1.4426950408889634
BF = jnp.bfloat16
F32 = jnp.float32


def time_embed(step, width):
    half = width // 2
    rate = jnp.exp(-math.log(10000.0) * jnp.arange(half, dtype=F32) / half)
    angle = step.astype(F32)[..., None] * rate
    return jnp.concatenate([jnp.cos(angle), jnp.sin(angle)], -1)


def rope_tables(sequence, wide, lanes):
    place = jnp.arange(sequence, dtype=jnp.int32)[None, :, None]
    wide = wide[:, None, None]
    lane = jnp.arange(lanes, dtype=jnp.int32)[None, None, :] % HP
    pair = lane // 2
    quarter = HD // 4
    upper = pair < quarter
    rank = jnp.where(upper, pair, pair - quarter).astype(F32)
    rate = jnp.exp(-math.log(10000.0) * rank / quarter)
    angle = jnp.where(upper, place // wide, place % wide).astype(F32) * rate
    sine = jnp.sin(angle)
    return jnp.cos(angle), jnp.where(lane % 2 == 0, -sine, sine)


def pad_heads(packed, local):
    rows, lanes = packed.shape
    groups = packed.reshape(rows, lanes // (local * HD), local, HD)
    groups = jnp.pad(groups, ((0, 0), (0, 0), (0, 0), (0, HP - HD)))
    groups = groups.reshape(rows, -1, local * HP)
    return jnp.pad(groups, ((0, 0), (0, 0), (0, -local * HP % 128))).reshape(rows, -1)


def cut_heads(padded, local):
    rows = padded.shape[0]
    groups = padded.reshape(rows, -1, local * HP + -local * HP % 128)[:, :, : local * HP]
    return groups.reshape(rows, -1, local, HP)[..., :HD].reshape(rows, -1)


def head_masks(shape, local):
    lane = lax.broadcasted_iota(jnp.int32, shape, len(shape) - 1)
    inside = lane % HP < HD
    return [((lane // HP == h) & inside).astype(F32) for h in range(local)]


def head_mean(value, masks):
    total = None
    for mask in masks:
        term = (jnp.sum(value * mask, -1, keepdims=True) * (1.0 / HD)) * mask
        total = term if total is None else total + term
    return total


def head_unit(value, masks):
    centre = value - head_mean(value, masks)
    spread = None
    square = centre * centre
    for mask in masks:
        mean = jnp.sum(square * mask, -1, keepdims=True) * (1.0 / HD)
        term = lax.rsqrt(mean + EPS) * mask
        spread = term if spread is None else spread + term
    return centre * spread, spread


def turn_pairs(value):
    lanes = value.shape[-1]
    after = pltpu.roll(value, lanes - 1, 1)
    before = pltpu.roll(value, 1, 1)
    lane = lax.broadcasted_iota(jnp.int32, value.shape, 1)
    return jnp.where(lane % 2 == 0, after, before)


def dot_nt(left, right):
    return lax.dot_general(left, right, (((1,), (1,)), ((), ())), preferred_element_type=F32)


def dot_nn(left, right):
    return lax.dot_general(left, right, (((1,), (0,)), ((), ())), preferred_element_type=F32)


def dot_tn(left, right):
    return lax.dot_general(left, right, (((0,), (0,)), ((), ())), preferred_element_type=F32)


def self_forward(raw, counts, cosine, sine, gain_q, gain_k):
    parts, micros, slots, packed = raw.shape
    lanes = packed // 3
    local = lanes // HP
    sequence = parts * slots
    factor = HD ** (-0.5) * LOG2E

    def kernel(count_ref, raw_ref, cos_ref, sin_ref, gq_ref, gk_ref, out_ref, q_ref, k_ref, lse_ref):
        count = count_ref[pl.program_id(0)]
        blocks = (count + slots - 1) // slots
        out_ref[...] = jnp.zeros_like(out_ref)
        masks = head_masks((1, lanes), local)

        def prepare(part, carry):
            spot = pl.ds(pl.multiple_of(part * slots, slots), slots)
            cosine, sine = cos_ref[0, spot, :], sin_ref[0, spot, :]
            for index, gain_ref, dest in ((0, gq_ref, q_ref), (1, gk_ref, k_ref)):
                value = raw_ref[part, 0, :, index * lanes : (index + 1) * lanes].astype(F32)
                scaled = head_unit(value, masks)[0] * gain_ref[...]
                dest[0, spot, :] = (scaled * cosine + turn_pairs(scaled) * sine).astype(BF)
            return carry

        lax.fori_loop(0, parts, prepare, 0)
        column = lax.broadcasted_iota(jnp.int32, (1, sequence), 1)
        bias = jnp.where(column < count, 0.0, MASKED)
        for h in range(local):
            cut = slice(h * HP, (h + 1) * HP)
            keys = k_ref[0, :, cut]
            values = raw_ref[:, 0, :, 2 * lanes + h * HP : 2 * lanes + (h + 1) * HP].reshape(sequence, HP)

            def one_block(part, carry):
                spot = pl.ds(pl.multiple_of(part * slots, slots), slots)
                scores = dot_nt(q_ref[0, spot, cut], keys) + bias
                top = jnp.max(scores, -1, keepdims=True)
                raised = jnp.exp2((scores - top) * factor)
                total = jnp.sum(raised, -1, keepdims=True)
                result = dot_nn(raised.astype(BF), values) / total
                out_ref[part, 0, :, cut] = result.astype(BF)
                norm = jnp.broadcast_to(top * factor + jnp.log2(total), (slots, 128))
                lse_ref[0, h : h + 1, spot] = jnp.transpose(norm)[0:1, :]
                return carry

            lax.fori_loop(0, blocks, one_block, 0)

    whole = lambda m, c: (0, m, 0, 0)
    table = lambda m, c: (m, 0, 0)
    fixed = lambda m, c: (0, 0)
    return pl.pallas_call(
        kernel,
        name="self_forward",
        grid_spec=pltpu.PrefetchScalarGridSpec(
            num_scalar_prefetch=1,
            grid=(micros,),
            in_specs=[
                pl.BlockSpec((parts, 1, slots, packed), whole),
                pl.BlockSpec((1, sequence, lanes), table),
                pl.BlockSpec((1, sequence, lanes), table),
                pl.BlockSpec((1, lanes), fixed),
                pl.BlockSpec((1, lanes), fixed),
            ],
            out_specs=[
                pl.BlockSpec((parts, 1, slots, lanes), whole),
                pl.BlockSpec((1, sequence, lanes), table),
                pl.BlockSpec((1, sequence, lanes), table),
                pl.BlockSpec((1, local, sequence), table),
            ],
        ),
        out_shape=[
            jax.ShapeDtypeStruct((parts, micros, slots, lanes), BF),
            jax.ShapeDtypeStruct((micros, sequence, lanes), BF),
            jax.ShapeDtypeStruct((micros, sequence, lanes), BF),
            jax.ShapeDtypeStruct((micros, local, sequence), F32),
        ],
        compiler_params=pltpu.CompilerParams(vmem_limit_bytes=48 << 20),
        cost_estimate=cost(4 * micros * local * sequence * sequence * HP),
    )(counts, raw, cosine, sine, gain_q, gain_k)


def self_backward(raw, counts, cosine, sine, gain_q, gain_k, turned_q, turned_k, norms, incoming):
    parts, micros, slots, packed = raw.shape
    lanes = packed // 3
    local = lanes // HP
    sequence = parts * slots
    scale = HD ** (-0.5)
    factor = scale * LOG2E

    def kernel(
        count_ref,
        raw_ref,
        cos_ref,
        sin_ref,
        gq_ref,
        gk_ref,
        q_ref,
        k_ref,
        lse_ref,
        in_ref,
        out_ref,
        dgq_ref,
        dgk_ref,
        dq_s,
        dk_s,
        dv_s,
    ):
        count = count_ref[pl.program_id(0)]
        blocks = (count + slots - 1) // slots
        dq_s[...] = jnp.zeros_like(dq_s)
        dk_s[...] = jnp.zeros_like(dk_s)
        dv_s[...] = jnp.zeros_like(dv_s)
        row = lax.broadcasted_iota(jnp.int32, (sequence, 1), 0)
        bias = jnp.where(row < count, 0.0, MASKED)
        for h in range(local):
            cut = slice(h * HP, (h + 1) * HP)
            keys = k_ref[0, :, cut]
            values = raw_ref[:, 0, :, 2 * lanes + h * HP : 2 * lanes + (h + 1) * HP].reshape(sequence, HP)

            def one_block(part, carry):
                spot = pl.ds(pl.multiple_of(part * slots, slots), slots)
                rows = q_ref[0, spot, cut]
                grads = in_ref[part, 0, :, cut]
                norm = lse_ref[0, h : h + 1, spot]
                probs = jnp.exp2(dot_nt(keys, rows) * factor + bias - norm)
                d_probs = dot_nt(values, grads)
                inner = jnp.sum(probs * d_probs, 0, keepdims=True)
                d_scores = (probs * (d_probs - inner)).astype(BF)
                dv_s[:, cut] += dot_nn(probs.astype(BF), grads)
                dk_s[:, cut] += dot_nn(d_scores, rows)
                dq_s[spot, cut] = dot_tn(d_scores, keys)
                return carry

            lax.fori_loop(0, blocks, one_block, 0)
        masks = head_masks((1, lanes), local)

        def finish(part, carry):
            spot = pl.ds(pl.multiple_of(part * slots, slots), slots)
            cosine, sine = cos_ref[0, spot, :], sin_ref[0, spot, :]
            sums = []
            for index, gain_ref, source in ((0, gq_ref, dq_s), (1, gk_ref, dk_s)):
                grad = source[spot, :] * scale
                grad = grad * cosine - turn_pairs(grad) * sine
                value = raw_ref[part, 0, :, index * lanes : (index + 1) * lanes].astype(F32)
                unit, spread = head_unit(value, masks)
                leading = grad * gain_ref[...]
                back = leading - head_mean(leading, masks) - unit * head_mean(leading * unit, masks)
                out_ref[part, 0, :, index * lanes : (index + 1) * lanes] = (spread * back).astype(BF)
                sums.append(carry[index] + jnp.sum(grad * unit, 0, keepdims=True))
            out_ref[part, 0, :, 2 * lanes : 3 * lanes] = dv_s[spot, :].astype(BF)
            return tuple(sums)

        zero = jnp.zeros((1, lanes), F32)
        d_gains = lax.fori_loop(0, parts, finish, (zero, zero))
        dgq_ref[0] = d_gains[0]
        dgk_ref[0] = d_gains[1]

    whole = lambda m, c: (0, m, 0, 0)
    table = lambda m, c: (m, 0, 0)
    fixed = lambda m, c: (0, 0)
    return pl.pallas_call(
        kernel,
        name="self_backward",
        grid_spec=pltpu.PrefetchScalarGridSpec(
            num_scalar_prefetch=1,
            grid=(micros,),
            in_specs=[
                pl.BlockSpec((parts, 1, slots, packed), whole),
                pl.BlockSpec((1, sequence, lanes), table),
                pl.BlockSpec((1, sequence, lanes), table),
                pl.BlockSpec((1, lanes), fixed),
                pl.BlockSpec((1, lanes), fixed),
                pl.BlockSpec((1, sequence, lanes), table),
                pl.BlockSpec((1, sequence, lanes), table),
                pl.BlockSpec((1, local, sequence), table),
                pl.BlockSpec((parts, 1, slots, lanes), whole),
            ],
            out_specs=[
                pl.BlockSpec((parts, 1, slots, packed), whole),
                pl.BlockSpec((1, 1, lanes), table),
                pl.BlockSpec((1, 1, lanes), table),
            ],
            scratch_shapes=[pltpu.VMEM((sequence, lanes), F32) for index in range(3)],
        ),
        out_shape=[
            jax.ShapeDtypeStruct((parts, micros, slots, packed), BF),
            jax.ShapeDtypeStruct((micros, 1, lanes), F32),
            jax.ShapeDtypeStruct((micros, 1, lanes), F32),
        ],
        compiler_params=pltpu.CompilerParams(vmem_limit_bytes=48 << 20),
        cost_estimate=cost(10 * micros * local * sequence * sequence * HP),
    )(counts, raw, cosine, sine, gain_q, gain_k, turned_q, turned_k, norms, incoming)


def cost(flops):
    return pl.CostEstimate(flops=flops // 16, bytes_accessed=flops // 16000, transcendentals=0)


def full(shape):
    return pl.BlockSpec(shape, lambda *index: (0,) * len(shape))


def params(megabytes=48):
    return pltpu.CompilerParams(vmem_limit_bytes=megabytes << 20)


class Lanes:
    def __init__(self, near, far, block=None, index=0):
        self.near, self.far = near, far
        self.block = block or near.shape[2]
        self.index = index

    def spec(self):
        index = self.index
        return pl.BlockSpec((1, self.near.shape[1], self.block), lambda p, *rest: (p, 0, index))


def to_lanes(value, weights, dtype=BF, name="to_lanes"):
    rows = value.shape[1]
    parts, half, _ = weights[0].near.shape
    total = sum(weight.block for weight in weights)

    def kernel(x_ref, *refs):
        out_ref = refs[-1]
        at = 0
        for index, weight in enumerate(weights):
            result = dot_nn(x_ref[0], refs[2 * index][0]) + dot_nn(x_ref[1], refs[2 * index + 1][0])
            out_ref[0, :, at : at + weight.block] = result.astype(dtype)
            at += weight.block

    return pl.pallas_call(
        kernel,
        name=name,
        grid=(parts,),
        in_specs=[full(value.shape)] + [weight.spec() for weight in weights for side in range(2)],
        out_specs=pl.BlockSpec((1, rows, total), lambda p: (p, 0, 0)),
        out_shape=jax.ShapeDtypeStruct((parts, rows, total), dtype),
        compiler_params=params(),
        cost_estimate=cost(4 * rows * half * parts * total),
    )(value, *[side for weight in weights for side in (weight.near, weight.far)])


def to_inputs(value, weights, kept):
    rows = value.shape[1]
    parts, half, _ = weights[0].near.shape
    sides = parts // 2

    def kernel(x_ref, *refs):
        out_ref = refs[-1]
        for side in range(sides):

            @pl.when(pl.program_id(0) % sides == side)
            def _():
                at = 0
                for index, weight in enumerate(weights):
                    result = dot_nn(x_ref[0], refs[2 * index][0]) + dot_nn(
                        x_ref[1], refs[2 * index + 1][0]
                    )
                    take = min(weight.block, kept - at)
                    start = side * kept + at
                    out_ref[0, :, start : start + take] = result[:, :take]
                    at += take

    return pl.pallas_call(
        kernel,
        name="to_inputs",
        grid=(parts,),
        in_specs=[full(value.shape)] + [weight.spec() for weight in weights for side in range(2)],
        out_specs=pl.BlockSpec((1, rows, sides * kept), lambda p: (p // sides, 0, 0)),
        out_shape=jax.ShapeDtypeStruct((2, rows, sides * kept), F32),
        compiler_params=params(),
        cost_estimate=cost(4 * rows * half * parts * kept),
    )(value, *[side for weight in weights for side in (weight.near, weight.far)])


def to_features(value, weights, extras, outs, finish, name="to_features"):
    parts, rows, total = value.shape
    half = weights[0].near.shape[1]
    count = 2 * len(weights)

    def kernel(*refs):
        y_ref, weight_refs = refs[0], refs[1 : 1 + count]
        extra_refs = refs[1 + count : 1 + count + len(extras)]
        out_refs = refs[1 + count + len(extras) : -1]
        sums = refs[-1]

        @pl.when(pl.program_id(0) == 0)
        def _():
            sums[...] = jnp.zeros_like(sums)

        at = 0
        for index, weight in enumerate(weights):
            left = y_ref[0, :, at : at + weight.block]
            for side in range(2):
                sums[side] += dot_nt(left, weight_refs[2 * index + side][0])
            at += weight.block

        @pl.when(pl.program_id(0) == parts - 1)
        def _():
            finish([sums[0], sums[1]], extra_refs, out_refs)

    return pl.pallas_call(
        kernel,
        name=name,
        grid=(parts,),
        in_specs=[pl.BlockSpec((1, rows, total), lambda p: (p, 0, 0))]
        + [weight.spec() for weight in weights for side in range(2)]
        + [full(extra.shape) for extra in extras],
        out_specs=[full(out.shape) for out in outs],
        out_shape=outs,
        scratch_shapes=[pltpu.VMEM((2, rows, half), F32)],
        compiler_params=params(56),
        cost_estimate=cost(4 * rows * half * parts * total),
    )(value, *[side for weight in weights for side in (weight.near, weight.far)], *extras)


def terms_of(pairs, name="terms_of"):
    half = pairs[0][0].shape[2]
    parts = pairs[0][1].shape[0]
    total = sum(pair[2] for pair in pairs)
    rows = [pair[0].shape[1] for pair in pairs]

    def kernel(*refs):
        count = len(pairs)
        lefts, rights = refs[:count], refs[count : 2 * count]
        near_ref, far_ref = refs[2 * count : 2 * count + 2]
        turned = refs[2 * count + 2 :]

        @pl.when(pl.program_id(0) == 0)
        def _():
            for left, flat in zip(lefts, turned):
                for side in range(2):
                    flat[side] = jnp.transpose(left[side])

        at = 0
        for pair, right, flat in zip(pairs, rights, turned):
            lanes = pair[2]
            near_ref[0, :, at : at + lanes] = dot_nn(flat[0], right[0]).astype(BF)
            far_ref[0, :, at : at + lanes] = dot_nn(flat[1], right[0]).astype(BF)
            at += lanes

    def right_spec(pair):
        return pl.BlockSpec((1, pair[1].shape[1], pair[2]), lambda p: (p, 0, pair[3]))

    out = jax.ShapeDtypeStruct((parts, half, total), BF)
    return pl.pallas_call(
        kernel,
        name=name,
        grid=(parts,),
        in_specs=[full(pair[0].shape) for pair in pairs] + [right_spec(pair) for pair in pairs],
        out_specs=[pl.BlockSpec((1, half, total), lambda p: (p, 0, 0))] * 2,
        out_shape=[out, out],
        scratch_shapes=[pltpu.VMEM((2, half, count), BF) for count in rows],
        compiler_params=params(),
        cost_estimate=cost(sum(4 * half * parts * pair[2] * count for pair, count in zip(pairs, rows))),
    )(*[pair[0] for pair in pairs], *[pair[1] for pair in pairs])


def norm_unit(halves):
    width = 2 * halves[0].shape[-1]
    mean = sum(jnp.sum(half, -1, keepdims=True) for half in halves) / width
    centre = [half - mean for half in halves]
    spread = sum(jnp.sum(half * half, -1, keepdims=True) for half in centre) / width
    scale = lax.rsqrt(spread + EPS)
    return [half * scale for half in centre], scale


def norm_back(halves, gain_ref, incoming):
    width = 2 * halves[0].shape[-1]
    unit, scale = norm_unit(halves)
    leading = [incoming[side] * gain_ref[side] for side in range(2)]
    mean = sum(jnp.sum(half, -1, keepdims=True) for half in leading) / width
    inner = sum(jnp.sum(leading[side] * unit[side], -1, keepdims=True) for side in range(2)) / width
    back = [scale * (leading[side] - mean - unit[side] * inner) for side in range(2)]
    gains = [jnp.sum(incoming[side] * unit[side], 0, keepdims=True) for side in range(2)]
    return back, gains


def join_rows(pieces, name="join_rows"):
    parts, rows, lanes = pieces[0].shape
    count = len(pieces)
    if rows % 16:
        return jnp.concatenate(pieces, 1)

    def kernel(*refs):
        for index in range(count):
            refs[-1][0, index * rows : (index + 1) * rows] = refs[index][0]

    return pl.pallas_call(
        kernel,
        name=name,
        grid=(parts,),
        in_specs=[pl.BlockSpec((1, rows, lanes), lambda p: (p, 0, 0))] * count,
        out_specs=pl.BlockSpec((1, count * rows, lanes), lambda p: (p, 0, 0)),
        out_shape=jax.ShapeDtypeStruct((parts, count * rows, lanes), BF),
        compiler_params=params(24),
        cost_estimate=cost(parts * count * rows * lanes),
    )(*pieces)


def sum_rows(terms, rows, count, name="sum_rows"):
    parts, _, lanes = terms[0][0].shape
    if rows % 16:
        value = 0.0
        for array, first, step in terms:
            blocks = array.reshape(parts, -1, rows, lanes)[:, first :: step][:, :count]
            value = value + blocks.astype(F32)
        return value.astype(BF).reshape(parts, count * rows, lanes)

    def kernel(*refs):
        for index in range(count):
            value = None
            for (array, first, step), ref in zip(terms, refs):
                start = 0 if array.shape[1] == rows else (first + step * index) % (array.shape[1] // rows)
                term = ref[0, start * rows : (start + 1) * rows].astype(F32)
                value = term if value is None else value + term
            refs[-1][0, index * rows : (index + 1) * rows] = value.astype(BF)

    def spec(size):
        return pl.BlockSpec((1, size, lanes), lambda p: (p, 0, 0))

    return pl.pallas_call(
        kernel,
        name=name,
        grid=(parts,),
        in_specs=[spec(term[0].shape[1]) for term in terms],
        out_specs=spec(count * rows),
        out_shape=jax.ShapeDtypeStruct((parts, count * rows, lanes), BF),
        compiler_params=params(32),
        cost_estimate=cost(parts * count * rows * lanes),
    )(*[term[0] for term in terms])


def side_by_side(left, right, kept, lanes):
    rows, width = left.shape
    count = width // kept

    def kernel(left_ref, right_ref, out_ref):
        for index, ref in enumerate((left_ref, right_ref)):
            for side in range(count):
                spot = count * index + side
                out_ref[spot, :, :kept] = ref[:, side * kept : (side + 1) * kept]
                if lanes > kept:
                    out_ref[spot, :, kept:] = jnp.zeros((rows, lanes - kept), BF)

    return pl.pallas_call(
        kernel,
        name="side_by_side",
        out_shape=jax.ShapeDtypeStruct((2 * count, rows, lanes), BF),
        compiler_params=params(24),
        cost_estimate=cost(4 * rows * lanes),
    )(left, right)


def mlp_forward(rows_in, grads, start, weight1, weight2, part, live=None):
    _, rows, half = rows_in.shape
    parts, _, lanes = weight1.near.shape
    ff = lanes // 2
    step = 384 if ff % 384 == 0 else ff
    steps = ff // step
    extras = [] if live is None else [live]

    def kernel(x_ref, g_ref, s_ref, n1_ref, f1_ref, n2_ref, f2_ref, *refs):
        hid_ref, act_ref, out_ref, dn2_ref, df2_ref, turned, sums = refs[len(extras) :]
        first = (pl.program_id(0) == 0) & (pl.program_id(1) == 0)
        last = (pl.program_id(0) == parts - 1) & (pl.program_id(1) == steps - 1)

        @pl.when(first)
        def _():
            for side in range(2):
                turned[side] = jnp.transpose(g_ref[side])
            sums[...] = s_ref[...]

        hidden = dot_nn(x_ref[0], n1_ref[0]) + dot_nn(x_ref[1], f1_ref[0])
        hid_ref[0] = hidden
        activ = jax.nn.gelu(hidden, approximate=True).astype(BF)
        act_ref[0] = activ
        sums[0] += dot_nt(activ, n2_ref[0])
        sums[1] += dot_nt(activ, f2_ref[0])
        dn2_ref[0] = dot_nn(turned[0], activ).astype(BF)
        df2_ref[0] = dot_nn(turned[1], activ).astype(BF)

        @pl.when(last)
        def _():
            if live is None:
                out_ref[...] = sums[...]
            else:
                out_ref[...] = (sums[...] * refs[0][...]).astype(BF)

    weight = pl.BlockSpec((1, half, step), lambda p, n: (p, 0, part * steps + n))
    grad = pl.BlockSpec((1, half, step), lambda p, n: (p, 0, n))
    unit = pl.BlockSpec((1, rows, step), lambda p, n: (p, 0, n))
    whole = full((2, rows, half))
    grad_shape = jax.ShapeDtypeStruct((parts, half, ff), BF)
    return pl.pallas_call(
        kernel,
        name="mlp_forward",
        grid=(parts, steps),
        in_specs=[whole, whole, whole, weight, weight, weight, weight] + [full(extra.shape) for extra in extras],
        out_specs=[unit, unit, whole, grad, grad],
        out_shape=[
            jax.ShapeDtypeStruct((parts, rows, ff), F32),
            jax.ShapeDtypeStruct((parts, rows, ff), BF),
            jax.ShapeDtypeStruct((2, rows, half), F32 if live is None else BF),
            grad_shape,
            grad_shape,
        ],
        scratch_shapes=[pltpu.VMEM((2, half, rows), BF), pltpu.VMEM((2, rows, half), F32)],
        compiler_params=params(),
        cost_estimate=cost(12 * rows * half * parts * ff),
    )(rows_in, grads, start, weight1.near, weight1.far, weight2.near, weight2.far, *extras)


def gelu_slope(value):
    root = math.sqrt(2.0 / math.pi)
    square = value * value
    curve = jnp.tanh(root * value * (1.0 + 0.044715 * square))
    return 0.5 * (1.0 + curve) + 0.5 * value * (1.0 - curve * curve) * root * (
        1.0 + 3.0 * 0.044715 * square
    )


def mlp_backward(grads, rows_in, hidden, weight1, weight2, part, start, finish=None):
    _, rows, half = rows_in.shape
    parts, _, lanes = weight1.near.shape
    ff = lanes // 2
    step = 384 if ff % 384 == 0 else ff
    steps = ff // step
    extras = list(finish or []) + ([] if start is None else [start])

    def kernel(g_ref, x_ref, hid_ref, n1_ref, f1_ref, n2_ref, f2_ref, *refs):
        extra_refs, refs = refs[: len(extras)], refs[len(extras) :]
        dn1_ref, df1_ref = refs[:2]
        out_refs = refs[2:-2]
        turned, sums = refs[-2:]
        first = (pl.program_id(0) == 0) & (pl.program_id(1) == 0)
        last = (pl.program_id(0) == parts - 1) & (pl.program_id(1) == steps - 1)

        @pl.when(first)
        def _():
            for side in range(2):
                turned[side] = jnp.transpose(x_ref[side])
            sums[...] = jnp.zeros_like(sums) if start is None else extra_refs[-1][...]

        d_activ = dot_nn(g_ref[0], n2_ref[0]) + dot_nn(g_ref[1], f2_ref[0])
        d_hidden = (d_activ * gelu_slope(hid_ref[0])).astype(BF)
        dn1_ref[0] = dot_nn(turned[0], d_hidden).astype(BF)
        df1_ref[0] = dot_nn(turned[1], d_hidden).astype(BF)
        sums[0] += dot_nt(d_hidden, n1_ref[0])
        sums[1] += dot_nt(d_hidden, f1_ref[0])

        @pl.when(last)
        def _():
            if finish is None:
                out_refs[0][...] = sums[...]
            else:
                value_ref, gain_ref, add_ref = extra_refs[:3]
                add_norm_back([sums[0], sums[1]], value_ref, gain_ref, add_ref, *out_refs)

    weight = pl.BlockSpec((1, half, step), lambda p, n: (p, 0, part * steps + n))
    grad = pl.BlockSpec((1, half, step), lambda p, n: (p, 0, n))
    unit = pl.BlockSpec((1, rows, step), lambda p, n: (p, 0, n))
    whole = full((2, rows, half))
    grad_shape = jax.ShapeDtypeStruct((parts, half, ff), BF)
    wide = jax.ShapeDtypeStruct((2, rows, half), F32)
    outs = [wide] if finish is None else [wide, *back_shapes(rows, half)]
    return pl.pallas_call(
        kernel,
        name="mlp_backward",
        grid=(parts, steps),
        in_specs=[whole, whole, unit, weight, weight, weight, weight] + [full(extra.shape) for extra in extras],
        out_specs=[grad, grad] + [full(out.shape) for out in outs],
        out_shape=[grad_shape, grad_shape] + outs,
        scratch_shapes=[pltpu.VMEM((2, half, rows), BF), pltpu.VMEM((2, rows, half), F32)],
        compiler_params=params(56),
        cost_estimate=cost(12 * rows * half * parts * ff),
    )(grads, rows_in, hidden, weight1.near, weight1.far, weight2.near, weight2.far, *extras)


def back_shapes(rows, half):
    return [jax.ShapeDtypeStruct((2, rows, half), BF), jax.ShapeDtypeStruct((2, 1, half), F32)]


def add_norm_back(incoming, value_ref, gain_ref, add_ref, out_ref, low_ref, d_gain_ref):
    back, gains = norm_back([value_ref[0], value_ref[1]], gain_ref, incoming)
    for side in range(2):
        total = add_ref[side] + back[side]
        out_ref[side] = total
        low_ref[side] = total.astype(BF)
        d_gain_ref[side] = gains[side]


def text_bias(lengths_ref, micro, words, strip, text_slots, axis):
    spot = lax.broadcasted_iota(jnp.int32, (1, words) if axis else (words, 1), axis)
    inner = spot % strip
    place = spot // strip * text_slots + inner
    live = (place < lengths_ref[micro, 0]) | (
        (place >= CLIP_LEN) & (place < CLIP_LEN + lengths_ref[micro, 1])
    )
    return jnp.where(live & (inner < text_slots), 0.0, MASKED)


def cross_forward(query, text_kv, lengths, text_slots):
    parts, micros, slots, lanes = query.shape
    zones, strip = text_kv.shape[1], text_kv.shape[3]
    words = zones * strip
    local = lanes // HP
    factor = HD ** (-0.5) * LOG2E

    def kernel(len_ref, q_ref, kv_ref, out_ref):
        bias = text_bias(len_ref, pl.program_id(1), words, strip, text_slots, 1)
        for h in range(local):
            cut = slice(h * HP, (h + 1) * HP)
            keys = kv_ref[0, :, 0, :, cut].reshape(words, HP)
            scores = dot_nt(q_ref[0, 0, :, cut], keys) + bias
            top = jnp.max(scores, -1, keepdims=True)
            raised = jnp.exp2((scores - top) * factor)
            total = jnp.sum(raised, -1, keepdims=True)
            values = kv_ref[0, :, 0, :, lanes + h * HP : lanes + (h + 1) * HP].reshape(words, HP)
            out_ref[0, 0, :, cut] = (dot_nn(raised.astype(BF), values) / total).astype(BF)

    spot = lambda p, m, c: (p, m, 0, 0)
    far = lambda p, m, c: (p, 0, m, 0, 0)
    return pl.pallas_call(
        kernel,
        name="cross_forward",
        grid_spec=pltpu.PrefetchScalarGridSpec(
            num_scalar_prefetch=1,
            grid=(parts, micros),
            in_specs=[
                pl.BlockSpec((1, 1, slots, lanes), spot),
                pl.BlockSpec((1, zones, 1, strip, 2 * lanes), far),
            ],
            out_specs=pl.BlockSpec((1, 1, slots, lanes), spot),
        ),
        out_shape=jax.ShapeDtypeStruct(query.shape, BF),
        compiler_params=pltpu.CompilerParams(vmem_limit_bytes=32 << 20),
        cost_estimate=cost(4 * parts * micros * slots * words * lanes),
    )(lengths, query, text_kv)


def cross_backward(query, text_kv, lengths, incoming, text_slots):
    parts, micros, slots, lanes = query.shape
    zones, strip = text_kv.shape[1], text_kv.shape[3]
    words = zones * strip
    local = lanes // HP
    scale = HD ** (-0.5)
    factor = scale * LOG2E

    def kernel(len_ref, q_ref, kv_ref, in_ref, dq_ref, dkv_ref):
        bias = text_bias(len_ref, pl.program_id(1), words, strip, text_slots, 0)
        for h in range(local):
            cut = slice(h * HP, (h + 1) * HP)
            far = slice(lanes + h * HP, lanes + (h + 1) * HP)
            rows = q_ref[0, 0, :, cut]
            keys = kv_ref[0, :, 0, :, cut].reshape(words, HP)
            values = kv_ref[0, :, 0, :, far].reshape(words, HP)
            grads = in_ref[0, 0, :, cut]
            scores = dot_nt(keys, rows) + bias
            top = jnp.max(scores, 0, keepdims=True)
            raised = jnp.exp2((scores - top) * factor)
            probs = raised * (1.0 / jnp.sum(raised, 0, keepdims=True))
            d_probs = dot_nt(values, grads)
            inner = jnp.sum(probs * d_probs, 0, keepdims=True)
            d_scores = (probs * (d_probs - inner)).astype(BF)
            shape = (zones, strip, HP)
            dkv_ref[0, :, 0, :, far] = dot_nn(probs.astype(BF), grads).astype(BF).reshape(shape)
            dkv_ref[0, :, 0, :, cut] = (dot_nn(d_scores, rows) * scale).astype(BF).reshape(shape)
            dq_ref[0, 0, :, cut] = (dot_tn(d_scores, keys) * scale).astype(BF)

    spot = lambda p, m, c: (p, m, 0, 0)
    far = lambda p, m, c: (p, 0, m, 0, 0)
    return pl.pallas_call(
        kernel,
        name="cross_backward",
        grid_spec=pltpu.PrefetchScalarGridSpec(
            num_scalar_prefetch=1,
            grid=(parts, micros),
            in_specs=[
                pl.BlockSpec((1, 1, slots, lanes), spot),
                pl.BlockSpec((1, zones, 1, strip, 2 * lanes), far),
                pl.BlockSpec((1, 1, slots, lanes), spot),
            ],
            out_specs=[
                pl.BlockSpec((1, 1, slots, lanes), spot),
                pl.BlockSpec((1, zones, 1, strip, 2 * lanes), far),
            ],
        ),
        out_shape=[
            jax.ShapeDtypeStruct(query.shape, BF),
            jax.ShapeDtypeStruct(text_kv.shape, BF),
        ],
        compiler_params=pltpu.CompilerParams(vmem_limit_bytes=32 << 20),
        cost_estimate=cost(10 * parts * micros * slots * words * lanes),
    )(lengths, query, text_kv, incoming)


def tie(*values):
    return lax.optimization_barrier(values)


class Cube:
    def __init__(self):
        self.size = lax.axis_size("dp")
        self.bits = self.size.bit_length() - 1
        self.outer = list(range(1, self.bits))
        self.rank = lax.axis_index("dp")
        self.masks = []
        for place in range(self.size):
            mask = place >> (self.bits - 1)
            for bit in self.outer:
                mask |= ((place >> (bit - 1)) & 1) << bit
            self.masks.append(mask)
        self.owners = self.rank ^ jnp.array(self.masks, jnp.int32)

    def swap(self, value, bit, axis="dp"):
        pairs = [(i, i ^ (1 << bit)) for i in range(lax.axis_size(axis))]
        return lax.ppermute(value, axis, pairs)

    def trade(self, value):
        blocks = {mask: value[mask] for mask in range(self.size)}
        for bit in range(self.bits):
            send = sorted(mask for mask in blocks if mask >> bit & 1)
            got = self.swap(jnp.stack([blocks[mask] for mask in send]), bit)
            for place, mask in enumerate(send):
                blocks[mask] = got[place]
        return jnp.stack([blocks[mask] for mask in range(self.size)])

    def spread(self, value):
        held = value[None]
        for bit in range(self.bits):
            held = jnp.concatenate([held, self.swap(held, bit)])
        return held

    def add(self, value, axis):
        for bit in range(lax.axis_size(axis).bit_length() - 1):
            value = value + self.swap(value, bit, axis)
        return value


class Gather:
    def __init__(self, cube, shard, flip):
        self.cube = cube
        self.masks = [0]
        self.pieces = [shard]
        self.todo = cube.outer[::-1] if flip else list(cube.outer)

    def move(self):
        bit = self.todo.pop(0)
        self.masks = self.masks + [mask | (1 << bit) for mask in self.masks]
        self.pieces = self.pieces + [self.cube.swap(piece, bit) for piece in self.pieces]

    def join(self):
        while self.todo:
            self.move()
        order = sorted(range(len(self.masks)), key=lambda i: self.cube.masks.index(self.masks[i]))
        self.pieces = [join_rows([self.pieces[i] for i in order])]

    def weight(self):
        near = self.pieces[0]
        return Lanes(near, self.cube.swap(near, 0))


class Scatter:
    def __init__(self, cube, near, far, flip):
        self.cube = cube
        self.todo = list(cube.outer) if flip else cube.outer[::-1]
        self.rows = near.shape[1] // (cube.size // 2)
        self.places = list(range(cube.size // 2))
        self.near = near
        self.got = []
        self.pieces = [cube.swap(far, 0)]
        self.arriving = self.places
        self.packed = False

    def total(self, places):
        first = places[0]
        step = places[1] - first if len(places) > 1 else 1
        terms = [(self.near, first, step)]
        for value, held in self.got:
            spots = [held.index(place) for place in places]
            terms.append((value, spots[0], spots[1] - spots[0] if len(spots) > 1 else 1))
        return sum_rows(terms, self.rows, len(places))

    def absorb(self):
        self.got.append((self.pieces[0], self.arriving))

    def pack(self):
        self.absorb()
        self.bit = self.todo.pop(0)
        weight = 1 << (self.bit - 1)
        sent = [place for place in self.places if place & weight]
        self.places = [place for place in self.places if not place & weight]
        self.arriving = [place ^ weight for place in sent]
        self.pieces = [self.total(sent)]
        self.packed = True

    def move(self):
        if not self.packed:
            self.pack()
        self.pieces = [self.cube.swap(self.pieces[0], self.bit)]
        self.packed = False

    def result(self):
        while self.todo or self.packed:
            self.move()
        self.absorb()
        return self.total([0])


def pin(value, *others):
    flat = []
    for other in others:
        flat += other.pieces if hasattr(other, "pieces") else [other]
    return tie(value, *flat)[0]


def bind(value, *movers):
    flat = [piece for mover in movers for piece in mover.pieces]
    held = tie(value, *flat)
    spot = 1
    for mover in movers:
        count = len(mover.pieces)
        mover.pieces = list(held[spot : spot + count])
        spot += count
    return held[0]


def hold(movers, *others):
    for mover in movers:
        mover.pieces = [pin(piece, *others) for piece in mover.pieces]


def on_device(
    tokens,
    skip_tokens,
    text,
    timestep,
    grid,
    text_len,
    w_skip,
    w_mod,
    w_qkv,
    w_out1,
    w_query2,
    w_text_kv,
    w_out2,
    w_fc1,
    w_fc2,
    gain_skip,
    gain_attn,
    gain_cross,
    gain_mlp,
    gain_query,
    gain_key,
    cotangent,
):
    micros, slots, width = tokens.shape
    parts = lax.axis_size("sp")
    zone = lax.axis_index("sp")
    cube = Cube()
    ranks = cube.size
    rows = micros * slots
    sequence = slots * parts
    local = H // parts
    lanes = local * HP + -local * HP % 128
    text_slots = text.shape[1]
    text_strip = -(-text_slots // 16) * 16
    features = text.shape[2]
    strip = width // ranks
    middle = width // 2
    kept = w_skip.shape[0]
    skip_lanes = -(-kept // 256) * 256
    skip_cut = skip_lanes // 2
    qkv_cut = (3 * lanes) // 256 * 128 + 128
    text_rows = w_text_kv.shape[0]

    def spread(shard, before=None):
        if before is not None:
            shard, before = tie(shard, before)
        return lax.all_gather(shard, "sp", axis=0, tiled=False)

    def fetch(value, cut):
        return [Gather(cube, value[:, :, :cut], 0), Gather(cube, value[:, :, cut:], 1)]

    def advance(movers):
        for mover in movers:
            mover.move()

    def join(movers):
        for mover in movers:
            mover.join()

    def exchange(value):
        return lax.all_to_all(value, "sp", split_axis=0, concat_axis=0, tiled=True)

    skip_z = spread(jnp.pad(w_skip.T, ((0, 0), (0, skip_lanes - kept))))
    qkv_z = spread(pad_heads(w_qkv.reshape(strip, -1), local), skip_z)
    fc1_z = spread(w_fc1, qkv_z)
    fc2_z = spread(w_fc2.T, fc1_z)
    skip_m = fetch(skip_z, skip_cut)
    while skip_m[0].todo:
        advance(skip_m)
    qkv_m = fetch(qkv_z, qkv_cut)
    hold(qkv_m, *skip_m)
    advance(qkv_m)
    hold(skip_m, qkv_z)
    join(skip_m)
    skip_w = [mover.weight() for mover in skip_m]

    def shuffle(count):
        block = count // ranks
        place = jnp.arange(count, dtype=jnp.int32)
        source = cube.owners[place // block] * block + place % block
        return (place[:, None] == source[None, :]).astype(BF)

    turn = shuffle(width)
    text_turn = shuffle(features)
    gains = jnp.stack([gain_skip, gain_attn, gain_cross, gain_mlp])
    gains = gains.reshape(4, ranks, strip)[:, cube.owners].reshape(4, 2, 1, middle)
    g_skip, g_attn, g_cross, g_mlp = gains

    wide = grid[:, 0, 1]
    counts = grid[:, 0, 0] * wide
    lengths = text_len[:, 0, :]
    place = zone * slots + jnp.arange(slots, dtype=jnp.int32)
    live = (place[None, :] < counts[:, None]).astype(F32).reshape(rows, 1)
    cosine, sine = rope_tables(sequence, wide, lanes)
    gain_q = pad_heads(jnp.tile(gain_query, local)[None, :], local)
    gain_k = pad_heads(jnp.tile(gain_key, local)[None, :], local)

    steps = cube.spread(timestep[:, 0])
    time_act = jax.nn.silu(time_embed(steps, width)).astype(BF).reshape(ranks * micros, parts, -1)
    time_part = lax.dynamic_index_in_dim(time_act, zone, 1, keepdims=False)
    shift = jnp.dot(time_part, w_mod, preferred_element_type=F32)
    shift = cube.trade(cube.add(shift, "sp").reshape(ranks, micros, strip))
    shift = jnp.stack([shift[mask] for mask in cube.masks]).reshape(2, ranks // 2, micros, strip)
    shift = jnp.transpose(shift, (0, 2, 1, 3)).reshape(2, micros, middle)

    grad3 = jnp.stack(
        [
            jnp.dot(cotangent.reshape(rows, width), side, preferred_element_type=F32) * live
            for side in (turn[:, :middle], turn[:, middle:])
        ]
    )
    d_mlp = grad3.astype(BF)

    wide_shape = jax.ShapeDtypeStruct((2, rows, middle), F32)
    low_shape = jax.ShapeDtypeStruct((2, rows, middle), BF)
    gain_shape = jax.ShapeDtypeStruct((2, 1, middle), F32)
    joined = side_by_side(tokens.reshape(rows, width), skip_tokens.reshape(rows, width), kept, skip_lanes)

    def first_norms(sums, extra, out):
        g0_ref, g1_ref, shift_ref = extra
        base_ref, stream_ref, pre_ref = out
        unit, _ = norm_unit(sums)
        stream = [unit[side] * g0_ref[side] for side in range(2)]
        unit, _ = norm_unit(stream)
        for side in range(2):
            base_ref[side] = sums[side]
            stream_ref[side] = stream[side]
            for micro in range(micros):
                cut = slice(micro * slots, (micro + 1) * slots)
                pre = unit[side][cut] * g1_ref[side] + shift_ref[side, micro : micro + 1]
                pre_ref[side, cut] = pre.astype(BF)

    def next_norm(sums, extra, out):
        before_ref, gain_ref = extra
        after_ref, pre_ref = out
        stream = [before_ref[side] + sums[side] for side in range(2)]
        unit, _ = norm_unit(stream)
        for side in range(2):
            after_ref[side] = stream[side]
            pre_ref[side] = (unit[side] * gain_ref[side]).astype(BF)

    base, stream, pre_attn = to_features(
        joined, skip_w, [g_skip, g_attn, shift], [wide_shape, wide_shape, low_shape], first_norms
    )
    while qkv_m[0].todo:
        advance(qkv_m)
    after_qkv = [mover.pieces[-1] for mover in qkv_m]
    hold(qkv_m, pre_attn)
    join(qkv_m)
    pre_attn, fc1_z = tie(pre_attn, fc1_z)
    qkv_w = [mover.weight() for mover in qkv_m]
    projected = to_lanes(pre_attn, qkv_w)
    projected, fc2_z = tie(projected, fc2_z)
    fc_m = [Gather(cube, fc1_z, 0), Gather(cube, fc2_z, 1)]
    hold(fc_m, *after_qkv)
    advance(fc_m)
    raw = exchange(projected.reshape(parts, micros, slots, 3 * lanes))
    cross_z = jnp.concatenate([pad_heads(side, local) for side in (w_out1.T, w_query2, w_out2.T)], 1)
    cross_z = spread(cross_z, raw)
    text_z = jnp.pad(pad_heads(w_text_kv.reshape(text_rows, -1), local), ((0, max(0, strip - text_rows)), (0, 0)))
    text_z = spread(text_z, cross_z)
    text_own = jnp.dot(text.reshape(-1, features), text_turn, preferred_element_type=F32).astype(BF)
    text_own = jnp.pad(
        text_own.reshape(micros, text_slots, features), ((0, 0), (0, text_strip - text_slots), (0, 0))
    ).reshape(micros * text_strip, features)
    text_all = spread(text_own, text_z).reshape(-1, features)
    text_all = jnp.stack([text_all[:, : features // 2], text_all[:, features // 2 :]])
    raw = pin(raw, *fc_m)
    while fc_m[0].todo:
        advance(fc_m)
    attended, turned_q, turned_k, norms = self_forward(raw, counts, cosine, sine, gain_q, gain_k)
    cross_m = fetch(cross_z, 2 * lanes)
    text_m = Gather(cube, text_z[:, :text_rows], 1)
    hold(cross_m, attended)
    advance(cross_m)
    attended = exchange(attended).reshape(parts, rows, lanes)
    hold(fc_m + cross_m + [text_m], attended)
    join(cross_m)
    first_w, out2_w = [mover.weight() for mover in cross_m]
    out1_w, query2_w = (Lanes(first_w.near, first_w.far, lanes, index) for index in range(2))
    join(fc_m)
    fc1_w, fc2_w = [mover.weight() for mover in fc_m]
    text_m.join()
    text_w = text_m.weight()
    stream1, pre_cross = to_features(
        attended, [out1_w], [stream, g_cross], [wide_shape, low_shape], next_norm
    )
    query2 = to_lanes(pre_cross, [query2_w]).reshape(parts, micros, slots, lanes)
    text_kv = to_lanes(text_all, [text_w]).reshape(parts, parts, micros, text_strip, 2 * lanes)
    crossed = cross_forward(query2, text_kv, lengths, text_slots).reshape(parts, rows, lanes)
    stream2, pre_mlp = to_features(
        crossed, [out2_w], [stream1, g_mlp], [wide_shape, low_shape], next_norm
    )
    hidden0, activ0, partial, fc2_n0, fc2_f0 = mlp_forward(pre_mlp, d_mlp, stream2, fc1_w, fc2_w, 0)
    hidden1, activ1, result, fc2_n1, fc2_f1 = mlp_forward(pre_mlp, d_mlp, partial, fc1_w, fc2_w, 1, live)
    fc2_s = [Scatter(cube, fc2_n0, fc2_f0, 0), Scatter(cube, fc2_n1, fc2_f1, 1)]

    def pack(movers):
        for mover in movers:
            mover.pack()

    def settle(values, before=None):
        value = values[0] if len(values) == 1 else jnp.concatenate(values, 2)
        if before is not None:
            value, before = tie(value, before)
        return lax.psum_scatter(value, "sp", scatter_dimension=0, tiled=False)

    fc1_n0, fc1_f0, partial = mlp_backward(d_mlp, pre_mlp, hidden0, fc1_w, fc2_w, 0, None)
    pack(fc2_s)
    partial = bind(partial, *fc2_s)
    advance(fc2_s)
    fc1_n1, fc1_f1, grad2, d_cross, d_gain_mlp = mlp_backward(
        d_mlp, pre_mlp, hidden1, fc1_w, fc2_w, 1, partial, [stream2, g_mlp, grad3]
    )
    fc1_s = [Scatter(cube, fc1_n0, fc1_f0, 0), Scatter(cube, fc1_n1, fc1_f1, 1)]
    d_crossed = to_lanes(d_cross, [out2_w])
    d_crossed = bind(d_crossed, *fc2_s)
    d_query2, d_text_kv = cross_backward(
        query2, text_kv, lengths, d_crossed.reshape(parts, micros, slots, lanes), text_slots
    )
    pack(fc2_s)
    pack(fc1_s)
    d_query2 = bind(d_query2, *fc2_s, *fc1_s)
    advance(fc2_s)
    advance(fc1_s)
    d_query2 = d_query2.reshape(parts, rows, lanes)
    d_text_kv = d_text_kv.reshape(parts, -1, 2 * lanes)

    def go_back(sums, extra, out):
        add_norm_back(sums, *extra, *out)

    grad1, d_attn, d_gain_cross = to_features(
        d_query2, [query2_w], [stream1, g_cross, grad2], [wide_shape, low_shape, gain_shape], go_back
    )
    d_attended = to_lanes(d_attn, [out1_w])
    d_heads = exchange(d_attended.reshape(parts, micros, slots, lanes))

    def words_back(sums, extra, out):
        size = micros * text_strip
        for zone in range(parts):
            for side in range(2):
                out[0][zone, side] = sums[side][zone * size : (zone + 1) * size].astype(BF)

    words_shape = jax.ShapeDtypeStruct((parts, 2, micros * text_strip, features // 2), BF)
    d_words = to_features(d_text_kv, [text_w], [], [words_shape], words_back)[0]
    d_words = settle([d_words])
    text_s = Scatter(cube, *terms_of([(text_all, d_text_kv, 2 * lanes, 0)]), 1)
    cross_s = Scatter(
        cube,
        *terms_of([(d_attn, attended, lanes, 0), (pre_cross, d_query2, lanes, 0), (d_cross, crossed, lanes, 0)]),
        0,
    )
    total_fc2 = [mover.result() for mover in fc2_s]
    term_fc2 = settle(total_fc2)
    d_raw, d_gain_q, d_gain_k = self_backward(
        raw, counts, cosine, sine, gain_q, gain_k, turned_q, turned_k, norms, d_heads
    )
    d_raw, term_fc2, d_words = tie(d_raw, term_fc2, d_words)
    d_raw = bind(d_raw, *fc1_s, cross_s, text_s)
    d_projected = exchange(d_raw).reshape(parts, rows, 3 * lanes)
    advance(fc1_s)
    pack([cross_s, text_s])
    hold([cross_s, text_s], d_raw)
    advance([cross_s, text_s])
    d_projected = bind(d_projected, *fc1_s, cross_s, text_s)
    total_fc1 = [mover.result() for mover in fc1_s]

    def last_norms(sums, extra, out):
        stream_ref, g1_ref, base_ref, g0_ref, add_ref = extra
        low_ref, d_shift_ref, d_g1_ref, d_g0_ref = out
        back, gains1 = norm_back([stream_ref[0], stream_ref[1]], g1_ref, sums)
        total = [add_ref[side] + back[side] for side in range(2)]
        back, gains0 = norm_back([base_ref[0], base_ref[1]], g0_ref, total)
        for side in range(2):
            low_ref[side] = back[side].astype(BF)
            d_g1_ref[side] = gains1[side]
            d_g0_ref[side] = gains0[side]
            for micro in range(micros):
                part = sums[side][micro * slots : (micro + 1) * slots]
                d_shift_ref[side, micro : micro + 1] = jnp.sum(part, 0, keepdims=True)

    qkv_s = [
        Scatter(cube, *terms_of([(pre_attn, d_projected, 2 * lanes, 0)]), 0),
        Scatter(cube, *terms_of([(pre_attn, d_projected, lanes, 2)]), 1),
    ]
    term_fc1 = settle(total_fc1, qkv_s[0].near)
    shift_shape = jax.ShapeDtypeStruct((2, micros, middle), F32)
    d_base, d_shift, d_gain_attn, d_gain_skip = to_features(
        d_projected,
        qkv_w,
        [stream, g_attn, base, g_skip, grad1],
        [low_shape, shift_shape, gain_shape, gain_shape],
        last_norms,
    )
    pack(qkv_s)
    d_base = bind(d_base, *qkv_s)
    advance(qkv_s)
    skip_s = [
        Scatter(cube, *terms_of([(d_base, joined, skip_cut, flip)]), flip) for flip in range(2)
    ]
    total_cross, total_text = cross_s.result(), text_s.result()
    pack(skip_s)
    hold(skip_s, total_cross, total_text, *qkv_s)
    advance(skip_s)
    term_cross = settle([total_cross])
    term_text = settle([total_text])
    term_qkv = settle([mover.result() for mover in qkv_s])
    term_skip = settle([mover.result() for mover in skip_s])
    d_joined = to_inputs(d_base, skip_w, kept)
    result = (
        jnp.dot(result[0], turn[:, :middle].T, preferred_element_type=F32)
        + jnp.dot(result[1], turn[:, middle:].T, preferred_element_type=F32)
    ).astype(BF)
    d_words = d_words.reshape(2, micros * text_strip, features // 2)
    d_words = jnp.dot(
        d_words[0], text_turn[:, : features // 2].T, preferred_element_type=F32
    ) + jnp.dot(d_words[1], text_turn[:, features // 2 :].T, preferred_element_type=F32)
    d_words = d_words.reshape(micros, text_strip, features)[:, :text_slots]

    d_shift = jnp.transpose(d_shift.reshape(2, micros, ranks // 2, strip), (0, 2, 1, 3))
    d_shift = d_shift.reshape(ranks, micros, strip)
    d_shift = jnp.stack([d_shift[cube.masks.index(mask)] for mask in range(ranks)])
    d_shift = cube.add(cube.trade(d_shift), "sp").reshape(ranks * micros, strip)
    term_mod = lax.dot_general(
        time_part.astype(F32), d_shift, (((0,), (0,)), ((), ())), precision=lax.Precision.HIGHEST
    )

    places = jnp.array([cube.masks.index(mask) for mask in range(ranks)], jnp.int32)
    places = places[jnp.arange(ranks, dtype=jnp.int32) ^ cube.rank]
    gains = jnp.stack([d_gain_skip, d_gain_attn, d_gain_cross, d_gain_mlp])
    gains = gains.reshape(4, ranks, strip)[:, places].reshape(-1)
    heads = jnp.stack([jnp.sum(d_gain_q, (0, 1)), jnp.sum(d_gain_k, (0, 1))])
    heads = jnp.sum(heads[:, : local * HP].reshape(2, local, HP)[:, :, :HD], 1)
    packed = jnp.concatenate([gains, heads.reshape(-1)])
    packed = cube.add(cube.add(packed, "sp"), "dp")
    gains = packed[: 4 * width].reshape(4, ranks * parts, -1)
    gains = lax.dynamic_index_in_dim(gains, cube.rank * parts + zone, 1, keepdims=False)
    heads = packed[4 * width :].reshape(2, HD)

    def whole(term, groups):
        return cut_heads(term.astype(F32), local).reshape(term.shape[0], groups, -1)

    return (
        result.reshape(tokens.shape),
        d_joined[0].reshape(tokens.shape),
        d_joined[1].reshape(tokens.shape),
        d_words.reshape(text.shape),
        term_skip.astype(F32)[:, :kept].T,
        term_mod,
        whole(term_qkv, 3),
        cut_heads(term_cross[:, :lanes].astype(F32), local).T,
        cut_heads(term_cross[:, lanes : 2 * lanes].astype(F32), local),
        whole(term_text, 2),
        cut_heads(term_cross[:, 2 * lanes :].astype(F32), local).T,
        term_fc1.astype(F32),
        term_fc2.astype(F32).T,
        gains[0],
        gains[1],
        gains[2],
        gains[3],
        heads[0],
        heads[1],
    )


def solution(mesh):
    rows = P(None, ("dp", "sp"), None)
    column = P("sp", "dp")
    row = P("dp", "sp")
    grouped = P("dp", None, "sp")
    in_specs = (
        (rows, rows, rows, P(None, "dp"), P(None, "dp", None), P(None, "dp", None))
        + (column, column, grouped, column, row, grouped, column, row, column)
        + (P(),) * 6
        + (rows,)
    )
    out_specs = (
        (rows, rows, rows, rows)
        + (column, column, grouped, column, row, grouped, column, row, column)
        + (P(("dp", "sp")),) * 4
        + (P(), P())
    )
    return jax.shard_map(
        on_device, mesh=mesh, in_specs=in_specs, out_specs=out_specs, check_vma=False
    )
```

```python
import math

import jax
import jax.numpy as jnp
from jax import lax
from jax.experimental import pallas as pl
from jax.experimental.pallas import tpu as pltpu
from jax.sharding import PartitionSpec as P

H = 16
HD = 88
HP = 96
CLIP_LEN = 77
ROWS = 256

EPS = 1e-06
MASKED = -1e30
LOG2E = 1.4426950408889634
BF = jnp.bfloat16
F32 = jnp.float32


def time_embed(step, width):
    half = width // 2
    rate = jnp.exp(-math.log(10000.0) * jnp.arange(half, dtype=F32) / half)
    angle = step.astype(F32)[..., None] * rate
    return jnp.concatenate([jnp.cos(angle), jnp.sin(angle)], -1)


def rope_tables(sequence, wide, lanes):
    place = jnp.arange(sequence, dtype=jnp.int32)[None, :, None]
    wide = wide[:, None, None]
    lane = jnp.arange(lanes, dtype=jnp.int32)[None, None, :] % HP
    pair = lane // 2
    quarter = HD // 4
    upper = pair < quarter
    rank = jnp.where(upper, pair, pair - quarter).astype(F32)
    rate = jnp.exp(-math.log(10000.0) * rank / quarter)
    angle = jnp.where(upper, place // wide, place % wide).astype(F32) * rate
    sine = jnp.sin(angle)
    return jnp.cos(angle), jnp.where(lane % 2 == 0, -sine, sine)


def pad_heads(packed, local):
    rows, lanes = packed.shape
    groups = packed.reshape(rows, lanes // (local * HD), local, HD)
    groups = jnp.pad(groups, ((0, 0), (0, 0), (0, 0), (0, HP - HD)))
    groups = groups.reshape(rows, -1, local * HP)
    return jnp.pad(groups, ((0, 0), (0, 0), (0, -local * HP % 128))).reshape(rows, -1)


def cut_heads(padded, local):
    rows = padded.shape[0]
    groups = padded.reshape(rows, -1, local * HP + -local * HP % 128)[:, :, : local * HP]
    return groups.reshape(rows, -1, local, HP)[..., :HD].reshape(rows, -1)


def head_masks(shape, local):
    lane = lax.broadcasted_iota(jnp.int32, shape, len(shape) - 1)
    inside = lane % HP < HD
    return [((lane // HP == h) & inside).astype(F32) for h in range(local)]


def head_mean(value, masks):
    total = None
    for mask in masks:
        term = (jnp.sum(value * mask, -1, keepdims=True) * (1.0 / HD)) * mask
        total = term if total is None else total + term
    return total


def head_unit(value, masks):
    centre = value - head_mean(value, masks)
    spread = None
    square = centre * centre
    for mask in masks:
        mean = jnp.sum(square * mask, -1, keepdims=True) * (1.0 / HD)
        term = lax.rsqrt(mean + EPS) * mask
        spread = term if spread is None else spread + term
    return centre * spread, spread


def turn_pairs(value):
    lanes = value.shape[-1]
    after = pltpu.roll(value, lanes - 1, 1)
    before = pltpu.roll(value, 1, 1)
    lane = lax.broadcasted_iota(jnp.int32, value.shape, 1)
    return jnp.where(lane % 2 == 0, after, before)


def dot_nt(left, right):
    return lax.dot_general(left, right, (((1,), (1,)), ((), ())), preferred_element_type=F32)


def dot_nn(left, right):
    return lax.dot_general(left, right, (((1,), (0,)), ((), ())), preferred_element_type=F32)


def dot_tn(left, right):
    return lax.dot_general(left, right, (((0,), (0,)), ((), ())), preferred_element_type=F32)


def self_forward(raw, counts, cosine, sine, gain_q, gain_k):
    parts, micros, slots, packed = raw.shape
    lanes = packed // 3
    local = lanes // HP
    sequence = parts * slots
    factor = HD ** (-0.5) * LOG2E

    def kernel(count_ref, raw_ref, cos_ref, sin_ref, gq_ref, gk_ref, out_ref, q_ref, k_ref, lse_ref):
        count = count_ref[pl.program_id(0)]
        blocks = (count + slots - 1) // slots
        out_ref[...] = jnp.zeros_like(out_ref)
        masks = head_masks((1, lanes), local)

        def prepare(part, carry):
            spot = pl.ds(pl.multiple_of(part * slots, slots), slots)
            cosine, sine = cos_ref[0, spot, :], sin_ref[0, spot, :]
            for index, gain_ref, dest in ((0, gq_ref, q_ref), (1, gk_ref, k_ref)):
                value = raw_ref[part, 0, :, index * lanes : (index + 1) * lanes].astype(F32)
                scaled = head_unit(value, masks)[0] * gain_ref[...]
                dest[0, spot, :] = (scaled * cosine + turn_pairs(scaled) * sine).astype(BF)
            return carry

        lax.fori_loop(0, parts, prepare, 0)
        column = lax.broadcasted_iota(jnp.int32, (1, sequence), 1)
        bias = jnp.where(column < count, 0.0, MASKED)
        for h in range(local):
            cut = slice(h * HP, (h + 1) * HP)
            keys = k_ref[0, :, cut]
            values = raw_ref[:, 0, :, 2 * lanes + h * HP : 2 * lanes + (h + 1) * HP].reshape(sequence, HP)

            def one_block(part, carry):
                spot = pl.ds(pl.multiple_of(part * slots, slots), slots)
                scores = dot_nt(q_ref[0, spot, cut], keys) + bias
                top = jnp.max(scores, -1, keepdims=True)
                raised = jnp.exp2((scores - top) * factor)
                total = jnp.sum(raised, -1, keepdims=True)
                result = dot_nn(raised.astype(BF), values) / total
                out_ref[part, 0, :, cut] = result.astype(BF)
                norm = jnp.broadcast_to(top * factor + jnp.log2(total), (slots, 128))
                lse_ref[0, h : h + 1, spot] = jnp.transpose(norm)[0:1, :]
                return carry

            lax.fori_loop(0, blocks, one_block, 0)

    whole = lambda m, c: (0, m, 0, 0)
    table = lambda m, c: (m, 0, 0)
    fixed = lambda m, c: (0, 0)
    return pl.pallas_call(
        kernel,
        name="self_forward",
        grid_spec=pltpu.PrefetchScalarGridSpec(
            num_scalar_prefetch=1,
            grid=(micros,),
            in_specs=[
                pl.BlockSpec((parts, 1, slots, packed), whole),
                pl.BlockSpec((1, sequence, lanes), table),
                pl.BlockSpec((1, sequence, lanes), table),
                pl.BlockSpec((1, lanes), fixed),
                pl.BlockSpec((1, lanes), fixed),
            ],
            out_specs=[
                pl.BlockSpec((parts, 1, slots, lanes), whole),
                pl.BlockSpec((1, sequence, lanes), table),
                pl.BlockSpec((1, sequence, lanes), table),
                pl.BlockSpec((1, local, sequence), table),
            ],
        ),
        out_shape=[
            jax.ShapeDtypeStruct((parts, micros, slots, lanes), BF),
            jax.ShapeDtypeStruct((micros, sequence, lanes), BF),
            jax.ShapeDtypeStruct((micros, sequence, lanes), BF),
            jax.ShapeDtypeStruct((micros, local, sequence), F32),
        ],
        compiler_params=params(),
        cost_estimate=cost(4 * micros * local * sequence * sequence * HP),
    )(counts, raw, cosine, sine, gain_q, gain_k)


def self_backward(raw, counts, cosine, sine, gain_q, gain_k, turned_q, turned_k, norms, incoming):
    parts, micros, slots, packed = raw.shape
    lanes = packed // 3
    local = lanes // HP
    sequence = parts * slots
    scale = HD ** (-0.5)
    factor = scale * LOG2E

    def kernel(
        count_ref,
        raw_ref,
        cos_ref,
        sin_ref,
        gq_ref,
        gk_ref,
        q_ref,
        k_ref,
        lse_ref,
        in_ref,
        out_ref,
        dgq_ref,
        dgk_ref,
        dq_s,
        dk_s,
        dv_s,
    ):
        count = count_ref[pl.program_id(0)]
        blocks = (count + slots - 1) // slots
        dq_s[...] = jnp.zeros_like(dq_s)
        dk_s[...] = jnp.zeros_like(dk_s)
        dv_s[...] = jnp.zeros_like(dv_s)
        row = lax.broadcasted_iota(jnp.int32, (sequence, 1), 0)
        bias = jnp.where(row < count, 0.0, MASKED)
        for h in range(local):
            cut = slice(h * HP, (h + 1) * HP)
            keys = k_ref[0, :, cut]
            values = raw_ref[:, 0, :, 2 * lanes + h * HP : 2 * lanes + (h + 1) * HP].reshape(sequence, HP)

            def one_block(part, carry):
                spot = pl.ds(pl.multiple_of(part * slots, slots), slots)
                rows = q_ref[0, spot, cut]
                grads = in_ref[part, 0, :, cut]
                norm = lse_ref[0, h : h + 1, spot]
                probs = jnp.exp2(dot_nt(keys, rows) * factor + bias - norm)
                d_probs = dot_nt(values, grads)
                inner = jnp.sum(probs * d_probs, 0, keepdims=True)
                d_scores = (probs * (d_probs - inner)).astype(BF)
                dv_s[:, cut] += dot_nn(probs.astype(BF), grads)
                dk_s[:, cut] += dot_nn(d_scores, rows)
                dq_s[spot, cut] = dot_tn(d_scores, keys)
                return carry

            lax.fori_loop(0, blocks, one_block, 0)
        masks = head_masks((1, lanes), local)

        def finish(part, carry):
            spot = pl.ds(pl.multiple_of(part * slots, slots), slots)
            cosine, sine = cos_ref[0, spot, :], sin_ref[0, spot, :]
            sums = []
            for index, gain_ref, source in ((0, gq_ref, dq_s), (1, gk_ref, dk_s)):
                grad = source[spot, :] * scale
                grad = grad * cosine - turn_pairs(grad) * sine
                value = raw_ref[part, 0, :, index * lanes : (index + 1) * lanes].astype(F32)
                unit, spread = head_unit(value, masks)
                leading = grad * gain_ref[...]
                back = leading - head_mean(leading, masks) - unit * head_mean(leading * unit, masks)
                out_ref[part, 0, :, index * lanes : (index + 1) * lanes] = (spread * back).astype(BF)
                sums.append(carry[index] + jnp.sum(grad * unit, 0, keepdims=True))
            out_ref[part, 0, :, 2 * lanes : 3 * lanes] = dv_s[spot, :].astype(BF)
            return tuple(sums)

        zero = jnp.zeros((1, lanes), F32)
        d_gains = lax.fori_loop(0, parts, finish, (zero, zero))
        dgq_ref[0] = d_gains[0]
        dgk_ref[0] = d_gains[1]

    whole = lambda m, c: (0, m, 0, 0)
    table = lambda m, c: (m, 0, 0)
    fixed = lambda m, c: (0, 0)
    return pl.pallas_call(
        kernel,
        name="self_backward",
        grid_spec=pltpu.PrefetchScalarGridSpec(
            num_scalar_prefetch=1,
            grid=(micros,),
            in_specs=[
                pl.BlockSpec((parts, 1, slots, packed), whole),
                pl.BlockSpec((1, sequence, lanes), table),
                pl.BlockSpec((1, sequence, lanes), table),
                pl.BlockSpec((1, lanes), fixed),
                pl.BlockSpec((1, lanes), fixed),
                pl.BlockSpec((1, sequence, lanes), table),
                pl.BlockSpec((1, sequence, lanes), table),
                pl.BlockSpec((1, local, sequence), table),
                pl.BlockSpec((parts, 1, slots, lanes), whole),
            ],
            out_specs=[
                pl.BlockSpec((parts, 1, slots, packed), whole),
                pl.BlockSpec((1, 1, lanes), table),
                pl.BlockSpec((1, 1, lanes), table),
            ],
            scratch_shapes=[pltpu.VMEM((sequence, lanes), F32) for index in range(3)],
        ),
        out_shape=[
            jax.ShapeDtypeStruct((parts, micros, slots, packed), BF),
            jax.ShapeDtypeStruct((micros, 1, lanes), F32),
            jax.ShapeDtypeStruct((micros, 1, lanes), F32),
        ],
        compiler_params=params(),
        cost_estimate=cost(10 * micros * local * sequence * sequence * HP),
    )(counts, raw, cosine, sine, gain_q, gain_k, turned_q, turned_k, norms, incoming)


def cost(flops):
    return pl.CostEstimate(flops=flops // 16, bytes_accessed=flops // 16000, transcendentals=0)


def full(shape):
    return pl.BlockSpec(shape, lambda *index: (0,) * len(shape))


def params(megabytes=60):
    return pltpu.CompilerParams(vmem_limit_bytes=megabytes << 20)


class Lanes:
    def __init__(self, near, far, block=None, index=0):
        self.near, self.far = near, far
        self.block = block or near.shape[2]
        self.index = index

    def spec(self):
        index = self.index
        return pl.BlockSpec((1, self.near.shape[1], self.block), lambda p, *rest: (p, 0, index))


def to_lanes(value, weights, dtype=BF, name="to_lanes"):
    rows = value.shape[1]
    parts, half, _ = weights[0].near.shape
    total = sum(weight.block for weight in weights)

    def kernel(x_ref, *refs):
        out_ref = refs[-1]
        at = 0
        for index, weight in enumerate(weights):
            result = dot_nn(x_ref[0], refs[2 * index][0]) + dot_nn(x_ref[1], refs[2 * index + 1][0])
            out_ref[0, :, at : at + weight.block] = result.astype(dtype)
            at += weight.block

    return pl.pallas_call(
        kernel,
        name=name,
        grid=(parts,),
        in_specs=[full(value.shape)] + [weight.spec() for weight in weights for side in range(2)],
        out_specs=pl.BlockSpec((1, rows, total), lambda p: (p, 0, 0)),
        out_shape=jax.ShapeDtypeStruct((parts, rows, total), dtype),
        compiler_params=params(),
        cost_estimate=cost(4 * rows * half * parts * total),
    )(value, *[side for weight in weights for side in (weight.near, weight.far)])


def to_inputs(value, weights, kept):
    rows = value.shape[1]
    parts, half, _ = weights[0].near.shape
    sides = parts // 2

    def kernel(x_ref, *refs):
        out_ref = refs[-1]
        for side in range(sides):

            @pl.when(pl.program_id(0) % sides == side)
            def _():
                at = 0
                for index, weight in enumerate(weights):
                    result = dot_nn(x_ref[0], refs[2 * index][0]) + dot_nn(
                        x_ref[1], refs[2 * index + 1][0]
                    )
                    take = min(weight.block, kept - at)
                    start = side * kept + at
                    out_ref[0, :, start : start + take] = result[:, :take]
                    at += take

    return pl.pallas_call(
        kernel,
        name="to_inputs",
        grid=(parts,),
        in_specs=[full(value.shape)] + [weight.spec() for weight in weights for side in range(2)],
        out_specs=pl.BlockSpec((1, rows, sides * kept), lambda p: (p // sides, 0, 0)),
        out_shape=jax.ShapeDtypeStruct((2, rows, sides * kept), F32),
        compiler_params=params(),
        cost_estimate=cost(4 * rows * half * parts * kept),
    )(value, *[side for weight in weights for side in (weight.near, weight.far)])


def to_features(value, weights, extras, outs, finish, name="to_features"):
    parts, rows, total = value.shape
    half = weights[0].near.shape[1]
    count = 2 * len(weights)

    def kernel(*refs):
        y_ref, weight_refs = refs[0], refs[1 : 1 + count]
        extra_refs = refs[1 + count : 1 + count + len(extras)]
        out_refs = refs[1 + count + len(extras) : -1]
        sums = refs[-1]

        @pl.when(pl.program_id(0) == 0)
        def _():
            sums[...] = jnp.zeros_like(sums)

        at = 0
        for index, weight in enumerate(weights):
            left = y_ref[0, :, at : at + weight.block]
            for side in range(2):
                sums[side] += dot_nt(left, weight_refs[2 * index + side][0])
            at += weight.block

        @pl.when(pl.program_id(0) == parts - 1)
        def _():
            finish([sums[0], sums[1]], extra_refs, out_refs)

    return pl.pallas_call(
        kernel,
        name=name,
        grid=(parts,),
        in_specs=[pl.BlockSpec((1, rows, total), lambda p: (p, 0, 0))]
        + [weight.spec() for weight in weights for side in range(2)]
        + [full(extra.shape) for extra in extras],
        out_specs=[full(out.shape) for out in outs],
        out_shape=outs,
        scratch_shapes=[pltpu.VMEM((2, rows, half), F32)],
        compiler_params=params(),
        cost_estimate=cost(4 * rows * half * parts * total),
    )(value, *[side for weight in weights for side in (weight.near, weight.far)], *extras)


def terms_of(pairs, name="terms_of"):
    half = pairs[0][0].shape[2]
    parts = pairs[0][1].shape[0]
    total = sum(pair[2] for pair in pairs)
    rows = [pair[0].shape[1] for pair in pairs]

    def kernel(*refs):
        count = len(pairs)
        lefts, rights = refs[:count], refs[count : 2 * count]
        near_ref, far_ref = refs[2 * count : 2 * count + 2]
        turned = refs[2 * count + 2 :]

        @pl.when(pl.program_id(0) == 0)
        def _():
            for left, flat in zip(lefts, turned):
                for side in range(2):
                    flat[side] = jnp.transpose(left[side])

        at = 0
        for pair, right, flat in zip(pairs, rights, turned):
            lanes = pair[2]
            near_ref[0, :, at : at + lanes] = dot_nn(flat[0], right[0]).astype(BF)
            far_ref[0, :, at : at + lanes] = dot_nn(flat[1], right[0]).astype(BF)
            at += lanes

    def right_spec(pair):
        return pl.BlockSpec((1, pair[1].shape[1], pair[2]), lambda p: (p, 0, pair[3]))

    out = jax.ShapeDtypeStruct((parts, half, total), BF)
    return pl.pallas_call(
        kernel,
        name=name,
        grid=(parts,),
        in_specs=[full(pair[0].shape) for pair in pairs] + [right_spec(pair) for pair in pairs],
        out_specs=[pl.BlockSpec((1, half, total), lambda p: (p, 0, 0))] * 2,
        out_shape=[out, out],
        scratch_shapes=[pltpu.VMEM((2, half, count), BF) for count in rows],
        compiler_params=params(),
        cost_estimate=cost(sum(4 * half * parts * pair[2] * count for pair, count in zip(pairs, rows))),
    )(*[pair[0] for pair in pairs], *[pair[1] for pair in pairs])


def norm_unit(halves):
    width = 2 * halves[0].shape[-1]
    mean = sum(jnp.sum(half, -1, keepdims=True) for half in halves) / width
    centre = [half - mean for half in halves]
    spread = sum(jnp.sum(half * half, -1, keepdims=True) for half in centre) / width
    scale = lax.rsqrt(spread + EPS)
    return [half * scale for half in centre], scale


def norm_back(halves, gain_ref, incoming):
    width = 2 * halves[0].shape[-1]
    unit, scale = norm_unit(halves)
    leading = [incoming[side] * gain_ref[side] for side in range(2)]
    mean = sum(jnp.sum(half, -1, keepdims=True) for half in leading) / width
    inner = sum(jnp.sum(leading[side] * unit[side], -1, keepdims=True) for side in range(2)) / width
    back = [scale * (leading[side] - mean - unit[side] * inner) for side in range(2)]
    gains = [jnp.sum(incoming[side] * unit[side], 0, keepdims=True) for side in range(2)]
    return back, gains


def join_rows(pieces, name="join_rows"):
    parts, rows, lanes = pieces[0].shape
    count = len(pieces)
    if rows % 16:
        return jnp.concatenate(pieces, 1)

    def kernel(*refs):
        for index in range(count):
            refs[-1][0, index * rows : (index + 1) * rows] = refs[index][0]

    return pl.pallas_call(
        kernel,
        name=name,
        grid=(parts,),
        in_specs=[pl.BlockSpec((1, rows, lanes), lambda p: (p, 0, 0))] * count,
        out_specs=pl.BlockSpec((1, count * rows, lanes), lambda p: (p, 0, 0)),
        out_shape=jax.ShapeDtypeStruct((parts, count * rows, lanes), BF),
        compiler_params=params(),
        cost_estimate=cost(parts * count * rows * lanes),
    )(*pieces)


def sum_rows(jobs, rows, name="sum_rows"):
    parts = jobs[0][0][0].shape[0]
    if rows % 16:
        results = []
        for terms in jobs:
            value = 0.0
            for array, blocks in terms:
                split = array.reshape(parts, -1, rows, array.shape[2])
                value = value + jnp.stack([split[:, block] for block in blocks], 1).astype(F32)
            results.append(value.astype(BF).reshape(parts, -1, value.shape[3]))
        return results
    arrays = [term[0] for terms in jobs for term in terms]

    def kernel(*refs):
        at = 0
        for spot, terms in enumerate(jobs):
            out_ref = refs[len(arrays) + spot]
            for index in range(len(terms[0][1])):
                value = None
                for offset, (_, blocks) in enumerate(terms):
                    start = blocks[index] * rows
                    term = refs[at + offset][0, start : start + rows].astype(F32)
                    value = term if value is None else value + term
                out_ref[0, index * rows : (index + 1) * rows] = value.astype(BF)
            at += len(terms)

    def spec(size, lanes):
        return pl.BlockSpec((1, size, lanes), lambda p: (p, 0, 0))

    shapes = [(len(terms[0][1]) * rows, terms[0][0].shape[2]) for terms in jobs]
    return pl.pallas_call(
        kernel,
        name=name,
        grid=(parts,),
        in_specs=[spec(*array.shape[1:]) for array in arrays],
        out_specs=[spec(*shape) for shape in shapes],
        out_shape=[jax.ShapeDtypeStruct((parts, *shape), BF) for shape in shapes],
        compiler_params=params(),
        cost_estimate=cost(sum(parts * size * lanes for size, lanes in shapes)),
    )(*arrays)


def side_by_side(left, right, kept, lanes):
    rows, width = left.shape
    count = width // kept

    def kernel(left_ref, right_ref, out_ref):
        for index, ref in enumerate((left_ref, right_ref)):
            for side in range(count):
                spot = count * index + side
                out_ref[spot, :, :kept] = ref[:, side * kept : (side + 1) * kept]
                if lanes > kept:
                    out_ref[spot, :, kept:] = jnp.zeros((rows, lanes - kept), BF)

    return pl.pallas_call(
        kernel,
        name="side_by_side",
        out_shape=jax.ShapeDtypeStruct((2 * count, rows, lanes), BF),
        compiler_params=params(),
        cost_estimate=cost(4 * rows * lanes),
    )(left, right)


def mlp_forward(rows_in, grads, start, weight1, weight2, part, live=None):
    _, rows, half = rows_in.shape
    parts, _, lanes = weight1.near.shape
    ff = lanes // 2
    step = 384 if ff % 384 == 0 else ff
    steps = ff // step
    extras = [] if live is None else [live]

    def kernel(x_ref, g_ref, s_ref, n1_ref, f1_ref, n2_ref, f2_ref, *refs):
        hid_ref, act_ref, out_ref, dn2_ref, df2_ref, turned, sums = refs[len(extras) :]
        first = (pl.program_id(0) == 0) & (pl.program_id(1) == 0)
        last = (pl.program_id(0) == parts - 1) & (pl.program_id(1) == steps - 1)

        @pl.when(first)
        def _():
            for side in range(2):
                turned[side] = jnp.transpose(g_ref[side])
            sums[...] = s_ref[...]

        hidden = dot_nn(x_ref[0], n1_ref[0]) + dot_nn(x_ref[1], f1_ref[0])
        hid_ref[0] = hidden
        activ = jax.nn.gelu(hidden, approximate=True).astype(BF)
        act_ref[0] = activ
        sums[0] += dot_nt(activ, n2_ref[0])
        sums[1] += dot_nt(activ, f2_ref[0])
        dn2_ref[0] = dot_nn(turned[0], activ).astype(BF)
        df2_ref[0] = dot_nn(turned[1], activ).astype(BF)

        @pl.when(last)
        def _():
            if live is None:
                out_ref[...] = sums[...]
            else:
                out_ref[...] = (sums[...] * refs[0][...]).astype(BF)

    weight = pl.BlockSpec((1, half, step), lambda p, n: (p, 0, part * steps + n))
    grad = pl.BlockSpec((1, half, step), lambda p, n: (p, 0, n))
    unit = pl.BlockSpec((1, rows, step), lambda p, n: (p, 0, n))
    whole = full((2, rows, half))
    grad_shape = jax.ShapeDtypeStruct((parts, half, ff), BF)
    return pl.pallas_call(
        kernel,
        name="mlp_forward",
        grid=(parts, steps),
        in_specs=[whole, whole, whole, weight, weight, weight, weight] + [full(extra.shape) for extra in extras],
        out_specs=[unit, unit, whole, grad, grad],
        out_shape=[
            jax.ShapeDtypeStruct((parts, rows, ff), F32),
            jax.ShapeDtypeStruct((parts, rows, ff), BF),
            jax.ShapeDtypeStruct((2, rows, half), F32 if live is None else BF),
            grad_shape,
            grad_shape,
        ],
        scratch_shapes=[pltpu.VMEM((2, half, rows), BF), pltpu.VMEM((2, rows, half), F32)],
        compiler_params=params(),
        cost_estimate=cost(12 * rows * half * parts * ff),
    )(rows_in, grads, start, weight1.near, weight1.far, weight2.near, weight2.far, *extras)


def gelu_slope(value):
    root = math.sqrt(2.0 / math.pi)
    square = value * value
    curve = jnp.tanh(root * value * (1.0 + 0.044715 * square))
    return 0.5 * (1.0 + curve) + 0.5 * value * (1.0 - curve * curve) * root * (
        1.0 + 3.0 * 0.044715 * square
    )


def mlp_backward(grads, rows_in, hidden, weight1, weight2, part, start, finish=None):
    _, rows, half = rows_in.shape
    parts, _, lanes = weight1.near.shape
    ff = lanes // 2
    step = 384 if ff % 384 == 0 else ff
    steps = ff // step
    extras = list(finish or []) + ([] if start is None else [start])

    def kernel(g_ref, x_ref, hid_ref, n1_ref, f1_ref, n2_ref, f2_ref, *refs):
        extra_refs, refs = refs[: len(extras)], refs[len(extras) :]
        dn1_ref, df1_ref = refs[:2]
        out_refs = refs[2:-2]
        turned, sums = refs[-2:]
        first = (pl.program_id(0) == 0) & (pl.program_id(1) == 0)
        last = (pl.program_id(0) == parts - 1) & (pl.program_id(1) == steps - 1)

        @pl.when(first)
        def _():
            for side in range(2):
                turned[side] = jnp.transpose(x_ref[side])
            sums[...] = jnp.zeros_like(sums) if start is None else extra_refs[-1][...]

        d_activ = dot_nn(g_ref[0], n2_ref[0]) + dot_nn(g_ref[1], f2_ref[0])
        d_hidden = (d_activ * gelu_slope(hid_ref[0])).astype(BF)
        dn1_ref[0] = dot_nn(turned[0], d_hidden).astype(BF)
        df1_ref[0] = dot_nn(turned[1], d_hidden).astype(BF)
        sums[0] += dot_nt(d_hidden, n1_ref[0])
        sums[1] += dot_nt(d_hidden, f1_ref[0])

        @pl.when(last)
        def _():
            if finish is None:
                out_refs[0][...] = sums[...]
            else:
                value_ref, gain_ref, add_ref = extra_refs[:3]
                add_norm_back([sums[0], sums[1]], value_ref, gain_ref, add_ref, *out_refs)

    weight = pl.BlockSpec((1, half, step), lambda p, n: (p, 0, part * steps + n))
    grad = pl.BlockSpec((1, half, step), lambda p, n: (p, 0, n))
    unit = pl.BlockSpec((1, rows, step), lambda p, n: (p, 0, n))
    whole = full((2, rows, half))
    grad_shape = jax.ShapeDtypeStruct((parts, half, ff), BF)
    wide = jax.ShapeDtypeStruct((2, rows, half), F32)
    outs = [wide] if finish is None else [wide, *back_shapes(rows, half)]
    return pl.pallas_call(
        kernel,
        name="mlp_backward",
        grid=(parts, steps),
        in_specs=[whole, whole, unit, weight, weight, weight, weight] + [full(extra.shape) for extra in extras],
        out_specs=[grad, grad] + [full(out.shape) for out in outs],
        out_shape=[grad_shape, grad_shape] + outs,
        scratch_shapes=[pltpu.VMEM((2, half, rows), BF), pltpu.VMEM((2, rows, half), F32)],
        compiler_params=params(),
        cost_estimate=cost(12 * rows * half * parts * ff),
    )(grads, rows_in, hidden, weight1.near, weight1.far, weight2.near, weight2.far, *extras)


def back_shapes(rows, half):
    return [jax.ShapeDtypeStruct((2, rows, half), BF), jax.ShapeDtypeStruct((2, 1, half), F32)]


def add_norm_back(incoming, value_ref, gain_ref, add_ref, out_ref, low_ref, d_gain_ref):
    back, gains = norm_back([value_ref[0], value_ref[1]], gain_ref, incoming)
    for side in range(2):
        total = add_ref[side] + back[side]
        out_ref[side] = total
        low_ref[side] = total.astype(BF)
        d_gain_ref[side] = gains[side]


def text_bias(lengths_ref, micro, words, strip, text_slots, axis):
    spot = lax.broadcasted_iota(jnp.int32, (1, words) if axis else (words, 1), axis)
    inner = spot % strip
    place = spot // strip * text_slots + inner
    live = (place < lengths_ref[micro, 0]) | (
        (place >= CLIP_LEN) & (place < CLIP_LEN + lengths_ref[micro, 1])
    )
    return jnp.where(live & (inner < text_slots), 0.0, MASKED)


def cross_forward(query, text_kv, lengths, text_slots):
    parts, micros, slots, lanes = query.shape
    zones, strip = text_kv.shape[1], text_kv.shape[3]
    words = zones * strip
    local = lanes // HP
    factor = HD ** (-0.5) * LOG2E

    def kernel(len_ref, q_ref, kv_ref, out_ref):
        bias = text_bias(len_ref, pl.program_id(1), words, strip, text_slots, 1)
        for h in range(local):
            cut = slice(h * HP, (h + 1) * HP)
            keys = kv_ref[0, :, 0, :, cut].reshape(words, HP)
            scores = dot_nt(q_ref[0, 0, :, cut], keys) + bias
            top = jnp.max(scores, -1, keepdims=True)
            raised = jnp.exp2((scores - top) * factor)
            total = jnp.sum(raised, -1, keepdims=True)
            values = kv_ref[0, :, 0, :, lanes + h * HP : lanes + (h + 1) * HP].reshape(words, HP)
            out_ref[0, 0, :, cut] = (dot_nn(raised.astype(BF), values) / total).astype(BF)

    spot = lambda p, m, c: (p, m, 0, 0)
    far = lambda p, m, c: (p, 0, m, 0, 0)
    return pl.pallas_call(
        kernel,
        name="cross_forward",
        grid_spec=pltpu.PrefetchScalarGridSpec(
            num_scalar_prefetch=1,
            grid=(parts, micros),
            in_specs=[
                pl.BlockSpec((1, 1, slots, lanes), spot),
                pl.BlockSpec((1, zones, 1, strip, 2 * lanes), far),
            ],
            out_specs=pl.BlockSpec((1, 1, slots, lanes), spot),
        ),
        out_shape=jax.ShapeDtypeStruct(query.shape, BF),
        compiler_params=params(),
        cost_estimate=cost(4 * parts * micros * slots * words * lanes),
    )(lengths, query, text_kv)


def cross_backward(query, text_kv, lengths, incoming, text_slots):
    parts, micros, slots, lanes = query.shape
    zones, strip = text_kv.shape[1], text_kv.shape[3]
    words = zones * strip
    local = lanes // HP
    scale = HD ** (-0.5)
    factor = scale * LOG2E

    def kernel(len_ref, q_ref, kv_ref, in_ref, dq_ref, dkv_ref):
        bias = text_bias(len_ref, pl.program_id(1), words, strip, text_slots, 0)
        for h in range(local):
            cut = slice(h * HP, (h + 1) * HP)
            far = slice(lanes + h * HP, lanes + (h + 1) * HP)
            rows = q_ref[0, 0, :, cut]
            keys = kv_ref[0, :, 0, :, cut].reshape(words, HP)
            values = kv_ref[0, :, 0, :, far].reshape(words, HP)
            grads = in_ref[0, 0, :, cut]
            scores = dot_nt(keys, rows) + bias
            top = jnp.max(scores, 0, keepdims=True)
            raised = jnp.exp2((scores - top) * factor)
            probs = raised * (1.0 / jnp.sum(raised, 0, keepdims=True))
            d_probs = dot_nt(values, grads)
            inner = jnp.sum(probs * d_probs, 0, keepdims=True)
            d_scores = (probs * (d_probs - inner)).astype(BF)
            shape = (zones, strip, HP)
            dkv_ref[0, :, 0, :, far] = dot_nn(probs.astype(BF), grads).astype(BF).reshape(shape)
            dkv_ref[0, :, 0, :, cut] = (dot_nn(d_scores, rows) * scale).astype(BF).reshape(shape)
            dq_ref[0, 0, :, cut] = (dot_tn(d_scores, keys) * scale).astype(BF)

    spot = lambda p, m, c: (p, m, 0, 0)
    far = lambda p, m, c: (p, 0, m, 0, 0)
    return pl.pallas_call(
        kernel,
        name="cross_backward",
        grid_spec=pltpu.PrefetchScalarGridSpec(
            num_scalar_prefetch=1,
            grid=(parts, micros),
            in_specs=[
                pl.BlockSpec((1, 1, slots, lanes), spot),
                pl.BlockSpec((1, zones, 1, strip, 2 * lanes), far),
                pl.BlockSpec((1, 1, slots, lanes), spot),
            ],
            out_specs=[
                pl.BlockSpec((1, 1, slots, lanes), spot),
                pl.BlockSpec((1, zones, 1, strip, 2 * lanes), far),
            ],
        ),
        out_shape=[
            jax.ShapeDtypeStruct(query.shape, BF),
            jax.ShapeDtypeStruct(text_kv.shape, BF),
        ],
        compiler_params=params(),
        cost_estimate=cost(10 * parts * micros * slots * words * lanes),
    )(lengths, query, text_kv, incoming)


def tie(*values):
    return lax.optimization_barrier(values)


class Cube:
    def __init__(self):
        self.size = lax.axis_size("dp")
        self.bits = self.size.bit_length() - 1
        self.outer = list(range(1, self.bits))
        self.rank = lax.axis_index("dp")
        self.masks = []
        for place in range(self.size):
            mask = place >> (self.bits - 1)
            for bit in self.outer:
                mask |= ((place >> (bit - 1)) & 1) << bit
            self.masks.append(mask)
        self.owners = self.rank ^ jnp.array(self.masks, jnp.int32)

    def swap(self, value, bit, axis="dp"):
        pairs = [(i, i ^ (1 << bit)) for i in range(lax.axis_size(axis))]
        return lax.ppermute(value, axis, pairs)

    def trade(self, value):
        blocks = {mask: value[mask] for mask in range(self.size)}
        for bit in range(self.bits):
            send = sorted(mask for mask in blocks if mask >> bit & 1)
            got = self.swap(jnp.stack([blocks[mask] for mask in send]), bit)
            for place, mask in enumerate(send):
                blocks[mask] = got[place]
        return jnp.stack([blocks[mask] for mask in range(self.size)])

    def spread(self, value):
        held = value[None]
        for bit in range(self.bits):
            held = jnp.concatenate([held, self.swap(held, bit)])
        return held

    def add(self, value, axis):
        for bit in range(lax.axis_size(axis).bit_length() - 1):
            value = value + self.swap(value, bit, axis)
        return value


class Gather:
    def __init__(self, cube, shard, flip):
        self.cube = cube
        self.masks = [0]
        self.pieces = [shard]
        self.todo = cube.outer[::-1] if flip else list(cube.outer)

    def move(self):
        bit = self.todo.pop(0)
        self.masks = self.masks + [mask | (1 << bit) for mask in self.masks]
        self.pieces = self.pieces + [self.cube.swap(piece, bit) for piece in self.pieces]

    def join(self):
        while self.todo:
            self.move()
        order = sorted(range(len(self.masks)), key=lambda i: self.cube.masks.index(self.masks[i]))
        self.pieces = [join_rows([self.pieces[i] for i in order])]

    def weight(self):
        near = self.pieces[0]
        return Lanes(near, self.cube.swap(near, 0))


class Scatter:
    def __init__(self, cube, near, far, flip):
        self.cube = cube
        self.todo = list(cube.outer) if flip else cube.outer[::-1]
        self.rows = near.shape[1] // (cube.size // 2)
        self.places = list(range(cube.size // 2))
        self.near = near
        self.got = []
        self.pieces = [cube.swap(far, 0)]
        self.arriving = self.places

    def job(self, places):
        return [(self.near, places)] + [
            (value, [held.index(place) for place in places]) for value, held in self.got
        ]

    def absorb(self):
        self.got.append((self.pieces[0], self.arriving))


def pack(movers):
    jobs = []
    for mover in movers:
        mover.absorb()
        mover.bit = mover.todo.pop(0)
        weight = 1 << (mover.bit - 1)
        sent = [place for place in mover.places if place & weight]
        mover.places = [place for place in mover.places if not place & weight]
        mover.arriving = [place ^ weight for place in sent]
        jobs.append(mover.job(sent))
    for mover, value in zip(movers, sum_rows(jobs, movers[0].rows)):
        mover.pieces = [value]


def send(movers):
    for mover in movers:
        mover.pieces = [mover.cube.swap(mover.pieces[0], mover.bit)]


def results(movers):
    while movers[0].todo:
        pack(movers)
        send(movers)
    for mover in movers:
        mover.absorb()
    return sum_rows([mover.job([0]) for mover in movers], movers[0].rows)


def pin(value, *others):
    flat = []
    for other in others:
        flat += other.pieces if hasattr(other, "pieces") else [other]
    return tie(value, *flat)[0]


def bind(value, *movers):
    flat = [piece for mover in movers for piece in mover.pieces]
    held = tie(value, *flat)
    spot = 1
    for mover in movers:
        count = len(mover.pieces)
        mover.pieces = list(held[spot : spot + count])
        spot += count
    return held[0]


def hold(movers, *others):
    for mover in movers:
        mover.pieces = [pin(piece, *others) for piece in mover.pieces]


def on_device(
    tokens,
    skip_tokens,
    text,
    timestep,
    grid,
    text_len,
    w_skip,
    w_mod,
    w_qkv,
    w_out1,
    w_query2,
    w_text_kv,
    w_out2,
    w_fc1,
    w_fc2,
    gain_skip,
    gain_attn,
    gain_cross,
    gain_mlp,
    gain_query,
    gain_key,
    cotangent,
):
    micros, slots, width = tokens.shape
    parts = lax.axis_size("sp")
    zone = lax.axis_index("sp")
    cube = Cube()
    ranks = cube.size
    rows = micros * slots
    sequence = slots * parts
    local = H // parts
    lanes = local * HP + -local * HP % 128
    text_slots = text.shape[1]
    text_strip = -(-text_slots // 16) * 16
    features = text.shape[2]
    strip = width // ranks
    middle = width // 2
    kept = w_skip.shape[0]
    skip_lanes = -(-kept // 256) * 256
    skip_cut = skip_lanes // 2
    qkv_cut = (3 * lanes) // 256 * 128 + 128
    text_rows = w_text_kv.shape[0]

    def spread(shard, before=None):
        if before is not None:
            shard, before = tie(shard, before)
        return lax.all_gather(shard, "sp", axis=0, tiled=False)

    def fetch(value, cut):
        return [Gather(cube, value[:, :, :cut], 0), Gather(cube, value[:, :, cut:], 1)]

    def advance(movers):
        for mover in movers:
            mover.move()

    def join(movers):
        for mover in movers:
            mover.join()

    def exchange(value):
        return lax.all_to_all(value, "sp", split_axis=0, concat_axis=0, tiled=True)

    skip_z = spread(jnp.pad(w_skip.T, ((0, 0), (0, skip_lanes - kept))))
    steps = cube.spread(timestep[:, 0])
    skip_z, steps = tie(skip_z, steps)
    skip_m = fetch(skip_z, skip_cut)
    qkv_z = spread(pad_heads(w_qkv.reshape(strip, -1), local), skip_z)
    advance(skip_m)

    time_act = jax.nn.silu(time_embed(steps, width)).astype(BF).reshape(ranks * micros, parts, -1)
    time_part = lax.dynamic_index_in_dim(time_act, zone, 1, keepdims=False)
    shift = cube.add(jnp.dot(time_part, w_mod, preferred_element_type=F32), "sp")
    skip_m[0].pieces[1], shift = tie(skip_m[0].pieces[1], shift)
    while skip_m[0].todo:
        advance(skip_m)
    shift = cube.trade(shift.reshape(ranks, micros, strip))
    skip_m[0].pieces[-1], shift = tie(skip_m[0].pieces[-1], shift)
    shift = jnp.stack([shift[mask] for mask in cube.masks]).reshape(2, ranks // 2, micros, strip)
    shift = jnp.transpose(shift, (0, 2, 1, 3)).reshape(2, micros, middle)
    qkv_m = fetch(qkv_z, qkv_cut)
    hold(qkv_m, *skip_m)
    advance(qkv_m)
    fc1_z = spread(pin(w_fc1, *skip_m))
    fc2_z = spread(pin(w_fc2.T, *qkv_m))
    join(skip_m)
    skip_w = [mover.weight() for mover in skip_m]

    def shuffle(count):
        block = count // ranks
        place = jnp.arange(count, dtype=jnp.int32)
        source = cube.owners[place // block] * block + place % block
        return (place[:, None] == source[None, :]).astype(BF)

    turn = shuffle(width)
    text_turn = shuffle(features)
    gains = jnp.stack([gain_skip, gain_attn, gain_cross, gain_mlp])
    gains = gains.reshape(4, ranks, strip)[:, cube.owners].reshape(4, 2, 1, middle)
    g_skip, g_attn, g_cross, g_mlp = gains

    wide = grid[:, 0, 1]
    counts = grid[:, 0, 0] * wide
    lengths = text_len[:, 0, :]
    place = zone * slots + jnp.arange(slots, dtype=jnp.int32)
    live = (place[None, :] < counts[:, None]).astype(F32).reshape(rows, 1)
    cosine, sine = rope_tables(sequence, wide, lanes)
    gain_q = pad_heads(jnp.tile(gain_query, local)[None, :], local)
    gain_k = pad_heads(jnp.tile(gain_key, local)[None, :], local)

    grad3 = jnp.stack(
        [
            jnp.dot(cotangent.reshape(rows, width), side, preferred_element_type=F32) * live
            for side in (turn[:, :middle], turn[:, middle:])
        ]
    )
    d_mlp = grad3.astype(BF)

    wide_shape = jax.ShapeDtypeStruct((2, rows, middle), F32)
    low_shape = jax.ShapeDtypeStruct((2, rows, middle), BF)
    gain_shape = jax.ShapeDtypeStruct((2, 1, middle), F32)
    joined = side_by_side(tokens.reshape(rows, width), skip_tokens.reshape(rows, width), kept, skip_lanes)

    def first_norms(sums, extra, out):
        g0_ref, g1_ref, shift_ref = extra
        base_ref, stream_ref, pre_ref = out
        unit, _ = norm_unit(sums)
        stream = [unit[side] * g0_ref[side] for side in range(2)]
        unit, _ = norm_unit(stream)
        for side in range(2):
            base_ref[side] = sums[side]
            stream_ref[side] = stream[side]
            for micro in range(micros):
                cut = slice(micro * slots, (micro + 1) * slots)
                pre = unit[side][cut] * g1_ref[side] + shift_ref[side, micro : micro + 1]
                pre_ref[side, cut] = pre.astype(BF)

    def next_norm(sums, extra, out):
        before_ref, gain_ref = extra
        after_ref, pre_ref = out
        stream = [before_ref[side] + sums[side] for side in range(2)]
        unit, _ = norm_unit(stream)
        for side in range(2):
            after_ref[side] = stream[side]
            pre_ref[side] = (unit[side] * gain_ref[side]).astype(BF)

    base, stream, pre_attn = to_features(
        joined, skip_w, [g_skip, g_attn, shift], [wide_shape, wide_shape, low_shape], first_norms
    )
    while qkv_m[0].todo:
        advance(qkv_m)
    after_qkv = [mover.pieces[-1] for mover in qkv_m]
    hold(qkv_m, pre_attn)
    join(qkv_m)
    pre_attn, fc1_z = tie(pre_attn, fc1_z)
    qkv_w = [mover.weight() for mover in qkv_m]
    projected = to_lanes(pre_attn, qkv_w)
    projected, fc2_z = tie(projected, fc2_z)
    fc_m = [Gather(cube, fc1_z, 0), Gather(cube, fc2_z, 1)]
    hold(fc_m, *after_qkv)
    advance(fc_m)
    raw = exchange(projected.reshape(parts, micros, slots, 3 * lanes))
    cross_z = jnp.concatenate([pad_heads(side, local) for side in (w_out1.T, w_query2, w_out2.T)], 1)
    cross_z = spread(pin(cross_z, *fc_m))
    text_own = jnp.dot(text.reshape(-1, features), text_turn, preferred_element_type=F32).astype(BF)
    text_own = jnp.pad(
        text_own.reshape(micros, text_slots, features), ((0, 0), (0, text_strip - text_slots), (0, 0))
    ).reshape(micros * text_strip, features)
    text_z = jnp.pad(pad_heads(w_text_kv.reshape(text_rows, -1), local), ((0, max(0, strip - text_rows)), (0, 0)))
    while fc_m[0].todo:
        advance(fc_m)
    attended, turned_q, turned_k, norms = self_forward(raw, counts, cosine, sine, gain_q, gain_k)
    attended = bind(attended, *fc_m)
    attended, cross_z = tie(attended, cross_z)
    text_z = spread(text_z, cross_z)
    cross_m = fetch(cross_z, 2 * lanes)
    advance(cross_m)
    attended = exchange(attended).reshape(parts, rows, lanes)
    attended, text_z = tie(attended, text_z)
    attended = bind(attended, *cross_m)
    text_all = spread(text_own, text_z).reshape(-1, features)
    text_all = jnp.stack([text_all[:, : features // 2], text_all[:, features // 2 :]])
    text_m = Gather(cube, text_z[:, :text_rows], 1)
    hold(fc_m, attended)
    join(cross_m)
    first_w, out2_w = [mover.weight() for mover in cross_m]
    out1_w, query2_w = (Lanes(first_w.near, first_w.far, lanes, index) for index in range(2))
    text_m.join()
    text_w = text_m.weight()
    join(fc_m)
    fc1_w, fc2_w = [mover.weight() for mover in fc_m]
    stream1, pre_cross = to_features(
        attended, [out1_w], [stream, g_cross], [wide_shape, low_shape], next_norm
    )
    query2 = to_lanes(pre_cross, [query2_w]).reshape(parts, micros, slots, lanes)
    text_kv = to_lanes(text_all, [text_w]).reshape(parts, parts, micros, text_strip, 2 * lanes)
    crossed = cross_forward(query2, text_kv, lengths, text_slots).reshape(parts, rows, lanes)
    stream2, pre_mlp = to_features(
        crossed, [out2_w], [stream1, g_mlp], [wide_shape, low_shape], next_norm
    )
    hidden0, activ0, partial, fc2_n0, fc2_f0 = mlp_forward(pre_mlp, d_mlp, stream2, fc1_w, fc2_w, 0)
    hidden1, activ1, result, fc2_n1, fc2_f1 = mlp_forward(pre_mlp, d_mlp, partial, fc1_w, fc2_w, 1, live)
    fc2_s = [Scatter(cube, fc2_n0, fc2_f0, 0), Scatter(cube, fc2_n1, fc2_f1, 1)]

    def settle(values, before=None):
        value = values[0] if len(values) == 1 else jnp.concatenate(values, 2)
        if before is not None:
            value, before = tie(value, before)
        return lax.psum_scatter(value, "sp", scatter_dimension=0, tiled=False)

    fc1_n0, fc1_f0, partial = mlp_backward(d_mlp, pre_mlp, hidden0, fc1_w, fc2_w, 0, None)
    fc1_s = [Scatter(cube, fc1_n0, fc1_f0, 0)]
    pack(fc2_s)
    partial = bind(partial, *fc2_s)
    send(fc2_s)
    fc1_n1, fc1_f1, grad2, d_cross, d_gain_mlp = mlp_backward(
        d_mlp, pre_mlp, hidden1, fc1_w, fc2_w, 1, partial, [stream2, g_mlp, grad3]
    )
    fc1_s.append(Scatter(cube, fc1_n1, fc1_f1, 1))
    d_cross = bind(d_cross, *fc2_s)
    d_crossed = to_lanes(d_cross, [out2_w])
    pack(fc2_s)
    d_crossed = bind(d_crossed, *fc2_s)
    send(fc2_s)
    d_query2, d_text_kv = cross_backward(
        query2, text_kv, lengths, d_crossed.reshape(parts, micros, slots, lanes), text_slots
    )
    d_query2 = bind(d_query2, *fc2_s)
    d_query2 = d_query2.reshape(parts, rows, lanes)
    d_text_kv = d_text_kv.reshape(parts, -1, 2 * lanes)
    total_fc2 = results(fc2_s)
    term_fc2 = settle(total_fc2)

    def go_back(sums, extra, out):
        add_norm_back(sums, *extra, *out)

    grad1, d_attn, d_gain_cross = to_features(
        d_query2, [query2_w], [stream1, g_cross, grad2], [wide_shape, low_shape, gain_shape], go_back
    )
    d_attn = bind(d_attn, *fc1_s)
    pack(fc1_s)
    d_attn = bind(d_attn, *fc1_s)
    send(fc1_s)
    d_attended = to_lanes(d_attn, [out1_w])
    d_attended, d_text_kv, pre_cross = tie(d_attended, d_text_kv, pre_cross)
    d_heads = exchange(d_attended.reshape(parts, micros, slots, lanes))

    def words_back(sums, extra, out):
        size = micros * text_strip
        for zone in range(parts):
            for side in range(2):
                out[0][zone, side] = sums[side][zone * size : (zone + 1) * size].astype(BF)

    words_shape = jax.ShapeDtypeStruct((parts, 2, micros * text_strip, features // 2), BF)
    d_words = to_features(d_text_kv, [text_w], [], [words_shape], words_back)[0]
    text_t = list(terms_of([(text_all, d_text_kv, 2 * lanes, 0)]))
    cross_t = terms_of(
        [(d_attn, attended, lanes, 0), (pre_cross, d_query2, lanes, 0), (d_cross, crossed, lanes, 0)]
    )
    cross_t = list(cross_t)
    d_heads, d_words, text_t[1], cross_t[1] = tie(d_heads, d_words, text_t[1], cross_t[1])
    d_words = settle([d_words])
    text_s, cross_s = Scatter(cube, *text_t, 1), Scatter(cube, *cross_t, 0)
    d_heads = bind(d_heads, *fc1_s)
    pack(fc1_s)
    d_heads = bind(d_heads, *fc1_s)
    send(fc1_s)
    d_raw, d_gain_q, d_gain_k = self_backward(
        raw, counts, cosine, sine, gain_q, gain_k, turned_q, turned_k, norms, d_heads
    )
    d_raw, term_fc2, d_words = tie(d_raw, term_fc2, d_words)
    d_raw = bind(d_raw, *fc1_s)
    d_projected = exchange(d_raw).reshape(parts, rows, 3 * lanes)
    other_s = [cross_s, text_s]
    total_fc1 = results(fc1_s)
    pack([cross_s])
    pack([text_s])
    send(other_s)
    d_projected = bind(d_projected, *other_s)
    pack([cross_s])
    pack([text_s])
    send(other_s)

    def last_norms(sums, extra, out):
        stream_ref, g1_ref, base_ref, g0_ref, add_ref = extra
        low_ref, d_shift_ref, d_g1_ref, d_g0_ref = out
        back, gains1 = norm_back([stream_ref[0], stream_ref[1]], g1_ref, sums)
        total = [add_ref[side] + back[side] for side in range(2)]
        back, gains0 = norm_back([base_ref[0], base_ref[1]], g0_ref, total)
        for side in range(2):
            low_ref[side] = back[side].astype(BF)
            d_g1_ref[side] = gains1[side]
            d_g0_ref[side] = gains0[side]
            for micro in range(micros):
                part = sums[side][micro * slots : (micro + 1) * slots]
                d_shift_ref[side, micro : micro + 1] = jnp.sum(part, 0, keepdims=True)

    qkv_s = [
        Scatter(cube, *terms_of([(pre_attn, d_projected, 2 * lanes, 0)]), 0),
        Scatter(cube, *terms_of([(pre_attn, d_projected, lanes, 2)]), 1),
    ]
    term_fc1 = settle(total_fc1, qkv_s[0].near)
    shift_shape = jax.ShapeDtypeStruct((2, micros, middle), F32)
    d_base, d_shift, d_gain_attn, d_gain_skip = to_features(
        d_projected,
        qkv_w,
        [stream, g_attn, base, g_skip, grad1],
        [low_shape, shift_shape, gain_shape, gain_shape],
        last_norms,
    )
    d_base = bind(d_base, *qkv_s, *other_s)
    pack(qkv_s)
    d_base = bind(d_base, *qkv_s)
    send(qkv_s)
    skip_s = [
        Scatter(cube, *terms_of([(d_base, joined, skip_cut, flip)]), flip) for flip in range(2)
    ]
    term_cross, term_text = settle(results([cross_s])), settle(results([text_s]))
    pack(skip_s)
    hold(skip_s, *qkv_s)
    send(skip_s)
    pack(qkv_s)
    send(qkv_s)
    term_qkv = settle(results(qkv_s))
    term_skip = settle(results(skip_s))
    d_joined = to_inputs(d_base, skip_w, kept)
    result = (
        jnp.dot(result[0], turn[:, :middle].T, preferred_element_type=F32)
        + jnp.dot(result[1], turn[:, middle:].T, preferred_element_type=F32)
    ).astype(BF)
    d_words = d_words.reshape(2, micros * text_strip, features // 2)
    d_words = jnp.dot(
        d_words[0], text_turn[:, : features // 2].T, preferred_element_type=F32
    ) + jnp.dot(d_words[1], text_turn[:, features // 2 :].T, preferred_element_type=F32)
    d_words = d_words.reshape(micros, text_strip, features)[:, :text_slots]

    d_shift = jnp.transpose(d_shift.reshape(2, micros, ranks // 2, strip), (0, 2, 1, 3))
    d_shift = d_shift.reshape(ranks, micros, strip)
    d_shift = jnp.stack([d_shift[cube.masks.index(mask)] for mask in range(ranks)])
    d_shift = cube.add(cube.trade(d_shift), "sp").reshape(ranks * micros, strip)
    term_mod = lax.dot_general(
        time_part.astype(F32), d_shift, (((0,), (0,)), ((), ())), precision=lax.Precision.HIGHEST
    )

    places = jnp.array([cube.masks.index(mask) for mask in range(ranks)], jnp.int32)
    places = places[jnp.arange(ranks, dtype=jnp.int32) ^ cube.rank]
    gains = jnp.stack([d_gain_skip, d_gain_attn, d_gain_cross, d_gain_mlp])
    gains = gains.reshape(4, ranks, strip)[:, places].reshape(-1)
    heads = jnp.stack([jnp.sum(d_gain_q, (0, 1)), jnp.sum(d_gain_k, (0, 1))])
    heads = jnp.sum(heads[:, : local * HP].reshape(2, local, HP)[:, :, :HD], 1)
    packed = jnp.concatenate([gains, heads.reshape(-1)])
    packed = cube.add(cube.add(packed, "sp"), "dp")
    gains = packed[: 4 * width].reshape(4, ranks * parts, -1)
    gains = lax.dynamic_index_in_dim(gains, cube.rank * parts + zone, 1, keepdims=False)
    heads = packed[4 * width :].reshape(2, HD)

    def whole(term, groups):
        return cut_heads(term.astype(F32), local).reshape(term.shape[0], groups, -1)

    return (
        result.reshape(tokens.shape),
        d_joined[0].reshape(tokens.shape),
        d_joined[1].reshape(tokens.shape),
        d_words.reshape(text.shape),
        term_skip.astype(F32)[:, :kept].T,
        term_mod,
        whole(term_qkv, 3),
        cut_heads(term_cross[:, :lanes].astype(F32), local).T,
        cut_heads(term_cross[:, lanes : 2 * lanes].astype(F32), local),
        whole(term_text, 2),
        cut_heads(term_cross[:, 2 * lanes :].astype(F32), local).T,
        term_fc1.astype(F32),
        term_fc2.astype(F32).T,
        gains[0],
        gains[1],
        gains[2],
        gains[3],
        heads[0],
        heads[1],
    )


def solution(mesh):
    rows = P(None, ("dp", "sp"), None)
    column = P("sp", "dp")
    row = P("dp", "sp")
    grouped = P("dp", None, "sp")
    in_specs = (
        (rows, rows, rows, P(None, "dp"), P(None, "dp", None), P(None, "dp", None))
        + (column, column, grouped, column, row, grouped, column, row, column)
        + (P(),) * 6
        + (rows,)
    )
    out_specs = (
        (rows, rows, rows, rows)
        + (column, column, grouped, column, row, grouped, column, row, column)
        + (P(("dp", "sp")),) * 4
        + (P(), P())
    )
    return jax.shard_map(
        on_device, mesh=mesh, in_specs=in_specs, out_specs=out_specs, check_vma=False
    )
```

```python
import math

import jax
import jax.numpy as jnp
from jax import lax
from jax.experimental import pallas as pl
from jax.experimental.pallas import tpu as pltpu
from jax.sharding import PartitionSpec as P

H = 16
HD = 88
HP = 96
CLIP_LEN = 77
ROWS = 256

EPS = 1e-06
MASKED = -1e30
LOG2E = 1.4426950408889634
BF = jnp.bfloat16
F32 = jnp.float32


def time_embed(step, width):
    half = width // 2
    rate = jnp.exp(-math.log(10000.0) * jnp.arange(half, dtype=F32) / half)
    angle = step.astype(F32)[..., None] * rate
    return jnp.concatenate([jnp.cos(angle), jnp.sin(angle)], -1)


def rope_tables(sequence, wide, lanes):
    place = jnp.arange(sequence, dtype=jnp.int32)[None, :, None]
    wide = wide[:, None, None]
    lane = jnp.arange(lanes, dtype=jnp.int32)[None, None, :] % HP
    pair = lane // 2
    quarter = HD // 4
    upper = pair < quarter
    rank = jnp.where(upper, pair, pair - quarter).astype(F32)
    rate = jnp.exp(-math.log(10000.0) * rank / quarter)
    angle = jnp.where(upper, place // wide, place % wide).astype(F32) * rate
    sine = jnp.sin(angle)
    return jnp.cos(angle), jnp.where(lane % 2 == 0, -sine, sine)


def pad_heads(packed, local):
    rows, lanes = packed.shape
    groups = packed.reshape(rows, lanes // (local * HD), local, HD)
    groups = jnp.pad(groups, ((0, 0), (0, 0), (0, 0), (0, HP - HD)))
    groups = groups.reshape(rows, -1, local * HP)
    return jnp.pad(groups, ((0, 0), (0, 0), (0, -local * HP % 128))).reshape(rows, -1)


def cut_heads(padded, local):
    rows = padded.shape[0]
    groups = padded.reshape(rows, -1, local * HP + -local * HP % 128)[:, :, : local * HP]
    return groups.reshape(rows, -1, local, HP)[..., :HD].reshape(rows, -1)


def head_masks(shape, local):
    lane = lax.broadcasted_iota(jnp.int32, shape, len(shape) - 1)
    inside = lane % HP < HD
    return [((lane // HP == h) & inside).astype(F32) for h in range(local)]


def head_mean(value, masks):
    total = None
    for mask in masks:
        term = (jnp.sum(value * mask, -1, keepdims=True) * (1.0 / HD)) * mask
        total = term if total is None else total + term
    return total


def head_unit(value, masks):
    centre = value - head_mean(value, masks)
    spread = None
    square = centre * centre
    for mask in masks:
        mean = jnp.sum(square * mask, -1, keepdims=True) * (1.0 / HD)
        term = lax.rsqrt(mean + EPS) * mask
        spread = term if spread is None else spread + term
    return centre * spread, spread


def turn_pairs(value):
    lanes = value.shape[-1]
    after = pltpu.roll(value, lanes - 1, 1)
    before = pltpu.roll(value, 1, 1)
    lane = lax.broadcasted_iota(jnp.int32, value.shape, 1)
    return jnp.where(lane % 2 == 0, after, before)


def dot_nt(left, right):
    return lax.dot_general(left, right, (((1,), (1,)), ((), ())), preferred_element_type=F32)


def dot_nn(left, right):
    return lax.dot_general(left, right, (((1,), (0,)), ((), ())), preferred_element_type=F32)


def dot_tn(left, right):
    return lax.dot_general(left, right, (((0,), (0,)), ((), ())), preferred_element_type=F32)


def self_forward(raw, counts, cosine, sine, gain_q, gain_k):
    parts, micros, slots, packed = raw.shape
    lanes = packed // 3
    local = lanes // HP
    sequence = parts * slots
    factor = HD ** (-0.5) * LOG2E

    def kernel(count_ref, raw_ref, cos_ref, sin_ref, gq_ref, gk_ref, out_ref, q_ref, k_ref, lse_ref):
        count = count_ref[pl.program_id(0)]
        blocks = (count + slots - 1) // slots
        out_ref[...] = jnp.zeros_like(out_ref)
        masks = head_masks((1, lanes), local)

        def prepare(part, carry):
            spot = pl.ds(pl.multiple_of(part * slots, slots), slots)
            cosine, sine = cos_ref[0, spot, :], sin_ref[0, spot, :]
            for index, gain_ref, dest in ((0, gq_ref, q_ref), (1, gk_ref, k_ref)):
                value = raw_ref[part, 0, :, index * lanes : (index + 1) * lanes].astype(F32)
                scaled = head_unit(value, masks)[0] * gain_ref[...]
                dest[0, spot, :] = (scaled * cosine + turn_pairs(scaled) * sine).astype(BF)
            return carry

        lax.fori_loop(0, parts, prepare, 0)
        column = lax.broadcasted_iota(jnp.int32, (1, sequence), 1)
        bias = jnp.where(column < count, 0.0, MASKED)
        for h in range(local):
            cut = slice(h * HP, (h + 1) * HP)
            keys = k_ref[0, :, cut]
            values = raw_ref[:, 0, :, 2 * lanes + h * HP : 2 * lanes + (h + 1) * HP].reshape(sequence, HP)

            def one_block(part, carry):
                spot = pl.ds(pl.multiple_of(part * slots, slots), slots)
                scores = dot_nt(q_ref[0, spot, cut], keys) + bias
                top = jnp.max(scores, -1, keepdims=True)
                raised = jnp.exp2((scores - top) * factor)
                total = jnp.sum(raised, -1, keepdims=True)
                result = dot_nn(raised.astype(BF), values) / total
                out_ref[part, 0, :, cut] = result.astype(BF)
                norm = jnp.broadcast_to(top * factor + jnp.log2(total), (slots, 128))
                lse_ref[0, h : h + 1, spot] = jnp.transpose(norm)[0:1, :]
                return carry

            lax.fori_loop(0, blocks, one_block, 0)

    whole = lambda m, c: (0, m, 0, 0)
    table = lambda m, c: (m, 0, 0)
    fixed = lambda m, c: (0, 0)
    return pl.pallas_call(
        kernel,
        name="self_forward",
        grid_spec=pltpu.PrefetchScalarGridSpec(
            num_scalar_prefetch=1,
            grid=(micros,),
            in_specs=[
                pl.BlockSpec((parts, 1, slots, packed), whole),
                pl.BlockSpec((1, sequence, lanes), table),
                pl.BlockSpec((1, sequence, lanes), table),
                pl.BlockSpec((1, lanes), fixed),
                pl.BlockSpec((1, lanes), fixed),
            ],
            out_specs=[
                pl.BlockSpec((parts, 1, slots, lanes), whole),
                pl.BlockSpec((1, sequence, lanes), table),
                pl.BlockSpec((1, sequence, lanes), table),
                pl.BlockSpec((1, local, sequence), table),
            ],
        ),
        out_shape=[
            jax.ShapeDtypeStruct((parts, micros, slots, lanes), BF),
            jax.ShapeDtypeStruct((micros, sequence, lanes), BF),
            jax.ShapeDtypeStruct((micros, sequence, lanes), BF),
            jax.ShapeDtypeStruct((micros, local, sequence), F32),
        ],
        compiler_params=params(),
        cost_estimate=cost(4 * micros * local * sequence * sequence * HP),
    )(counts, raw, cosine, sine, gain_q, gain_k)


def self_backward(raw, counts, cosine, sine, gain_q, gain_k, turned_q, turned_k, norms, incoming):
    parts, micros, slots, packed = raw.shape
    lanes = packed // 3
    local = lanes // HP
    sequence = parts * slots
    scale = HD ** (-0.5)
    factor = scale * LOG2E

    def kernel(
        count_ref,
        raw_ref,
        cos_ref,
        sin_ref,
        gq_ref,
        gk_ref,
        q_ref,
        k_ref,
        lse_ref,
        in_ref,
        out_ref,
        dgq_ref,
        dgk_ref,
        dq_s,
        dk_s,
        dv_s,
    ):
        count = count_ref[pl.program_id(0)]
        blocks = (count + slots - 1) // slots
        dq_s[...] = jnp.zeros_like(dq_s)
        dk_s[...] = jnp.zeros_like(dk_s)
        dv_s[...] = jnp.zeros_like(dv_s)
        row = lax.broadcasted_iota(jnp.int32, (sequence, 1), 0)
        bias = jnp.where(row < count, 0.0, MASKED)
        for h in range(local):
            cut = slice(h * HP, (h + 1) * HP)
            keys = k_ref[0, :, cut]
            values = raw_ref[:, 0, :, 2 * lanes + h * HP : 2 * lanes + (h + 1) * HP].reshape(sequence, HP)

            def one_block(part, carry):
                spot = pl.ds(pl.multiple_of(part * slots, slots), slots)
                rows = q_ref[0, spot, cut]
                grads = in_ref[part, 0, :, cut]
                norm = lse_ref[0, h : h + 1, spot]
                probs = jnp.exp2(dot_nt(keys, rows) * factor + bias - norm)
                d_probs = dot_nt(values, grads)
                inner = jnp.sum(probs * d_probs, 0, keepdims=True)
                d_scores = (probs * (d_probs - inner)).astype(BF)
                dv_s[:, cut] += dot_nn(probs.astype(BF), grads)
                dk_s[:, cut] += dot_nn(d_scores, rows)
                dq_s[spot, cut] = dot_tn(d_scores, keys)
                return carry

            lax.fori_loop(0, blocks, one_block, 0)
        masks = head_masks((1, lanes), local)

        def finish(part, carry):
            spot = pl.ds(pl.multiple_of(part * slots, slots), slots)
            cosine, sine = cos_ref[0, spot, :], sin_ref[0, spot, :]
            sums = []
            for index, gain_ref, source in ((0, gq_ref, dq_s), (1, gk_ref, dk_s)):
                grad = source[spot, :] * scale
                grad = grad * cosine - turn_pairs(grad) * sine
                value = raw_ref[part, 0, :, index * lanes : (index + 1) * lanes].astype(F32)
                unit, spread = head_unit(value, masks)
                leading = grad * gain_ref[...]
                back = leading - head_mean(leading, masks) - unit * head_mean(leading * unit, masks)
                out_ref[part, 0, :, index * lanes : (index + 1) * lanes] = (spread * back).astype(BF)
                sums.append(carry[index] + jnp.sum(grad * unit, 0, keepdims=True))
            out_ref[part, 0, :, 2 * lanes : 3 * lanes] = dv_s[spot, :].astype(BF)
            return tuple(sums)

        zero = jnp.zeros((1, lanes), F32)
        d_gains = lax.fori_loop(0, parts, finish, (zero, zero))
        dgq_ref[0] = d_gains[0]
        dgk_ref[0] = d_gains[1]

    whole = lambda m, c: (0, m, 0, 0)
    table = lambda m, c: (m, 0, 0)
    fixed = lambda m, c: (0, 0)
    return pl.pallas_call(
        kernel,
        name="self_backward",
        grid_spec=pltpu.PrefetchScalarGridSpec(
            num_scalar_prefetch=1,
            grid=(micros,),
            in_specs=[
                pl.BlockSpec((parts, 1, slots, packed), whole),
                pl.BlockSpec((1, sequence, lanes), table),
                pl.BlockSpec((1, sequence, lanes), table),
                pl.BlockSpec((1, lanes), fixed),
                pl.BlockSpec((1, lanes), fixed),
                pl.BlockSpec((1, sequence, lanes), table),
                pl.BlockSpec((1, sequence, lanes), table),
                pl.BlockSpec((1, local, sequence), table),
                pl.BlockSpec((parts, 1, slots, lanes), whole),
            ],
            out_specs=[
                pl.BlockSpec((parts, 1, slots, packed), whole),
                pl.BlockSpec((1, 1, lanes), table),
                pl.BlockSpec((1, 1, lanes), table),
            ],
            scratch_shapes=[pltpu.VMEM((sequence, lanes), F32) for index in range(3)],
        ),
        out_shape=[
            jax.ShapeDtypeStruct((parts, micros, slots, packed), BF),
            jax.ShapeDtypeStruct((micros, 1, lanes), F32),
            jax.ShapeDtypeStruct((micros, 1, lanes), F32),
        ],
        compiler_params=params(),
        cost_estimate=cost(10 * micros * local * sequence * sequence * HP),
    )(counts, raw, cosine, sine, gain_q, gain_k, turned_q, turned_k, norms, incoming)


def cost(flops):
    return pl.CostEstimate(flops=flops // 16, bytes_accessed=flops // 16000, transcendentals=0)


def full(shape):
    return pl.BlockSpec(shape, lambda *index: (0,) * len(shape))


def params(megabytes=60):
    return pltpu.CompilerParams(vmem_limit_bytes=megabytes << 20)


class Lanes:
    def __init__(self, near, far, block=None, index=0):
        self.near, self.far = near, far
        self.block = block or near.shape[2]
        self.index = index

    def spec(self):
        index = self.index
        return pl.BlockSpec((1, self.near.shape[1], self.block), lambda p, *rest: (p, 0, index))


def to_lanes(value, weights, dtype=BF, name="to_lanes"):
    rows = value.shape[1]
    parts, half, _ = weights[0].near.shape
    total = sum(weight.block for weight in weights)

    def kernel(x_ref, *refs):
        out_ref = refs[-1]
        at = 0
        for index, weight in enumerate(weights):
            result = dot_nn(x_ref[0], refs[2 * index][0]) + dot_nn(x_ref[1], refs[2 * index + 1][0])
            out_ref[0, :, at : at + weight.block] = result.astype(dtype)
            at += weight.block

    return pl.pallas_call(
        kernel,
        name=name,
        grid=(parts,),
        in_specs=[full(value.shape)] + [weight.spec() for weight in weights for side in range(2)],
        out_specs=pl.BlockSpec((1, rows, total), lambda p: (p, 0, 0)),
        out_shape=jax.ShapeDtypeStruct((parts, rows, total), dtype),
        compiler_params=params(),
        cost_estimate=cost(4 * rows * half * parts * total),
    )(value, *[side for weight in weights for side in (weight.near, weight.far)])


def to_inputs(value, weights, kept):
    rows = value.shape[1]
    parts, half, _ = weights[0].near.shape
    sides = parts // 2

    def kernel(x_ref, *refs):
        out_ref = refs[-1]
        for side in range(sides):

            @pl.when(pl.program_id(0) % sides == side)
            def _():
                at = 0
                for index, weight in enumerate(weights):
                    result = dot_nn(x_ref[0], refs[2 * index][0]) + dot_nn(
                        x_ref[1], refs[2 * index + 1][0]
                    )
                    take = min(weight.block, kept - at)
                    start = side * kept + at
                    out_ref[0, :, start : start + take] = result[:, :take]
                    at += take

    return pl.pallas_call(
        kernel,
        name="to_inputs",
        grid=(parts,),
        in_specs=[full(value.shape)] + [weight.spec() for weight in weights for side in range(2)],
        out_specs=pl.BlockSpec((1, rows, sides * kept), lambda p: (p // sides, 0, 0)),
        out_shape=jax.ShapeDtypeStruct((2, rows, sides * kept), F32),
        compiler_params=params(),
        cost_estimate=cost(4 * rows * half * parts * kept),
    )(value, *[side for weight in weights for side in (weight.near, weight.far)])


def to_features(value, weights, extras, outs, finish, name="to_features"):
    parts, rows, total = value.shape
    half = weights[0].near.shape[1]
    count = 2 * len(weights)

    def kernel(*refs):
        y_ref, weight_refs = refs[0], refs[1 : 1 + count]
        extra_refs = refs[1 + count : 1 + count + len(extras)]
        out_refs = refs[1 + count + len(extras) : -1]
        sums = refs[-1]

        @pl.when(pl.program_id(0) == 0)
        def _():
            sums[...] = jnp.zeros_like(sums)

        at = 0
        for index, weight in enumerate(weights):
            left = y_ref[0, :, at : at + weight.block]
            for side in range(2):
                sums[side] += dot_nt(left, weight_refs[2 * index + side][0])
            at += weight.block

        @pl.when(pl.program_id(0) == parts - 1)
        def _():
            finish([sums[0], sums[1]], extra_refs, out_refs)

    return pl.pallas_call(
        kernel,
        name=name,
        grid=(parts,),
        in_specs=[pl.BlockSpec((1, rows, total), lambda p: (p, 0, 0))]
        + [weight.spec() for weight in weights for side in range(2)]
        + [full(extra.shape) for extra in extras],
        out_specs=[full(out.shape) for out in outs],
        out_shape=outs,
        scratch_shapes=[pltpu.VMEM((2, rows, half), F32)],
        compiler_params=params(),
        cost_estimate=cost(4 * rows * half * parts * total),
    )(value, *[side for weight in weights for side in (weight.near, weight.far)], *extras)


def terms_of(pairs, name="terms_of"):
    half = pairs[0][0].shape[2]
    parts = pairs[0][1].shape[0]
    total = sum(pair[2] for pair in pairs)
    rows = [pair[0].shape[1] for pair in pairs]

    def kernel(*refs):
        count = len(pairs)
        lefts, rights = refs[:count], refs[count : 2 * count]
        near_ref, far_ref = refs[2 * count : 2 * count + 2]
        turned = refs[2 * count + 2 :]

        @pl.when(pl.program_id(0) == 0)
        def _():
            for left, flat in zip(lefts, turned):
                for side in range(2):
                    flat[side] = jnp.transpose(left[side])

        at = 0
        for pair, right, flat in zip(pairs, rights, turned):
            lanes = pair[2]
            near_ref[0, :, at : at + lanes] = dot_nn(flat[0], right[0]).astype(BF)
            far_ref[0, :, at : at + lanes] = dot_nn(flat[1], right[0]).astype(BF)
            at += lanes

    def right_spec(pair):
        return pl.BlockSpec((1, pair[1].shape[1], pair[2]), lambda p: (p, 0, pair[3]))

    out = jax.ShapeDtypeStruct((parts, half, total), BF)
    return pl.pallas_call(
        kernel,
        name=name,
        grid=(parts,),
        in_specs=[full(pair[0].shape) for pair in pairs] + [right_spec(pair) for pair in pairs],
        out_specs=[pl.BlockSpec((1, half, total), lambda p: (p, 0, 0))] * 2,
        out_shape=[out, out],
        scratch_shapes=[pltpu.VMEM((2, half, count), BF) for count in rows],
        compiler_params=params(),
        cost_estimate=cost(sum(4 * half * parts * pair[2] * count for pair, count in zip(pairs, rows))),
    )(*[pair[0] for pair in pairs], *[pair[1] for pair in pairs])


def norm_unit(halves):
    width = 2 * halves[0].shape[-1]
    mean = sum(jnp.sum(half, -1, keepdims=True) for half in halves) / width
    centre = [half - mean for half in halves]
    spread = sum(jnp.sum(half * half, -1, keepdims=True) for half in centre) / width
    scale = lax.rsqrt(spread + EPS)
    return [half * scale for half in centre], scale


def norm_back(halves, gain_ref, incoming):
    width = 2 * halves[0].shape[-1]
    unit, scale = norm_unit(halves)
    leading = [incoming[side] * gain_ref[side] for side in range(2)]
    mean = sum(jnp.sum(half, -1, keepdims=True) for half in leading) / width
    inner = sum(jnp.sum(leading[side] * unit[side], -1, keepdims=True) for side in range(2)) / width
    back = [scale * (leading[side] - mean - unit[side] * inner) for side in range(2)]
    gains = [jnp.sum(incoming[side] * unit[side], 0, keepdims=True) for side in range(2)]
    return back, gains


def join_rows(pieces, name="join_rows"):
    parts, rows, lanes = pieces[0].shape
    count = len(pieces)
    if rows % 16:
        return jnp.concatenate(pieces, 1)

    def kernel(*refs):
        for index in range(count):
            refs[-1][0, index * rows : (index + 1) * rows] = refs[index][0]

    return pl.pallas_call(
        kernel,
        name=name,
        grid=(parts,),
        in_specs=[pl.BlockSpec((1, rows, lanes), lambda p: (p, 0, 0))] * count,
        out_specs=pl.BlockSpec((1, count * rows, lanes), lambda p: (p, 0, 0)),
        out_shape=jax.ShapeDtypeStruct((parts, count * rows, lanes), BF),
        compiler_params=params(),
        cost_estimate=cost(parts * count * rows * lanes),
    )(*pieces)


def sum_rows(jobs, rows, name="sum_rows"):
    parts = jobs[0][0][0].shape[0]
    if rows % 16:
        results = []
        for terms in jobs:
            value = 0.0
            for array, blocks in terms:
                split = array.reshape(parts, -1, rows, array.shape[2])
                value = value + jnp.stack([split[:, block] for block in blocks], 1).astype(F32)
            results.append(value.astype(BF).reshape(parts, -1, value.shape[3]))
        return results
    spots = [
        (array, blocks[index])
        for terms in jobs
        for index in range(len(terms[0][1]))
        for array, blocks in terms
    ]

    def kernel(*refs):
        at = 0
        for spot, terms in enumerate(jobs):
            out_ref = refs[len(spots) + spot]
            for index in range(len(terms[0][1])):
                value = refs[at][0].astype(F32)
                for offset in range(1, len(terms)):
                    value = value + refs[at + offset][0].astype(F32)
                out_ref[0, index * rows : (index + 1) * rows] = value.astype(BF)
                at += len(terms)

    def spec(block, lanes):
        return pl.BlockSpec((1, rows, lanes), lambda p: (p, block, 0))

    shapes = [(len(terms[0][1]) * rows, terms[0][0].shape[2]) for terms in jobs]
    return pl.pallas_call(
        kernel,
        name=name,
        grid=(parts,),
        in_specs=[spec(block, array.shape[2]) for array, block in spots],
        out_specs=[pl.BlockSpec((1, *shape), lambda p: (p, 0, 0)) for shape in shapes],
        out_shape=[jax.ShapeDtypeStruct((parts, *shape), BF) for shape in shapes],
        compiler_params=params(),
        cost_estimate=cost(sum(parts * size * lanes for size, lanes in shapes)),
    )(*[array for array, _ in spots])


def side_by_side(left, right, kept, lanes):
    rows, width = left.shape
    count = width // kept

    def kernel(left_ref, right_ref, out_ref):
        for index, ref in enumerate((left_ref, right_ref)):
            for side in range(count):
                spot = count * index + side
                out_ref[spot, :, :kept] = ref[:, side * kept : (side + 1) * kept]
                if lanes > kept:
                    out_ref[spot, :, kept:] = jnp.zeros((rows, lanes - kept), BF)

    return pl.pallas_call(
        kernel,
        name="side_by_side",
        out_shape=jax.ShapeDtypeStruct((2 * count, rows, lanes), BF),
        compiler_params=params(),
        cost_estimate=cost(4 * rows * lanes),
    )(left, right)


def mlp_forward(rows_in, grads, start, weight1, weight2, part, live=None):
    _, rows, half = rows_in.shape
    parts, _, lanes = weight1.near.shape
    ff = lanes // 2
    step = 384 if ff % 384 == 0 else ff
    steps = ff // step
    extras = [] if live is None else [live]

    def kernel(x_ref, g_ref, s_ref, n1_ref, f1_ref, n2_ref, f2_ref, *refs):
        hid_ref, act_ref, out_ref, dn2_ref, df2_ref, turned, sums = refs[len(extras) :]
        first = (pl.program_id(0) == 0) & (pl.program_id(1) == 0)
        last = (pl.program_id(0) == parts - 1) & (pl.program_id(1) == steps - 1)

        @pl.when(first)
        def _():
            for side in range(2):
                turned[side] = jnp.transpose(g_ref[side])
            sums[...] = s_ref[...]

        hidden = dot_nn(x_ref[0], n1_ref[0]) + dot_nn(x_ref[1], f1_ref[0])
        hid_ref[0] = hidden
        activ = jax.nn.gelu(hidden, approximate=True).astype(BF)
        act_ref[0] = activ
        sums[0] += dot_nt(activ, n2_ref[0])
        sums[1] += dot_nt(activ, f2_ref[0])
        dn2_ref[0] = dot_nn(turned[0], activ).astype(BF)
        df2_ref[0] = dot_nn(turned[1], activ).astype(BF)

        @pl.when(last)
        def _():
            if live is None:
                out_ref[...] = sums[...]
            else:
                out_ref[...] = (sums[...] * refs[0][...]).astype(BF)

    weight = pl.BlockSpec((1, half, step), lambda p, n: (p, 0, part * steps + n))
    grad = pl.BlockSpec((1, half, step), lambda p, n: (p, 0, n))
    unit = pl.BlockSpec((1, rows, step), lambda p, n: (p, 0, n))
    whole = full((2, rows, half))
    grad_shape = jax.ShapeDtypeStruct((parts, half, ff), BF)
    return pl.pallas_call(
        kernel,
        name="mlp_forward",
        grid=(parts, steps),
        in_specs=[whole, whole, whole, weight, weight, weight, weight] + [full(extra.shape) for extra in extras],
        out_specs=[unit, unit, whole, grad, grad],
        out_shape=[
            jax.ShapeDtypeStruct((parts, rows, ff), F32),
            jax.ShapeDtypeStruct((parts, rows, ff), BF),
            jax.ShapeDtypeStruct((2, rows, half), F32 if live is None else BF),
            grad_shape,
            grad_shape,
        ],
        scratch_shapes=[pltpu.VMEM((2, half, rows), BF), pltpu.VMEM((2, rows, half), F32)],
        compiler_params=params(),
        cost_estimate=cost(12 * rows * half * parts * ff),
    )(rows_in, grads, start, weight1.near, weight1.far, weight2.near, weight2.far, *extras)


def gelu_slope(value):
    root = math.sqrt(2.0 / math.pi)
    square = value * value
    curve = jnp.tanh(root * value * (1.0 + 0.044715 * square))
    return 0.5 * (1.0 + curve) + 0.5 * value * (1.0 - curve * curve) * root * (
        1.0 + 3.0 * 0.044715 * square
    )


def mlp_backward(grads, rows_in, hidden, weight1, weight2, part, start, finish=None):
    _, rows, half = rows_in.shape
    parts, _, lanes = weight1.near.shape
    ff = lanes // 2
    step = 384 if ff % 384 == 0 else ff
    steps = ff // step
    extras = list(finish or []) + ([] if start is None else [start])

    def kernel(g_ref, x_ref, hid_ref, n1_ref, f1_ref, n2_ref, f2_ref, *refs):
        extra_refs, refs = refs[: len(extras)], refs[len(extras) :]
        dn1_ref, df1_ref = refs[:2]
        out_refs = refs[2:-2]
        turned, sums = refs[-2:]
        first = (pl.program_id(0) == 0) & (pl.program_id(1) == 0)
        last = (pl.program_id(0) == parts - 1) & (pl.program_id(1) == steps - 1)

        @pl.when(first)
        def _():
            for side in range(2):
                turned[side] = jnp.transpose(x_ref[side])
            sums[...] = jnp.zeros_like(sums) if start is None else extra_refs[-1][...]

        d_activ = dot_nn(g_ref[0], n2_ref[0]) + dot_nn(g_ref[1], f2_ref[0])
        d_hidden = (d_activ * gelu_slope(hid_ref[0])).astype(BF)
        dn1_ref[0] = dot_nn(turned[0], d_hidden).astype(BF)
        df1_ref[0] = dot_nn(turned[1], d_hidden).astype(BF)
        sums[0] += dot_nt(d_hidden, n1_ref[0])
        sums[1] += dot_nt(d_hidden, f1_ref[0])

        @pl.when(last)
        def _():
            if finish is None:
                out_refs[0][...] = sums[...]
            else:
                value_ref, gain_ref, add_ref = extra_refs[:3]
                add_norm_back([sums[0], sums[1]], value_ref, gain_ref, add_ref, *out_refs)

    weight = pl.BlockSpec((1, half, step), lambda p, n: (p, 0, part * steps + n))
    grad = pl.BlockSpec((1, half, step), lambda p, n: (p, 0, n))
    unit = pl.BlockSpec((1, rows, step), lambda p, n: (p, 0, n))
    whole = full((2, rows, half))
    grad_shape = jax.ShapeDtypeStruct((parts, half, ff), BF)
    wide = jax.ShapeDtypeStruct((2, rows, half), F32)
    outs = [wide] if finish is None else [wide, *back_shapes(rows, half)]
    return pl.pallas_call(
        kernel,
        name="mlp_backward",
        grid=(parts, steps),
        in_specs=[whole, whole, unit, weight, weight, weight, weight] + [full(extra.shape) for extra in extras],
        out_specs=[grad, grad] + [full(out.shape) for out in outs],
        out_shape=[grad_shape, grad_shape] + outs,
        scratch_shapes=[pltpu.VMEM((2, half, rows), BF), pltpu.VMEM((2, rows, half), F32)],
        compiler_params=params(),
        cost_estimate=cost(12 * rows * half * parts * ff),
    )(grads, rows_in, hidden, weight1.near, weight1.far, weight2.near, weight2.far, *extras)


def back_shapes(rows, half):
    return [jax.ShapeDtypeStruct((2, rows, half), BF), jax.ShapeDtypeStruct((2, 1, half), F32)]


def add_norm_back(incoming, value_ref, gain_ref, add_ref, out_ref, low_ref, d_gain_ref):
    back, gains = norm_back([value_ref[0], value_ref[1]], gain_ref, incoming)
    for side in range(2):
        total = add_ref[side] + back[side]
        out_ref[side] = total
        low_ref[side] = total.astype(BF)
        d_gain_ref[side] = gains[side]


def text_bias(lengths_ref, micro, words, strip, text_slots, axis):
    spot = lax.broadcasted_iota(jnp.int32, (1, words) if axis else (words, 1), axis)
    inner = spot % strip
    place = spot // strip * text_slots + inner
    live = (place < lengths_ref[micro, 0]) | (
        (place >= CLIP_LEN) & (place < CLIP_LEN + lengths_ref[micro, 1])
    )
    return jnp.where(live & (inner < text_slots), 0.0, MASKED)


def cross_forward(query, text_kv, lengths, text_slots):
    parts, micros, slots, lanes = query.shape
    zones, strip = text_kv.shape[1], text_kv.shape[3]
    words = zones * strip
    local = lanes // HP
    factor = HD ** (-0.5) * LOG2E

    def kernel(len_ref, q_ref, kv_ref, out_ref):
        bias = text_bias(len_ref, pl.program_id(1), words, strip, text_slots, 1)
        for h in range(local):
            cut = slice(h * HP, (h + 1) * HP)
            keys = kv_ref[0, :, 0, :, cut].reshape(words, HP)
            scores = dot_nt(q_ref[0, 0, :, cut], keys) + bias
            top = jnp.max(scores, -1, keepdims=True)
            raised = jnp.exp2((scores - top) * factor)
            total = jnp.sum(raised, -1, keepdims=True)
            values = kv_ref[0, :, 0, :, lanes + h * HP : lanes + (h + 1) * HP].reshape(words, HP)
            out_ref[0, 0, :, cut] = (dot_nn(raised.astype(BF), values) / total).astype(BF)

    spot = lambda p, m, c: (p, m, 0, 0)
    far = lambda p, m, c: (p, 0, m, 0, 0)
    return pl.pallas_call(
        kernel,
        name="cross_forward",
        grid_spec=pltpu.PrefetchScalarGridSpec(
            num_scalar_prefetch=1,
            grid=(parts, micros),
            in_specs=[
                pl.BlockSpec((1, 1, slots, lanes), spot),
                pl.BlockSpec((1, zones, 1, strip, 2 * lanes), far),
            ],
            out_specs=pl.BlockSpec((1, 1, slots, lanes), spot),
        ),
        out_shape=jax.ShapeDtypeStruct(query.shape, BF),
        compiler_params=params(),
        cost_estimate=cost(4 * parts * micros * slots * words * lanes),
    )(lengths, query, text_kv)


def cross_backward(query, text_kv, lengths, incoming, text_slots):
    parts, micros, slots, lanes = query.shape
    zones, strip = text_kv.shape[1], text_kv.shape[3]
    words = zones * strip
    local = lanes // HP
    scale = HD ** (-0.5)
    factor = scale * LOG2E

    def kernel(len_ref, q_ref, kv_ref, in_ref, dq_ref, dkv_ref):
        bias = text_bias(len_ref, pl.program_id(1), words, strip, text_slots, 0)
        for h in range(local):
            cut = slice(h * HP, (h + 1) * HP)
            far = slice(lanes + h * HP, lanes + (h + 1) * HP)
            rows = q_ref[0, 0, :, cut]
            keys = kv_ref[0, :, 0, :, cut].reshape(words, HP)
            values = kv_ref[0, :, 0, :, far].reshape(words, HP)
            grads = in_ref[0, 0, :, cut]
            scores = dot_nt(keys, rows) + bias
            top = jnp.max(scores, 0, keepdims=True)
            raised = jnp.exp2((scores - top) * factor)
            probs = raised * (1.0 / jnp.sum(raised, 0, keepdims=True))
            d_probs = dot_nt(values, grads)
            inner = jnp.sum(probs * d_probs, 0, keepdims=True)
            d_scores = (probs * (d_probs - inner)).astype(BF)
            shape = (zones, strip, HP)
            dkv_ref[0, :, 0, :, far] = dot_nn(probs.astype(BF), grads).astype(BF).reshape(shape)
            dkv_ref[0, :, 0, :, cut] = (dot_nn(d_scores, rows) * scale).astype(BF).reshape(shape)
            dq_ref[0, 0, :, cut] = (dot_tn(d_scores, keys) * scale).astype(BF)

    spot = lambda p, m, c: (p, m, 0, 0)
    far = lambda p, m, c: (p, 0, m, 0, 0)
    return pl.pallas_call(
        kernel,
        name="cross_backward",
        grid_spec=pltpu.PrefetchScalarGridSpec(
            num_scalar_prefetch=1,
            grid=(parts, micros),
            in_specs=[
                pl.BlockSpec((1, 1, slots, lanes), spot),
                pl.BlockSpec((1, zones, 1, strip, 2 * lanes), far),
                pl.BlockSpec((1, 1, slots, lanes), spot),
            ],
            out_specs=[
                pl.BlockSpec((1, 1, slots, lanes), spot),
                pl.BlockSpec((1, zones, 1, strip, 2 * lanes), far),
            ],
        ),
        out_shape=[
            jax.ShapeDtypeStruct(query.shape, BF),
            jax.ShapeDtypeStruct(text_kv.shape, BF),
        ],
        compiler_params=params(),
        cost_estimate=cost(10 * parts * micros * slots * words * lanes),
    )(lengths, query, text_kv, incoming)


def tie(*values):
    return lax.optimization_barrier(values)


class Cube:
    def __init__(self):
        self.size = lax.axis_size("dp")
        self.bits = self.size.bit_length() - 1
        self.outer = list(range(1, self.bits))
        self.rank = lax.axis_index("dp")
        self.masks = []
        for place in range(self.size):
            mask = place >> (self.bits - 1)
            for bit in self.outer:
                mask |= ((place >> (bit - 1)) & 1) << bit
            self.masks.append(mask)
        self.owners = self.rank ^ jnp.array(self.masks, jnp.int32)

    def swap(self, value, bit, axis="dp"):
        pairs = [(i, i ^ (1 << bit)) for i in range(lax.axis_size(axis))]
        return lax.ppermute(value, axis, pairs)

    def trade(self, value):
        blocks = {mask: value[mask] for mask in range(self.size)}
        for bit in range(self.bits):
            send = sorted(mask for mask in blocks if mask >> bit & 1)
            got = self.swap(jnp.stack([blocks[mask] for mask in send]), bit)
            for place, mask in enumerate(send):
                blocks[mask] = got[place]
        return jnp.stack([blocks[mask] for mask in range(self.size)])

    def spread(self, value):
        held = value[None]
        for bit in range(self.bits):
            held = jnp.concatenate([held, self.swap(held, bit)])
        return held

    def add(self, value, axis):
        for bit in range(lax.axis_size(axis).bit_length() - 1):
            value = value + self.swap(value, bit, axis)
        return value


class Gather:
    def __init__(self, cube, shard, flip):
        self.cube = cube
        self.masks = [0]
        self.pieces = [shard]
        self.todo = cube.outer[::-1] if flip else list(cube.outer)

    def move(self):
        bit = self.todo.pop(0)
        self.masks = self.masks + [mask | (1 << bit) for mask in self.masks]
        self.pieces = self.pieces + [self.cube.swap(piece, bit) for piece in self.pieces]

    def join(self):
        while self.todo:
            self.move()
        order = sorted(range(len(self.masks)), key=lambda i: self.cube.masks.index(self.masks[i]))
        self.pieces = [join_rows([self.pieces[i] for i in order])]

    def weight(self):
        near = self.pieces[0]
        return Lanes(near, self.cube.swap(near, 0))


class Scatter:
    def __init__(self, cube, near, far, flip):
        self.cube = cube
        self.todo = list(cube.outer) if flip else cube.outer[::-1]
        self.rows = near.shape[1] // (cube.size // 2)
        self.places = list(range(cube.size // 2))
        self.near = near
        self.got = []
        self.pieces = [cube.swap(far, 0)]
        self.arriving = self.places

    def job(self, places):
        return [(self.near, places)] + [
            (value, [held.index(place) for place in places]) for value, held in self.got
        ]

    def absorb(self):
        self.got.append((self.pieces[0], self.arriving))


def pack(movers):
    jobs = []
    for mover in movers:
        mover.absorb()
        mover.bit = mover.todo.pop(0)
        weight = 1 << (mover.bit - 1)
        sent = [place for place in mover.places if place & weight]
        mover.places = [place for place in mover.places if not place & weight]
        mover.arriving = [place ^ weight for place in sent]
        jobs.append(mover.job(sent))
    for mover, value in zip(movers, sum_rows(jobs, movers[0].rows)):
        mover.pieces = [value]


def send(movers):
    for mover in movers:
        mover.pieces = [mover.cube.swap(mover.pieces[0], mover.bit)]


def results(movers):
    while movers[0].todo:
        pack(movers)
        send(movers)
    for mover in movers:
        mover.absorb()
    return sum_rows([mover.job([0]) for mover in movers], movers[0].rows)


def pin(value, *others):
    flat = []
    for other in others:
        flat += other.pieces if hasattr(other, "pieces") else [other]
    return tie(value, *flat)[0]


def bind(value, *movers):
    flat = [piece for mover in movers for piece in mover.pieces]
    held = tie(value, *flat)
    spot = 1
    for mover in movers:
        count = len(mover.pieces)
        mover.pieces = list(held[spot : spot + count])
        spot += count
    return held[0]


def hold(movers, *others):
    for mover in movers:
        mover.pieces = [pin(piece, *others) for piece in mover.pieces]


def on_device(
    tokens,
    skip_tokens,
    text,
    timestep,
    grid,
    text_len,
    w_skip,
    w_mod,
    w_qkv,
    w_out1,
    w_query2,
    w_text_kv,
    w_out2,
    w_fc1,
    w_fc2,
    gain_skip,
    gain_attn,
    gain_cross,
    gain_mlp,
    gain_query,
    gain_key,
    cotangent,
):
    micros, slots, width = tokens.shape
    parts = lax.axis_size("sp")
    zone = lax.axis_index("sp")
    cube = Cube()
    ranks = cube.size
    rows = micros * slots
    sequence = slots * parts
    local = H // parts
    lanes = local * HP + -local * HP % 128
    text_slots = text.shape[1]
    text_strip = -(-text_slots // 16) * 16
    features = text.shape[2]
    strip = width // ranks
    middle = width // 2
    kept = w_skip.shape[0]
    skip_lanes = -(-kept // 256) * 256
    skip_cut = skip_lanes // 2
    qkv_cut = (3 * lanes) // 256 * 128 + 128
    text_rows = w_text_kv.shape[0]

    def spread(shard, before=None):
        if before is not None:
            shard, before = tie(shard, before)
        return lax.all_gather(shard, "sp", axis=0, tiled=False)

    def fetch(value, cut):
        return [Gather(cube, value[:, :, :cut], 0), Gather(cube, value[:, :, cut:], 1)]

    def advance(movers):
        for mover in movers:
            mover.move()

    def join(movers):
        for mover in movers:
            mover.join()

    def exchange(value):
        return lax.all_to_all(value, "sp", split_axis=0, concat_axis=0, tiled=True)

    skip_z = spread(jnp.pad(w_skip.T, ((0, 0), (0, skip_lanes - kept))))
    steps = cube.spread(timestep[:, 0])
    joined = side_by_side(tokens.reshape(rows, width), skip_tokens.reshape(rows, width), kept, skip_lanes)
    skip_z, steps, joined = tie(skip_z, steps, joined)
    skip_m = fetch(skip_z, skip_cut)
    qkv_z = spread(pad_heads(w_qkv.reshape(strip, -1), local), skip_z)
    advance(skip_m)

    time_act = jax.nn.silu(time_embed(steps, width)).astype(BF).reshape(ranks * micros, parts, -1)
    time_part = lax.dynamic_index_in_dim(time_act, zone, 1, keepdims=False)
    shift = cube.add(jnp.dot(time_part, w_mod, preferred_element_type=F32), "sp")
    skip_m[0].pieces[1], shift = tie(skip_m[0].pieces[1], shift)
    while skip_m[0].todo:
        advance(skip_m)
    shift = cube.trade(shift.reshape(ranks, micros, strip))
    skip_m[0].pieces[-1], shift = tie(skip_m[0].pieces[-1], shift)
    shift = jnp.stack([shift[mask] for mask in cube.masks]).reshape(2, ranks // 2, micros, strip)
    shift = jnp.transpose(shift, (0, 2, 1, 3)).reshape(2, micros, middle)
    qkv_m = fetch(qkv_z, qkv_cut)
    hold(qkv_m, *skip_m)
    advance(qkv_m)
    fc1_z = spread(pin(w_fc1, *skip_m))
    fc2_z = spread(pin(w_fc2.T, *qkv_m))
    join(skip_m)
    skip_w = [mover.weight() for mover in skip_m]

    def shuffle(count):
        block = count // ranks
        place = jnp.arange(count, dtype=jnp.int32)
        source = cube.owners[place // block] * block + place % block
        return (place[:, None] == source[None, :]).astype(BF)

    turn = shuffle(width)
    text_turn = shuffle(features)
    gains = jnp.stack([gain_skip, gain_attn, gain_cross, gain_mlp])
    gains = gains.reshape(4, ranks, strip)[:, cube.owners].reshape(4, 2, 1, middle)
    g_skip, g_attn, g_cross, g_mlp = gains

    wide = grid[:, 0, 1]
    counts = grid[:, 0, 0] * wide
    lengths = text_len[:, 0, :]
    place = zone * slots + jnp.arange(slots, dtype=jnp.int32)
    live = (place[None, :] < counts[:, None]).astype(F32).reshape(rows, 1)
    cosine, sine = rope_tables(sequence, wide, lanes)
    gain_q = pad_heads(jnp.tile(gain_query, local)[None, :], local)
    gain_k = pad_heads(jnp.tile(gain_key, local)[None, :], local)

    grad3 = jnp.stack(
        [
            jnp.dot(cotangent.reshape(rows, width), side, preferred_element_type=F32) * live
            for side in (turn[:, :middle], turn[:, middle:])
        ]
    )
    d_mlp = grad3.astype(BF)

    wide_shape = jax.ShapeDtypeStruct((2, rows, middle), F32)
    low_shape = jax.ShapeDtypeStruct((2, rows, middle), BF)
    gain_shape = jax.ShapeDtypeStruct((2, 1, middle), F32)

    def first_norms(sums, extra, out):
        g0_ref, g1_ref, shift_ref = extra
        base_ref, stream_ref, pre_ref = out
        unit, _ = norm_unit(sums)
        stream = [unit[side] * g0_ref[side] for side in range(2)]
        unit, _ = norm_unit(stream)
        for side in range(2):
            base_ref[side] = sums[side]
            stream_ref[side] = stream[side]
            for micro in range(micros):
                cut = slice(micro * slots, (micro + 1) * slots)
                pre = unit[side][cut] * g1_ref[side] + shift_ref[side, micro : micro + 1]
                pre_ref[side, cut] = pre.astype(BF)

    def next_norm(sums, extra, out):
        before_ref, gain_ref = extra
        after_ref, pre_ref = out
        stream = [before_ref[side] + sums[side] for side in range(2)]
        unit, _ = norm_unit(stream)
        for side in range(2):
            after_ref[side] = stream[side]
            pre_ref[side] = (unit[side] * gain_ref[side]).astype(BF)

    base, stream, pre_attn = to_features(
        joined, skip_w, [g_skip, g_attn, shift], [wide_shape, wide_shape, low_shape], first_norms
    )
    while qkv_m[0].todo:
        advance(qkv_m)
    after_qkv = [mover.pieces[-1] for mover in qkv_m]
    hold(qkv_m, pre_attn)
    join(qkv_m)
    pre_attn, fc1_z = tie(pre_attn, fc1_z)
    qkv_w = [mover.weight() for mover in qkv_m]
    projected = to_lanes(pre_attn, qkv_w)
    projected, fc2_z = tie(projected, fc2_z)
    fc_m = [Gather(cube, fc1_z, 0), Gather(cube, fc2_z, 1)]
    hold(fc_m, *after_qkv)
    advance(fc_m)
    raw = exchange(projected.reshape(parts, micros, slots, 3 * lanes))
    cross_z = jnp.concatenate([pad_heads(side, local) for side in (w_out1.T, w_query2, w_out2.T)], 1)
    cross_z = spread(pin(cross_z, *fc_m))
    text_own = jnp.dot(text.reshape(-1, features), text_turn, preferred_element_type=F32).astype(BF)
    text_own = jnp.pad(
        text_own.reshape(micros, text_slots, features), ((0, 0), (0, text_strip - text_slots), (0, 0))
    ).reshape(micros * text_strip, features)
    text_z = jnp.pad(pad_heads(w_text_kv.reshape(text_rows, -1), local), ((0, max(0, strip - text_rows)), (0, 0)))
    while fc_m[0].todo:
        advance(fc_m)
    text_z = spread(text_z, cross_z)
    cross_m = fetch(cross_z, 2 * lanes)
    advance(cross_m)
    raw, d_mlp = tie(raw, d_mlp)
    attended, turned_q, turned_k, norms = self_forward(raw, counts, cosine, sine, gain_q, gain_k)
    attended = bind(attended, *fc_m, *cross_m)
    attended, text_z = tie(attended, text_z)
    text_m = Gather(cube, text_z[:, :text_rows], 1)
    text_m.move()
    attended = exchange(attended).reshape(parts, rows, lanes)
    while cross_m[0].todo:
        advance(cross_m)
    text_all = spread(text_own, text_z)
    hold(cross_m, attended)
    join(cross_m)
    first_w, out2_w = [mover.weight() for mover in cross_m]
    out1_w, query2_w = (Lanes(first_w.near, first_w.far, lanes, index) for index in range(2))
    attended, text_all = tie(attended, text_all)
    stream1, pre_cross = to_features(
        attended, [out1_w], [stream, g_cross], [wide_shape, low_shape], next_norm
    )
    pre_cross = bind(pre_cross, text_m, *fc_m)
    while text_m.todo:
        text_m.move()
    query2 = to_lanes(pre_cross, [query2_w]).reshape(parts, micros, slots, lanes)
    query2 = bind(query2, text_m)
    text_all = text_all.reshape(-1, features)
    text_all = jnp.stack([text_all[:, : features // 2], text_all[:, features // 2 :]])
    text_m.join()
    text_w = text_m.weight()
    join(fc_m)
    fc1_w, fc2_w = [mover.weight() for mover in fc_m]
    text_kv = to_lanes(text_all, [text_w]).reshape(parts, parts, micros, text_strip, 2 * lanes)
    crossed = cross_forward(query2, text_kv, lengths, text_slots).reshape(parts, rows, lanes)
    stream2, pre_mlp = to_features(
        crossed, [out2_w], [stream1, g_mlp], [wide_shape, low_shape], next_norm
    )
    hidden0, activ0, partial, fc2_n0, fc2_f0 = mlp_forward(pre_mlp, d_mlp, stream2, fc1_w, fc2_w, 0)
    hidden1, activ1, result, fc2_n1, fc2_f1 = mlp_forward(pre_mlp, d_mlp, partial, fc1_w, fc2_w, 1, live)
    fc2_s = [Scatter(cube, fc2_n0, fc2_f0, 0), Scatter(cube, fc2_n1, fc2_f1, 1)]

    def settle(values, before=None):
        value = values[0] if len(values) == 1 else jnp.concatenate(values, 2)
        if before is not None:
            value, before = tie(value, before)
        return lax.psum_scatter(value, "sp", scatter_dimension=0, tiled=False)

    fc1_n0, fc1_f0, partial = mlp_backward(d_mlp, pre_mlp, hidden0, fc1_w, fc2_w, 0, None)
    fc1_s = [Scatter(cube, fc1_n0, fc1_f0, 0)]
    pack(fc2_s)
    partial = bind(partial, *fc2_s)
    send(fc2_s)
    fc1_n1, fc1_f1, grad2, d_cross, d_gain_mlp = mlp_backward(
        d_mlp, pre_mlp, hidden1, fc1_w, fc2_w, 1, partial, [stream2, g_mlp, grad3]
    )
    fc1_s.append(Scatter(cube, fc1_n1, fc1_f1, 1))
    d_cross = bind(d_cross, *fc2_s)
    d_crossed = to_lanes(d_cross, [out2_w])
    pack(fc2_s)
    d_crossed = bind(d_crossed, *fc2_s)
    send(fc2_s)
    d_query2, d_text_kv = cross_backward(
        query2, text_kv, lengths, d_crossed.reshape(parts, micros, slots, lanes), text_slots
    )
    d_query2 = bind(d_query2, *fc2_s)
    d_query2 = d_query2.reshape(parts, rows, lanes)
    d_text_kv = d_text_kv.reshape(parts, -1, 2 * lanes)
    total_fc2 = results(fc2_s)
    term_fc2 = settle(total_fc2)

    def go_back(sums, extra, out):
        add_norm_back(sums, *extra, *out)

    grad1, d_attn, d_gain_cross = to_features(
        d_query2, [query2_w], [stream1, g_cross, grad2], [wide_shape, low_shape, gain_shape], go_back
    )
    d_attn = bind(d_attn, *fc1_s)
    pack(fc1_s)
    d_attn = bind(d_attn, *fc1_s)
    send(fc1_s)
    d_attended = to_lanes(d_attn, [out1_w])
    d_attended, d_text_kv, pre_cross = tie(d_attended, d_text_kv, pre_cross)
    d_heads = exchange(d_attended.reshape(parts, micros, slots, lanes))

    def words_back(sums, extra, out):
        size = micros * text_strip
        for zone in range(parts):
            for side in range(2):
                out[0][zone, side] = sums[side][zone * size : (zone + 1) * size].astype(BF)

    words_shape = jax.ShapeDtypeStruct((parts, 2, micros * text_strip, features // 2), BF)
    d_words = to_features(d_text_kv, [text_w], [], [words_shape], words_back)[0]
    text_t = list(terms_of([(text_all, d_text_kv, 2 * lanes, 0)]))
    cross_t = terms_of(
        [(d_attn, attended, lanes, 0), (pre_cross, d_query2, lanes, 0), (d_cross, crossed, lanes, 0)]
    )
    cross_t = list(cross_t)
    d_heads, d_words, text_t[1], cross_t[1] = tie(d_heads, d_words, text_t[1], cross_t[1])
    d_words = settle([d_words])
    text_s, cross_s = Scatter(cube, *text_t, 1), Scatter(cube, *cross_t, 0)
    d_heads = bind(d_heads, *fc1_s)
    pack(fc1_s)
    d_heads = bind(d_heads, *fc1_s)
    send(fc1_s)
    d_raw, d_gain_q, d_gain_k = self_backward(
        raw, counts, cosine, sine, gain_q, gain_k, turned_q, turned_k, norms, d_heads
    )
    d_raw, term_fc2, d_words = tie(d_raw, term_fc2, d_words)
    d_raw = bind(d_raw, *fc1_s)
    d_projected = exchange(d_raw).reshape(parts, rows, 3 * lanes)
    other_s = [cross_s, text_s]
    total_fc1 = results(fc1_s)
    pack([cross_s])
    pack([text_s])
    send(other_s)
    d_projected = bind(d_projected, *other_s)
    term_fc1 = settle(total_fc1, d_projected)
    qkv_s = [
        Scatter(cube, *terms_of([(pre_attn, d_projected, 2 * lanes, 0)]), 0),
        Scatter(cube, *terms_of([(pre_attn, d_projected, lanes, 2)]), 1),
    ]
    pack([cross_s])
    pack([text_s])
    send(other_s)
    pack(qkv_s)
    d_projected = bind(d_projected, *qkv_s)
    send(qkv_s)

    def last_norms(sums, extra, out):
        stream_ref, g1_ref, base_ref, g0_ref, add_ref = extra
        low_ref, d_shift_ref, d_g1_ref, d_g0_ref = out
        back, gains1 = norm_back([stream_ref[0], stream_ref[1]], g1_ref, sums)
        total = [add_ref[side] + back[side] for side in range(2)]
        back, gains0 = norm_back([base_ref[0], base_ref[1]], g0_ref, total)
        for side in range(2):
            low_ref[side] = back[side].astype(BF)
            d_g1_ref[side] = gains1[side]
            d_g0_ref[side] = gains0[side]
            for micro in range(micros):
                part = sums[side][micro * slots : (micro + 1) * slots]
                d_shift_ref[side, micro : micro + 1] = jnp.sum(part, 0, keepdims=True)

    shift_shape = jax.ShapeDtypeStruct((2, micros, middle), F32)
    d_base, d_shift, d_gain_attn, d_gain_skip = to_features(
        d_projected,
        qkv_w,
        [stream, g_attn, base, g_skip, grad1],
        [low_shape, shift_shape, gain_shape, gain_shape],
        last_norms,
    )
    d_base = bind(d_base, *other_s)
    skip_s = [
        Scatter(cube, *terms_of([(d_base, joined, skip_cut, flip)]), flip) for flip in range(2)
    ]
    pack(skip_s)
    hold(skip_s, *qkv_s)
    pack(qkv_s)
    send(qkv_s)
    term_cross, term_text = settle(results([cross_s])), settle(results([text_s]))
    send(skip_s)
    term_qkv = settle(results(qkv_s))
    term_skip = settle(results(skip_s))
    d_joined = to_inputs(d_base, skip_w, kept)
    result = (
        jnp.dot(result[0], turn[:, :middle].T, preferred_element_type=F32)
        + jnp.dot(result[1], turn[:, middle:].T, preferred_element_type=F32)
    ).astype(BF)
    d_words = d_words.reshape(2, micros * text_strip, features // 2)
    d_words = jnp.dot(
        d_words[0], text_turn[:, : features // 2].T, preferred_element_type=F32
    ) + jnp.dot(d_words[1], text_turn[:, features // 2 :].T, preferred_element_type=F32)
    d_words = d_words.reshape(micros, text_strip, features)[:, :text_slots]

    d_shift = jnp.transpose(d_shift.reshape(2, micros, ranks // 2, strip), (0, 2, 1, 3))
    d_shift = d_shift.reshape(ranks, micros, strip)
    d_shift = jnp.stack([d_shift[cube.masks.index(mask)] for mask in range(ranks)])
    d_shift = cube.add(cube.trade(d_shift), "sp").reshape(ranks * micros, strip)
    term_mod = lax.dot_general(
        time_part.astype(F32), d_shift, (((0,), (0,)), ((), ())), precision=lax.Precision.HIGHEST
    )

    places = jnp.array([cube.masks.index(mask) for mask in range(ranks)], jnp.int32)
    places = places[jnp.arange(ranks, dtype=jnp.int32) ^ cube.rank]
    gains = jnp.stack([d_gain_skip, d_gain_attn, d_gain_cross, d_gain_mlp])
    gains = gains.reshape(4, ranks, strip)[:, places].reshape(-1)
    heads = jnp.stack([jnp.sum(d_gain_q, (0, 1)), jnp.sum(d_gain_k, (0, 1))])
    heads = jnp.sum(heads[:, : local * HP].reshape(2, local, HP)[:, :, :HD], 1)
    packed = jnp.concatenate([gains, heads.reshape(-1)])
    packed = cube.add(cube.add(packed, "sp"), "dp")
    gains = packed[: 4 * width].reshape(4, ranks * parts, -1)
    gains = lax.dynamic_index_in_dim(gains, cube.rank * parts + zone, 1, keepdims=False)
    heads = packed[4 * width :].reshape(2, HD)

    def whole(term, groups):
        return cut_heads(term.astype(F32), local).reshape(term.shape[0], groups, -1)

    return (
        result.reshape(tokens.shape),
        d_joined[0].reshape(tokens.shape),
        d_joined[1].reshape(tokens.shape),
        d_words.reshape(text.shape),
        term_skip.astype(F32)[:, :kept].T,
        term_mod,
        whole(term_qkv, 3),
        cut_heads(term_cross[:, :lanes].astype(F32), local).T,
        cut_heads(term_cross[:, lanes : 2 * lanes].astype(F32), local),
        whole(term_text, 2),
        cut_heads(term_cross[:, 2 * lanes :].astype(F32), local).T,
        term_fc1.astype(F32),
        term_fc2.astype(F32).T,
        gains[0],
        gains[1],
        gains[2],
        gains[3],
        heads[0],
        heads[1],
    )


def solution(mesh):
    rows = P(None, ("dp", "sp"), None)
    column = P("sp", "dp")
    row = P("dp", "sp")
    grouped = P("dp", None, "sp")
    in_specs = (
        (rows, rows, rows, P(None, "dp"), P(None, "dp", None), P(None, "dp", None))
        + (column, column, grouped, column, row, grouped, column, row, column)
        + (P(),) * 6
        + (rows,)
    )
    out_specs = (
        (rows, rows, rows, rows)
        + (column, column, grouped, column, row, grouped, column, row, column)
        + (P(("dp", "sp")),) * 4
        + (P(), P())
    )
    return jax.shard_map(
        on_device, mesh=mesh, in_specs=in_specs, out_specs=out_specs, check_vma=False
    )
```

```python
import math

import jax
import jax.numpy as jnp
from jax import lax
from jax.experimental import pallas as pl
from jax.experimental.pallas import tpu as pltpu
from jax.sharding import PartitionSpec as P

H = 16
HD = 88
HP = 96
CLIP_LEN = 77
ROWS = 256

EPS = 1e-06
MASKED = -1e30
LOG2E = 1.4426950408889634
BF = jnp.bfloat16
F32 = jnp.float32


def time_embed(step, width):
    half = width // 2
    rate = jnp.exp(-math.log(10000.0) * jnp.arange(half, dtype=F32) / half)
    angle = step.astype(F32)[..., None] * rate
    return jnp.concatenate([jnp.cos(angle), jnp.sin(angle)], -1)


def rope_tables(sequence, wide, lanes):
    place = jnp.arange(sequence, dtype=jnp.int32)[None, :, None]
    wide = wide[:, None, None]
    lane = jnp.arange(lanes, dtype=jnp.int32)[None, None, :] % HP
    pair = lane // 2
    quarter = HD // 4
    upper = pair < quarter
    rank = jnp.where(upper, pair, pair - quarter).astype(F32)
    rate = jnp.exp(-math.log(10000.0) * rank / quarter)
    angle = jnp.where(upper, place // wide, place % wide).astype(F32) * rate
    sine = jnp.sin(angle)
    return jnp.cos(angle), jnp.where(lane % 2 == 0, -sine, sine)


def pad_heads(packed, local):
    rows, lanes = packed.shape
    groups = packed.reshape(rows, lanes // (local * HD), local, HD)
    groups = jnp.pad(groups, ((0, 0), (0, 0), (0, 0), (0, HP - HD)))
    groups = groups.reshape(rows, -1, local * HP)
    return jnp.pad(groups, ((0, 0), (0, 0), (0, -local * HP % 128))).reshape(rows, -1)


def cut_heads(padded, local):
    rows = padded.shape[0]
    groups = padded.reshape(rows, -1, local * HP + -local * HP % 128)[:, :, : local * HP]
    return groups.reshape(rows, -1, local, HP)[..., :HD].reshape(rows, -1)


def head_masks(shape, local):
    lane = lax.broadcasted_iota(jnp.int32, shape, len(shape) - 1)
    inside = lane % HP < HD
    return [((lane // HP == h) & inside).astype(F32) for h in range(local)]


def head_mean(value, masks):
    total = None
    for mask in masks:
        term = (jnp.sum(value * mask, -1, keepdims=True) * (1.0 / HD)) * mask
        total = term if total is None else total + term
    return total


def head_unit(value, masks):
    centre = value - head_mean(value, masks)
    spread = None
    square = centre * centre
    for mask in masks:
        mean = jnp.sum(square * mask, -1, keepdims=True) * (1.0 / HD)
        term = lax.rsqrt(mean + EPS) * mask
        spread = term if spread is None else spread + term
    return centre * spread, spread


def turn_pairs(value):
    lanes = value.shape[-1]
    after = pltpu.roll(value, lanes - 1, 1)
    before = pltpu.roll(value, 1, 1)
    lane = lax.broadcasted_iota(jnp.int32, value.shape, 1)
    return jnp.where(lane % 2 == 0, after, before)


def dot_nt(left, right):
    return lax.dot_general(left, right, (((1,), (1,)), ((), ())), preferred_element_type=F32)


def dot_nn(left, right):
    return lax.dot_general(left, right, (((1,), (0,)), ((), ())), preferred_element_type=F32)


def dot_tn(left, right):
    return lax.dot_general(left, right, (((0,), (0,)), ((), ())), preferred_element_type=F32)


def self_forward(raw, counts, cosine, sine, gain_q, gain_k):
    parts, micros, slots, packed = raw.shape
    lanes = packed // 3
    local = lanes // HP
    sequence = parts * slots
    factor = HD ** (-0.5) * LOG2E

    def kernel(count_ref, raw_ref, cos_ref, sin_ref, gq_ref, gk_ref, out_ref, q_ref, k_ref, lse_ref):
        count = count_ref[pl.program_id(0)]
        blocks = (count + slots - 1) // slots
        out_ref[...] = jnp.zeros_like(out_ref)
        masks = head_masks((1, lanes), local)

        def prepare(part, carry):
            spot = pl.ds(pl.multiple_of(part * slots, slots), slots)
            cosine, sine = cos_ref[0, spot, :], sin_ref[0, spot, :]
            for index, gain_ref, dest in ((0, gq_ref, q_ref), (1, gk_ref, k_ref)):
                value = raw_ref[part, 0, :, index * lanes : (index + 1) * lanes].astype(F32)
                scaled = head_unit(value, masks)[0] * gain_ref[...]
                dest[0, spot, :] = (scaled * cosine + turn_pairs(scaled) * sine).astype(BF)
            return carry

        lax.fori_loop(0, parts, prepare, 0)
        column = lax.broadcasted_iota(jnp.int32, (1, sequence), 1)
        bias = jnp.where(column < count, 0.0, MASKED)
        for h in range(local):
            cut = slice(h * HP, (h + 1) * HP)
            keys = k_ref[0, :, cut]
            values = raw_ref[:, 0, :, 2 * lanes + h * HP : 2 * lanes + (h + 1) * HP].reshape(sequence, HP)

            def one_block(part, carry):
                spot = pl.ds(pl.multiple_of(part * slots, slots), slots)
                scores = dot_nt(q_ref[0, spot, cut], keys) + bias
                top = jnp.max(scores, -1, keepdims=True)
                raised = jnp.exp2((scores - top) * factor)
                total = jnp.sum(raised, -1, keepdims=True)
                result = dot_nn(raised.astype(BF), values) / total
                out_ref[part, 0, :, cut] = result.astype(BF)
                norm = jnp.broadcast_to(top * factor + jnp.log2(total), (slots, 128))
                lse_ref[0, h : h + 1, spot] = jnp.transpose(norm)[0:1, :]
                return carry

            lax.fori_loop(0, blocks, one_block, 0)

    whole = lambda m, c: (0, m, 0, 0)
    table = lambda m, c: (m, 0, 0)
    fixed = lambda m, c: (0, 0)
    return pl.pallas_call(
        kernel,
        name="self_forward",
        grid_spec=pltpu.PrefetchScalarGridSpec(
            num_scalar_prefetch=1,
            grid=(micros,),
            in_specs=[
                pl.BlockSpec((parts, 1, slots, packed), whole),
                pl.BlockSpec((1, sequence, lanes), table),
                pl.BlockSpec((1, sequence, lanes), table),
                pl.BlockSpec((1, lanes), fixed),
                pl.BlockSpec((1, lanes), fixed),
            ],
            out_specs=[
                pl.BlockSpec((parts, 1, slots, lanes), whole),
                pl.BlockSpec((1, sequence, lanes), table),
                pl.BlockSpec((1, sequence, lanes), table),
                pl.BlockSpec((1, local, sequence), table),
            ],
        ),
        out_shape=[
            jax.ShapeDtypeStruct((parts, micros, slots, lanes), BF),
            jax.ShapeDtypeStruct((micros, sequence, lanes), BF),
            jax.ShapeDtypeStruct((micros, sequence, lanes), BF),
            jax.ShapeDtypeStruct((micros, local, sequence), F32),
        ],
        compiler_params=params(),
        cost_estimate=cost(4 * micros * local * sequence * sequence * HP),
    )(counts, raw, cosine, sine, gain_q, gain_k)


def self_backward(raw, counts, cosine, sine, gain_q, gain_k, turned_q, turned_k, norms, incoming):
    parts, micros, slots, packed = raw.shape
    lanes = packed // 3
    local = lanes // HP
    sequence = parts * slots
    scale = HD ** (-0.5)
    factor = scale * LOG2E

    def kernel(
        count_ref,
        raw_ref,
        cos_ref,
        sin_ref,
        gq_ref,
        gk_ref,
        q_ref,
        k_ref,
        lse_ref,
        in_ref,
        out_ref,
        dgq_ref,
        dgk_ref,
        dq_s,
        dk_s,
        dv_s,
    ):
        count = count_ref[pl.program_id(0)]
        blocks = (count + slots - 1) // slots
        dq_s[...] = jnp.zeros_like(dq_s)
        dk_s[...] = jnp.zeros_like(dk_s)
        dv_s[...] = jnp.zeros_like(dv_s)
        row = lax.broadcasted_iota(jnp.int32, (sequence, 1), 0)
        bias = jnp.where(row < count, 0.0, MASKED)
        for h in range(local):
            cut = slice(h * HP, (h + 1) * HP)
            keys = k_ref[0, :, cut]
            values = raw_ref[:, 0, :, 2 * lanes + h * HP : 2 * lanes + (h + 1) * HP].reshape(sequence, HP)

            def one_block(part, carry):
                spot = pl.ds(pl.multiple_of(part * slots, slots), slots)
                rows = q_ref[0, spot, cut]
                grads = in_ref[part, 0, :, cut]
                norm = lse_ref[0, h : h + 1, spot]
                probs = jnp.exp2(dot_nt(keys, rows) * factor + bias - norm)
                d_probs = dot_nt(values, grads)
                inner = jnp.sum(probs * d_probs, 0, keepdims=True)
                d_scores = (probs * (d_probs - inner)).astype(BF)
                dv_s[:, cut] += dot_nn(probs.astype(BF), grads)
                dk_s[:, cut] += dot_nn(d_scores, rows)
                dq_s[spot, cut] = dot_tn(d_scores, keys)
                return carry

            lax.fori_loop(0, blocks, one_block, 0)
        masks = head_masks((1, lanes), local)

        def finish(part, carry):
            spot = pl.ds(pl.multiple_of(part * slots, slots), slots)
            cosine, sine = cos_ref[0, spot, :], sin_ref[0, spot, :]
            sums = []
            for index, gain_ref, source in ((0, gq_ref, dq_s), (1, gk_ref, dk_s)):
                grad = source[spot, :] * scale
                grad = grad * cosine - turn_pairs(grad) * sine
                value = raw_ref[part, 0, :, index * lanes : (index + 1) * lanes].astype(F32)
                unit, spread = head_unit(value, masks)
                leading = grad * gain_ref[...]
                back = leading - head_mean(leading, masks) - unit * head_mean(leading * unit, masks)
                out_ref[part, 0, :, index * lanes : (index + 1) * lanes] = (spread * back).astype(BF)
                sums.append(carry[index] + jnp.sum(grad * unit, 0, keepdims=True))
            out_ref[part, 0, :, 2 * lanes : 3 * lanes] = dv_s[spot, :].astype(BF)
            return tuple(sums)

        zero = jnp.zeros((1, lanes), F32)
        d_gains = lax.fori_loop(0, parts, finish, (zero, zero))
        dgq_ref[0] = d_gains[0]
        dgk_ref[0] = d_gains[1]

    whole = lambda m, c: (0, m, 0, 0)
    table = lambda m, c: (m, 0, 0)
    fixed = lambda m, c: (0, 0)
    return pl.pallas_call(
        kernel,
        name="self_backward",
        grid_spec=pltpu.PrefetchScalarGridSpec(
            num_scalar_prefetch=1,
            grid=(micros,),
            in_specs=[
                pl.BlockSpec((parts, 1, slots, packed), whole),
                pl.BlockSpec((1, sequence, lanes), table),
                pl.BlockSpec((1, sequence, lanes), table),
                pl.BlockSpec((1, lanes), fixed),
                pl.BlockSpec((1, lanes), fixed),
                pl.BlockSpec((1, sequence, lanes), table),
                pl.BlockSpec((1, sequence, lanes), table),
                pl.BlockSpec((1, local, sequence), table),
                pl.BlockSpec((parts, 1, slots, lanes), whole),
            ],
            out_specs=[
                pl.BlockSpec((parts, 1, slots, packed), whole),
                pl.BlockSpec((1, 1, lanes), table),
                pl.BlockSpec((1, 1, lanes), table),
            ],
            scratch_shapes=[pltpu.VMEM((sequence, lanes), F32) for index in range(3)],
        ),
        out_shape=[
            jax.ShapeDtypeStruct((parts, micros, slots, packed), BF),
            jax.ShapeDtypeStruct((micros, 1, lanes), F32),
            jax.ShapeDtypeStruct((micros, 1, lanes), F32),
        ],
        compiler_params=params(),
        cost_estimate=cost(10 * micros * local * sequence * sequence * HP),
    )(counts, raw, cosine, sine, gain_q, gain_k, turned_q, turned_k, norms, incoming)


def cost(flops):
    return pl.CostEstimate(flops=flops // 16, bytes_accessed=flops // 16000, transcendentals=0)


def full(shape):
    return pl.BlockSpec(shape, lambda *index: (0,) * len(shape))


def params(megabytes=60):
    return pltpu.CompilerParams(vmem_limit_bytes=megabytes << 20)


class Lanes:
    def __init__(self, near, far, block=None, index=0):
        self.near, self.far = near, far
        self.block = block or near.shape[2]
        self.index = index

    def spec(self):
        index = self.index
        return pl.BlockSpec((1, self.near.shape[1], self.block), lambda p, *rest: (p, 0, index))


def to_lanes(value, weights, dtype=BF, name="to_lanes"):
    rows = value.shape[1]
    parts, half, _ = weights[0].near.shape
    total = sum(weight.block for weight in weights)

    def kernel(x_ref, *refs):
        out_ref = refs[-1]
        at = 0
        for index, weight in enumerate(weights):
            result = dot_nn(x_ref[0], refs[2 * index][0]) + dot_nn(x_ref[1], refs[2 * index + 1][0])
            out_ref[0, :, at : at + weight.block] = result.astype(dtype)
            at += weight.block

    return pl.pallas_call(
        kernel,
        name=name,
        grid=(parts,),
        in_specs=[full(value.shape)] + [weight.spec() for weight in weights for side in range(2)],
        out_specs=pl.BlockSpec((1, rows, total), lambda p: (p, 0, 0)),
        out_shape=jax.ShapeDtypeStruct((parts, rows, total), dtype),
        compiler_params=params(),
        cost_estimate=cost(4 * rows * half * parts * total),
    )(value, *[side for weight in weights for side in (weight.near, weight.far)])


def to_inputs(value, weights, kept):
    rows = value.shape[1]
    parts, half, _ = weights[0].near.shape
    sides = parts // 2

    def kernel(x_ref, *refs):
        out_ref = refs[-1]
        for side in range(sides):

            @pl.when(pl.program_id(0) % sides == side)
            def _():
                at = 0
                for index, weight in enumerate(weights):
                    result = dot_nn(x_ref[0], refs[2 * index][0]) + dot_nn(
                        x_ref[1], refs[2 * index + 1][0]
                    )
                    take = min(weight.block, kept - at)
                    start = side * kept + at
                    out_ref[0, :, start : start + take] = result[:, :take]
                    at += take

    return pl.pallas_call(
        kernel,
        name="to_inputs",
        grid=(parts,),
        in_specs=[full(value.shape)] + [weight.spec() for weight in weights for side in range(2)],
        out_specs=pl.BlockSpec((1, rows, sides * kept), lambda p: (p // sides, 0, 0)),
        out_shape=jax.ShapeDtypeStruct((2, rows, sides * kept), F32),
        compiler_params=params(),
        cost_estimate=cost(4 * rows * half * parts * kept),
    )(value, *[side for weight in weights for side in (weight.near, weight.far)])


def to_features(value, weights, extras, outs, finish, name="to_features"):
    parts, rows, total = value.shape
    half = weights[0].near.shape[1]
    count = 2 * len(weights)

    def kernel(*refs):
        y_ref, weight_refs = refs[0], refs[1 : 1 + count]
        extra_refs = refs[1 + count : 1 + count + len(extras)]
        out_refs = refs[1 + count + len(extras) : -1]
        sums = refs[-1]

        @pl.when(pl.program_id(0) == 0)
        def _():
            sums[...] = jnp.zeros_like(sums)

        at = 0
        for index, weight in enumerate(weights):
            left = y_ref[0, :, at : at + weight.block]
            for side in range(2):
                sums[side] += dot_nt(left, weight_refs[2 * index + side][0])
            at += weight.block

        @pl.when(pl.program_id(0) == parts - 1)
        def _():
            finish([sums[0], sums[1]], extra_refs, out_refs)

    return pl.pallas_call(
        kernel,
        name=name,
        grid=(parts,),
        in_specs=[pl.BlockSpec((1, rows, total), lambda p: (p, 0, 0))]
        + [weight.spec() for weight in weights for side in range(2)]
        + [full(extra.shape) for extra in extras],
        out_specs=[full(out.shape) for out in outs],
        out_shape=outs,
        scratch_shapes=[pltpu.VMEM((2, rows, half), F32)],
        compiler_params=params(),
        cost_estimate=cost(4 * rows * half * parts * total),
    )(value, *[side for weight in weights for side in (weight.near, weight.far)], *extras)


def terms_of(pairs, name="terms_of"):
    half = pairs[0][0].shape[2]
    parts = pairs[0][1].shape[0]
    total = sum(pair[2] for pair in pairs)
    rows = [pair[0].shape[1] for pair in pairs]

    def kernel(*refs):
        count = len(pairs)
        lefts, rights = refs[:count], refs[count : 2 * count]
        near_ref, far_ref = refs[2 * count : 2 * count + 2]
        turned = refs[2 * count + 2 :]

        @pl.when(pl.program_id(0) == 0)
        def _():
            for left, flat in zip(lefts, turned):
                for side in range(2):
                    flat[side] = jnp.transpose(left[side])

        at = 0
        for pair, right, flat in zip(pairs, rights, turned):
            lanes = pair[2]
            near_ref[0, :, at : at + lanes] = dot_nn(flat[0], right[0]).astype(BF)
            far_ref[0, :, at : at + lanes] = dot_nn(flat[1], right[0]).astype(BF)
            at += lanes

    def right_spec(pair):
        return pl.BlockSpec((1, pair[1].shape[1], pair[2]), lambda p: (p, 0, pair[3]))

    out = jax.ShapeDtypeStruct((parts, half, total), BF)
    return pl.pallas_call(
        kernel,
        name=name,
        grid=(parts,),
        in_specs=[full(pair[0].shape) for pair in pairs] + [right_spec(pair) for pair in pairs],
        out_specs=[pl.BlockSpec((1, half, total), lambda p: (p, 0, 0))] * 2,
        out_shape=[out, out],
        scratch_shapes=[pltpu.VMEM((2, half, count), BF) for count in rows],
        compiler_params=params(),
        cost_estimate=cost(sum(4 * half * parts * pair[2] * count for pair, count in zip(pairs, rows))),
    )(*[pair[0] for pair in pairs], *[pair[1] for pair in pairs])


def norm_unit(halves):
    width = 2 * halves[0].shape[-1]
    mean = sum(jnp.sum(half, -1, keepdims=True) for half in halves) / width
    centre = [half - mean for half in halves]
    spread = sum(jnp.sum(half * half, -1, keepdims=True) for half in centre) / width
    scale = lax.rsqrt(spread + EPS)
    return [half * scale for half in centre], scale


def norm_back(halves, gain_ref, incoming):
    width = 2 * halves[0].shape[-1]
    unit, scale = norm_unit(halves)
    leading = [incoming[side] * gain_ref[side] for side in range(2)]
    mean = sum(jnp.sum(half, -1, keepdims=True) for half in leading) / width
    inner = sum(jnp.sum(leading[side] * unit[side], -1, keepdims=True) for side in range(2)) / width
    back = [scale * (leading[side] - mean - unit[side] * inner) for side in range(2)]
    gains = [jnp.sum(incoming[side] * unit[side], 0, keepdims=True) for side in range(2)]
    return back, gains


def join_rows(pieces, name="join_rows"):
    parts, rows, lanes = pieces[0].shape
    count = len(pieces)
    if rows % 16:
        return jnp.concatenate(pieces, 1)

    def kernel(*refs):
        for index in range(count):
            refs[-1][0, index * rows : (index + 1) * rows] = refs[index][0]

    return pl.pallas_call(
        kernel,
        name=name,
        grid=(parts,),
        in_specs=[pl.BlockSpec((1, rows, lanes), lambda p: (p, 0, 0))] * count,
        out_specs=pl.BlockSpec((1, count * rows, lanes), lambda p: (p, 0, 0)),
        out_shape=jax.ShapeDtypeStruct((parts, count * rows, lanes), BF),
        compiler_params=params(),
        cost_estimate=cost(parts * count * rows * lanes),
    )(*pieces)


def sum_rows(jobs, rows, name="sum_rows"):
    parts = jobs[0][0][0].shape[0]
    if rows % 16:
        results = []
        for terms in jobs:
            value = 0.0
            for array, blocks in terms:
                split = array.reshape(parts, -1, rows, array.shape[2])
                value = value + jnp.stack([split[:, block] for block in blocks], 1).astype(F32)
            results.append(value.astype(BF).reshape(parts, -1, value.shape[3]))
        return results
    spots = [
        (array, blocks[index])
        for terms in jobs
        for index in range(len(terms[0][1]))
        for array, blocks in terms
    ]

    def kernel(*refs):
        at = 0
        for spot, terms in enumerate(jobs):
            out_ref = refs[len(spots) + spot]
            for index in range(len(terms[0][1])):
                value = refs[at][0].astype(F32)
                for offset in range(1, len(terms)):
                    value = value + refs[at + offset][0].astype(F32)
                out_ref[0, index * rows : (index + 1) * rows] = value.astype(BF)
                at += len(terms)

    def spec(block, lanes):
        return pl.BlockSpec((1, rows, lanes), lambda p: (p, block, 0))

    shapes = [(len(terms[0][1]) * rows, terms[0][0].shape[2]) for terms in jobs]
    return pl.pallas_call(
        kernel,
        name=name,
        grid=(parts,),
        in_specs=[spec(block, array.shape[2]) for array, block in spots],
        out_specs=[pl.BlockSpec((1, *shape), lambda p: (p, 0, 0)) for shape in shapes],
        out_shape=[jax.ShapeDtypeStruct((parts, *shape), BF) for shape in shapes],
        compiler_params=params(),
        cost_estimate=cost(sum(parts * size * lanes for size, lanes in shapes)),
    )(*[array for array, _ in spots])


def side_by_side(left, right, kept, lanes):
    rows, width = left.shape
    count = width // kept

    def kernel(left_ref, right_ref, out_ref):
        for index, ref in enumerate((left_ref, right_ref)):
            for side in range(count):
                spot = count * index + side
                out_ref[spot, :, :kept] = ref[:, side * kept : (side + 1) * kept]
                if lanes > kept:
                    out_ref[spot, :, kept:] = jnp.zeros((rows, lanes - kept), BF)

    return pl.pallas_call(
        kernel,
        name="side_by_side",
        out_shape=jax.ShapeDtypeStruct((2 * count, rows, lanes), BF),
        compiler_params=params(),
        cost_estimate=cost(4 * rows * lanes),
    )(left, right)


def mlp_forward(rows_in, grads, start, weight1, weight2, part, live=None):
    _, rows, half = rows_in.shape
    parts, _, lanes = weight1.near.shape
    ff = lanes // 2
    step = 384 if ff % 384 == 0 else ff
    steps = ff // step
    extras = [] if live is None else [live]

    def kernel(x_ref, g_ref, s_ref, n1_ref, f1_ref, n2_ref, f2_ref, *refs):
        hid_ref, act_ref, out_ref, dn2_ref, df2_ref, turned, sums = refs[len(extras) :]
        first = (pl.program_id(0) == 0) & (pl.program_id(1) == 0)
        last = (pl.program_id(0) == parts - 1) & (pl.program_id(1) == steps - 1)

        @pl.when(first)
        def _():
            for side in range(2):
                turned[side] = jnp.transpose(g_ref[side])
            sums[...] = s_ref[...]

        hidden = dot_nn(x_ref[0], n1_ref[0]) + dot_nn(x_ref[1], f1_ref[0])
        hid_ref[0] = hidden
        activ = jax.nn.gelu(hidden, approximate=True).astype(BF)
        act_ref[0] = activ
        sums[0] += dot_nt(activ, n2_ref[0])
        sums[1] += dot_nt(activ, f2_ref[0])
        dn2_ref[0] = dot_nn(turned[0], activ).astype(BF)
        df2_ref[0] = dot_nn(turned[1], activ).astype(BF)

        @pl.when(last)
        def _():
            if live is None:
                out_ref[...] = sums[...]
            else:
                out_ref[...] = (sums[...] * refs[0][...]).astype(BF)

    weight = pl.BlockSpec((1, half, step), lambda p, n: (p, 0, part * steps + n))
    grad = pl.BlockSpec((1, half, step), lambda p, n: (p, 0, n))
    unit = pl.BlockSpec((1, rows, step), lambda p, n: (p, 0, n))
    whole = full((2, rows, half))
    grad_shape = jax.ShapeDtypeStruct((parts, half, ff), BF)
    return pl.pallas_call(
        kernel,
        name="mlp_forward",
        grid=(parts, steps),
        in_specs=[whole, whole, whole, weight, weight, weight, weight] + [full(extra.shape) for extra in extras],
        out_specs=[unit, unit, whole, grad, grad],
        out_shape=[
            jax.ShapeDtypeStruct((parts, rows, ff), F32),
            jax.ShapeDtypeStruct((parts, rows, ff), BF),
            jax.ShapeDtypeStruct((2, rows, half), F32 if live is None else BF),
            grad_shape,
            grad_shape,
        ],
        scratch_shapes=[pltpu.VMEM((2, half, rows), BF), pltpu.VMEM((2, rows, half), F32)],
        compiler_params=params(),
        cost_estimate=cost(12 * rows * half * parts * ff),
    )(rows_in, grads, start, weight1.near, weight1.far, weight2.near, weight2.far, *extras)


def gelu_slope(value):
    root = math.sqrt(2.0 / math.pi)
    square = value * value
    curve = jnp.tanh(root * value * (1.0 + 0.044715 * square))
    return 0.5 * (1.0 + curve) + 0.5 * value * (1.0 - curve * curve) * root * (
        1.0 + 3.0 * 0.044715 * square
    )


def mlp_backward(grads, rows_in, hidden, weight1, weight2, part, start, finish=None):
    _, rows, half = rows_in.shape
    parts, _, lanes = weight1.near.shape
    ff = lanes // 2
    step = 384 if ff % 384 == 0 else ff
    steps = ff // step
    extras = list(finish or []) + ([] if start is None else [start])

    def kernel(g_ref, x_ref, hid_ref, n1_ref, f1_ref, n2_ref, f2_ref, *refs):
        extra_refs, refs = refs[: len(extras)], refs[len(extras) :]
        dn1_ref, df1_ref = refs[:2]
        out_refs = refs[2:-2]
        turned, sums = refs[-2:]
        first = (pl.program_id(0) == 0) & (pl.program_id(1) == 0)
        last = (pl.program_id(0) == parts - 1) & (pl.program_id(1) == steps - 1)

        @pl.when(first)
        def _():
            for side in range(2):
                turned[side] = jnp.transpose(x_ref[side])
            sums[...] = jnp.zeros_like(sums) if start is None else extra_refs[-1][...]

        d_activ = dot_nn(g_ref[0], n2_ref[0]) + dot_nn(g_ref[1], f2_ref[0])
        d_hidden = (d_activ * gelu_slope(hid_ref[0])).astype(BF)
        dn1_ref[0] = dot_nn(turned[0], d_hidden).astype(BF)
        df1_ref[0] = dot_nn(turned[1], d_hidden).astype(BF)
        sums[0] += dot_nt(d_hidden, n1_ref[0])
        sums[1] += dot_nt(d_hidden, f1_ref[0])

        @pl.when(last)
        def _():
            if finish is None:
                out_refs[0][...] = sums[...]
            else:
                value_ref, gain_ref, add_ref = extra_refs[:3]
                add_norm_back([sums[0], sums[1]], value_ref, gain_ref, add_ref, *out_refs)

    weight = pl.BlockSpec((1, half, step), lambda p, n: (p, 0, part * steps + n))
    grad = pl.BlockSpec((1, half, step), lambda p, n: (p, 0, n))
    unit = pl.BlockSpec((1, rows, step), lambda p, n: (p, 0, n))
    whole = full((2, rows, half))
    grad_shape = jax.ShapeDtypeStruct((parts, half, ff), BF)
    wide = jax.ShapeDtypeStruct((2, rows, half), F32)
    outs = [wide] if finish is None else [wide, *back_shapes(rows, half)]
    return pl.pallas_call(
        kernel,
        name="mlp_backward",
        grid=(parts, steps),
        in_specs=[whole, whole, unit, weight, weight, weight, weight] + [full(extra.shape) for extra in extras],
        out_specs=[grad, grad] + [full(out.shape) for out in outs],
        out_shape=[grad_shape, grad_shape] + outs,
        scratch_shapes=[pltpu.VMEM((2, half, rows), BF), pltpu.VMEM((2, rows, half), F32)],
        compiler_params=params(),
        cost_estimate=cost(12 * rows * half * parts * ff),
    )(grads, rows_in, hidden, weight1.near, weight1.far, weight2.near, weight2.far, *extras)


def back_shapes(rows, half):
    return [jax.ShapeDtypeStruct((2, rows, half), BF), jax.ShapeDtypeStruct((2, 1, half), F32)]


def add_norm_back(incoming, value_ref, gain_ref, add_ref, out_ref, low_ref, d_gain_ref):
    back, gains = norm_back([value_ref[0], value_ref[1]], gain_ref, incoming)
    for side in range(2):
        total = add_ref[side] + back[side]
        out_ref[side] = total
        low_ref[side] = total.astype(BF)
        d_gain_ref[side] = gains[side]


def text_bias(lengths_ref, micro, words, strip, text_slots, axis):
    spot = lax.broadcasted_iota(jnp.int32, (1, words) if axis else (words, 1), axis)
    inner = spot % strip
    place = spot // strip * text_slots + inner
    live = (place < lengths_ref[micro, 0]) | (
        (place >= CLIP_LEN) & (place < CLIP_LEN + lengths_ref[micro, 1])
    )
    return jnp.where(live & (inner < text_slots), 0.0, MASKED)


def cross_forward(query, text_kv, lengths, text_slots):
    parts, micros, slots, lanes = query.shape
    zones, strip = text_kv.shape[1], text_kv.shape[3]
    words = zones * strip
    local = lanes // HP
    factor = HD ** (-0.5) * LOG2E

    def kernel(len_ref, q_ref, kv_ref, out_ref):
        bias = text_bias(len_ref, pl.program_id(1), words, strip, text_slots, 1)
        for h in range(local):
            cut = slice(h * HP, (h + 1) * HP)
            keys = kv_ref[0, :, 0, :, cut].reshape(words, HP)
            scores = dot_nt(q_ref[0, 0, :, cut], keys) + bias
            top = jnp.max(scores, -1, keepdims=True)
            raised = jnp.exp2((scores - top) * factor)
            total = jnp.sum(raised, -1, keepdims=True)
            values = kv_ref[0, :, 0, :, lanes + h * HP : lanes + (h + 1) * HP].reshape(words, HP)
            out_ref[0, 0, :, cut] = (dot_nn(raised.astype(BF), values) / total).astype(BF)

    spot = lambda p, m, c: (p, m, 0, 0)
    far = lambda p, m, c: (p, 0, m, 0, 0)
    return pl.pallas_call(
        kernel,
        name="cross_forward",
        grid_spec=pltpu.PrefetchScalarGridSpec(
            num_scalar_prefetch=1,
            grid=(parts, micros),
            in_specs=[
                pl.BlockSpec((1, 1, slots, lanes), spot),
                pl.BlockSpec((1, zones, 1, strip, 2 * lanes), far),
            ],
            out_specs=pl.BlockSpec((1, 1, slots, lanes), spot),
        ),
        out_shape=jax.ShapeDtypeStruct(query.shape, BF),
        compiler_params=params(),
        cost_estimate=cost(4 * parts * micros * slots * words * lanes),
    )(lengths, query, text_kv)


def cross_backward(query, text_kv, lengths, incoming, text_slots):
    parts, micros, slots, lanes = query.shape
    zones, strip = text_kv.shape[1], text_kv.shape[3]
    words = zones * strip
    local = lanes // HP
    scale = HD ** (-0.5)
    factor = scale * LOG2E

    def kernel(len_ref, q_ref, kv_ref, in_ref, dq_ref, dkv_ref):
        bias = text_bias(len_ref, pl.program_id(1), words, strip, text_slots, 0)
        for h in range(local):
            cut = slice(h * HP, (h + 1) * HP)
            far = slice(lanes + h * HP, lanes + (h + 1) * HP)
            rows = q_ref[0, 0, :, cut]
            keys = kv_ref[0, :, 0, :, cut].reshape(words, HP)
            values = kv_ref[0, :, 0, :, far].reshape(words, HP)
            grads = in_ref[0, 0, :, cut]
            scores = dot_nt(keys, rows) + bias
            top = jnp.max(scores, 0, keepdims=True)
            raised = jnp.exp2((scores - top) * factor)
            probs = raised * (1.0 / jnp.sum(raised, 0, keepdims=True))
            d_probs = dot_nt(values, grads)
            inner = jnp.sum(probs * d_probs, 0, keepdims=True)
            d_scores = (probs * (d_probs - inner)).astype(BF)
            shape = (zones, strip, HP)
            dkv_ref[0, :, 0, :, far] = dot_nn(probs.astype(BF), grads).astype(BF).reshape(shape)
            dkv_ref[0, :, 0, :, cut] = (dot_nn(d_scores, rows) * scale).astype(BF).reshape(shape)
            dq_ref[0, 0, :, cut] = (dot_tn(d_scores, keys) * scale).astype(BF)

    spot = lambda p, m, c: (p, m, 0, 0)
    far = lambda p, m, c: (p, 0, m, 0, 0)
    return pl.pallas_call(
        kernel,
        name="cross_backward",
        grid_spec=pltpu.PrefetchScalarGridSpec(
            num_scalar_prefetch=1,
            grid=(parts, micros),
            in_specs=[
                pl.BlockSpec((1, 1, slots, lanes), spot),
                pl.BlockSpec((1, zones, 1, strip, 2 * lanes), far),
                pl.BlockSpec((1, 1, slots, lanes), spot),
            ],
            out_specs=[
                pl.BlockSpec((1, 1, slots, lanes), spot),
                pl.BlockSpec((1, zones, 1, strip, 2 * lanes), far),
            ],
        ),
        out_shape=[
            jax.ShapeDtypeStruct(query.shape, BF),
            jax.ShapeDtypeStruct(text_kv.shape, BF),
        ],
        compiler_params=params(),
        cost_estimate=cost(10 * parts * micros * slots * words * lanes),
    )(lengths, query, text_kv, incoming)


def tie(*values):
    return lax.optimization_barrier(values)


class Cube:
    def __init__(self):
        self.size = lax.axis_size("dp")
        self.bits = self.size.bit_length() - 1
        self.outer = list(range(1, self.bits))
        self.rank = lax.axis_index("dp")
        self.masks = []
        for place in range(self.size):
            mask = place >> (self.bits - 1)
            for bit in self.outer:
                mask |= ((place >> (bit - 1)) & 1) << bit
            self.masks.append(mask)
        self.owners = self.rank ^ jnp.array(self.masks, jnp.int32)

    def swap(self, value, bit, axis="dp"):
        pairs = [(i, i ^ (1 << bit)) for i in range(lax.axis_size(axis))]
        return lax.ppermute(value, axis, pairs)

    def trade(self, value):
        blocks = {mask: value[mask] for mask in range(self.size)}
        for bit in range(self.bits):
            send = sorted(mask for mask in blocks if mask >> bit & 1)
            got = self.swap(jnp.stack([blocks[mask] for mask in send]), bit)
            for place, mask in enumerate(send):
                blocks[mask] = got[place]
        return jnp.stack([blocks[mask] for mask in range(self.size)])

    def spread(self, value):
        held = value[None]
        for bit in range(self.bits):
            held = jnp.concatenate([held, self.swap(held, bit)])
        return held

    def add(self, value, axis):
        for bit in range(lax.axis_size(axis).bit_length() - 1):
            value = value + self.swap(value, bit, axis)
        return value


class Gather:
    def __init__(self, cube, shard, flip):
        self.cube = cube
        self.masks = [0]
        self.pieces = [shard]
        self.todo = cube.outer[::-1] if flip else list(cube.outer)

    def move(self):
        bit = self.todo.pop(0)
        self.masks = self.masks + [mask | (1 << bit) for mask in self.masks]
        self.pieces = self.pieces + [self.cube.swap(piece, bit) for piece in self.pieces]

    def join(self):
        while self.todo:
            self.move()
        order = sorted(range(len(self.masks)), key=lambda i: self.cube.masks.index(self.masks[i]))
        self.pieces = [join_rows([self.pieces[i] for i in order])]

    def weight(self):
        near = self.pieces[0]
        return Lanes(near, self.cube.swap(near, 0))


class Scatter:
    def __init__(self, cube, near, far, flip):
        self.cube = cube
        self.todo = list(cube.outer) if flip else cube.outer[::-1]
        self.rows = near.shape[1] // (cube.size // 2)
        self.places = list(range(cube.size // 2))
        self.near = near
        self.got = []
        self.pieces = [cube.swap(far, 0)]
        self.arriving = self.places

    def job(self, places):
        return [(self.near, places)] + [
            (value, [held.index(place) for place in places]) for value, held in self.got
        ]

    def absorb(self):
        self.got.append((self.pieces[0], self.arriving))


def pack(movers):
    jobs = []
    for mover in movers:
        mover.absorb()
        mover.bit = mover.todo.pop(0)
        weight = 1 << (mover.bit - 1)
        sent = [place for place in mover.places if place & weight]
        mover.places = [place for place in mover.places if not place & weight]
        mover.arriving = [place ^ weight for place in sent]
        jobs.append(mover.job(sent))
    for mover, value in zip(movers, sum_rows(jobs, movers[0].rows)):
        mover.pieces = [value]


def send(movers):
    for mover in movers:
        mover.pieces = [mover.cube.swap(mover.pieces[0], mover.bit)]


def results(movers):
    while movers[0].todo:
        pack(movers)
        send(movers)
    for mover in movers:
        mover.absorb()
    return sum_rows([mover.job([0]) for mover in movers], movers[0].rows)


def pin(value, *others):
    flat = []
    for other in others:
        flat += other.pieces if hasattr(other, "pieces") else [other]
    return tie(value, *flat)[0]


def bind(value, *movers):
    flat = [piece for mover in movers for piece in mover.pieces]
    held = tie(value, *flat)
    spot = 1
    for mover in movers:
        count = len(mover.pieces)
        mover.pieces = list(held[spot : spot + count])
        spot += count
    return held[0]


def hold(movers, *others):
    for mover in movers:
        mover.pieces = [pin(piece, *others) for piece in mover.pieces]


def on_device(
    tokens,
    skip_tokens,
    text,
    timestep,
    grid,
    text_len,
    w_skip,
    w_mod,
    w_qkv,
    w_out1,
    w_query2,
    w_text_kv,
    w_out2,
    w_fc1,
    w_fc2,
    gain_skip,
    gain_attn,
    gain_cross,
    gain_mlp,
    gain_query,
    gain_key,
    cotangent,
):
    micros, slots, width = tokens.shape
    parts = lax.axis_size("sp")
    zone = lax.axis_index("sp")
    cube = Cube()
    ranks = cube.size
    rows = micros * slots
    sequence = slots * parts
    local = H // parts
    lanes = local * HP + -local * HP % 128
    text_slots = text.shape[1]
    text_strip = -(-text_slots // 16) * 16
    features = text.shape[2]
    strip = width // ranks
    middle = width // 2
    kept = w_skip.shape[0]
    skip_lanes = -(-kept // 256) * 256
    skip_cut = skip_lanes // 2
    qkv_cut = (3 * lanes) // 256 * 128 + 128
    text_rows = w_text_kv.shape[0]

    def spread(shard, before=None):
        if before is not None:
            shard, before = tie(shard, before)
        return lax.all_gather(shard, "sp", axis=0, tiled=False)

    def fetch(value, cut):
        return [Gather(cube, value[:, :, :cut], 0), Gather(cube, value[:, :, cut:], 1)]

    def advance(movers):
        for mover in movers:
            mover.move()

    def join(movers):
        for mover in movers:
            mover.join()

    def exchange(value):
        return lax.all_to_all(value, "sp", split_axis=0, concat_axis=0, tiled=True)

    skip_z = spread(jnp.pad(w_skip.T, ((0, 0), (0, skip_lanes - kept))))
    steps = cube.spread(timestep[:, 0])
    joined = side_by_side(tokens.reshape(rows, width), skip_tokens.reshape(rows, width), kept, skip_lanes)
    wide = grid[:, 0, 1]
    counts = grid[:, 0, 0] * wide
    cosine, sine = rope_tables(sequence, wide, lanes)
    skip_z, steps, joined, cosine, sine = tie(skip_z, steps, joined, cosine, sine)
    skip_m = fetch(skip_z, skip_cut)
    qkv_z = spread(pad_heads(w_qkv.reshape(strip, -1), local), skip_z)
    advance(skip_m)

    time_act = jax.nn.silu(time_embed(steps, width)).astype(BF).reshape(ranks * micros, parts, -1)
    time_part = lax.dynamic_index_in_dim(time_act, zone, 1, keepdims=False)
    shift = cube.add(jnp.dot(time_part, w_mod, preferred_element_type=F32), "sp")
    skip_m[0].pieces[1], shift = tie(skip_m[0].pieces[1], shift)
    while skip_m[0].todo:
        advance(skip_m)
    shift = cube.trade(shift.reshape(ranks, micros, strip))
    skip_m[0].pieces[-1], shift = tie(skip_m[0].pieces[-1], shift)
    shift = jnp.stack([shift[mask] for mask in cube.masks]).reshape(2, ranks // 2, micros, strip)
    shift = jnp.transpose(shift, (0, 2, 1, 3)).reshape(2, micros, middle)
    qkv_m = fetch(qkv_z, qkv_cut)
    hold(qkv_m, *skip_m)
    advance(qkv_m)
    fc1_z = spread(pin(w_fc1, *skip_m))
    fc2_z = spread(pin(w_fc2.T, *qkv_m))
    join(skip_m)
    skip_w = [mover.weight() for mover in skip_m]

    def shuffle(count):
        block = count // ranks
        place = jnp.arange(count, dtype=jnp.int32)
        source = cube.owners[place // block] * block + place % block
        return (place[:, None] == source[None, :]).astype(BF)

    turn = shuffle(width)
    text_turn = shuffle(features)
    gains = jnp.stack([gain_skip, gain_attn, gain_cross, gain_mlp])
    gains = gains.reshape(4, ranks, strip)[:, cube.owners].reshape(4, 2, 1, middle)
    g_skip, g_attn, g_cross, g_mlp = gains

    lengths = text_len[:, 0, :]
    place = zone * slots + jnp.arange(slots, dtype=jnp.int32)
    live = (place[None, :] < counts[:, None]).astype(F32).reshape(rows, 1)
    gain_q = pad_heads(jnp.tile(gain_query, local)[None, :], local)
    gain_k = pad_heads(jnp.tile(gain_key, local)[None, :], local)

    grad3 = jnp.stack(
        [
            jnp.dot(cotangent.reshape(rows, width), side, preferred_element_type=F32) * live
            for side in (turn[:, :middle], turn[:, middle:])
        ]
    )
    d_mlp = grad3.astype(BF)

    wide_shape = jax.ShapeDtypeStruct((2, rows, middle), F32)
    low_shape = jax.ShapeDtypeStruct((2, rows, middle), BF)
    gain_shape = jax.ShapeDtypeStruct((2, 1, middle), F32)

    def first_norms(sums, extra, out):
        g0_ref, g1_ref, shift_ref = extra
        base_ref, stream_ref, pre_ref = out
        unit, _ = norm_unit(sums)
        stream = [unit[side] * g0_ref[side] for side in range(2)]
        unit, _ = norm_unit(stream)
        for side in range(2):
            base_ref[side] = sums[side]
            stream_ref[side] = stream[side]
            for micro in range(micros):
                cut = slice(micro * slots, (micro + 1) * slots)
                pre = unit[side][cut] * g1_ref[side] + shift_ref[side, micro : micro + 1]
                pre_ref[side, cut] = pre.astype(BF)

    def next_norm(sums, extra, out):
        before_ref, gain_ref = extra
        after_ref, pre_ref = out
        stream = [before_ref[side] + sums[side] for side in range(2)]
        unit, _ = norm_unit(stream)
        for side in range(2):
            after_ref[side] = stream[side]
            pre_ref[side] = (unit[side] * gain_ref[side]).astype(BF)

    base, stream, pre_attn = to_features(
        joined, skip_w, [g_skip, g_attn, shift], [wide_shape, wide_shape, low_shape], first_norms
    )
    while qkv_m[0].todo:
        advance(qkv_m)
    after_qkv = [mover.pieces[-1] for mover in qkv_m]
    hold(qkv_m, pre_attn)
    join(qkv_m)
    pre_attn, fc1_z = tie(pre_attn, fc1_z)
    qkv_w = [mover.weight() for mover in qkv_m]
    projected = to_lanes(pre_attn, qkv_w)
    projected, fc2_z = tie(projected, fc2_z)
    fc_m = [Gather(cube, fc1_z, 0), Gather(cube, fc2_z, 1)]
    hold(fc_m, *after_qkv)
    advance(fc_m)
    raw = exchange(projected.reshape(parts, micros, slots, 3 * lanes))
    cross_z = jnp.concatenate([pad_heads(side, local) for side in (w_out1.T, w_query2, w_out2.T)], 1)
    cross_z = spread(pin(cross_z, *fc_m))
    text_own = jnp.dot(text.reshape(-1, features), text_turn, preferred_element_type=F32).astype(BF)
    text_own = jnp.pad(
        text_own.reshape(micros, text_slots, features), ((0, 0), (0, text_strip - text_slots), (0, 0))
    ).reshape(micros * text_strip, features)
    text_z = jnp.pad(pad_heads(w_text_kv.reshape(text_rows, -1), local), ((0, max(0, strip - text_rows)), (0, 0)))
    while fc_m[0].todo:
        advance(fc_m)
    text_z = spread(text_z, cross_z)
    text_all = spread(text_own, cross_z)
    cross_m = fetch(cross_z, 2 * lanes)
    advance(cross_m)
    raw, d_mlp, turn, text_turn = tie(raw, d_mlp, turn, text_turn)
    text_m = Gather(cube, text_z[:, :text_rows], 1)
    attended, turned_q, turned_k, norms = self_forward(raw, counts, cosine, sine, gain_q, gain_k)
    attended = bind(attended, *fc_m, *cross_m, text_m)
    attended, text_all = tie(attended, text_all)
    text_m.move()
    attended = exchange(attended).reshape(parts, rows, lanes)
    while cross_m[0].todo:
        advance(cross_m)
    join(fc_m)
    hold(cross_m, attended)
    attended = bind(attended, text_m, *fc_m)
    while text_m.todo:
        text_m.move()
    join(cross_m[:1])
    first_w = cross_m[0].weight()
    out1_w, query2_w = (Lanes(first_w.near, first_w.far, lanes, index) for index in range(2))
    attended, first_w.far = tie(attended, first_w.far)
    out1_w.far = query2_w.far = first_w.far
    text_all = text_all.reshape(-1, features)
    text_all = jnp.stack([text_all[:, : features // 2], text_all[:, features // 2 :]])
    stream1, pre_cross = to_features(
        attended, [out1_w], [stream, g_cross], [wide_shape, low_shape], next_norm
    )
    pre_cross = bind(pre_cross, text_m, *cross_m[1:])
    text_m.join()
    text_w = text_m.weight()
    join(cross_m[1:])
    out2_w = cross_m[1].weight()
    query2 = to_lanes(pre_cross, [query2_w]).reshape(parts, micros, slots, lanes)
    fc1_w, fc2_w = [mover.weight() for mover in fc_m]
    text_kv = to_lanes(text_all, [text_w]).reshape(parts, parts, micros, text_strip, 2 * lanes)
    crossed = cross_forward(query2, text_kv, lengths, text_slots).reshape(parts, rows, lanes)
    stream2, pre_mlp = to_features(
        crossed, [out2_w], [stream1, g_mlp], [wide_shape, low_shape], next_norm
    )
    hidden0, activ0, partial, fc2_n0, fc2_f0 = mlp_forward(pre_mlp, d_mlp, stream2, fc1_w, fc2_w, 0)
    hidden1, activ1, result, fc2_n1, fc2_f1 = mlp_forward(pre_mlp, d_mlp, partial, fc1_w, fc2_w, 1, live)
    fc2_s = [Scatter(cube, fc2_n0, fc2_f0, 0), Scatter(cube, fc2_n1, fc2_f1, 1)]

    def settle(values, before=None):
        value = values[0] if len(values) == 1 else jnp.concatenate(values, 2)
        if before is not None:
            value, before = tie(value, before)
        return lax.psum_scatter(value, "sp", scatter_dimension=0, tiled=False)

    fc1_n0, fc1_f0, partial = mlp_backward(d_mlp, pre_mlp, hidden0, fc1_w, fc2_w, 0, None)
    fc1_s = [Scatter(cube, fc1_n0, fc1_f0, 0)]
    pack(fc2_s)
    partial = bind(partial, *fc2_s)
    send(fc2_s)
    fc1_n1, fc1_f1, grad2, d_cross, d_gain_mlp = mlp_backward(
        d_mlp, pre_mlp, hidden1, fc1_w, fc2_w, 1, partial, [stream2, g_mlp, grad3]
    )
    fc1_s.append(Scatter(cube, fc1_n1, fc1_f1, 1))
    d_cross = bind(d_cross, *fc2_s)
    d_crossed = to_lanes(d_cross, [out2_w])
    pack(fc2_s)
    d_crossed = bind(d_crossed, *fc2_s)
    send(fc2_s)
    d_query2, d_text_kv = cross_backward(
        query2, text_kv, lengths, d_crossed.reshape(parts, micros, slots, lanes), text_slots
    )
    d_query2 = bind(d_query2, *fc2_s)
    d_query2 = d_query2.reshape(parts, rows, lanes)
    d_text_kv = d_text_kv.reshape(parts, -1, 2 * lanes)
    total_fc2 = results(fc2_s)
    term_fc2 = settle(total_fc2)

    def go_back(sums, extra, out):
        add_norm_back(sums, *extra, *out)

    grad1, d_attn, d_gain_cross = to_features(
        d_query2, [query2_w], [stream1, g_cross, grad2], [wide_shape, low_shape, gain_shape], go_back
    )
    d_attn = bind(d_attn, *fc1_s)
    pack(fc1_s)
    d_attn = bind(d_attn, *fc1_s)
    send(fc1_s)
    d_attended = to_lanes(d_attn, [out1_w])
    d_attended, d_text_kv, pre_cross = tie(d_attended, d_text_kv, pre_cross)
    d_heads = exchange(d_attended.reshape(parts, micros, slots, lanes))

    def words_back(sums, extra, out):
        size = micros * text_strip
        for zone in range(parts):
            for side in range(2):
                out[0][zone, side] = sums[side][zone * size : (zone + 1) * size].astype(BF)

    words_shape = jax.ShapeDtypeStruct((parts, 2, micros * text_strip, features // 2), BF)
    d_words = to_features(d_text_kv, [text_w], [], [words_shape], words_back)[0]
    text_t = list(terms_of([(text_all, d_text_kv, 2 * lanes, 0)]))
    cross_t = terms_of(
        [(d_attn, attended, lanes, 0), (pre_cross, d_query2, lanes, 0), (d_cross, crossed, lanes, 0)]
    )
    cross_t = list(cross_t)
    d_heads, d_words, text_t[1], cross_t[1] = tie(d_heads, d_words, text_t[1], cross_t[1])
    d_words = settle([d_words])
    text_s, cross_s = Scatter(cube, *text_t, 1), Scatter(cube, *cross_t, 0)
    d_heads = bind(d_heads, *fc1_s)
    pack(fc1_s)
    d_heads = bind(d_heads, *fc1_s)
    send(fc1_s)
    d_raw, d_gain_q, d_gain_k = self_backward(
        raw, counts, cosine, sine, gain_q, gain_k, turned_q, turned_k, norms, d_heads
    )
    d_raw, term_fc2, d_words = tie(d_raw, term_fc2, d_words)
    d_raw = bind(d_raw, *fc1_s)
    d_projected = exchange(d_raw).reshape(parts, rows, 3 * lanes)
    other_s = [cross_s, text_s]
    total_fc1 = results(fc1_s)
    pack([cross_s])
    pack([text_s])
    send(other_s)
    d_projected = bind(d_projected, *other_s)
    term_fc1 = settle(total_fc1, d_projected)
    qkv_s = [
        Scatter(cube, *terms_of([(pre_attn, d_projected, 2 * lanes, 0)]), 0),
        Scatter(cube, *terms_of([(pre_attn, d_projected, lanes, 2)]), 1),
    ]
    pack([cross_s])
    pack([text_s])
    send(other_s)
    pack(qkv_s)
    d_projected = bind(d_projected, *qkv_s)
    send(qkv_s)

    def last_norms(sums, extra, out):
        stream_ref, g1_ref, base_ref, g0_ref, add_ref = extra
        low_ref, d_shift_ref, d_g1_ref, d_g0_ref = out
        back, gains1 = norm_back([stream_ref[0], stream_ref[1]], g1_ref, sums)
        total = [add_ref[side] + back[side] for side in range(2)]
        back, gains0 = norm_back([base_ref[0], base_ref[1]], g0_ref, total)
        for side in range(2):
            low_ref[side] = back[side].astype(BF)
            d_g1_ref[side] = gains1[side]
            d_g0_ref[side] = gains0[side]
            for micro in range(micros):
                part = sums[side][micro * slots : (micro + 1) * slots]
                d_shift_ref[side, micro : micro + 1] = jnp.sum(part, 0, keepdims=True)

    shift_shape = jax.ShapeDtypeStruct((2, micros, middle), F32)
    d_base, d_shift, d_gain_attn, d_gain_skip = to_features(
        d_projected,
        qkv_w,
        [stream, g_attn, base, g_skip, grad1],
        [low_shape, shift_shape, gain_shape, gain_shape],
        last_norms,
    )
    d_base = bind(d_base, *other_s)
    skip_t = [list(terms_of([(d_base, joined, skip_cut, flip)])) for flip in range(2)]
    skip_t[0][1] = bind(skip_t[0][1], *qkv_s)
    skip_s = [Scatter(cube, *pair, flip) for flip, pair in enumerate(skip_t)]
    pack(qkv_s)
    send(qkv_s)
    pack(skip_s)
    term_cross, term_text = settle(results([cross_s])), settle(results([text_s]))
    send(skip_s)
    term_qkv = settle(results(qkv_s))
    term_skip = settle(results(skip_s))
    d_joined = to_inputs(d_base, skip_w, kept)
    result = (
        jnp.dot(result[0], turn[:, :middle].T, preferred_element_type=F32)
        + jnp.dot(result[1], turn[:, middle:].T, preferred_element_type=F32)
    ).astype(BF)
    d_words = d_words.reshape(2, micros * text_strip, features // 2)
    d_words = jnp.dot(
        d_words[0], text_turn[:, : features // 2].T, preferred_element_type=F32
    ) + jnp.dot(d_words[1], text_turn[:, features // 2 :].T, preferred_element_type=F32)
    d_words = d_words.reshape(micros, text_strip, features)[:, :text_slots]

    d_shift = jnp.transpose(d_shift.reshape(2, micros, ranks // 2, strip), (0, 2, 1, 3))
    d_shift = d_shift.reshape(ranks, micros, strip)
    d_shift = jnp.stack([d_shift[cube.masks.index(mask)] for mask in range(ranks)])
    d_shift = cube.add(cube.trade(d_shift), "sp").reshape(ranks * micros, strip)
    term_mod = lax.dot_general(
        time_part.astype(F32), d_shift, (((0,), (0,)), ((), ())), precision=lax.Precision.HIGHEST
    )

    places = jnp.array([cube.masks.index(mask) for mask in range(ranks)], jnp.int32)
    places = places[jnp.arange(ranks, dtype=jnp.int32) ^ cube.rank]
    gains = jnp.stack([d_gain_skip, d_gain_attn, d_gain_cross, d_gain_mlp])
    gains = gains.reshape(4, ranks, strip)[:, places].reshape(-1)
    heads = jnp.stack([jnp.sum(d_gain_q, (0, 1)), jnp.sum(d_gain_k, (0, 1))])
    heads = jnp.sum(heads[:, : local * HP].reshape(2, local, HP)[:, :, :HD], 1)
    packed = jnp.concatenate([gains, heads.reshape(-1)])
    packed = cube.add(cube.add(packed, "sp"), "dp")
    gains = packed[: 4 * width].reshape(4, ranks * parts, -1)
    gains = lax.dynamic_index_in_dim(gains, cube.rank * parts + zone, 1, keepdims=False)
    heads = packed[4 * width :].reshape(2, HD)

    def whole(term, groups):
        return cut_heads(term.astype(F32), local).reshape(term.shape[0], groups, -1)

    return (
        result.reshape(tokens.shape),
        d_joined[0].reshape(tokens.shape),
        d_joined[1].reshape(tokens.shape),
        d_words.reshape(text.shape),
        term_skip.astype(F32)[:, :kept].T,
        term_mod,
        whole(term_qkv, 3),
        cut_heads(term_cross[:, :lanes].astype(F32), local).T,
        cut_heads(term_cross[:, lanes : 2 * lanes].astype(F32), local),
        whole(term_text, 2),
        cut_heads(term_cross[:, 2 * lanes :].astype(F32), local).T,
        term_fc1.astype(F32),
        term_fc2.astype(F32).T,
        gains[0],
        gains[1],
        gains[2],
        gains[3],
        heads[0],
        heads[1],
    )


def solution(mesh):
    rows = P(None, ("dp", "sp"), None)
    column = P("sp", "dp")
    row = P("dp", "sp")
    grouped = P("dp", None, "sp")
    in_specs = (
        (rows, rows, rows, P(None, "dp"), P(None, "dp", None), P(None, "dp", None))
        + (column, column, grouped, column, row, grouped, column, row, column)
        + (P(),) * 6
        + (rows,)
    )
    out_specs = (
        (rows, rows, rows, rows)
        + (column, column, grouped, column, row, grouped, column, row, column)
        + (P(("dp", "sp")),) * 4
        + (P(), P())
    )
    return jax.shard_map(
        on_device, mesh=mesh, in_specs=in_specs, out_specs=out_specs, check_vma=False
    )
```

```python
import math

import jax
import jax.numpy as jnp
from jax import lax
from jax.experimental import pallas as pl
from jax.experimental.pallas import tpu as pltpu
from jax.sharding import PartitionSpec as P

H = 16
HD = 88
HP = 96
CLIP_LEN = 77
ROWS = 256

EPS = 1e-06
MASKED = -1e30
LOG2E = 1.4426950408889634
BF = jnp.bfloat16
F32 = jnp.float32


def time_embed(step, width):
    half = width // 2
    rate = jnp.exp(-math.log(10000.0) * jnp.arange(half, dtype=F32) / half)
    angle = step.astype(F32)[..., None] * rate
    return jnp.concatenate([jnp.cos(angle), jnp.sin(angle)], -1)


def rope_tables(sequence, wide, lanes):
    place = jnp.arange(sequence, dtype=jnp.int32)[None, :, None]
    wide = wide[:, None, None]
    lane = jnp.arange(lanes, dtype=jnp.int32)[None, None, :] % HP
    pair = lane // 2
    quarter = HD // 4
    upper = pair < quarter
    rank = jnp.where(upper, pair, pair - quarter).astype(F32)
    rate = jnp.exp(-math.log(10000.0) * rank / quarter)
    angle = jnp.where(upper, place // wide, place % wide).astype(F32) * rate
    sine = jnp.sin(angle)
    return jnp.cos(angle), jnp.where(lane % 2 == 0, -sine, sine)


def pad_heads(packed, local):
    rows, lanes = packed.shape
    groups = packed.reshape(rows, lanes // (local * HD), local, HD)
    groups = jnp.pad(groups, ((0, 0), (0, 0), (0, 0), (0, HP - HD)))
    groups = groups.reshape(rows, -1, local * HP)
    return jnp.pad(groups, ((0, 0), (0, 0), (0, -local * HP % 128))).reshape(rows, -1)


def cut_heads(padded, local):
    rows = padded.shape[0]
    groups = padded.reshape(rows, -1, local * HP + -local * HP % 128)[:, :, : local * HP]
    return groups.reshape(rows, -1, local, HP)[..., :HD].reshape(rows, -1)


def head_masks(shape, local):
    lane = lax.broadcasted_iota(jnp.int32, shape, len(shape) - 1)
    inside = lane % HP < HD
    return [((lane // HP == h) & inside).astype(F32) for h in range(local)]


def head_mean(value, masks):
    total = None
    for mask in masks:
        term = (jnp.sum(value * mask, -1, keepdims=True) * (1.0 / HD)) * mask
        total = term if total is None else total + term
    return total


def head_unit(value, masks):
    centre = value - head_mean(value, masks)
    spread = None
    square = centre * centre
    for mask in masks:
        mean = jnp.sum(square * mask, -1, keepdims=True) * (1.0 / HD)
        term = lax.rsqrt(mean + EPS) * mask
        spread = term if spread is None else spread + term
    return centre * spread, spread


def turn_pairs(value):
    lanes = value.shape[-1]
    after = pltpu.roll(value, lanes - 1, 1)
    before = pltpu.roll(value, 1, 1)
    lane = lax.broadcasted_iota(jnp.int32, value.shape, 1)
    return jnp.where(lane % 2 == 0, after, before)


def dot_nt(left, right):
    return lax.dot_general(left, right, (((1,), (1,)), ((), ())), preferred_element_type=F32)


def dot_nn(left, right):
    return lax.dot_general(left, right, (((1,), (0,)), ((), ())), preferred_element_type=F32)


def dot_tn(left, right):
    return lax.dot_general(left, right, (((0,), (0,)), ((), ())), preferred_element_type=F32)


def self_forward(raw, counts, cosine, sine, gain_q, gain_k):
    parts, micros, slots, packed = raw.shape
    lanes = packed // 3
    local = lanes // HP
    sequence = parts * slots
    factor = HD ** (-0.5) * LOG2E

    def kernel(count_ref, raw_ref, cos_ref, sin_ref, gq_ref, gk_ref, out_ref, q_ref, k_ref, lse_ref):
        count = count_ref[pl.program_id(0)]
        blocks = (count + slots - 1) // slots
        out_ref[...] = jnp.zeros_like(out_ref)
        masks = head_masks((1, lanes), local)

        def prepare(part, carry):
            spot = pl.ds(pl.multiple_of(part * slots, slots), slots)
            cosine, sine = cos_ref[0, spot, :], sin_ref[0, spot, :]
            for index, gain_ref, dest in ((0, gq_ref, q_ref), (1, gk_ref, k_ref)):
                value = raw_ref[part, 0, :, index * lanes : (index + 1) * lanes].astype(F32)
                scaled = head_unit(value, masks)[0] * gain_ref[...]
                dest[0, spot, :] = (scaled * cosine + turn_pairs(scaled) * sine).astype(BF)
            return carry

        lax.fori_loop(0, parts, prepare, 0)
        column = lax.broadcasted_iota(jnp.int32, (1, sequence), 1)
        bias = jnp.where(column < count, 0.0, MASKED)
        for h in range(local):
            cut = slice(h * HP, (h + 1) * HP)
            keys = k_ref[0, :, cut]
            values = raw_ref[:, 0, :, 2 * lanes + h * HP : 2 * lanes + (h + 1) * HP].reshape(sequence, HP)

            def one_block(part, carry):
                spot = pl.ds(pl.multiple_of(part * slots, slots), slots)
                scores = dot_nt(q_ref[0, spot, cut], keys) + bias
                top = jnp.max(scores, -1, keepdims=True)
                raised = jnp.exp2((scores - top) * factor)
                total = jnp.sum(raised, -1, keepdims=True)
                result = dot_nn(raised.astype(BF), values) / total
                out_ref[part, 0, :, cut] = result.astype(BF)
                norm = jnp.broadcast_to(top * factor + jnp.log2(total), (slots, 128))
                lse_ref[0, h : h + 1, spot] = jnp.transpose(norm)[0:1, :]
                return carry

            lax.fori_loop(0, blocks, one_block, 0)

    whole = lambda m, c: (0, m, 0, 0)
    table = lambda m, c: (m, 0, 0)
    fixed = lambda m, c: (0, 0)
    return pl.pallas_call(
        kernel,
        name="self_forward",
        grid_spec=pltpu.PrefetchScalarGridSpec(
            num_scalar_prefetch=1,
            grid=(micros,),
            in_specs=[
                pl.BlockSpec((parts, 1, slots, packed), whole),
                pl.BlockSpec((1, sequence, lanes), table),
                pl.BlockSpec((1, sequence, lanes), table),
                pl.BlockSpec((1, lanes), fixed),
                pl.BlockSpec((1, lanes), fixed),
            ],
            out_specs=[
                pl.BlockSpec((parts, 1, slots, lanes), whole),
                pl.BlockSpec((1, sequence, lanes), table),
                pl.BlockSpec((1, sequence, lanes), table),
                pl.BlockSpec((1, local, sequence), table),
            ],
        ),
        out_shape=[
            jax.ShapeDtypeStruct((parts, micros, slots, lanes), BF),
            jax.ShapeDtypeStruct((micros, sequence, lanes), BF),
            jax.ShapeDtypeStruct((micros, sequence, lanes), BF),
            jax.ShapeDtypeStruct((micros, local, sequence), F32),
        ],
        compiler_params=params(),
        cost_estimate=cost(4 * micros * local * sequence * sequence * HP),
    )(counts, raw, cosine, sine, gain_q, gain_k)


def self_backward(raw, counts, cosine, sine, gain_q, gain_k, turned_q, turned_k, norms, incoming):
    parts, micros, slots, packed = raw.shape
    lanes = packed // 3
    local = lanes // HP
    sequence = parts * slots
    scale = HD ** (-0.5)
    factor = scale * LOG2E

    def kernel(
        count_ref,
        raw_ref,
        cos_ref,
        sin_ref,
        gq_ref,
        gk_ref,
        q_ref,
        k_ref,
        lse_ref,
        in_ref,
        out_ref,
        dgq_ref,
        dgk_ref,
        dq_s,
        dk_s,
        dv_s,
    ):
        count = count_ref[pl.program_id(0)]
        blocks = (count + slots - 1) // slots
        dq_s[...] = jnp.zeros_like(dq_s)
        dk_s[...] = jnp.zeros_like(dk_s)
        dv_s[...] = jnp.zeros_like(dv_s)
        row = lax.broadcasted_iota(jnp.int32, (sequence, 1), 0)
        bias = jnp.where(row < count, 0.0, MASKED)
        for h in range(local):
            cut = slice(h * HP, (h + 1) * HP)
            keys = k_ref[0, :, cut]
            values = raw_ref[:, 0, :, 2 * lanes + h * HP : 2 * lanes + (h + 1) * HP].reshape(sequence, HP)

            def one_block(part, carry):
                spot = pl.ds(pl.multiple_of(part * slots, slots), slots)
                rows = q_ref[0, spot, cut]
                grads = in_ref[part, 0, :, cut]
                norm = lse_ref[0, h : h + 1, spot]
                probs = jnp.exp2(dot_nt(keys, rows) * factor + bias - norm)
                d_probs = dot_nt(values, grads)
                inner = jnp.sum(probs * d_probs, 0, keepdims=True)
                d_scores = (probs * (d_probs - inner)).astype(BF)
                dv_s[:, cut] += dot_nn(probs.astype(BF), grads)
                dk_s[:, cut] += dot_nn(d_scores, rows)
                dq_s[spot, cut] = dot_tn(d_scores, keys)
                return carry

            lax.fori_loop(0, blocks, one_block, 0)
        masks = head_masks((1, lanes), local)

        def finish(part, carry):
            spot = pl.ds(pl.multiple_of(part * slots, slots), slots)
            cosine, sine = cos_ref[0, spot, :], sin_ref[0, spot, :]
            sums = []
            for index, gain_ref, source in ((0, gq_ref, dq_s), (1, gk_ref, dk_s)):
                grad = source[spot, :] * scale
                grad = grad * cosine - turn_pairs(grad) * sine
                value = raw_ref[part, 0, :, index * lanes : (index + 1) * lanes].astype(F32)
                unit, spread = head_unit(value, masks)
                leading = grad * gain_ref[...]
                back = leading - head_mean(leading, masks) - unit * head_mean(leading * unit, masks)
                out_ref[part, 0, :, index * lanes : (index + 1) * lanes] = (spread * back).astype(BF)
                sums.append(carry[index] + jnp.sum(grad * unit, 0, keepdims=True))
            out_ref[part, 0, :, 2 * lanes : 3 * lanes] = dv_s[spot, :].astype(BF)
            return tuple(sums)

        zero = jnp.zeros((1, lanes), F32)
        d_gains = lax.fori_loop(0, parts, finish, (zero, zero))
        dgq_ref[0] = d_gains[0]
        dgk_ref[0] = d_gains[1]

    whole = lambda m, c: (0, m, 0, 0)
    table = lambda m, c: (m, 0, 0)
    fixed = lambda m, c: (0, 0)
    return pl.pallas_call(
        kernel,
        name="self_backward",
        grid_spec=pltpu.PrefetchScalarGridSpec(
            num_scalar_prefetch=1,
            grid=(micros,),
            in_specs=[
                pl.BlockSpec((parts, 1, slots, packed), whole),
                pl.BlockSpec((1, sequence, lanes), table),
                pl.BlockSpec((1, sequence, lanes), table),
                pl.BlockSpec((1, lanes), fixed),
                pl.BlockSpec((1, lanes), fixed),
                pl.BlockSpec((1, sequence, lanes), table),
                pl.BlockSpec((1, sequence, lanes), table),
                pl.BlockSpec((1, local, sequence), table),
                pl.BlockSpec((parts, 1, slots, lanes), whole),
            ],
            out_specs=[
                pl.BlockSpec((parts, 1, slots, packed), whole),
                pl.BlockSpec((1, 1, lanes), table),
                pl.BlockSpec((1, 1, lanes), table),
            ],
            scratch_shapes=[pltpu.VMEM((sequence, lanes), F32) for index in range(3)],
        ),
        out_shape=[
            jax.ShapeDtypeStruct((parts, micros, slots, packed), BF),
            jax.ShapeDtypeStruct((micros, 1, lanes), F32),
            jax.ShapeDtypeStruct((micros, 1, lanes), F32),
        ],
        compiler_params=params(),
        cost_estimate=cost(10 * micros * local * sequence * sequence * HP),
    )(counts, raw, cosine, sine, gain_q, gain_k, turned_q, turned_k, norms, incoming)


def cost(flops):
    return pl.CostEstimate(flops=flops // 16, bytes_accessed=flops // 16000, transcendentals=0)


def full(shape):
    return pl.BlockSpec(shape, lambda *index: (0,) * len(shape))


def params(megabytes=60):
    return pltpu.CompilerParams(vmem_limit_bytes=megabytes << 20)


class Lanes:
    def __init__(self, near, far, block=None, index=0):
        self.near, self.far = near, far
        self.block = block or near.shape[2]
        self.index = index

    def spec(self):
        index = self.index
        return pl.BlockSpec((1, self.near.shape[1], self.block), lambda p, *rest: (p, 0, index))


def to_lanes(value, weights, dtype=BF, name="to_lanes"):
    rows = value.shape[1]
    parts, half, _ = weights[0].near.shape
    total = sum(weight.block for weight in weights)

    def kernel(x_ref, *refs):
        out_ref = refs[-1]
        at = 0
        for index, weight in enumerate(weights):
            result = dot_nn(x_ref[0], refs[2 * index][0]) + dot_nn(x_ref[1], refs[2 * index + 1][0])
            out_ref[0, :, at : at + weight.block] = result.astype(dtype)
            at += weight.block

    return pl.pallas_call(
        kernel,
        name=name,
        grid=(parts,),
        in_specs=[full(value.shape)] + [weight.spec() for weight in weights for side in range(2)],
        out_specs=pl.BlockSpec((1, rows, total), lambda p: (p, 0, 0)),
        out_shape=jax.ShapeDtypeStruct((parts, rows, total), dtype),
        compiler_params=params(),
        cost_estimate=cost(4 * rows * half * parts * total),
    )(value, *[side for weight in weights for side in (weight.near, weight.far)])


def to_inputs(value, weights, kept):
    rows = value.shape[1]
    parts, half, _ = weights[0].near.shape
    sides = parts // 2

    def kernel(x_ref, *refs):
        out_ref = refs[-1]
        for side in range(sides):

            @pl.when(pl.program_id(0) % sides == side)
            def _():
                at = 0
                for index, weight in enumerate(weights):
                    result = dot_nn(x_ref[0], refs[2 * index][0]) + dot_nn(
                        x_ref[1], refs[2 * index + 1][0]
                    )
                    take = min(weight.block, kept - at)
                    start = side * kept + at
                    out_ref[0, :, start : start + take] = result[:, :take]
                    at += take

    return pl.pallas_call(
        kernel,
        name="to_inputs",
        grid=(parts,),
        in_specs=[full(value.shape)] + [weight.spec() for weight in weights for side in range(2)],
        out_specs=pl.BlockSpec((1, rows, sides * kept), lambda p: (p // sides, 0, 0)),
        out_shape=jax.ShapeDtypeStruct((2, rows, sides * kept), F32),
        compiler_params=params(),
        cost_estimate=cost(4 * rows * half * parts * kept),
    )(value, *[side for weight in weights for side in (weight.near, weight.far)])


def to_features(value, weights, extras, outs, finish, name="to_features"):
    parts, rows, total = value.shape
    half = weights[0].near.shape[1]
    count = 2 * len(weights)

    def kernel(*refs):
        y_ref, weight_refs = refs[0], refs[1 : 1 + count]
        extra_refs = refs[1 + count : 1 + count + len(extras)]
        out_refs = refs[1 + count + len(extras) : -1]
        sums = refs[-1]

        @pl.when(pl.program_id(0) == 0)
        def _():
            sums[...] = jnp.zeros_like(sums)

        at = 0
        for index, weight in enumerate(weights):
            left = y_ref[0, :, at : at + weight.block]
            for side in range(2):
                sums[side] += dot_nt(left, weight_refs[2 * index + side][0])
            at += weight.block

        @pl.when(pl.program_id(0) == parts - 1)
        def _():
            finish([sums[0], sums[1]], extra_refs, out_refs)

    return pl.pallas_call(
        kernel,
        name=name,
        grid=(parts,),
        in_specs=[pl.BlockSpec((1, rows, total), lambda p: (p, 0, 0))]
        + [weight.spec() for weight in weights for side in range(2)]
        + [full(extra.shape) for extra in extras],
        out_specs=[full(out.shape) for out in outs],
        out_shape=outs,
        scratch_shapes=[pltpu.VMEM((2, rows, half), F32)],
        compiler_params=params(),
        cost_estimate=cost(4 * rows * half * parts * total),
    )(value, *[side for weight in weights for side in (weight.near, weight.far)], *extras)


def terms_of(pairs, name="terms_of"):
    half = pairs[0][0].shape[2]
    parts = pairs[0][1].shape[0]
    total = sum(pair[2] for pair in pairs)
    rows = [pair[0].shape[1] for pair in pairs]

    def kernel(*refs):
        count = len(pairs)
        lefts, rights = refs[:count], refs[count : 2 * count]
        near_ref, far_ref = refs[2 * count : 2 * count + 2]
        turned = refs[2 * count + 2 :]

        @pl.when(pl.program_id(0) == 0)
        def _():
            for left, flat in zip(lefts, turned):
                for side in range(2):
                    flat[side] = jnp.transpose(left[side])

        at = 0
        for pair, right, flat in zip(pairs, rights, turned):
            lanes = pair[2]
            near_ref[0, :, at : at + lanes] = dot_nn(flat[0], right[0]).astype(BF)
            far_ref[0, :, at : at + lanes] = dot_nn(flat[1], right[0]).astype(BF)
            at += lanes

    def right_spec(pair):
        return pl.BlockSpec((1, pair[1].shape[1], pair[2]), lambda p: (p, 0, pair[3]))

    out = jax.ShapeDtypeStruct((parts, half, total), BF)
    return pl.pallas_call(
        kernel,
        name=name,
        grid=(parts,),
        in_specs=[full(pair[0].shape) for pair in pairs] + [right_spec(pair) for pair in pairs],
        out_specs=[pl.BlockSpec((1, half, total), lambda p: (p, 0, 0))] * 2,
        out_shape=[out, out],
        scratch_shapes=[pltpu.VMEM((2, half, count), BF) for count in rows],
        compiler_params=params(),
        cost_estimate=cost(sum(4 * half * parts * pair[2] * count for pair, count in zip(pairs, rows))),
    )(*[pair[0] for pair in pairs], *[pair[1] for pair in pairs])


def norm_unit(halves):
    width = 2 * halves[0].shape[-1]
    mean = sum(jnp.sum(half, -1, keepdims=True) for half in halves) / width
    centre = [half - mean for half in halves]
    spread = sum(jnp.sum(half * half, -1, keepdims=True) for half in centre) / width
    scale = lax.rsqrt(spread + EPS)
    return [half * scale for half in centre], scale


def norm_back(halves, gain_ref, incoming):
    width = 2 * halves[0].shape[-1]
    unit, scale = norm_unit(halves)
    leading = [incoming[side] * gain_ref[side] for side in range(2)]
    mean = sum(jnp.sum(half, -1, keepdims=True) for half in leading) / width
    inner = sum(jnp.sum(leading[side] * unit[side], -1, keepdims=True) for side in range(2)) / width
    back = [scale * (leading[side] - mean - unit[side] * inner) for side in range(2)]
    gains = [jnp.sum(incoming[side] * unit[side], 0, keepdims=True) for side in range(2)]
    return back, gains


def join_rows(pieces, rows, name="join_rows"):
    parts, _, lanes = pieces[0][0].shape
    count = len(pieces)
    if rows % 16:
        return jnp.concatenate([array[:, block * rows : (block + 1) * rows] for array, block in pieces], 1)

    def kernel(*refs):
        for index in range(count):
            refs[-1][0, index * rows : (index + 1) * rows] = refs[index][0]

    def spec(block):
        return pl.BlockSpec((1, rows, lanes), lambda p: (p, block, 0))

    return pl.pallas_call(
        kernel,
        name=name,
        grid=(parts,),
        in_specs=[spec(block) for _, block in pieces],
        out_specs=pl.BlockSpec((1, count * rows, lanes), lambda p: (p, 0, 0)),
        out_shape=jax.ShapeDtypeStruct((parts, count * rows, lanes), BF),
        compiler_params=params(),
        cost_estimate=cost(parts * count * rows * lanes),
    )(*[array for array, _ in pieces])


def sum_rows(jobs, rows, name="sum_rows"):
    parts = jobs[0][0][0].shape[0]
    if rows % 16:
        results = []
        for terms in jobs:
            value = 0.0
            for array, blocks in terms:
                split = array.reshape(parts, -1, rows, array.shape[2])
                value = value + jnp.stack([split[:, block] for block in blocks], 1).astype(F32)
            results.append(value.astype(BF).reshape(parts, -1, value.shape[3]))
        return results
    spots = [
        (array, blocks[index])
        for terms in jobs
        for index in range(len(terms[0][1]))
        for array, blocks in terms
    ]

    def kernel(*refs):
        at = 0
        for spot, terms in enumerate(jobs):
            out_ref = refs[len(spots) + spot]
            for index in range(len(terms[0][1])):
                value = refs[at][0].astype(F32)
                for offset in range(1, len(terms)):
                    value = value + refs[at + offset][0].astype(F32)
                out_ref[0, index * rows : (index + 1) * rows] = value.astype(BF)
                at += len(terms)

    def spec(block, lanes):
        return pl.BlockSpec((1, rows, lanes), lambda p: (p, block, 0))

    shapes = [(len(terms[0][1]) * rows, terms[0][0].shape[2]) for terms in jobs]
    return pl.pallas_call(
        kernel,
        name=name,
        grid=(parts,),
        in_specs=[spec(block, array.shape[2]) for array, block in spots],
        out_specs=[pl.BlockSpec((1, *shape), lambda p: (p, 0, 0)) for shape in shapes],
        out_shape=[jax.ShapeDtypeStruct((parts, *shape), BF) for shape in shapes],
        compiler_params=params(),
        cost_estimate=cost(sum(parts * size * lanes for size, lanes in shapes)),
    )(*[array for array, _ in spots])


def side_by_side(left, right, kept, lanes):
    rows, width = left.shape
    count = width // kept

    def kernel(left_ref, right_ref, out_ref):
        for index, ref in enumerate((left_ref, right_ref)):
            for side in range(count):
                spot = count * index + side
                out_ref[spot, :, :kept] = ref[:, side * kept : (side + 1) * kept]
                if lanes > kept:
                    out_ref[spot, :, kept:] = jnp.zeros((rows, lanes - kept), BF)

    return pl.pallas_call(
        kernel,
        name="side_by_side",
        out_shape=jax.ShapeDtypeStruct((2 * count, rows, lanes), BF),
        compiler_params=params(),
        cost_estimate=cost(4 * rows * lanes),
    )(left, right)


def mlp_forward(rows_in, grads, start, weight1, weight2, part, live=None):
    _, rows, half = rows_in.shape
    parts, _, lanes = weight1.near.shape
    ff = lanes // 2
    step = 384 if ff % 384 == 0 else ff
    steps = ff // step
    extras = [] if live is None else [live]

    def kernel(x_ref, g_ref, s_ref, n1_ref, f1_ref, n2_ref, f2_ref, *refs):
        hid_ref, act_ref, out_ref, dn2_ref, df2_ref, turned, sums = refs[len(extras) :]
        first = (pl.program_id(0) == 0) & (pl.program_id(1) == 0)
        last = (pl.program_id(0) == parts - 1) & (pl.program_id(1) == steps - 1)

        @pl.when(first)
        def _():
            for side in range(2):
                turned[side] = jnp.transpose(g_ref[side])
            sums[...] = s_ref[...]

        hidden = dot_nn(x_ref[0], n1_ref[0]) + dot_nn(x_ref[1], f1_ref[0])
        hid_ref[0] = hidden
        activ = jax.nn.gelu(hidden, approximate=True).astype(BF)
        act_ref[0] = activ
        sums[0] += dot_nt(activ, n2_ref[0])
        sums[1] += dot_nt(activ, f2_ref[0])
        dn2_ref[0] = dot_nn(turned[0], activ).astype(BF)
        df2_ref[0] = dot_nn(turned[1], activ).astype(BF)

        @pl.when(last)
        def _():
            if live is None:
                out_ref[...] = sums[...]
            else:
                out_ref[...] = (sums[...] * refs[0][...]).astype(BF)

    weight = pl.BlockSpec((1, half, step), lambda p, n: (p, 0, part * steps + n))
    grad = pl.BlockSpec((1, half, step), lambda p, n: (p, 0, n))
    unit = pl.BlockSpec((1, rows, step), lambda p, n: (p, 0, n))
    whole = full((2, rows, half))
    grad_shape = jax.ShapeDtypeStruct((parts, half, ff), BF)
    return pl.pallas_call(
        kernel,
        name="mlp_forward",
        grid=(parts, steps),
        in_specs=[whole, whole, whole, weight, weight, weight, weight] + [full(extra.shape) for extra in extras],
        out_specs=[unit, unit, whole, grad, grad],
        out_shape=[
            jax.ShapeDtypeStruct((parts, rows, ff), F32),
            jax.ShapeDtypeStruct((parts, rows, ff), BF),
            jax.ShapeDtypeStruct((2, rows, half), F32 if live is None else BF),
            grad_shape,
            grad_shape,
        ],
        scratch_shapes=[pltpu.VMEM((2, half, rows), BF), pltpu.VMEM((2, rows, half), F32)],
        compiler_params=params(),
        cost_estimate=cost(12 * rows * half * parts * ff),
    )(rows_in, grads, start, weight1.near, weight1.far, weight2.near, weight2.far, *extras)


def gelu_slope(value):
    root = math.sqrt(2.0 / math.pi)
    square = value * value
    curve = jnp.tanh(root * value * (1.0 + 0.044715 * square))
    return 0.5 * (1.0 + curve) + 0.5 * value * (1.0 - curve * curve) * root * (
        1.0 + 3.0 * 0.044715 * square
    )


def mlp_backward(grads, rows_in, hidden, weight1, weight2, part, start, finish=None):
    _, rows, half = rows_in.shape
    parts, _, lanes = weight1.near.shape
    ff = lanes // 2
    step = 384 if ff % 384 == 0 else ff
    steps = ff // step
    extras = list(finish or []) + ([] if start is None else [start])

    def kernel(g_ref, x_ref, hid_ref, n1_ref, f1_ref, n2_ref, f2_ref, *refs):
        extra_refs, refs = refs[: len(extras)], refs[len(extras) :]
        dn1_ref, df1_ref = refs[:2]
        out_refs = refs[2:-2]
        turned, sums = refs[-2:]
        first = (pl.program_id(0) == 0) & (pl.program_id(1) == 0)
        last = (pl.program_id(0) == parts - 1) & (pl.program_id(1) == steps - 1)

        @pl.when(first)
        def _():
            for side in range(2):
                turned[side] = jnp.transpose(x_ref[side])
            sums[...] = jnp.zeros_like(sums) if start is None else extra_refs[-1][...]

        d_activ = dot_nn(g_ref[0], n2_ref[0]) + dot_nn(g_ref[1], f2_ref[0])
        d_hidden = (d_activ * gelu_slope(hid_ref[0])).astype(BF)
        dn1_ref[0] = dot_nn(turned[0], d_hidden).astype(BF)
        df1_ref[0] = dot_nn(turned[1], d_hidden).astype(BF)
        sums[0] += dot_nt(d_hidden, n1_ref[0])
        sums[1] += dot_nt(d_hidden, f1_ref[0])

        @pl.when(last)
        def _():
            if finish is None:
                out_refs[0][...] = sums[...]
            else:
                value_ref, gain_ref, add_ref = extra_refs[:3]
                add_norm_back([sums[0], sums[1]], value_ref, gain_ref, add_ref, *out_refs)

    weight = pl.BlockSpec((1, half, step), lambda p, n: (p, 0, part * steps + n))
    grad = pl.BlockSpec((1, half, step), lambda p, n: (p, 0, n))
    unit = pl.BlockSpec((1, rows, step), lambda p, n: (p, 0, n))
    whole = full((2, rows, half))
    grad_shape = jax.ShapeDtypeStruct((parts, half, ff), BF)
    wide = jax.ShapeDtypeStruct((2, rows, half), F32)
    outs = [wide] if finish is None else [wide, *back_shapes(rows, half)]
    return pl.pallas_call(
        kernel,
        name="mlp_backward",
        grid=(parts, steps),
        in_specs=[whole, whole, unit, weight, weight, weight, weight] + [full(extra.shape) for extra in extras],
        out_specs=[grad, grad] + [full(out.shape) for out in outs],
        out_shape=[grad_shape, grad_shape] + outs,
        scratch_shapes=[pltpu.VMEM((2, half, rows), BF), pltpu.VMEM((2, rows, half), F32)],
        compiler_params=params(),
        cost_estimate=cost(12 * rows * half * parts * ff),
    )(grads, rows_in, hidden, weight1.near, weight1.far, weight2.near, weight2.far, *extras)


def back_shapes(rows, half):
    return [jax.ShapeDtypeStruct((2, rows, half), BF), jax.ShapeDtypeStruct((2, 1, half), F32)]


def add_norm_back(incoming, value_ref, gain_ref, add_ref, out_ref, low_ref, d_gain_ref):
    back, gains = norm_back([value_ref[0], value_ref[1]], gain_ref, incoming)
    for side in range(2):
        total = add_ref[side] + back[side]
        out_ref[side] = total
        low_ref[side] = total.astype(BF)
        d_gain_ref[side] = gains[side]


def text_bias(lengths_ref, micro, words, strip, text_slots, axis):
    spot = lax.broadcasted_iota(jnp.int32, (1, words) if axis else (words, 1), axis)
    inner = spot % strip
    place = spot // strip * text_slots + inner
    live = (place < lengths_ref[micro, 0]) | (
        (place >= CLIP_LEN) & (place < CLIP_LEN + lengths_ref[micro, 1])
    )
    return jnp.where(live & (inner < text_slots), 0.0, MASKED)


def cross_forward(query, text_kv, lengths, text_slots):
    parts, micros, slots, lanes = query.shape
    zones, strip = text_kv.shape[1], text_kv.shape[3]
    words = zones * strip
    local = lanes // HP
    factor = HD ** (-0.5) * LOG2E

    def kernel(len_ref, q_ref, kv_ref, out_ref):
        bias = text_bias(len_ref, pl.program_id(1), words, strip, text_slots, 1)
        for h in range(local):
            cut = slice(h * HP, (h + 1) * HP)
            keys = kv_ref[0, :, 0, :, cut].reshape(words, HP)
            scores = dot_nt(q_ref[0, 0, :, cut], keys) + bias
            top = jnp.max(scores, -1, keepdims=True)
            raised = jnp.exp2((scores - top) * factor)
            total = jnp.sum(raised, -1, keepdims=True)
            values = kv_ref[0, :, 0, :, lanes + h * HP : lanes + (h + 1) * HP].reshape(words, HP)
            out_ref[0, 0, :, cut] = (dot_nn(raised.astype(BF), values) / total).astype(BF)

    spot = lambda p, m, c: (p, m, 0, 0)
    far = lambda p, m, c: (p, 0, m, 0, 0)
    return pl.pallas_call(
        kernel,
        name="cross_forward",
        grid_spec=pltpu.PrefetchScalarGridSpec(
            num_scalar_prefetch=1,
            grid=(parts, micros),
            in_specs=[
                pl.BlockSpec((1, 1, slots, lanes), spot),
                pl.BlockSpec((1, zones, 1, strip, 2 * lanes), far),
            ],
            out_specs=pl.BlockSpec((1, 1, slots, lanes), spot),
        ),
        out_shape=jax.ShapeDtypeStruct(query.shape, BF),
        compiler_params=params(),
        cost_estimate=cost(4 * parts * micros * slots * words * lanes),
    )(lengths, query, text_kv)


def cross_backward(query, text_kv, lengths, incoming, text_slots):
    parts, micros, slots, lanes = query.shape
    zones, strip = text_kv.shape[1], text_kv.shape[3]
    words = zones * strip
    local = lanes // HP
    scale = HD ** (-0.5)
    factor = scale * LOG2E

    def kernel(len_ref, q_ref, kv_ref, in_ref, dq_ref, dkv_ref):
        bias = text_bias(len_ref, pl.program_id(1), words, strip, text_slots, 0)
        for h in range(local):
            cut = slice(h * HP, (h + 1) * HP)
            far = slice(lanes + h * HP, lanes + (h + 1) * HP)
            rows = q_ref[0, 0, :, cut]
            keys = kv_ref[0, :, 0, :, cut].reshape(words, HP)
            values = kv_ref[0, :, 0, :, far].reshape(words, HP)
            grads = in_ref[0, 0, :, cut]
            scores = dot_nt(keys, rows) + bias
            top = jnp.max(scores, 0, keepdims=True)
            raised = jnp.exp2((scores - top) * factor)
            probs = raised * (1.0 / jnp.sum(raised, 0, keepdims=True))
            d_probs = dot_nt(values, grads)
            inner = jnp.sum(probs * d_probs, 0, keepdims=True)
            d_scores = (probs * (d_probs - inner)).astype(BF)
            shape = (zones, strip, HP)
            dkv_ref[0, :, 0, :, far] = dot_nn(probs.astype(BF), grads).astype(BF).reshape(shape)
            dkv_ref[0, :, 0, :, cut] = (dot_nn(d_scores, rows) * scale).astype(BF).reshape(shape)
            dq_ref[0, 0, :, cut] = (dot_tn(d_scores, keys) * scale).astype(BF)

    spot = lambda p, m, c: (p, m, 0, 0)
    far = lambda p, m, c: (p, 0, m, 0, 0)
    return pl.pallas_call(
        kernel,
        name="cross_backward",
        grid_spec=pltpu.PrefetchScalarGridSpec(
            num_scalar_prefetch=1,
            grid=(parts, micros),
            in_specs=[
                pl.BlockSpec((1, 1, slots, lanes), spot),
                pl.BlockSpec((1, zones, 1, strip, 2 * lanes), far),
                pl.BlockSpec((1, 1, slots, lanes), spot),
            ],
            out_specs=[
                pl.BlockSpec((1, 1, slots, lanes), spot),
                pl.BlockSpec((1, zones, 1, strip, 2 * lanes), far),
            ],
        ),
        out_shape=[
            jax.ShapeDtypeStruct(query.shape, BF),
            jax.ShapeDtypeStruct(text_kv.shape, BF),
        ],
        compiler_params=params(),
        cost_estimate=cost(10 * parts * micros * slots * words * lanes),
    )(lengths, query, text_kv, incoming)


def tie(*values):
    return lax.optimization_barrier(values)


class Cube:
    def __init__(self):
        self.size = lax.axis_size("dp")
        self.bits = self.size.bit_length() - 1
        self.outer = list(range(1, self.bits))
        self.rank = lax.axis_index("dp")
        self.masks = []
        for place in range(self.size):
            mask = place >> (self.bits - 1)
            for bit in self.outer:
                mask |= ((place >> (bit - 1)) & 1) << bit
            self.masks.append(mask)
        self.owners = self.rank ^ jnp.array(self.masks, jnp.int32)

    def swap(self, value, bit, axis="dp"):
        pairs = [(i, i ^ (1 << bit)) for i in range(lax.axis_size(axis))]
        return lax.ppermute(value, axis, pairs)

    def trade(self, value):
        blocks = {mask: value[mask] for mask in range(self.size)}
        for bit in range(self.bits):
            send = sorted(mask for mask in blocks if mask >> bit & 1)
            got = self.swap(jnp.stack([blocks[mask] for mask in send]), bit)
            for place, mask in enumerate(send):
                blocks[mask] = got[place]
        return jnp.stack([blocks[mask] for mask in range(self.size)])

    def spread(self, value):
        held = value[None]
        for bit in range(self.bits):
            held = jnp.concatenate([held, self.swap(held, bit)])
        return held

    def add(self, value, axis):
        for bit in range(lax.axis_size(axis).bit_length() - 1):
            value = value + self.swap(value, bit, axis)
        return value


class Gather:
    def __init__(self, cube, shard, flip, joined=False):
        self.cube = cube
        self.rows = shard.shape[1]
        self.masks = [[0]]
        self.pieces = [shard]
        self.todo = cube.outer[::-1] if flip else list(cube.outer)
        self.joined = joined

    def blocks(self, order):
        spots = {
            mask: (piece, index)
            for piece, masks in zip(self.pieces, self.masks)
            for index, mask in enumerate(masks)
        }
        return join_rows([spots[mask] for mask in order], self.rows)

    def move(self):
        bit = self.todo.pop(0)
        if self.joined and len(self.pieces) > 1:
            order = [mask for masks in self.masks for mask in masks]
            self.pieces, self.masks = [self.blocks(order)], [order]
        self.masks = self.masks + [[mask | (1 << bit) for mask in masks] for masks in self.masks]
        self.pieces = self.pieces + [self.cube.swap(piece, bit) for piece in self.pieces]

    def join(self):
        while self.todo:
            self.move()
        self.pieces = [self.blocks(self.cube.masks[: self.cube.size // 2])]

    def weight(self):
        near = self.pieces[0]
        return Lanes(near, self.cube.swap(near, 0))


class Scatter:
    def __init__(self, cube, near, far, flip):
        self.cube = cube
        self.todo = list(cube.outer) if flip else cube.outer[::-1]
        self.rows = near.shape[1] // (cube.size // 2)
        self.places = list(range(cube.size // 2))
        self.near = near
        self.got = []
        self.pieces = [cube.swap(far, 0)]
        self.arriving = self.places

    def job(self, places):
        return [(self.near, places)] + [
            (value, [held.index(place) for place in places]) for value, held in self.got
        ]

    def absorb(self):
        self.got.append((self.pieces[0], self.arriving))


def pack(movers):
    jobs = []
    for mover in movers:
        mover.absorb()
        mover.bit = mover.todo.pop(0)
        weight = 1 << (mover.bit - 1)
        sent = [place for place in mover.places if place & weight]
        mover.places = [place for place in mover.places if not place & weight]
        mover.arriving = [place ^ weight for place in sent]
        jobs.append(mover.job(sent))
    for mover, value in zip(movers, sum_rows(jobs, movers[0].rows)):
        mover.pieces = [value]


def send(movers):
    for mover in movers:
        mover.pieces = [mover.cube.swap(mover.pieces[0], mover.bit)]


def results(movers):
    while movers[0].todo:
        pack(movers)
        send(movers)
    for mover in movers:
        mover.absorb()
    return sum_rows([mover.job([0]) for mover in movers], movers[0].rows)


def pin(value, *others):
    flat = []
    for other in others:
        flat += other.pieces if hasattr(other, "pieces") else [other]
    return tie(value, *flat)[0]


def bind(value, *movers):
    flat = [piece for mover in movers for piece in mover.pieces]
    held = tie(value, *flat)
    spot = 1
    for mover in movers:
        count = len(mover.pieces)
        mover.pieces = list(held[spot : spot + count])
        spot += count
    return held[0]


def hold(movers, *others):
    for mover in movers:
        mover.pieces = [pin(piece, *others) for piece in mover.pieces]


def on_device(
    tokens,
    skip_tokens,
    text,
    timestep,
    grid,
    text_len,
    w_skip,
    w_mod,
    w_qkv,
    w_out1,
    w_query2,
    w_text_kv,
    w_out2,
    w_fc1,
    w_fc2,
    gain_skip,
    gain_attn,
    gain_cross,
    gain_mlp,
    gain_query,
    gain_key,
    cotangent,
):
    micros, slots, width = tokens.shape
    parts = lax.axis_size("sp")
    zone = lax.axis_index("sp")
    cube = Cube()
    ranks = cube.size
    rows = micros * slots
    sequence = slots * parts
    local = H // parts
    lanes = local * HP + -local * HP % 128
    text_slots = text.shape[1]
    text_strip = -(-text_slots // 16) * 16
    features = text.shape[2]
    strip = width // ranks
    middle = width // 2
    kept = w_skip.shape[0]
    skip_lanes = -(-kept // 256) * 256
    skip_cut = skip_lanes // 2
    qkv_cut = (3 * lanes) // 256 * 128 + 128
    text_rows = w_text_kv.shape[0]

    def spread(shard, before=None):
        if before is not None:
            shard, before = tie(shard, before)
        return lax.all_gather(shard, "sp", axis=0, tiled=False)

    def fetch(value, cut, joined=False):
        return [Gather(cube, value[:, :, :cut], 0, joined), Gather(cube, value[:, :, cut:], 1, joined)]

    def advance(movers):
        for mover in movers:
            mover.move()

    def join(movers):
        for mover in movers:
            mover.join()

    def exchange(value):
        return lax.all_to_all(value, "sp", split_axis=0, concat_axis=0, tiled=True)

    skip_z = spread(jnp.pad(w_skip.T, ((0, 0), (0, skip_lanes - kept))))
    steps = cube.spread(timestep[:, 0])
    joined = side_by_side(tokens.reshape(rows, width), skip_tokens.reshape(rows, width), kept, skip_lanes)
    wide = grid[:, 0, 1]
    counts = grid[:, 0, 0] * wide
    cosine, sine = rope_tables(sequence, wide, lanes)
    skip_z, steps, joined, cosine, sine = tie(skip_z, steps, joined, cosine, sine)
    skip_m = fetch(skip_z, skip_cut)
    qkv_z = spread(pad_heads(w_qkv.reshape(strip, -1), local), skip_z)
    advance(skip_m)

    time_act = jax.nn.silu(time_embed(steps, width)).astype(BF).reshape(ranks * micros, parts, -1)
    time_part = lax.dynamic_index_in_dim(time_act, zone, 1, keepdims=False)
    shift = cube.add(jnp.dot(time_part, w_mod, preferred_element_type=F32), "sp")
    skip_m[0].pieces[1], shift = tie(skip_m[0].pieces[1], shift)
    while skip_m[0].todo:
        advance(skip_m)
    shift = cube.trade(shift.reshape(ranks, micros, strip))
    skip_m[0].pieces[-1], shift = tie(skip_m[0].pieces[-1], shift)
    shift = jnp.stack([shift[mask] for mask in cube.masks]).reshape(2, ranks // 2, micros, strip)
    shift = jnp.transpose(shift, (0, 2, 1, 3)).reshape(2, micros, middle)
    qkv_m = fetch(qkv_z, qkv_cut)
    hold(qkv_m, *skip_m)
    advance(qkv_m)
    fc1_z = spread(pin(w_fc1, *skip_m))
    fc2_z = spread(pin(w_fc2.T, *qkv_m))
    join(skip_m)
    skip_w = [mover.weight() for mover in skip_m]

    def shuffle(count):
        block = count // ranks
        place = jnp.arange(count, dtype=jnp.int32)
        source = cube.owners[place // block] * block + place % block
        return (place[:, None] == source[None, :]).astype(BF)

    turn = shuffle(width)
    text_turn = shuffle(features)
    gains = jnp.stack([gain_skip, gain_attn, gain_cross, gain_mlp])
    gains = gains.reshape(4, ranks, strip)[:, cube.owners].reshape(4, 2, 1, middle)
    g_skip, g_attn, g_cross, g_mlp = gains

    lengths = text_len[:, 0, :]
    place = zone * slots + jnp.arange(slots, dtype=jnp.int32)
    live = (place[None, :] < counts[:, None]).astype(F32).reshape(rows, 1)
    gain_q = pad_heads(jnp.tile(gain_query, local)[None, :], local)
    gain_k = pad_heads(jnp.tile(gain_key, local)[None, :], local)

    grad3 = jnp.stack(
        [
            jnp.dot(cotangent.reshape(rows, width), side, preferred_element_type=F32) * live
            for side in (turn[:, :middle], turn[:, middle:])
        ]
    )
    d_mlp = grad3.astype(BF)

    wide_shape = jax.ShapeDtypeStruct((2, rows, middle), F32)
    low_shape = jax.ShapeDtypeStruct((2, rows, middle), BF)
    gain_shape = jax.ShapeDtypeStruct((2, 1, middle), F32)

    def first_norms(sums, extra, out):
        g0_ref, g1_ref, shift_ref = extra
        base_ref, stream_ref, pre_ref = out
        unit, _ = norm_unit(sums)
        stream = [unit[side] * g0_ref[side] for side in range(2)]
        unit, _ = norm_unit(stream)
        for side in range(2):
            base_ref[side] = sums[side]
            stream_ref[side] = stream[side]
            for micro in range(micros):
                cut = slice(micro * slots, (micro + 1) * slots)
                pre = unit[side][cut] * g1_ref[side] + shift_ref[side, micro : micro + 1]
                pre_ref[side, cut] = pre.astype(BF)

    def next_norm(sums, extra, out):
        before_ref, gain_ref = extra
        after_ref, pre_ref = out
        stream = [before_ref[side] + sums[side] for side in range(2)]
        unit, _ = norm_unit(stream)
        for side in range(2):
            after_ref[side] = stream[side]
            pre_ref[side] = (unit[side] * gain_ref[side]).astype(BF)

    base, stream, pre_attn = to_features(
        joined, skip_w, [g_skip, g_attn, shift], [wide_shape, wide_shape, low_shape], first_norms
    )
    while qkv_m[0].todo:
        advance(qkv_m)
    after_qkv = [mover.pieces[-1] for mover in qkv_m]
    hold(qkv_m, pre_attn)
    join(qkv_m)
    pre_attn, fc1_z = tie(pre_attn, fc1_z)
    qkv_w = [mover.weight() for mover in qkv_m]
    projected = to_lanes(pre_attn, qkv_w)
    projected, fc2_z = tie(projected, fc2_z)
    fc_m = [Gather(cube, fc1_z, 0, True), Gather(cube, fc2_z, 1, True)]
    hold(fc_m, *after_qkv)
    advance(fc_m)
    raw = exchange(projected.reshape(parts, micros, slots, 3 * lanes))
    cross_z = jnp.concatenate([pad_heads(side, local) for side in (w_out1.T, w_query2, w_out2.T)], 1)
    arrived = fc_m[0].pieces + fc_m[1].pieces
    cross_z = spread(pin(cross_z, *arrived))
    text_own = jnp.dot(text.reshape(-1, features), text_turn, preferred_element_type=F32).astype(BF)
    text_own = jnp.pad(
        text_own.reshape(micros, text_slots, features), ((0, 0), (0, text_strip - text_slots), (0, 0))
    ).reshape(micros * text_strip, features)
    text_z = jnp.pad(pad_heads(w_text_kv.reshape(text_rows, -1), local), ((0, max(0, strip - text_rows)), (0, 0)))
    while fc_m[0].todo:
        advance(fc_m)
    text_z = spread(pin(text_z, *arrived))
    text_all = spread(pin(text_own, *arrived))
    cross_m = fetch(cross_z, 2 * lanes, True)
    advance(cross_m)
    raw, d_mlp, turn, text_turn = tie(raw, d_mlp, turn, text_turn)
    attended, turned_q, turned_k, norms = self_forward(raw, counts, cosine, sine, gain_q, gain_k)
    attended = bind(attended, *fc_m, *cross_m)
    attended, text_all, text_z = tie(attended, text_all, text_z)
    text_m = Gather(cube, text_z[:, :text_rows], 1, True)
    text_m.move()
    attended = exchange(attended).reshape(parts, rows, lanes)
    while cross_m[0].todo:
        advance(cross_m)
    join(fc_m)
    attended = bind(attended, text_m, *fc_m, cross_m[0])
    while text_m.todo:
        text_m.move()
    join(cross_m[:1])
    first_w = cross_m[0].weight()
    out1_w, query2_w = (Lanes(first_w.near, first_w.far, lanes, index) for index in range(2))
    attended, first_w.far = tie(attended, first_w.far)
    out1_w.far = query2_w.far = first_w.far
    text_all = text_all.reshape(-1, features)
    text_all = jnp.stack([text_all[:, : features // 2], text_all[:, features // 2 :]])
    stream1, pre_cross = to_features(
        attended, [out1_w], [stream, g_cross], [wide_shape, low_shape], next_norm
    )
    hold(fc_m, out1_w.far)
    fc1_w, fc2_w = [mover.weight() for mover in fc_m]
    text_m.join()
    text_w = text_m.weight()
    query2 = to_lanes(pre_cross, [query2_w]).reshape(parts, micros, slots, lanes)
    query2 = bind(query2, *cross_m[1:])
    join(cross_m[1:])
    out2_w = cross_m[1].weight()
    text_kv = to_lanes(text_all, [text_w]).reshape(parts, parts, micros, text_strip, 2 * lanes)
    crossed = cross_forward(query2, text_kv, lengths, text_slots).reshape(parts, rows, lanes)
    stream2, pre_mlp = to_features(
        crossed, [out2_w], [stream1, g_mlp], [wide_shape, low_shape], next_norm
    )
    hidden0, activ0, partial, fc2_n0, fc2_f0 = mlp_forward(pre_mlp, d_mlp, stream2, fc1_w, fc2_w, 0)
    hidden1, activ1, result, fc2_n1, fc2_f1 = mlp_forward(pre_mlp, d_mlp, partial, fc1_w, fc2_w, 1, live)
    fc2_s = [Scatter(cube, fc2_n0, fc2_f0, 0), Scatter(cube, fc2_n1, fc2_f1, 1)]

    def settle(values, before=None):
        value = values[0] if len(values) == 1 else jnp.concatenate(values, 2)
        if before is not None:
            value, before = tie(value, before)
        return lax.psum_scatter(value, "sp", scatter_dimension=0, tiled=False)

    fc1_n0, fc1_f0, partial = mlp_backward(d_mlp, pre_mlp, hidden0, fc1_w, fc2_w, 0, None)
    fc1_s = [Scatter(cube, fc1_n0, fc1_f0, 0)]
    pack(fc2_s)
    partial = bind(partial, *fc2_s)
    send(fc2_s)
    fc1_n1, fc1_f1, grad2, d_cross, d_gain_mlp = mlp_backward(
        d_mlp, pre_mlp, hidden1, fc1_w, fc2_w, 1, partial, [stream2, g_mlp, grad3]
    )
    fc1_s.append(Scatter(cube, fc1_n1, fc1_f1, 1))
    d_cross = bind(d_cross, *fc2_s)
    d_crossed = to_lanes(d_cross, [out2_w])
    pack(fc2_s)
    d_crossed = bind(d_crossed, *fc2_s)
    send(fc2_s)
    d_query2, d_text_kv = cross_backward(
        query2, text_kv, lengths, d_crossed.reshape(parts, micros, slots, lanes), text_slots
    )
    d_query2 = bind(d_query2, *fc2_s)
    d_query2 = d_query2.reshape(parts, rows, lanes)
    d_text_kv = d_text_kv.reshape(parts, -1, 2 * lanes)
    total_fc2 = results(fc2_s)
    term_fc2 = settle(total_fc2)

    def go_back(sums, extra, out):
        add_norm_back(sums, *extra, *out)

    grad1, d_attn, d_gain_cross = to_features(
        d_query2, [query2_w], [stream1, g_cross, grad2], [wide_shape, low_shape, gain_shape], go_back
    )
    d_attn = bind(d_attn, *fc1_s)
    pack(fc1_s)
    d_attn = bind(d_attn, *fc1_s)
    send(fc1_s)
    d_attended = to_lanes(d_attn, [out1_w])
    d_attended, d_text_kv, pre_cross = tie(d_attended, d_text_kv, pre_cross)
    d_heads = exchange(d_attended.reshape(parts, micros, slots, lanes))

    def words_back(sums, extra, out):
        size = micros * text_strip
        for zone in range(parts):
            for side in range(2):
                out[0][zone, side] = sums[side][zone * size : (zone + 1) * size].astype(BF)

    words_shape = jax.ShapeDtypeStruct((parts, 2, micros * text_strip, features // 2), BF)
    d_words = to_features(d_text_kv, [text_w], [], [words_shape], words_back)[0]
    text_t = list(terms_of([(text_all, d_text_kv, 2 * lanes, 0)]))
    cross_t = terms_of(
        [(d_attn, attended, lanes, 0), (pre_cross, d_query2, lanes, 0), (d_cross, crossed, lanes, 0)]
    )
    cross_t = list(cross_t)
    d_heads, d_words, text_t[1], cross_t[1] = tie(d_heads, d_words, text_t[1], cross_t[1])
    d_words = settle([d_words])
    text_s, cross_s = Scatter(cube, *text_t, 1), Scatter(cube, *cross_t, 0)
    d_heads = bind(d_heads, *fc1_s)
    pack(fc1_s)
    d_heads = bind(d_heads, *fc1_s)
    send(fc1_s)
    d_raw, d_gain_q, d_gain_k = self_backward(
        raw, counts, cosine, sine, gain_q, gain_k, turned_q, turned_k, norms, d_heads
    )
    d_raw, term_fc2, d_words = tie(d_raw, term_fc2, d_words)
    d_raw = bind(d_raw, *fc1_s)
    d_projected = exchange(d_raw).reshape(parts, rows, 3 * lanes)
    other_s = [cross_s, text_s]
    total_fc1 = results(fc1_s)
    pack([cross_s])
    pack([text_s])
    send(other_s)
    d_projected = bind(d_projected, *other_s)
    term_fc1 = settle(total_fc1, d_projected)
    qkv_s = [
        Scatter(cube, *terms_of([(pre_attn, d_projected, 2 * lanes, 0)]), 0),
        Scatter(cube, *terms_of([(pre_attn, d_projected, lanes, 2)]), 1),
    ]
    pack([cross_s])
    pack([text_s])
    send(other_s)
    pack(qkv_s)
    d_projected = bind(d_projected, *qkv_s)
    send(qkv_s)

    def last_norms(sums, extra, out):
        stream_ref, g1_ref, base_ref, g0_ref, add_ref = extra
        low_ref, d_shift_ref, d_g1_ref, d_g0_ref = out
        back, gains1 = norm_back([stream_ref[0], stream_ref[1]], g1_ref, sums)
        total = [add_ref[side] + back[side] for side in range(2)]
        back, gains0 = norm_back([base_ref[0], base_ref[1]], g0_ref, total)
        for side in range(2):
            low_ref[side] = back[side].astype(BF)
            d_g1_ref[side] = gains1[side]
            d_g0_ref[side] = gains0[side]
            for micro in range(micros):
                part = sums[side][micro * slots : (micro + 1) * slots]
                d_shift_ref[side, micro : micro + 1] = jnp.sum(part, 0, keepdims=True)

    shift_shape = jax.ShapeDtypeStruct((2, micros, middle), F32)
    d_base, d_shift, d_gain_attn, d_gain_skip = to_features(
        d_projected,
        qkv_w,
        [stream, g_attn, base, g_skip, grad1],
        [low_shape, shift_shape, gain_shape, gain_shape],
        last_norms,
    )
    d_base = bind(d_base, *other_s)
    skip_t = [list(terms_of([(d_base, joined, skip_cut, flip)])) for flip in range(2)]
    skip_t[0][1] = bind(skip_t[0][1], *qkv_s)
    skip_s = [Scatter(cube, *pair, flip) for flip, pair in enumerate(skip_t)]
    pack(qkv_s)
    send(qkv_s)
    pack(skip_s)
    term_cross, term_text = settle(results([cross_s])), settle(results([text_s]))
    send(skip_s)
    term_qkv = settle(results(qkv_s))
    term_skip = settle(results(skip_s))
    d_joined = to_inputs(d_base, skip_w, kept)
    result = (
        jnp.dot(result[0], turn[:, :middle].T, preferred_element_type=F32)
        + jnp.dot(result[1], turn[:, middle:].T, preferred_element_type=F32)
    ).astype(BF)
    d_words = d_words.reshape(2, micros * text_strip, features // 2)
    d_words = jnp.dot(
        d_words[0], text_turn[:, : features // 2].T, preferred_element_type=F32
    ) + jnp.dot(d_words[1], text_turn[:, features // 2 :].T, preferred_element_type=F32)
    d_words = d_words.reshape(micros, text_strip, features)[:, :text_slots]

    d_shift = jnp.transpose(d_shift.reshape(2, micros, ranks // 2, strip), (0, 2, 1, 3))
    d_shift = d_shift.reshape(ranks, micros, strip)
    d_shift = jnp.stack([d_shift[cube.masks.index(mask)] for mask in range(ranks)])
    d_shift = cube.add(cube.trade(d_shift), "sp").reshape(ranks * micros, strip)
    term_mod = lax.dot_general(
        time_part.astype(F32), d_shift, (((0,), (0,)), ((), ())), precision=lax.Precision.HIGHEST
    )

    places = jnp.array([cube.masks.index(mask) for mask in range(ranks)], jnp.int32)
    places = places[jnp.arange(ranks, dtype=jnp.int32) ^ cube.rank]
    gains = jnp.stack([d_gain_skip, d_gain_attn, d_gain_cross, d_gain_mlp])
    gains = gains.reshape(4, ranks, strip)[:, places].reshape(-1)
    heads = jnp.stack([jnp.sum(d_gain_q, (0, 1)), jnp.sum(d_gain_k, (0, 1))])
    heads = jnp.sum(heads[:, : local * HP].reshape(2, local, HP)[:, :, :HD], 1)
    packed = jnp.concatenate([gains, heads.reshape(-1)])
    packed = cube.add(cube.add(packed, "sp"), "dp")
    gains = packed[: 4 * width].reshape(4, ranks * parts, -1)
    gains = lax.dynamic_index_in_dim(gains, cube.rank * parts + zone, 1, keepdims=False)
    heads = packed[4 * width :].reshape(2, HD)

    def whole(term, groups):
        return cut_heads(term.astype(F32), local).reshape(term.shape[0], groups, -1)

    return (
        result.reshape(tokens.shape),
        d_joined[0].reshape(tokens.shape),
        d_joined[1].reshape(tokens.shape),
        d_words.reshape(text.shape),
        term_skip.astype(F32)[:, :kept].T,
        term_mod,
        whole(term_qkv, 3),
        cut_heads(term_cross[:, :lanes].astype(F32), local).T,
        cut_heads(term_cross[:, lanes : 2 * lanes].astype(F32), local),
        whole(term_text, 2),
        cut_heads(term_cross[:, 2 * lanes :].astype(F32), local).T,
        term_fc1.astype(F32),
        term_fc2.astype(F32).T,
        gains[0],
        gains[1],
        gains[2],
        gains[3],
        heads[0],
        heads[1],
    )


def solution(mesh):
    rows = P(None, ("dp", "sp"), None)
    column = P("sp", "dp")
    row = P("dp", "sp")
    grouped = P("dp", None, "sp")
    in_specs = (
        (rows, rows, rows, P(None, "dp"), P(None, "dp", None), P(None, "dp", None))
        + (column, column, grouped, column, row, grouped, column, row, column)
        + (P(),) * 6
        + (rows,)
    )
    out_specs = (
        (rows, rows, rows, rows)
        + (column, column, grouped, column, row, grouped, column, row, column)
        + (P(("dp", "sp")),) * 4
        + (P(), P())
    )
    return jax.shard_map(
        on_device, mesh=mesh, in_specs=in_specs, out_specs=out_specs, check_vma=False
    )
```

```python
import math

import jax
import jax.numpy as jnp
from jax import lax
from jax.experimental import pallas as pl
from jax.experimental.pallas import tpu as pltpu
from jax.sharding import PartitionSpec as P

H = 16
HD = 88
HP = 96
CLIP_LEN = 77
ROWS = 256

EPS = 1e-06
MASKED = -1e30
LOG2E = 1.4426950408889634
BF = jnp.bfloat16
F32 = jnp.float32


def time_embed(step, width):
    half = width // 2
    rate = jnp.exp(-math.log(10000.0) * jnp.arange(half, dtype=F32) / half)
    angle = step.astype(F32)[..., None] * rate
    return jnp.concatenate([jnp.cos(angle), jnp.sin(angle)], -1)


def rope_tables(sequence, wide, lanes):
    place = jnp.arange(sequence, dtype=jnp.int32)[None, :, None]
    wide = wide[:, None, None]
    lane = jnp.arange(lanes, dtype=jnp.int32)[None, None, :] % HP
    pair = lane // 2
    quarter = HD // 4
    upper = pair < quarter
    rank = jnp.where(upper, pair, pair - quarter).astype(F32)
    rate = jnp.exp(-math.log(10000.0) * rank / quarter)
    angle = jnp.where(upper, place // wide, place % wide).astype(F32) * rate
    sine = jnp.sin(angle)
    return jnp.cos(angle), jnp.where(lane % 2 == 0, -sine, sine)


def pad_heads(packed, local):
    rows, lanes = packed.shape
    groups = packed.reshape(rows, lanes // (local * HD), local, HD)
    groups = jnp.pad(groups, ((0, 0), (0, 0), (0, 0), (0, HP - HD)))
    groups = groups.reshape(rows, -1, local * HP)
    return jnp.pad(groups, ((0, 0), (0, 0), (0, -local * HP % 128))).reshape(rows, -1)


def cut_heads(padded, local):
    rows = padded.shape[0]
    groups = padded.reshape(rows, -1, local * HP + -local * HP % 128)[:, :, : local * HP]
    return groups.reshape(rows, -1, local, HP)[..., :HD].reshape(rows, -1)


def head_masks(shape, local):
    lane = lax.broadcasted_iota(jnp.int32, shape, len(shape) - 1)
    inside = lane % HP < HD
    return [((lane // HP == h) & inside).astype(F32) for h in range(local)]


def head_mean(value, masks):
    total = None
    for mask in masks:
        term = (jnp.sum(value * mask, -1, keepdims=True) * (1.0 / HD)) * mask
        total = term if total is None else total + term
    return total


def head_unit(value, masks):
    centre = value - head_mean(value, masks)
    spread = None
    square = centre * centre
    for mask in masks:
        mean = jnp.sum(square * mask, -1, keepdims=True) * (1.0 / HD)
        term = lax.rsqrt(mean + EPS) * mask
        spread = term if spread is None else spread + term
    return centre * spread, spread


def turn_pairs(value):
    lanes = value.shape[-1]
    after = pltpu.roll(value, lanes - 1, 1)
    before = pltpu.roll(value, 1, 1)
    lane = lax.broadcasted_iota(jnp.int32, value.shape, 1)
    return jnp.where(lane % 2 == 0, after, before)


def dot_nt(left, right):
    return lax.dot_general(left, right, (((1,), (1,)), ((), ())), preferred_element_type=F32)


def dot_nn(left, right):
    return lax.dot_general(left, right, (((1,), (0,)), ((), ())), preferred_element_type=F32)


def dot_tn(left, right):
    return lax.dot_general(left, right, (((0,), (0,)), ((), ())), preferred_element_type=F32)


def self_forward(raw, counts, cosine, sine, gain_q, gain_k):
    parts, micros, slots, packed = raw.shape
    lanes = packed // 3
    local = lanes // HP
    sequence = parts * slots
    factor = HD ** (-0.5) * LOG2E

    def kernel(count_ref, raw_ref, cos_ref, sin_ref, gq_ref, gk_ref, out_ref, q_ref, k_ref, lse_ref):
        count = count_ref[pl.program_id(0)]
        blocks = (count + slots - 1) // slots
        out_ref[...] = jnp.zeros_like(out_ref)
        masks = head_masks((1, lanes), local)

        def prepare(part, carry):
            spot = pl.ds(pl.multiple_of(part * slots, slots), slots)
            cosine, sine = cos_ref[0, spot, :], sin_ref[0, spot, :]
            for index, gain_ref, dest in ((0, gq_ref, q_ref), (1, gk_ref, k_ref)):
                value = raw_ref[part, 0, :, index * lanes : (index + 1) * lanes].astype(F32)
                scaled = head_unit(value, masks)[0] * gain_ref[...]
                dest[0, spot, :] = (scaled * cosine + turn_pairs(scaled) * sine).astype(BF)
            return carry

        lax.fori_loop(0, parts, prepare, 0)
        column = lax.broadcasted_iota(jnp.int32, (1, sequence), 1)
        bias = jnp.where(column < count, 0.0, MASKED)
        for h in range(local):
            cut = slice(h * HP, (h + 1) * HP)
            keys = k_ref[0, :, cut]
            values = raw_ref[:, 0, :, 2 * lanes + h * HP : 2 * lanes + (h + 1) * HP].reshape(sequence, HP)

            def one_block(part, carry):
                spot = pl.ds(pl.multiple_of(part * slots, slots), slots)
                scores = dot_nt(q_ref[0, spot, cut], keys) + bias
                top = jnp.max(scores, -1, keepdims=True)
                raised = jnp.exp2((scores - top) * factor)
                total = jnp.sum(raised, -1, keepdims=True)
                result = dot_nn(raised.astype(BF), values) / total
                out_ref[part, 0, :, cut] = result.astype(BF)
                norm = jnp.broadcast_to(top * factor + jnp.log2(total), (slots, 128))
                lse_ref[0, h : h + 1, spot] = jnp.transpose(norm)[0:1, :]
                return carry

            lax.fori_loop(0, blocks, one_block, 0)

    whole = lambda m, c: (0, m, 0, 0)
    table = lambda m, c: (m, 0, 0)
    fixed = lambda m, c: (0, 0)
    return pl.pallas_call(
        kernel,
        name="self_forward",
        grid_spec=pltpu.PrefetchScalarGridSpec(
            num_scalar_prefetch=1,
            grid=(micros,),
            in_specs=[
                pl.BlockSpec((parts, 1, slots, packed), whole),
                pl.BlockSpec((1, sequence, lanes), table),
                pl.BlockSpec((1, sequence, lanes), table),
                pl.BlockSpec((1, lanes), fixed),
                pl.BlockSpec((1, lanes), fixed),
            ],
            out_specs=[
                pl.BlockSpec((parts, 1, slots, lanes), whole),
                pl.BlockSpec((1, sequence, lanes), table),
                pl.BlockSpec((1, sequence, lanes), table),
                pl.BlockSpec((1, local, sequence), table),
            ],
        ),
        out_shape=[
            jax.ShapeDtypeStruct((parts, micros, slots, lanes), BF),
            jax.ShapeDtypeStruct((micros, sequence, lanes), BF),
            jax.ShapeDtypeStruct((micros, sequence, lanes), BF),
            jax.ShapeDtypeStruct((micros, local, sequence), F32),
        ],
        compiler_params=params(),
        cost_estimate=cost(4 * micros * local * sequence * sequence * HP),
    )(counts, raw, cosine, sine, gain_q, gain_k)


def self_backward(raw, counts, cosine, sine, gain_q, gain_k, turned_q, turned_k, norms, incoming):
    parts, micros, slots, packed = raw.shape
    lanes = packed // 3
    local = lanes // HP
    sequence = parts * slots
    scale = HD ** (-0.5)
    factor = scale * LOG2E

    def kernel(
        count_ref,
        raw_ref,
        cos_ref,
        sin_ref,
        gq_ref,
        gk_ref,
        q_ref,
        k_ref,
        lse_ref,
        in_ref,
        out_ref,
        dgq_ref,
        dgk_ref,
        dq_s,
        dk_s,
        dv_s,
    ):
        count = count_ref[pl.program_id(0)]
        blocks = (count + slots - 1) // slots
        dq_s[...] = jnp.zeros_like(dq_s)
        dk_s[...] = jnp.zeros_like(dk_s)
        dv_s[...] = jnp.zeros_like(dv_s)
        row = lax.broadcasted_iota(jnp.int32, (sequence, 1), 0)
        bias = jnp.where(row < count, 0.0, MASKED)
        for h in range(local):
            cut = slice(h * HP, (h + 1) * HP)
            keys = k_ref[0, :, cut]
            values = raw_ref[:, 0, :, 2 * lanes + h * HP : 2 * lanes + (h + 1) * HP].reshape(sequence, HP)

            def one_block(part, carry):
                spot = pl.ds(pl.multiple_of(part * slots, slots), slots)
                rows = q_ref[0, spot, cut]
                grads = in_ref[part, 0, :, cut]
                norm = lse_ref[0, h : h + 1, spot]
                probs = jnp.exp2(dot_nt(keys, rows) * factor + bias - norm)
                d_probs = dot_nt(values, grads)
                inner = jnp.sum(probs * d_probs, 0, keepdims=True)
                d_scores = (probs * (d_probs - inner)).astype(BF)
                dv_s[:, cut] += dot_nn(probs.astype(BF), grads)
                dk_s[:, cut] += dot_nn(d_scores, rows)
                dq_s[spot, cut] = dot_tn(d_scores, keys)
                return carry

            lax.fori_loop(0, blocks, one_block, 0)
        masks = head_masks((1, lanes), local)

        def finish(part, carry):
            spot = pl.ds(pl.multiple_of(part * slots, slots), slots)
            cosine, sine = cos_ref[0, spot, :], sin_ref[0, spot, :]
            sums = []
            for index, gain_ref, source in ((0, gq_ref, dq_s), (1, gk_ref, dk_s)):
                grad = source[spot, :] * scale
                grad = grad * cosine - turn_pairs(grad) * sine
                value = raw_ref[part, 0, :, index * lanes : (index + 1) * lanes].astype(F32)
                unit, spread = head_unit(value, masks)
                leading = grad * gain_ref[...]
                back = leading - head_mean(leading, masks) - unit * head_mean(leading * unit, masks)
                out_ref[part, 0, :, index * lanes : (index + 1) * lanes] = (spread * back).astype(BF)
                sums.append(carry[index] + jnp.sum(grad * unit, 0, keepdims=True))
            out_ref[part, 0, :, 2 * lanes : 3 * lanes] = dv_s[spot, :].astype(BF)
            return tuple(sums)

        zero = jnp.zeros((1, lanes), F32)
        d_gains = lax.fori_loop(0, parts, finish, (zero, zero))
        dgq_ref[0] = d_gains[0]
        dgk_ref[0] = d_gains[1]

    whole = lambda m, c: (0, m, 0, 0)
    table = lambda m, c: (m, 0, 0)
    fixed = lambda m, c: (0, 0)
    return pl.pallas_call(
        kernel,
        name="self_backward",
        grid_spec=pltpu.PrefetchScalarGridSpec(
            num_scalar_prefetch=1,
            grid=(micros,),
            in_specs=[
                pl.BlockSpec((parts, 1, slots, packed), whole),
                pl.BlockSpec((1, sequence, lanes), table),
                pl.BlockSpec((1, sequence, lanes), table),
                pl.BlockSpec((1, lanes), fixed),
                pl.BlockSpec((1, lanes), fixed),
                pl.BlockSpec((1, sequence, lanes), table),
                pl.BlockSpec((1, sequence, lanes), table),
                pl.BlockSpec((1, local, sequence), table),
                pl.BlockSpec((parts, 1, slots, lanes), whole),
            ],
            out_specs=[
                pl.BlockSpec((parts, 1, slots, packed), whole),
                pl.BlockSpec((1, 1, lanes), table),
                pl.BlockSpec((1, 1, lanes), table),
            ],
            scratch_shapes=[pltpu.VMEM((sequence, lanes), F32) for index in range(3)],
        ),
        out_shape=[
            jax.ShapeDtypeStruct((parts, micros, slots, packed), BF),
            jax.ShapeDtypeStruct((micros, 1, lanes), F32),
            jax.ShapeDtypeStruct((micros, 1, lanes), F32),
        ],
        compiler_params=params(),
        cost_estimate=cost(10 * micros * local * sequence * sequence * HP),
    )(counts, raw, cosine, sine, gain_q, gain_k, turned_q, turned_k, norms, incoming)


def cost(flops):
    return pl.CostEstimate(flops=flops // 16, bytes_accessed=flops // 16000, transcendentals=0)


def full(shape):
    return pl.BlockSpec(shape, lambda *index: (0,) * len(shape))


def params(megabytes=60):
    return pltpu.CompilerParams(vmem_limit_bytes=megabytes << 20)


class Lanes:
    def __init__(self, near, far, block=None, index=0):
        self.near, self.far = near, far
        self.block = block or near.shape[2]
        self.index = index

    def spec(self):
        index = self.index
        return pl.BlockSpec((1, self.near.shape[1], self.block), lambda p, *rest: (p, 0, index))


def to_lanes(value, weights, dtype=BF, name="to_lanes"):
    rows = value.shape[1]
    parts, half, _ = weights[0].near.shape
    total = sum(weight.block for weight in weights)

    def kernel(x_ref, *refs):
        out_ref = refs[-1]
        at = 0
        for index, weight in enumerate(weights):
            result = dot_nn(x_ref[0], refs[2 * index][0]) + dot_nn(x_ref[1], refs[2 * index + 1][0])
            out_ref[0, :, at : at + weight.block] = result.astype(dtype)
            at += weight.block

    return pl.pallas_call(
        kernel,
        name=name,
        grid=(parts,),
        in_specs=[full(value.shape)] + [weight.spec() for weight in weights for side in range(2)],
        out_specs=pl.BlockSpec((1, rows, total), lambda p: (p, 0, 0)),
        out_shape=jax.ShapeDtypeStruct((parts, rows, total), dtype),
        compiler_params=params(),
        cost_estimate=cost(4 * rows * half * parts * total),
    )(value, *[side for weight in weights for side in (weight.near, weight.far)])


def to_inputs(value, weights, kept):
    rows = value.shape[1]
    parts, half, _ = weights[0].near.shape
    sides = parts // 2

    def kernel(x_ref, *refs):
        out_ref = refs[-1]
        for side in range(sides):

            @pl.when(pl.program_id(0) % sides == side)
            def _():
                at = 0
                for index, weight in enumerate(weights):
                    result = dot_nn(x_ref[0], refs[2 * index][0]) + dot_nn(
                        x_ref[1], refs[2 * index + 1][0]
                    )
                    take = min(weight.block, kept - at)
                    start = side * kept + at
                    out_ref[0, :, start : start + take] = result[:, :take]
                    at += take

    return pl.pallas_call(
        kernel,
        name="to_inputs",
        grid=(parts,),
        in_specs=[full(value.shape)] + [weight.spec() for weight in weights for side in range(2)],
        out_specs=pl.BlockSpec((1, rows, sides * kept), lambda p: (p // sides, 0, 0)),
        out_shape=jax.ShapeDtypeStruct((2, rows, sides * kept), F32),
        compiler_params=params(),
        cost_estimate=cost(4 * rows * half * parts * kept),
    )(value, *[side for weight in weights for side in (weight.near, weight.far)])


def to_features(value, weights, extras, outs, finish, name="to_features"):
    parts, rows, total = value.shape
    half = weights[0].near.shape[1]
    count = 2 * len(weights)

    def kernel(*refs):
        y_ref, weight_refs = refs[0], refs[1 : 1 + count]
        extra_refs = refs[1 + count : 1 + count + len(extras)]
        out_refs = refs[1 + count + len(extras) : -1]
        sums = refs[-1]

        @pl.when(pl.program_id(0) == 0)
        def _():
            sums[...] = jnp.zeros_like(sums)

        at = 0
        for index, weight in enumerate(weights):
            left = y_ref[0, :, at : at + weight.block]
            for side in range(2):
                sums[side] += dot_nt(left, weight_refs[2 * index + side][0])
            at += weight.block

        @pl.when(pl.program_id(0) == parts - 1)
        def _():
            finish([sums[0], sums[1]], extra_refs, out_refs)

    return pl.pallas_call(
        kernel,
        name=name,
        grid=(parts,),
        in_specs=[pl.BlockSpec((1, rows, total), lambda p: (p, 0, 0))]
        + [weight.spec() for weight in weights for side in range(2)]
        + [full(extra.shape) for extra in extras],
        out_specs=[full(out.shape) for out in outs],
        out_shape=outs,
        scratch_shapes=[pltpu.VMEM((2, rows, half), F32)],
        compiler_params=params(),
        cost_estimate=cost(4 * rows * half * parts * total),
    )(value, *[side for weight in weights for side in (weight.near, weight.far)], *extras)


def terms_of(pairs, name="terms_of"):
    half = pairs[0][0].shape[2]
    parts = pairs[0][1].shape[0]
    total = sum(pair[2] for pair in pairs)
    rows = [pair[0].shape[1] for pair in pairs]

    def kernel(*refs):
        count = len(pairs)
        lefts, rights = refs[:count], refs[count : 2 * count]
        near_ref, far_ref = refs[2 * count : 2 * count + 2]
        turned = refs[2 * count + 2 :]

        @pl.when(pl.program_id(0) == 0)
        def _():
            for left, flat in zip(lefts, turned):
                for side in range(2):
                    flat[side] = jnp.transpose(left[side])

        at = 0
        for pair, right, flat in zip(pairs, rights, turned):
            lanes = pair[2]
            near_ref[0, :, at : at + lanes] = dot_nn(flat[0], right[0]).astype(BF)
            far_ref[0, :, at : at + lanes] = dot_nn(flat[1], right[0]).astype(BF)
            at += lanes

    def right_spec(pair):
        return pl.BlockSpec((1, pair[1].shape[1], pair[2]), lambda p: (p, 0, pair[3]))

    out = jax.ShapeDtypeStruct((parts, half, total), BF)
    return pl.pallas_call(
        kernel,
        name=name,
        grid=(parts,),
        in_specs=[full(pair[0].shape) for pair in pairs] + [right_spec(pair) for pair in pairs],
        out_specs=[pl.BlockSpec((1, half, total), lambda p: (p, 0, 0))] * 2,
        out_shape=[out, out],
        scratch_shapes=[pltpu.VMEM((2, half, count), BF) for count in rows],
        compiler_params=params(),
        cost_estimate=cost(sum(4 * half * parts * pair[2] * count for pair, count in zip(pairs, rows))),
    )(*[pair[0] for pair in pairs], *[pair[1] for pair in pairs])


def norm_unit(halves):
    width = 2 * halves[0].shape[-1]
    mean = sum(jnp.sum(half, -1, keepdims=True) for half in halves) / width
    centre = [half - mean for half in halves]
    spread = sum(jnp.sum(half * half, -1, keepdims=True) for half in centre) / width
    scale = lax.rsqrt(spread + EPS)
    return [half * scale for half in centre], scale


def norm_back(halves, gain_ref, incoming):
    width = 2 * halves[0].shape[-1]
    unit, scale = norm_unit(halves)
    leading = [incoming[side] * gain_ref[side] for side in range(2)]
    mean = sum(jnp.sum(half, -1, keepdims=True) for half in leading) / width
    inner = sum(jnp.sum(leading[side] * unit[side], -1, keepdims=True) for side in range(2)) / width
    back = [scale * (leading[side] - mean - unit[side] * inner) for side in range(2)]
    gains = [jnp.sum(incoming[side] * unit[side], 0, keepdims=True) for side in range(2)]
    return back, gains


def join_rows(pieces, rows, name="join_rows"):
    parts, _, lanes = pieces[0][0].shape
    count = len(pieces)
    if rows % 16:
        return jnp.concatenate([array[:, block * rows : (block + 1) * rows] for array, block in pieces], 1)

    def kernel(*refs):
        for index in range(count):
            refs[-1][0, index * rows : (index + 1) * rows] = refs[index][0]

    def spec(block):
        return pl.BlockSpec((1, rows, lanes), lambda p: (p, block, 0))

    return pl.pallas_call(
        kernel,
        name=name,
        grid=(parts,),
        in_specs=[spec(block) for _, block in pieces],
        out_specs=pl.BlockSpec((1, count * rows, lanes), lambda p: (p, 0, 0)),
        out_shape=jax.ShapeDtypeStruct((parts, count * rows, lanes), BF),
        compiler_params=params(),
        cost_estimate=cost(parts * count * rows * lanes),
    )(*[array for array, _ in pieces])


def sum_rows(jobs, rows, name="sum_rows"):
    parts = jobs[0][1][0][0].shape[0]
    if rows % 16:
        results = []
        for lanes, terms in jobs:
            value = 0.0
            for array, blocks, spot in terms:
                split = array[:, :, spot * lanes : (spot + 1) * lanes].reshape(parts, -1, rows, lanes)
                value = value + jnp.stack([split[:, block] for block in blocks], 1).astype(F32)
            results.append(value.astype(BF).reshape(parts, -1, lanes))
        return results
    spots = [
        (array, blocks[index], spot, lanes)
        for lanes, terms in jobs
        for index in range(len(terms[0][1]))
        for array, blocks, spot in terms
    ]

    def kernel(*refs):
        at = 0
        for order, (_, terms) in enumerate(jobs):
            out_ref = refs[len(spots) + order]
            for index in range(len(terms[0][1])):
                value = refs[at][0].astype(F32)
                for offset in range(1, len(terms)):
                    value = value + refs[at + offset][0].astype(F32)
                out_ref[0, index * rows : (index + 1) * rows] = value.astype(BF)
                at += len(terms)

    def spec(block, spot, lanes):
        return pl.BlockSpec((1, rows, lanes), lambda p: (p, block, spot))

    shapes = [(len(terms[0][1]) * rows, lanes) for lanes, terms in jobs]
    return pl.pallas_call(
        kernel,
        name=name,
        grid=(parts,),
        in_specs=[spec(*rest) for _, *rest in spots],
        out_specs=[pl.BlockSpec((1, *shape), lambda p: (p, 0, 0)) for shape in shapes],
        out_shape=[jax.ShapeDtypeStruct((parts, *shape), BF) for shape in shapes],
        compiler_params=params(),
        cost_estimate=cost(sum(parts * size * lanes for size, lanes in shapes)),
    )(*[array for array, *_ in spots])


def side_by_side(left, right, kept, lanes):
    rows, width = left.shape
    count = width // kept

    def kernel(left_ref, right_ref, out_ref):
        for index, ref in enumerate((left_ref, right_ref)):
            for side in range(count):
                spot = count * index + side
                out_ref[spot, :, :kept] = ref[:, side * kept : (side + 1) * kept]
                if lanes > kept:
                    out_ref[spot, :, kept:] = jnp.zeros((rows, lanes - kept), BF)

    return pl.pallas_call(
        kernel,
        name="side_by_side",
        out_shape=jax.ShapeDtypeStruct((2 * count, rows, lanes), BF),
        compiler_params=params(),
        cost_estimate=cost(4 * rows * lanes),
    )(left, right)


def mlp_forward(rows_in, grads, start, weight1, weight2, part, live=None):
    _, rows, half = rows_in.shape
    parts, _, lanes = weight1.near.shape
    ff = lanes // 2
    step = 768 if ff % 768 == 0 else ff
    steps = ff // step
    extras = [] if live is None else [live]

    def kernel(x_ref, g_ref, s_ref, n1_ref, f1_ref, n2_ref, f2_ref, *refs):
        hid_ref, act_ref, out_ref, dn2_ref, df2_ref, turned, sums = refs[len(extras) :]
        first = (pl.program_id(0) == 0) & (pl.program_id(1) == 0)
        last = (pl.program_id(0) == parts - 1) & (pl.program_id(1) == steps - 1)

        @pl.when(first)
        def _():
            for side in range(2):
                turned[side] = jnp.transpose(g_ref[side])
            sums[...] = s_ref[...]

        hidden = dot_nn(x_ref[0], n1_ref[0]) + dot_nn(x_ref[1], f1_ref[0])
        hid_ref[0] = hidden
        activ = jax.nn.gelu(hidden, approximate=True).astype(BF)
        act_ref[0] = activ
        sums[0] += dot_nt(activ, n2_ref[0])
        sums[1] += dot_nt(activ, f2_ref[0])
        dn2_ref[0] = dot_nn(turned[0], activ).astype(BF)
        df2_ref[0] = dot_nn(turned[1], activ).astype(BF)

        @pl.when(last)
        def _():
            if live is None:
                out_ref[...] = sums[...]
            else:
                out_ref[...] = (sums[...] * refs[0][...]).astype(BF)

    weight = pl.BlockSpec((1, half, step), lambda p, n: (p, 0, part * steps + n))
    grad = pl.BlockSpec((1, half, step), lambda p, n: (p, 0, n))
    unit = pl.BlockSpec((1, rows, step), lambda p, n: (p, 0, n))
    whole = full((2, rows, half))
    grad_shape = jax.ShapeDtypeStruct((parts, half, ff), BF)
    return pl.pallas_call(
        kernel,
        name="mlp_forward",
        grid=(parts, steps),
        in_specs=[whole, whole, whole, weight, weight, weight, weight] + [full(extra.shape) for extra in extras],
        out_specs=[unit, unit, whole, grad, grad],
        out_shape=[
            jax.ShapeDtypeStruct((parts, rows, ff), F32),
            jax.ShapeDtypeStruct((parts, rows, ff), BF),
            jax.ShapeDtypeStruct((2, rows, half), F32 if live is None else BF),
            grad_shape,
            grad_shape,
        ],
        scratch_shapes=[pltpu.VMEM((2, half, rows), BF), pltpu.VMEM((2, rows, half), F32)],
        compiler_params=params(),
        cost_estimate=cost(12 * rows * half * parts * ff),
    )(rows_in, grads, start, weight1.near, weight1.far, weight2.near, weight2.far, *extras)


def gelu_slope(value):
    root = math.sqrt(2.0 / math.pi)
    square = value * value
    curve = jnp.tanh(root * value * (1.0 + 0.044715 * square))
    return 0.5 * (1.0 + curve) + 0.5 * value * (1.0 - curve * curve) * root * (
        1.0 + 3.0 * 0.044715 * square
    )


def mlp_backward(grads, rows_in, hidden, weight1, weight2, part, start, finish=None):
    _, rows, half = rows_in.shape
    parts, _, lanes = weight1.near.shape
    ff = lanes // 2
    step = 768 if ff % 768 == 0 else ff
    steps = ff // step
    extras = list(finish or []) + ([] if start is None else [start])

    def kernel(g_ref, x_ref, hid_ref, n1_ref, f1_ref, n2_ref, f2_ref, *refs):
        extra_refs, refs = refs[: len(extras)], refs[len(extras) :]
        dn1_ref, df1_ref = refs[:2]
        out_refs = refs[2:-2]
        turned, sums = refs[-2:]
        first = (pl.program_id(0) == 0) & (pl.program_id(1) == 0)
        last = (pl.program_id(0) == parts - 1) & (pl.program_id(1) == steps - 1)

        @pl.when(first)
        def _():
            for side in range(2):
                turned[side] = jnp.transpose(x_ref[side])
            sums[...] = jnp.zeros_like(sums) if start is None else extra_refs[-1][...]

        d_activ = dot_nn(g_ref[0], n2_ref[0]) + dot_nn(g_ref[1], f2_ref[0])
        d_hidden = (d_activ * gelu_slope(hid_ref[0])).astype(BF)
        dn1_ref[0] = dot_nn(turned[0], d_hidden).astype(BF)
        df1_ref[0] = dot_nn(turned[1], d_hidden).astype(BF)
        sums[0] += dot_nt(d_hidden, n1_ref[0])
        sums[1] += dot_nt(d_hidden, f1_ref[0])

        @pl.when(last)
        def _():
            if finish is None:
                out_refs[0][...] = sums[...]
            else:
                value_ref, gain_ref, add_ref = extra_refs[:3]
                add_norm_back([sums[0], sums[1]], value_ref, gain_ref, add_ref, *out_refs)

    weight = pl.BlockSpec((1, half, step), lambda p, n: (p, 0, part * steps + n))
    grad = pl.BlockSpec((1, half, step), lambda p, n: (p, 0, n))
    unit = pl.BlockSpec((1, rows, step), lambda p, n: (p, 0, n))
    whole = full((2, rows, half))
    grad_shape = jax.ShapeDtypeStruct((parts, half, ff), BF)
    wide = jax.ShapeDtypeStruct((2, rows, half), F32)
    outs = [wide] if finish is None else [wide, *back_shapes(rows, half)]
    return pl.pallas_call(
        kernel,
        name="mlp_backward",
        grid=(parts, steps),
        in_specs=[whole, whole, unit, weight, weight, weight, weight] + [full(extra.shape) for extra in extras],
        out_specs=[grad, grad] + [full(out.shape) for out in outs],
        out_shape=[grad_shape, grad_shape] + outs,
        scratch_shapes=[pltpu.VMEM((2, half, rows), BF), pltpu.VMEM((2, rows, half), F32)],
        compiler_params=params(),
        cost_estimate=cost(12 * rows * half * parts * ff),
    )(grads, rows_in, hidden, weight1.near, weight1.far, weight2.near, weight2.far, *extras)


def back_shapes(rows, half):
    return [jax.ShapeDtypeStruct((2, rows, half), BF), jax.ShapeDtypeStruct((2, 1, half), F32)]


def add_norm_back(incoming, value_ref, gain_ref, add_ref, out_ref, low_ref, d_gain_ref):
    back, gains = norm_back([value_ref[0], value_ref[1]], gain_ref, incoming)
    for side in range(2):
        total = add_ref[side] + back[side]
        out_ref[side] = total
        low_ref[side] = total.astype(BF)
        d_gain_ref[side] = gains[side]


def text_bias(lengths_ref, micro, words, strip, text_slots, axis):
    spot = lax.broadcasted_iota(jnp.int32, (1, words) if axis else (words, 1), axis)
    inner = spot % strip
    place = spot // strip * text_slots + inner
    live = (place < lengths_ref[micro, 0]) | (
        (place >= CLIP_LEN) & (place < CLIP_LEN + lengths_ref[micro, 1])
    )
    return jnp.where(live & (inner < text_slots), 0.0, MASKED)


def cross_forward(query, text_kv, lengths, text_slots):
    parts, micros, slots, lanes = query.shape
    zones, strip = text_kv.shape[1], text_kv.shape[3]
    words = zones * strip
    local = lanes // HP
    factor = HD ** (-0.5) * LOG2E

    def kernel(len_ref, q_ref, kv_ref, out_ref):
        bias = text_bias(len_ref, pl.program_id(1), words, strip, text_slots, 1)
        for h in range(local):
            cut = slice(h * HP, (h + 1) * HP)
            keys = kv_ref[0, :, 0, :, cut].reshape(words, HP)
            scores = dot_nt(q_ref[0, 0, :, cut], keys) + bias
            top = jnp.max(scores, -1, keepdims=True)
            raised = jnp.exp2((scores - top) * factor)
            total = jnp.sum(raised, -1, keepdims=True)
            values = kv_ref[0, :, 0, :, lanes + h * HP : lanes + (h + 1) * HP].reshape(words, HP)
            out_ref[0, 0, :, cut] = (dot_nn(raised.astype(BF), values) / total).astype(BF)

    spot = lambda p, m, c: (p, m, 0, 0)
    far = lambda p, m, c: (p, 0, m, 0, 0)
    return pl.pallas_call(
        kernel,
        name="cross_forward",
        grid_spec=pltpu.PrefetchScalarGridSpec(
            num_scalar_prefetch=1,
            grid=(parts, micros),
            in_specs=[
                pl.BlockSpec((1, 1, slots, lanes), spot),
                pl.BlockSpec((1, zones, 1, strip, 2 * lanes), far),
            ],
            out_specs=pl.BlockSpec((1, 1, slots, lanes), spot),
        ),
        out_shape=jax.ShapeDtypeStruct(query.shape, BF),
        compiler_params=params(),
        cost_estimate=cost(4 * parts * micros * slots * words * lanes),
    )(lengths, query, text_kv)


def cross_backward(query, text_kv, lengths, incoming, text_slots):
    parts, micros, slots, lanes = query.shape
    zones, strip = text_kv.shape[1], text_kv.shape[3]
    words = zones * strip
    local = lanes // HP
    scale = HD ** (-0.5)
    factor = scale * LOG2E

    def kernel(len_ref, q_ref, kv_ref, in_ref, dq_ref, dkv_ref):
        bias = text_bias(len_ref, pl.program_id(1), words, strip, text_slots, 0)
        for h in range(local):
            cut = slice(h * HP, (h + 1) * HP)
            far = slice(lanes + h * HP, lanes + (h + 1) * HP)
            rows = q_ref[0, 0, :, cut]
            keys = kv_ref[0, :, 0, :, cut].reshape(words, HP)
            values = kv_ref[0, :, 0, :, far].reshape(words, HP)
            grads = in_ref[0, 0, :, cut]
            scores = dot_nt(keys, rows) + bias
            top = jnp.max(scores, 0, keepdims=True)
            raised = jnp.exp2((scores - top) * factor)
            probs = raised * (1.0 / jnp.sum(raised, 0, keepdims=True))
            d_probs = dot_nt(values, grads)
            inner = jnp.sum(probs * d_probs, 0, keepdims=True)
            d_scores = (probs * (d_probs - inner)).astype(BF)
            shape = (zones, strip, HP)
            dkv_ref[0, :, 0, :, far] = dot_nn(probs.astype(BF), grads).astype(BF).reshape(shape)
            dkv_ref[0, :, 0, :, cut] = (dot_nn(d_scores, rows) * scale).astype(BF).reshape(shape)
            dq_ref[0, 0, :, cut] = (dot_tn(d_scores, keys) * scale).astype(BF)

    spot = lambda p, m, c: (p, m, 0, 0)
    far = lambda p, m, c: (p, 0, m, 0, 0)
    return pl.pallas_call(
        kernel,
        name="cross_backward",
        grid_spec=pltpu.PrefetchScalarGridSpec(
            num_scalar_prefetch=1,
            grid=(parts, micros),
            in_specs=[
                pl.BlockSpec((1, 1, slots, lanes), spot),
                pl.BlockSpec((1, zones, 1, strip, 2 * lanes), far),
                pl.BlockSpec((1, 1, slots, lanes), spot),
            ],
            out_specs=[
                pl.BlockSpec((1, 1, slots, lanes), spot),
                pl.BlockSpec((1, zones, 1, strip, 2 * lanes), far),
            ],
        ),
        out_shape=[
            jax.ShapeDtypeStruct(query.shape, BF),
            jax.ShapeDtypeStruct(text_kv.shape, BF),
        ],
        compiler_params=params(),
        cost_estimate=cost(10 * parts * micros * slots * words * lanes),
    )(lengths, query, text_kv, incoming)


def tie(*values):
    return lax.optimization_barrier(values)


class Cube:
    def __init__(self):
        self.size = lax.axis_size("dp")
        self.bits = self.size.bit_length() - 1
        self.outer = list(range(1, self.bits))
        self.rank = lax.axis_index("dp")
        self.masks = []
        for place in range(self.size):
            mask = place >> (self.bits - 1)
            for bit in self.outer:
                mask |= ((place >> (bit - 1)) & 1) << bit
            self.masks.append(mask)
        self.owners = self.rank ^ jnp.array(self.masks, jnp.int32)

    def swap(self, value, bit, axis="dp"):
        pairs = [(i, i ^ (1 << bit)) for i in range(lax.axis_size(axis))]
        return lax.ppermute(value, axis, pairs)

    def trade(self, value):
        blocks = {mask: value[mask] for mask in range(self.size)}
        for bit in range(self.bits):
            send = sorted(mask for mask in blocks if mask >> bit & 1)
            got = self.swap(jnp.stack([blocks[mask] for mask in send]), bit)
            for place, mask in enumerate(send):
                blocks[mask] = got[place]
        return jnp.stack([blocks[mask] for mask in range(self.size)])

    def spread(self, value):
        held = value[None]
        for bit in range(self.bits):
            held = jnp.concatenate([held, self.swap(held, bit)])
        return held

    def add(self, value, axis):
        for bit in range(lax.axis_size(axis).bit_length() - 1):
            value = value + self.swap(value, bit, axis)
        return value


class Gather:
    def __init__(self, cube, shard, flip, joined=False):
        self.cube = cube
        self.rows = shard.shape[1]
        self.masks = [[0]]
        self.pieces = [shard]
        self.todo = cube.outer[::-1] if flip else list(cube.outer)
        self.joined = joined

    def blocks(self, order):
        spots = {
            mask: (piece, index)
            for piece, masks in zip(self.pieces, self.masks)
            for index, mask in enumerate(masks)
        }
        return join_rows([spots[mask] for mask in order], self.rows)

    def move(self):
        bit = self.todo.pop(0)
        if self.joined and len(self.pieces) > 1:
            order = [mask for masks in self.masks for mask in masks]
            self.pieces, self.masks = [self.blocks(order)], [order]
        self.masks = self.masks + [[mask | (1 << bit) for mask in masks] for masks in self.masks]
        self.pieces = self.pieces + [self.cube.swap(piece, bit) for piece in self.pieces]

    def join(self):
        while self.todo:
            self.move()
        self.pieces = [self.blocks(self.cube.masks[: self.cube.size // 2])]

    def weight(self):
        near = self.pieces[0]
        return Lanes(near, self.cube.swap(near, 0))


class Scatter:
    def __init__(self, cube, near, other, flip, lanes=None, spot=0):
        self.cube = cube
        self.todo = list(cube.outer) if flip else cube.outer[::-1]
        self.rows = near.shape[1] // (cube.size // 2)
        self.places = list(range(cube.size // 2))
        self.near = near
        self.lanes = lanes or near.shape[2]
        self.spot = spot
        self.got = []
        self.pieces = [other]
        self.arriving = self.places

    def job(self, places):
        terms = [(self.near, places, self.spot)]
        for value, held, spot in self.got:
            terms.append((value, [held.index(place) for place in places], spot))
        return self.lanes, terms

    def absorb(self):
        self.got.append((self.pieces[0], self.arriving, 0 if self.got else self.spot))


def scatter(cube, terms, *shares):
    near, far = terms
    other = cube.swap(far, 0)
    return [Scatter(cube, near, other, flip, lanes, spot) for lanes, spot, flip in shares]


def pack(movers):
    jobs = []
    for mover in movers:
        mover.absorb()
        mover.bit = mover.todo.pop(0)
        weight = 1 << (mover.bit - 1)
        sent = [place for place in mover.places if place & weight]
        mover.places = [place for place in mover.places if not place & weight]
        mover.arriving = [place ^ weight for place in sent]
        jobs.append(mover.job(sent))
    for mover, value in zip(movers, sum_rows(jobs, movers[0].rows)):
        mover.pieces = [value]


def send(movers):
    for mover in movers:
        mover.pieces = [mover.cube.swap(mover.pieces[0], mover.bit)]


def results(movers):
    while movers[0].todo:
        pack(movers)
        send(movers)
    for mover in movers:
        mover.absorb()
    return sum_rows([mover.job([0]) for mover in movers], movers[0].rows)


def pin(value, *others):
    flat = []
    for other in others:
        flat += other.pieces if hasattr(other, "pieces") else [other]
    return tie(value, *flat)[0]


def bind(value, *movers):
    flat = [piece for mover in movers for piece in mover.pieces]
    held = tie(value, *flat)
    spot = 1
    for mover in movers:
        count = len(mover.pieces)
        mover.pieces = list(held[spot : spot + count])
        spot += count
    return held[0]


def hold(movers, *others):
    for mover in movers:
        mover.pieces = [pin(piece, *others) for piece in mover.pieces]


def on_device(
    tokens,
    skip_tokens,
    text,
    timestep,
    grid,
    text_len,
    w_skip,
    w_mod,
    w_qkv,
    w_out1,
    w_query2,
    w_text_kv,
    w_out2,
    w_fc1,
    w_fc2,
    gain_skip,
    gain_attn,
    gain_cross,
    gain_mlp,
    gain_query,
    gain_key,
    cotangent,
):
    micros, slots, width = tokens.shape
    parts = lax.axis_size("sp")
    zone = lax.axis_index("sp")
    cube = Cube()
    ranks = cube.size
    rows = micros * slots
    sequence = slots * parts
    local = H // parts
    lanes = local * HP + -local * HP % 128
    text_slots = text.shape[1]
    text_strip = -(-text_slots // 16) * 16
    features = text.shape[2]
    strip = width // ranks
    middle = width // 2
    kept = w_skip.shape[0]
    skip_lanes = -(-kept // 256) * 256
    skip_cut = skip_lanes // 2
    qkv_cut = (3 * lanes) // 256 * 128 + 128
    text_rows = w_text_kv.shape[0]

    def spread(shard, before=None):
        if before is not None:
            shard, before = tie(shard, before)
        return lax.all_gather(shard, "sp", axis=0, tiled=False)

    def fetch(value, cut, joined=False):
        return [Gather(cube, value[:, :, :cut], 0, joined), Gather(cube, value[:, :, cut:], 1, joined)]

    def advance(movers):
        for mover in movers:
            mover.move()

    def join(movers):
        for mover in movers:
            mover.join()

    def exchange(value):
        return lax.all_to_all(value, "sp", split_axis=0, concat_axis=0, tiled=True)

    skip_z = spread(jnp.pad(w_skip.T, ((0, 0), (0, skip_lanes - kept))))
    steps = cube.spread(timestep[:, 0])
    joined = side_by_side(tokens.reshape(rows, width), skip_tokens.reshape(rows, width), kept, skip_lanes)
    wide = grid[:, 0, 1]
    counts = grid[:, 0, 0] * wide
    cosine, sine = rope_tables(sequence, wide, lanes)
    skip_z, steps, joined, cosine, sine = tie(skip_z, steps, joined, cosine, sine)
    skip_m = fetch(skip_z, skip_cut)
    qkv_z = spread(pad_heads(w_qkv.reshape(strip, -1), local), skip_z)
    advance(skip_m)

    time_act = jax.nn.silu(time_embed(steps, width)).astype(BF).reshape(ranks * micros, parts, -1)
    time_part = lax.dynamic_index_in_dim(time_act, zone, 1, keepdims=False)
    shift = cube.add(jnp.dot(time_part, w_mod, preferred_element_type=F32), "sp")
    skip_m[0].pieces[1], shift = tie(skip_m[0].pieces[1], shift)
    while skip_m[0].todo:
        advance(skip_m)
    shift = cube.trade(shift.reshape(ranks, micros, strip))
    skip_m[0].pieces[-1], shift = tie(skip_m[0].pieces[-1], shift)
    shift = jnp.stack([shift[mask] for mask in cube.masks]).reshape(2, ranks // 2, micros, strip)
    shift = jnp.transpose(shift, (0, 2, 1, 3)).reshape(2, micros, middle)
    qkv_m = fetch(qkv_z, qkv_cut)
    hold(qkv_m, *skip_m)
    advance(qkv_m)
    fc1_z = spread(pin(w_fc1, *skip_m))
    fc2_z = spread(pin(w_fc2.T, *qkv_m))
    join(skip_m)
    skip_w = [mover.weight() for mover in skip_m]

    def shuffle(count):
        block = count // ranks
        place = jnp.arange(count, dtype=jnp.int32)
        source = cube.owners[place // block] * block + place % block
        return (place[:, None] == source[None, :]).astype(BF)

    turn = shuffle(width)
    text_turn = shuffle(features)
    gains = jnp.stack([gain_skip, gain_attn, gain_cross, gain_mlp])
    gains = gains.reshape(4, ranks, strip)[:, cube.owners].reshape(4, 2, 1, middle)
    g_skip, g_attn, g_cross, g_mlp = gains

    lengths = text_len[:, 0, :]
    place = zone * slots + jnp.arange(slots, dtype=jnp.int32)
    live = (place[None, :] < counts[:, None]).astype(F32).reshape(rows, 1)
    gain_q = pad_heads(jnp.tile(gain_query, local)[None, :], local)
    gain_k = pad_heads(jnp.tile(gain_key, local)[None, :], local)

    grad3 = jnp.stack(
        [
            jnp.dot(cotangent.reshape(rows, width), side, preferred_element_type=F32) * live
            for side in (turn[:, :middle], turn[:, middle:])
        ]
    )
    d_mlp = grad3.astype(BF)

    wide_shape = jax.ShapeDtypeStruct((2, rows, middle), F32)
    low_shape = jax.ShapeDtypeStruct((2, rows, middle), BF)
    gain_shape = jax.ShapeDtypeStruct((2, 1, middle), F32)

    def first_norms(sums, extra, out):
        g0_ref, g1_ref, shift_ref = extra
        base_ref, stream_ref, pre_ref = out
        unit, _ = norm_unit(sums)
        stream = [unit[side] * g0_ref[side] for side in range(2)]
        unit, _ = norm_unit(stream)
        for side in range(2):
            base_ref[side] = sums[side]
            stream_ref[side] = stream[side]
            for micro in range(micros):
                cut = slice(micro * slots, (micro + 1) * slots)
                pre = unit[side][cut] * g1_ref[side] + shift_ref[side, micro : micro + 1]
                pre_ref[side, cut] = pre.astype(BF)

    def next_norm(sums, extra, out):
        before_ref, gain_ref = extra
        after_ref, pre_ref = out
        stream = [before_ref[side] + sums[side] for side in range(2)]
        unit, _ = norm_unit(stream)
        for side in range(2):
            after_ref[side] = stream[side]
            pre_ref[side] = (unit[side] * gain_ref[side]).astype(BF)

    base, stream, pre_attn = to_features(
        joined, skip_w, [g_skip, g_attn, shift], [wide_shape, wide_shape, low_shape], first_norms
    )
    while qkv_m[0].todo:
        advance(qkv_m)
    after_qkv = [mover.pieces[-1] for mover in qkv_m]
    hold(qkv_m, pre_attn)
    join(qkv_m)
    pre_attn, fc1_z = tie(pre_attn, fc1_z)
    qkv_w = [mover.weight() for mover in qkv_m]
    projected = to_lanes(pre_attn, qkv_w)
    projected, fc2_z = tie(projected, fc2_z)
    fc_m = [Gather(cube, fc1_z, 0, True), Gather(cube, fc2_z, 1, True)]
    hold(fc_m, *after_qkv)
    advance(fc_m)
    raw = exchange(projected.reshape(parts, micros, slots, 3 * lanes))
    cross_z = jnp.concatenate([pad_heads(side, local) for side in (w_out1.T, w_query2, w_out2.T)], 1)
    arrived = fc_m[0].pieces + fc_m[1].pieces
    cross_z = spread(pin(cross_z, *arrived))
    text_own = jnp.dot(text.reshape(-1, features), text_turn, preferred_element_type=F32).astype(BF)
    text_own = jnp.pad(
        text_own.reshape(micros, text_slots, features), ((0, 0), (0, text_strip - text_slots), (0, 0))
    ).reshape(micros * text_strip, features)
    text_z = jnp.pad(pad_heads(w_text_kv.reshape(text_rows, -1), local), ((0, max(0, strip - text_rows)), (0, 0)))
    while fc_m[0].todo:
        advance(fc_m)
    text_z = spread(pin(text_z, *arrived))
    text_all = spread(pin(text_own, *arrived))
    cross_z, d_mlp, turn, text_turn = tie(cross_z, d_mlp, turn, text_turn)
    cross_m = fetch(cross_z, 2 * lanes, True)
    advance(cross_m)
    attended, turned_q, turned_k, norms = self_forward(raw, counts, cosine, sine, gain_q, gain_k)
    attended = bind(attended, *fc_m, *cross_m)
    attended, text_all, text_z = tie(attended, text_all, text_z)
    text_m = Gather(cube, text_z[:, :text_rows], 0, True)
    text_m.move()
    attended = exchange(attended).reshape(parts, rows, lanes)
    while cross_m[0].todo:
        advance(cross_m)
    join(fc_m)
    attended = bind(attended, text_m, *fc_m, cross_m[0])
    while text_m.todo:
        text_m.move()
    join(cross_m[:1])
    first_w = cross_m[0].weight()
    out1_w, query2_w = (Lanes(first_w.near, first_w.far, lanes, index) for index in range(2))
    attended, first_w.far = tie(attended, first_w.far)
    out1_w.far = query2_w.far = first_w.far
    text_all = text_all.reshape(-1, features)
    text_all = jnp.stack([text_all[:, : features // 2], text_all[:, features // 2 :]])
    stream1, pre_cross = to_features(
        attended, [out1_w], [stream, g_cross], [wide_shape, low_shape], next_norm
    )
    hold(fc_m, out1_w.far)
    fc1_w, fc2_w = [mover.weight() for mover in fc_m]
    hold([text_m], pre_cross)
    text_m.join()
    text_w = text_m.weight()
    query2 = to_lanes(pre_cross, [query2_w]).reshape(parts, micros, slots, lanes)
    query2 = bind(query2, *cross_m[1:])
    join(cross_m[1:])
    out2_w = cross_m[1].weight()
    text_kv = to_lanes(text_all, [text_w]).reshape(parts, parts, micros, text_strip, 2 * lanes)
    crossed = cross_forward(query2, text_kv, lengths, text_slots).reshape(parts, rows, lanes)
    stream2, pre_mlp = to_features(
        crossed, [out2_w], [stream1, g_mlp], [wide_shape, low_shape], next_norm
    )
    hidden0, activ0, partial, fc2_n0, fc2_f0 = mlp_forward(pre_mlp, d_mlp, stream2, fc1_w, fc2_w, 0)
    hidden1, activ1, result, fc2_n1, fc2_f1 = mlp_forward(pre_mlp, d_mlp, partial, fc1_w, fc2_w, 1, live)
    share = fc2_n0.shape[2]
    fc2_s = scatter(cube, (fc2_n0, fc2_f0), (share, 0, 0)) + scatter(cube, (fc2_n1, fc2_f1), (share, 0, 1))

    def settle(values, before=None):
        value = values[0] if len(values) == 1 else jnp.concatenate(values, 2)
        if before is not None:
            value, before = tie(value, before)
        return lax.psum_scatter(value, "sp", scatter_dimension=0, tiled=False)

    fc1_n0, fc1_f0, partial = mlp_backward(d_mlp, pre_mlp, hidden0, fc1_w, fc2_w, 0, None)
    fc1_s = scatter(cube, (fc1_n0, fc1_f0), (share, 0, 0))
    pack(fc2_s)
    partial = bind(partial, *fc2_s)
    send(fc2_s)
    fc1_n1, fc1_f1, grad2, d_cross, d_gain_mlp = mlp_backward(
        d_mlp, pre_mlp, hidden1, fc1_w, fc2_w, 1, partial, [stream2, g_mlp, grad3]
    )
    fc1_s += scatter(cube, (fc1_n1, fc1_f1), (share, 0, 1))
    d_cross = bind(d_cross, *fc2_s)
    d_crossed = to_lanes(d_cross, [out2_w])
    pack(fc2_s)
    d_crossed = bind(d_crossed, *fc2_s)
    send(fc2_s)
    d_query2, d_text_kv = cross_backward(
        query2, text_kv, lengths, d_crossed.reshape(parts, micros, slots, lanes), text_slots
    )
    d_query2 = bind(d_query2, *fc2_s)
    d_query2 = d_query2.reshape(parts, rows, lanes)
    d_text_kv = d_text_kv.reshape(parts, -1, 2 * lanes)
    total_fc2 = results(fc2_s)
    term_fc2 = settle(total_fc2)

    def go_back(sums, extra, out):
        add_norm_back(sums, *extra, *out)

    grad1, d_attn, d_gain_cross = to_features(
        d_query2, [query2_w], [stream1, g_cross, grad2], [wide_shape, low_shape, gain_shape], go_back
    )
    d_attn = bind(d_attn, *fc1_s)
    pack(fc1_s)
    d_attn = bind(d_attn, *fc1_s)
    send(fc1_s)
    d_attended = to_lanes(d_attn, [out1_w])
    d_attended, d_text_kv, pre_cross = tie(d_attended, d_text_kv, pre_cross)
    d_heads = exchange(d_attended.reshape(parts, micros, slots, lanes))

    def words_back(sums, extra, out):
        size = micros * text_strip
        for zone in range(parts):
            for side in range(2):
                out[0][zone, side] = sums[side][zone * size : (zone + 1) * size].astype(BF)

    words_shape = jax.ShapeDtypeStruct((parts, 2, micros * text_strip, features // 2), BF)
    d_words = to_features(d_text_kv, [text_w], [], [words_shape], words_back)[0]
    text_t = list(terms_of([(text_all, d_text_kv, 2 * lanes, 0)]))
    cross_t = terms_of(
        [(d_attn, attended, lanes, 0), (pre_cross, d_query2, lanes, 0), (d_cross, crossed, lanes, 0)]
    )
    cross_t = list(cross_t)
    d_heads, d_words, text_t[1], cross_t[1] = tie(d_heads, d_words, text_t[1], cross_t[1])
    d_words = settle([d_words])
    text_s = scatter(cube, text_t, (lanes, 0, 0), (lanes, 1, 1))
    cross_s = scatter(cube, cross_t, (2 * lanes, 0, 0), (lanes, 2, 1))
    d_heads = bind(d_heads, *fc1_s)
    pack(fc1_s)
    d_heads = bind(d_heads, *fc1_s)
    send(fc1_s)
    d_raw, d_gain_q, d_gain_k = self_backward(
        raw, counts, cosine, sine, gain_q, gain_k, turned_q, turned_k, norms, d_heads
    )
    d_raw, term_fc2, d_words = tie(d_raw, term_fc2, d_words)
    d_raw = bind(d_raw, *fc1_s)
    d_projected = exchange(d_raw).reshape(parts, rows, 3 * lanes)
    other_s = cross_s + text_s
    total_fc1 = results(fc1_s)
    pack(cross_s)
    pack(text_s)
    send(other_s)
    d_projected = bind(d_projected, *other_s)
    term_fc1 = settle(total_fc1, d_projected)
    qkv_t = terms_of([(pre_attn, d_projected, 3 * lanes, 0)])
    qkv_s = scatter(cube, qkv_t, (2 * lanes, 0, 0), (lanes, 2, 1))
    pack(cross_s)
    pack(text_s)
    send(other_s)
    pack(qkv_s)
    d_projected = bind(d_projected, *qkv_s)
    send(qkv_s)

    def last_norms(sums, extra, out):
        stream_ref, g1_ref, base_ref, g0_ref, add_ref = extra
        low_ref, d_shift_ref, d_g1_ref, d_g0_ref = out
        back, gains1 = norm_back([stream_ref[0], stream_ref[1]], g1_ref, sums)
        total = [add_ref[side] + back[side] for side in range(2)]
        back, gains0 = norm_back([base_ref[0], base_ref[1]], g0_ref, total)
        for side in range(2):
            low_ref[side] = back[side].astype(BF)
            d_g1_ref[side] = gains1[side]
            d_g0_ref[side] = gains0[side]
            for micro in range(micros):
                part = sums[side][micro * slots : (micro + 1) * slots]
                d_shift_ref[side, micro : micro + 1] = jnp.sum(part, 0, keepdims=True)

    shift_shape = jax.ShapeDtypeStruct((2, micros, middle), F32)
    d_base, d_shift, d_gain_attn, d_gain_skip = to_features(
        d_projected,
        qkv_w,
        [stream, g_attn, base, g_skip, grad1],
        [low_shape, shift_shape, gain_shape, gain_shape],
        last_norms,
    )
    d_base = bind(d_base, *other_s)
    skip_t = terms_of([(d_base, joined, skip_lanes, 0)])
    skip_s = scatter(cube, skip_t, (skip_cut, 0, 0), (skip_cut, 1, 1))
    pack(skip_s)
    pack(qkv_s)
    skip_s[0].pieces[0] = bind(skip_s[0].pieces[0], *qkv_s)
    send(qkv_s)
    send(skip_s)
    term_cross, term_text = settle(results(cross_s)), settle(results(text_s))
    total_qkv = results(qkv_s)
    term_qkv = settle(total_qkv)
    term_skip = settle(results(skip_s), total_qkv[0])
    d_joined = to_inputs(d_base, skip_w, kept)
    result = (
        jnp.dot(result[0], turn[:, :middle].T, preferred_element_type=F32)
        + jnp.dot(result[1], turn[:, middle:].T, preferred_element_type=F32)
    ).astype(BF)
    d_words = d_words.reshape(2, micros * text_strip, features // 2)
    d_words = jnp.dot(
        d_words[0], text_turn[:, : features // 2].T, preferred_element_type=F32
    ) + jnp.dot(d_words[1], text_turn[:, features // 2 :].T, preferred_element_type=F32)
    d_words = d_words.reshape(micros, text_strip, features)[:, :text_slots]

    d_shift = jnp.transpose(d_shift.reshape(2, micros, ranks // 2, strip), (0, 2, 1, 3))
    d_shift = d_shift.reshape(ranks, micros, strip)
    d_shift = jnp.stack([d_shift[cube.masks.index(mask)] for mask in range(ranks)])
    d_shift = cube.add(cube.trade(d_shift), "sp").reshape(ranks * micros, strip)
    term_mod = lax.dot_general(
        time_part.astype(F32), d_shift, (((0,), (0,)), ((), ())), precision=lax.Precision.HIGHEST
    )

    places = jnp.array([cube.masks.index(mask) for mask in range(ranks)], jnp.int32)
    places = places[jnp.arange(ranks, dtype=jnp.int32) ^ cube.rank]
    gains = jnp.stack([d_gain_skip, d_gain_attn, d_gain_cross, d_gain_mlp])
    gains = gains.reshape(4, ranks, strip)[:, places].reshape(-1)
    heads = jnp.stack([jnp.sum(d_gain_q, (0, 1)), jnp.sum(d_gain_k, (0, 1))])
    heads = jnp.sum(heads[:, : local * HP].reshape(2, local, HP)[:, :, :HD], 1)
    packed = jnp.concatenate([gains, heads.reshape(-1)])
    packed = cube.add(cube.add(packed, "sp"), "dp")
    gains = packed[: 4 * width].reshape(4, ranks * parts, -1)
    gains = lax.dynamic_index_in_dim(gains, cube.rank * parts + zone, 1, keepdims=False)
    heads = packed[4 * width :].reshape(2, HD)

    def whole(term, groups):
        return cut_heads(term.astype(F32), local).reshape(term.shape[0], groups, -1)

    return (
        result.reshape(tokens.shape),
        d_joined[0].reshape(tokens.shape),
        d_joined[1].reshape(tokens.shape),
        d_words.reshape(text.shape),
        term_skip.astype(F32)[:, :kept].T,
        term_mod,
        whole(term_qkv, 3),
        cut_heads(term_cross[:, :lanes].astype(F32), local).T,
        cut_heads(term_cross[:, lanes : 2 * lanes].astype(F32), local),
        whole(term_text, 2),
        cut_heads(term_cross[:, 2 * lanes :].astype(F32), local).T,
        term_fc1.astype(F32),
        term_fc2.astype(F32).T,
        gains[0],
        gains[1],
        gains[2],
        gains[3],
        heads[0],
        heads[1],
    )


def solution(mesh):
    rows = P(None, ("dp", "sp"), None)
    column = P("sp", "dp")
    row = P("dp", "sp")
    grouped = P("dp", None, "sp")
    in_specs = (
        (rows, rows, rows, P(None, "dp"), P(None, "dp", None), P(None, "dp", None))
        + (column, column, grouped, column, row, grouped, column, row, column)
        + (P(),) * 6
        + (rows,)
    )
    out_specs = (
        (rows, rows, rows, rows)
        + (column, column, grouped, column, row, grouped, column, row, column)
        + (P(("dp", "sp")),) * 4
        + (P(), P())
    )
    return jax.shard_map(
        on_device, mesh=mesh, in_specs=in_specs, out_specs=out_specs, check_vma=False
    )
```

```python
import math

import jax
import jax.numpy as jnp
from jax import lax
from jax.experimental import pallas as pl
from jax.experimental.pallas import tpu as pltpu
from jax.sharding import PartitionSpec as P

H = 16
HD = 88
HP = 96
CLIP_LEN = 77
ROWS = 256

EPS = 1e-06
MASKED = -1e30
LOG2E = 1.4426950408889634
BF = jnp.bfloat16
F32 = jnp.float32


def time_embed(step, width):
    half = width // 2
    rate = jnp.exp(-math.log(10000.0) * jnp.arange(half, dtype=F32) / half)
    angle = step.astype(F32)[..., None] * rate
    return jnp.concatenate([jnp.cos(angle), jnp.sin(angle)], -1)


def rope_tables(sequence, wide, lanes):
    place = jnp.arange(sequence, dtype=jnp.int32)[None, :, None]
    wide = wide[:, None, None]
    lane = jnp.arange(lanes, dtype=jnp.int32)[None, None, :] % HP
    pair = lane // 2
    quarter = HD // 4
    upper = pair < quarter
    rank = jnp.where(upper, pair, pair - quarter).astype(F32)
    rate = jnp.exp(-math.log(10000.0) * rank / quarter)
    angle = jnp.where(upper, place // wide, place % wide).astype(F32) * rate
    sine = jnp.sin(angle)
    return jnp.cos(angle), jnp.where(lane % 2 == 0, -sine, sine)


def pad_heads(packed, local):
    rows, lanes = packed.shape
    groups = packed.reshape(rows, lanes // (local * HD), local, HD)
    groups = jnp.pad(groups, ((0, 0), (0, 0), (0, 0), (0, HP - HD)))
    groups = groups.reshape(rows, -1, local * HP)
    return jnp.pad(groups, ((0, 0), (0, 0), (0, -local * HP % 128))).reshape(rows, -1)


def cut_heads(padded, local):
    rows = padded.shape[0]
    groups = padded.reshape(rows, -1, local * HP + -local * HP % 128)[:, :, : local * HP]
    return groups.reshape(rows, -1, local, HP)[..., :HD].reshape(rows, -1)


def head_masks(shape, local):
    lane = lax.broadcasted_iota(jnp.int32, shape, len(shape) - 1)
    inside = lane % HP < HD
    return [((lane // HP == h) & inside).astype(F32) for h in range(local)]


def head_mean(value, masks):
    total = None
    for mask in masks:
        term = (jnp.sum(value * mask, -1, keepdims=True) * (1.0 / HD)) * mask
        total = term if total is None else total + term
    return total


def head_unit(value, masks):
    centre = value - head_mean(value, masks)
    spread = None
    square = centre * centre
    for mask in masks:
        mean = jnp.sum(square * mask, -1, keepdims=True) * (1.0 / HD)
        term = lax.rsqrt(mean + EPS) * mask
        spread = term if spread is None else spread + term
    return centre * spread, spread


def turn_pairs(value):
    lanes = value.shape[-1]
    after = pltpu.roll(value, lanes - 1, 1)
    before = pltpu.roll(value, 1, 1)
    lane = lax.broadcasted_iota(jnp.int32, value.shape, 1)
    return jnp.where(lane % 2 == 0, after, before)


def dot_nt(left, right):
    return lax.dot_general(left, right, (((1,), (1,)), ((), ())), preferred_element_type=F32)


def dot_nn(left, right):
    return lax.dot_general(left, right, (((1,), (0,)), ((), ())), preferred_element_type=F32)


def dot_tn(left, right):
    return lax.dot_general(left, right, (((0,), (0,)), ((), ())), preferred_element_type=F32)


def self_forward(raw, counts, cosine, sine, gain_q, gain_k):
    parts, micros, slots, packed = raw.shape
    lanes = packed // 3
    local = lanes // HP
    sequence = parts * slots
    factor = HD ** (-0.5) * LOG2E

    def kernel(count_ref, raw_ref, cos_ref, sin_ref, gq_ref, gk_ref, out_ref, q_ref, k_ref, lse_ref):
        count = count_ref[pl.program_id(0)]
        blocks = (count + slots - 1) // slots
        out_ref[...] = jnp.zeros_like(out_ref)
        masks = head_masks((1, lanes), local)

        def prepare(part, carry):
            spot = pl.ds(pl.multiple_of(part * slots, slots), slots)
            cosine, sine = cos_ref[0, spot, :], sin_ref[0, spot, :]
            for index, gain_ref, dest in ((0, gq_ref, q_ref), (1, gk_ref, k_ref)):
                value = raw_ref[part, 0, :, index * lanes : (index + 1) * lanes].astype(F32)
                scaled = head_unit(value, masks)[0] * gain_ref[...]
                dest[0, spot, :] = (scaled * cosine + turn_pairs(scaled) * sine).astype(BF)
            return carry

        lax.fori_loop(0, parts, prepare, 0)
        column = lax.broadcasted_iota(jnp.int32, (1, sequence), 1)
        bias = jnp.where(column < count, 0.0, MASKED)
        for h in range(local):
            cut = slice(h * HP, (h + 1) * HP)
            keys = k_ref[0, :, cut]
            values = raw_ref[:, 0, :, 2 * lanes + h * HP : 2 * lanes + (h + 1) * HP].reshape(sequence, HP)

            def one_block(part, carry):
                spot = pl.ds(pl.multiple_of(part * slots, slots), slots)
                scores = dot_nt(q_ref[0, spot, cut], keys) + bias
                top = jnp.max(scores, -1, keepdims=True)
                raised = jnp.exp2((scores - top) * factor)
                total = jnp.sum(raised, -1, keepdims=True)
                result = dot_nn(raised.astype(BF), values) / total
                out_ref[part, 0, :, cut] = result.astype(BF)
                norm = jnp.broadcast_to(top * factor + jnp.log2(total), (slots, 128))
                lse_ref[0, h : h + 1, spot] = jnp.transpose(norm)[0:1, :]
                return carry

            lax.fori_loop(0, blocks, one_block, 0)

    whole = lambda m, c: (0, m, 0, 0)
    table = lambda m, c: (m, 0, 0)
    fixed = lambda m, c: (0, 0)
    return pl.pallas_call(
        kernel,
        name="self_forward",
        grid_spec=pltpu.PrefetchScalarGridSpec(
            num_scalar_prefetch=1,
            grid=(micros,),
            in_specs=[
                pl.BlockSpec((parts, 1, slots, packed), whole),
                pl.BlockSpec((1, sequence, lanes), table),
                pl.BlockSpec((1, sequence, lanes), table),
                pl.BlockSpec((1, lanes), fixed),
                pl.BlockSpec((1, lanes), fixed),
            ],
            out_specs=[
                pl.BlockSpec((parts, 1, slots, lanes), whole),
                pl.BlockSpec((1, sequence, lanes), table),
                pl.BlockSpec((1, sequence, lanes), table),
                pl.BlockSpec((1, local, sequence), table),
            ],
        ),
        out_shape=[
            jax.ShapeDtypeStruct((parts, micros, slots, lanes), BF),
            jax.ShapeDtypeStruct((micros, sequence, lanes), BF),
            jax.ShapeDtypeStruct((micros, sequence, lanes), BF),
            jax.ShapeDtypeStruct((micros, local, sequence), F32),
        ],
        compiler_params=params(),
        cost_estimate=cost(4 * micros * local * sequence * sequence * HP),
    )(counts, raw, cosine, sine, gain_q, gain_k)


def self_backward(raw, counts, cosine, sine, gain_q, gain_k, turned_q, turned_k, norms, incoming):
    parts, micros, slots, packed = raw.shape
    lanes = packed // 3
    local = lanes // HP
    sequence = parts * slots
    scale = HD ** (-0.5)
    factor = scale * LOG2E

    def kernel(
        count_ref,
        raw_ref,
        cos_ref,
        sin_ref,
        gq_ref,
        gk_ref,
        q_ref,
        k_ref,
        lse_ref,
        in_ref,
        out_ref,
        dgq_ref,
        dgk_ref,
        dq_s,
        dk_s,
        dv_s,
    ):
        count = count_ref[pl.program_id(0)]
        blocks = (count + slots - 1) // slots
        dq_s[...] = jnp.zeros_like(dq_s)
        dk_s[...] = jnp.zeros_like(dk_s)
        dv_s[...] = jnp.zeros_like(dv_s)
        row = lax.broadcasted_iota(jnp.int32, (sequence, 1), 0)
        bias = jnp.where(row < count, 0.0, MASKED)
        for h in range(local):
            cut = slice(h * HP, (h + 1) * HP)
            keys = k_ref[0, :, cut]
            values = raw_ref[:, 0, :, 2 * lanes + h * HP : 2 * lanes + (h + 1) * HP].reshape(sequence, HP)

            def one_block(part, carry):
                spot = pl.ds(pl.multiple_of(part * slots, slots), slots)
                rows = q_ref[0, spot, cut]
                grads = in_ref[part, 0, :, cut]
                norm = lse_ref[0, h : h + 1, spot]
                probs = jnp.exp2(dot_nt(keys, rows) * factor + bias - norm)
                d_probs = dot_nt(values, grads)
                inner = jnp.sum(probs * d_probs, 0, keepdims=True)
                d_scores = (probs * (d_probs - inner)).astype(BF)
                dv_s[:, cut] += dot_nn(probs.astype(BF), grads)
                dk_s[:, cut] += dot_nn(d_scores, rows)
                dq_s[spot, cut] = dot_tn(d_scores, keys)
                return carry

            lax.fori_loop(0, blocks, one_block, 0)
        masks = head_masks((1, lanes), local)

        def finish(part, carry):
            spot = pl.ds(pl.multiple_of(part * slots, slots), slots)
            cosine, sine = cos_ref[0, spot, :], sin_ref[0, spot, :]
            sums = []
            for index, gain_ref, source in ((0, gq_ref, dq_s), (1, gk_ref, dk_s)):
                grad = source[spot, :] * scale
                grad = grad * cosine - turn_pairs(grad) * sine
                value = raw_ref[part, 0, :, index * lanes : (index + 1) * lanes].astype(F32)
                unit, spread = head_unit(value, masks)
                leading = grad * gain_ref[...]
                back = leading - head_mean(leading, masks) - unit * head_mean(leading * unit, masks)
                out_ref[part, 0, :, index * lanes : (index + 1) * lanes] = (spread * back).astype(BF)
                sums.append(carry[index] + jnp.sum(grad * unit, 0, keepdims=True))
            out_ref[part, 0, :, 2 * lanes : 3 * lanes] = dv_s[spot, :].astype(BF)
            return tuple(sums)

        zero = jnp.zeros((1, lanes), F32)
        d_gains = lax.fori_loop(0, parts, finish, (zero, zero))
        dgq_ref[0] = d_gains[0]
        dgk_ref[0] = d_gains[1]

    whole = lambda m, c: (0, m, 0, 0)
    table = lambda m, c: (m, 0, 0)
    fixed = lambda m, c: (0, 0)
    return pl.pallas_call(
        kernel,
        name="self_backward",
        grid_spec=pltpu.PrefetchScalarGridSpec(
            num_scalar_prefetch=1,
            grid=(micros,),
            in_specs=[
                pl.BlockSpec((parts, 1, slots, packed), whole),
                pl.BlockSpec((1, sequence, lanes), table),
                pl.BlockSpec((1, sequence, lanes), table),
                pl.BlockSpec((1, lanes), fixed),
                pl.BlockSpec((1, lanes), fixed),
                pl.BlockSpec((1, sequence, lanes), table),
                pl.BlockSpec((1, sequence, lanes), table),
                pl.BlockSpec((1, local, sequence), table),
                pl.BlockSpec((parts, 1, slots, lanes), whole),
            ],
            out_specs=[
                pl.BlockSpec((parts, 1, slots, packed), whole),
                pl.BlockSpec((1, 1, lanes), table),
                pl.BlockSpec((1, 1, lanes), table),
            ],
            scratch_shapes=[pltpu.VMEM((sequence, lanes), F32) for index in range(3)],
        ),
        out_shape=[
            jax.ShapeDtypeStruct((parts, micros, slots, packed), BF),
            jax.ShapeDtypeStruct((micros, 1, lanes), F32),
            jax.ShapeDtypeStruct((micros, 1, lanes), F32),
        ],
        compiler_params=params(),
        cost_estimate=cost(10 * micros * local * sequence * sequence * HP),
    )(counts, raw, cosine, sine, gain_q, gain_k, turned_q, turned_k, norms, incoming)


def cost(flops):
    return pl.CostEstimate(flops=flops // 16, bytes_accessed=flops // 16000, transcendentals=0)


def full(shape):
    return pl.BlockSpec(shape, lambda *index: (0,) * len(shape))


def params(megabytes=60):
    return pltpu.CompilerParams(vmem_limit_bytes=megabytes << 20)


class Lanes:
    def __init__(self, near, far, block=None, index=0):
        self.near, self.far = near, far
        self.block = block or near.shape[2]
        self.index = index

    def spec(self):
        index = self.index
        return pl.BlockSpec((1, self.near.shape[1], self.block), lambda p, *rest: (p, 0, index))


def to_lanes(value, weights, dtype=BF, name="to_lanes"):
    rows = value.shape[1]
    parts, half, _ = weights[0].near.shape
    total = sum(weight.block for weight in weights)

    def kernel(x_ref, *refs):
        out_ref = refs[-1]
        at = 0
        for index, weight in enumerate(weights):
            result = dot_nn(x_ref[0], refs[2 * index][0]) + dot_nn(x_ref[1], refs[2 * index + 1][0])
            out_ref[0, :, at : at + weight.block] = result.astype(dtype)
            at += weight.block

    return pl.pallas_call(
        kernel,
        name=name,
        grid=(parts,),
        in_specs=[full(value.shape)] + [weight.spec() for weight in weights for side in range(2)],
        out_specs=pl.BlockSpec((1, rows, total), lambda p: (p, 0, 0)),
        out_shape=jax.ShapeDtypeStruct((parts, rows, total), dtype),
        compiler_params=params(),
        cost_estimate=cost(4 * rows * half * parts * total),
    )(value, *[side for weight in weights for side in (weight.near, weight.far)])


def to_inputs(value, weights, kept):
    rows = value.shape[1]
    parts, half, _ = weights[0].near.shape
    sides = parts // 2

    def kernel(x_ref, *refs):
        out_ref = refs[-1]
        for side in range(sides):

            @pl.when(pl.program_id(0) % sides == side)
            def _():
                at = 0
                for index, weight in enumerate(weights):
                    result = dot_nn(x_ref[0], refs[2 * index][0]) + dot_nn(
                        x_ref[1], refs[2 * index + 1][0]
                    )
                    take = min(weight.block, kept - at)
                    start = side * kept + at
                    out_ref[0, :, start : start + take] = result[:, :take]
                    at += take

    return pl.pallas_call(
        kernel,
        name="to_inputs",
        grid=(parts,),
        in_specs=[full(value.shape)] + [weight.spec() for weight in weights for side in range(2)],
        out_specs=pl.BlockSpec((1, rows, sides * kept), lambda p: (p // sides, 0, 0)),
        out_shape=jax.ShapeDtypeStruct((2, rows, sides * kept), F32),
        compiler_params=params(),
        cost_estimate=cost(4 * rows * half * parts * kept),
    )(value, *[side for weight in weights for side in (weight.near, weight.far)])


def to_features(value, weights, extras, outs, finish, name="to_features"):
    parts, rows, total = value.shape
    half = weights[0].near.shape[1]
    count = 2 * len(weights)

    def kernel(*refs):
        y_ref, weight_refs = refs[0], refs[1 : 1 + count]
        extra_refs = refs[1 + count : 1 + count + len(extras)]
        out_refs = refs[1 + count + len(extras) : -1]
        sums = refs[-1]

        @pl.when(pl.program_id(0) == 0)
        def _():
            sums[...] = jnp.zeros_like(sums)

        at = 0
        for index, weight in enumerate(weights):
            left = y_ref[0, :, at : at + weight.block]
            for side in range(2):
                sums[side] += dot_nt(left, weight_refs[2 * index + side][0])
            at += weight.block

        @pl.when(pl.program_id(0) == parts - 1)
        def _():
            finish([sums[0], sums[1]], extra_refs, out_refs)

    return pl.pallas_call(
        kernel,
        name=name,
        grid=(parts,),
        in_specs=[pl.BlockSpec((1, rows, total), lambda p: (p, 0, 0))]
        + [weight.spec() for weight in weights for side in range(2)]
        + [full(extra.shape) for extra in extras],
        out_specs=[full(out.shape) for out in outs],
        out_shape=outs,
        scratch_shapes=[pltpu.VMEM((2, rows, half), F32)],
        compiler_params=params(),
        cost_estimate=cost(4 * rows * half * parts * total),
    )(value, *[side for weight in weights for side in (weight.near, weight.far)], *extras)


def terms_of(pairs, name="terms_of"):
    half = pairs[0][0].shape[2]
    parts = pairs[0][1].shape[0]
    total = sum(pair[2] for pair in pairs)
    rows = [pair[0].shape[1] for pair in pairs]

    def kernel(*refs):
        count = len(pairs)
        lefts, rights = refs[:count], refs[count : 2 * count]
        near_ref, far_ref = refs[2 * count : 2 * count + 2]
        turned = refs[2 * count + 2 :]

        @pl.when(pl.program_id(0) == 0)
        def _():
            for left, flat in zip(lefts, turned):
                for side in range(2):
                    flat[side] = jnp.transpose(left[side])

        at = 0
        for pair, right, flat in zip(pairs, rights, turned):
            lanes = pair[2]
            near_ref[0, :, at : at + lanes] = dot_nn(flat[0], right[0]).astype(BF)
            far_ref[0, :, at : at + lanes] = dot_nn(flat[1], right[0]).astype(BF)
            at += lanes

    def right_spec(pair):
        return pl.BlockSpec((1, pair[1].shape[1], pair[2]), lambda p: (p, 0, pair[3]))

    out = jax.ShapeDtypeStruct((parts, half, total), BF)
    return pl.pallas_call(
        kernel,
        name=name,
        grid=(parts,),
        in_specs=[full(pair[0].shape) for pair in pairs] + [right_spec(pair) for pair in pairs],
        out_specs=[pl.BlockSpec((1, half, total), lambda p: (p, 0, 0))] * 2,
        out_shape=[out, out],
        scratch_shapes=[pltpu.VMEM((2, half, count), BF) for count in rows],
        compiler_params=params(),
        cost_estimate=cost(sum(4 * half * parts * pair[2] * count for pair, count in zip(pairs, rows))),
    )(*[pair[0] for pair in pairs], *[pair[1] for pair in pairs])


def norm_unit(halves):
    width = 2 * halves[0].shape[-1]
    mean = sum(jnp.sum(half, -1, keepdims=True) for half in halves) / width
    centre = [half - mean for half in halves]
    spread = sum(jnp.sum(half * half, -1, keepdims=True) for half in centre) / width
    scale = lax.rsqrt(spread + EPS)
    return [half * scale for half in centre], scale


def norm_back(halves, gain_ref, incoming):
    width = 2 * halves[0].shape[-1]
    unit, scale = norm_unit(halves)
    leading = [incoming[side] * gain_ref[side] for side in range(2)]
    mean = sum(jnp.sum(half, -1, keepdims=True) for half in leading) / width
    inner = sum(jnp.sum(leading[side] * unit[side], -1, keepdims=True) for side in range(2)) / width
    back = [scale * (leading[side] - mean - unit[side] * inner) for side in range(2)]
    gains = [jnp.sum(incoming[side] * unit[side], 0, keepdims=True) for side in range(2)]
    return back, gains


def join_rows(pieces, rows, name="join_rows"):
    parts, _, lanes = pieces[0][0].shape
    count = len(pieces)
    if rows % 16:
        return jnp.concatenate([array[:, block * rows : (block + 1) * rows] for array, block in pieces], 1)

    def kernel(*refs):
        for index in range(count):
            refs[-1][0, index * rows : (index + 1) * rows] = refs[index][0]

    def spec(block):
        return pl.BlockSpec((1, rows, lanes), lambda p: (p, block, 0))

    return pl.pallas_call(
        kernel,
        name=name,
        grid=(parts,),
        in_specs=[spec(block) for _, block in pieces],
        out_specs=pl.BlockSpec((1, count * rows, lanes), lambda p: (p, 0, 0)),
        out_shape=jax.ShapeDtypeStruct((parts, count * rows, lanes), BF),
        compiler_params=params(),
        cost_estimate=cost(parts * count * rows * lanes),
    )(*[array for array, _ in pieces])


def sum_rows(jobs, rows, name="sum_rows"):
    parts = jobs[0][1][0][0].shape[0]
    if rows % 16:
        results = []
        for lanes, terms in jobs:
            value = 0.0
            for array, blocks, spot in terms:
                split = array[:, :, spot * lanes : (spot + 1) * lanes].reshape(parts, -1, rows, lanes)
                value = value + jnp.stack([split[:, block] for block in blocks], 1).astype(F32)
            results.append(value.astype(BF).reshape(parts, -1, lanes))
        return results
    spots = [
        (array, blocks[index], spot, lanes)
        for lanes, terms in jobs
        for index in range(len(terms[0][1]))
        for array, blocks, spot in terms
    ]

    def kernel(*refs):
        at = 0
        for order, (_, terms) in enumerate(jobs):
            out_ref = refs[len(spots) + order]
            for index in range(len(terms[0][1])):
                value = refs[at][0].astype(F32)
                for offset in range(1, len(terms)):
                    value = value + refs[at + offset][0].astype(F32)
                out_ref[0, index * rows : (index + 1) * rows] = value.astype(BF)
                at += len(terms)

    def spec(block, spot, lanes):
        return pl.BlockSpec((1, rows, lanes), lambda p: (p, block, spot))

    shapes = [(len(terms[0][1]) * rows, lanes) for lanes, terms in jobs]
    return pl.pallas_call(
        kernel,
        name=name,
        grid=(parts,),
        in_specs=[spec(*rest) for _, *rest in spots],
        out_specs=[pl.BlockSpec((1, *shape), lambda p: (p, 0, 0)) for shape in shapes],
        out_shape=[jax.ShapeDtypeStruct((parts, *shape), BF) for shape in shapes],
        compiler_params=params(),
        cost_estimate=cost(sum(parts * size * lanes for size, lanes in shapes)),
    )(*[array for array, *_ in spots])


def side_by_side(left, right, kept, lanes):
    rows, width = left.shape
    count = width // kept

    def kernel(left_ref, right_ref, out_ref):
        for index, ref in enumerate((left_ref, right_ref)):
            for side in range(count):
                spot = count * index + side
                out_ref[spot, :, :kept] = ref[:, side * kept : (side + 1) * kept]
                if lanes > kept:
                    out_ref[spot, :, kept:] = jnp.zeros((rows, lanes - kept), BF)

    return pl.pallas_call(
        kernel,
        name="side_by_side",
        out_shape=jax.ShapeDtypeStruct((2 * count, rows, lanes), BF),
        compiler_params=params(),
        cost_estimate=cost(4 * rows * lanes),
    )(left, right)


def mlp_forward(rows_in, grads, start, weight1, weight2, part, live=None):
    _, rows, half = rows_in.shape
    parts, _, lanes = weight1.near.shape
    ff = lanes // 2
    step = 768 if ff % 768 == 0 else ff
    steps = ff // step
    extras = [] if live is None else [live]

    def kernel(x_ref, g_ref, s_ref, n1_ref, f1_ref, n2_ref, f2_ref, *refs):
        hid_ref, act_ref, out_ref, dn2_ref, df2_ref, turned, sums = refs[len(extras) :]
        first = (pl.program_id(0) == 0) & (pl.program_id(1) == 0)
        last = (pl.program_id(0) == parts - 1) & (pl.program_id(1) == steps - 1)

        @pl.when(first)
        def _():
            for side in range(2):
                turned[side] = jnp.transpose(g_ref[side])
            sums[...] = s_ref[...]

        hidden = dot_nn(x_ref[0], n1_ref[0]) + dot_nn(x_ref[1], f1_ref[0])
        hid_ref[0] = hidden
        activ = jax.nn.gelu(hidden, approximate=True).astype(BF)
        act_ref[0] = activ
        sums[0] += dot_nt(activ, n2_ref[0])
        sums[1] += dot_nt(activ, f2_ref[0])
        dn2_ref[0] = dot_nn(turned[0], activ).astype(BF)
        df2_ref[0] = dot_nn(turned[1], activ).astype(BF)

        @pl.when(last)
        def _():
            if live is None:
                out_ref[...] = sums[...]
            else:
                out_ref[...] = (sums[...] * refs[0][...]).astype(BF)

    weight = pl.BlockSpec((1, half, step), lambda p, n: (p, 0, part * steps + n))
    grad = pl.BlockSpec((1, half, step), lambda p, n: (p, 0, n))
    unit = pl.BlockSpec((1, rows, step), lambda p, n: (p, 0, n))
    whole = full((2, rows, half))
    grad_shape = jax.ShapeDtypeStruct((parts, half, ff), BF)
    return pl.pallas_call(
        kernel,
        name="mlp_forward",
        grid=(parts, steps),
        in_specs=[whole, whole, whole, weight, weight, weight, weight] + [full(extra.shape) for extra in extras],
        out_specs=[unit, unit, whole, grad, grad],
        out_shape=[
            jax.ShapeDtypeStruct((parts, rows, ff), F32),
            jax.ShapeDtypeStruct((parts, rows, ff), BF),
            jax.ShapeDtypeStruct((2, rows, half), F32 if live is None else BF),
            grad_shape,
            grad_shape,
        ],
        scratch_shapes=[pltpu.VMEM((2, half, rows), BF), pltpu.VMEM((2, rows, half), F32)],
        compiler_params=params(),
        cost_estimate=cost(12 * rows * half * parts * ff),
    )(rows_in, grads, start, weight1.near, weight1.far, weight2.near, weight2.far, *extras)


def gelu_slope(value):
    root = math.sqrt(2.0 / math.pi)
    square = value * value
    curve = jnp.tanh(root * value * (1.0 + 0.044715 * square))
    return 0.5 * (1.0 + curve) + 0.5 * value * (1.0 - curve * curve) * root * (
        1.0 + 3.0 * 0.044715 * square
    )


def mlp_backward(grads, rows_in, hidden, weight1, weight2, part, start, finish=None):
    _, rows, half = rows_in.shape
    parts, _, lanes = weight1.near.shape
    ff = lanes // 2
    step = 768 if ff % 768 == 0 else ff
    steps = ff // step
    extras = list(finish or []) + ([] if start is None else [start])

    def kernel(g_ref, x_ref, hid_ref, n1_ref, f1_ref, n2_ref, f2_ref, *refs):
        extra_refs, refs = refs[: len(extras)], refs[len(extras) :]
        dn1_ref, df1_ref = refs[:2]
        out_refs = refs[2:-2]
        turned, sums = refs[-2:]
        first = (pl.program_id(0) == 0) & (pl.program_id(1) == 0)
        last = (pl.program_id(0) == parts - 1) & (pl.program_id(1) == steps - 1)

        @pl.when(first)
        def _():
            for side in range(2):
                turned[side] = jnp.transpose(x_ref[side])
            sums[...] = jnp.zeros_like(sums) if start is None else extra_refs[-1][...]

        d_activ = dot_nn(g_ref[0], n2_ref[0]) + dot_nn(g_ref[1], f2_ref[0])
        d_hidden = (d_activ * gelu_slope(hid_ref[0])).astype(BF)
        dn1_ref[0] = dot_nn(turned[0], d_hidden).astype(BF)
        df1_ref[0] = dot_nn(turned[1], d_hidden).astype(BF)
        sums[0] += dot_nt(d_hidden, n1_ref[0])
        sums[1] += dot_nt(d_hidden, f1_ref[0])

        @pl.when(last)
        def _():
            if finish is None:
                out_refs[0][...] = sums[...]
            else:
                value_ref, gain_ref, add_ref = extra_refs[:3]
                add_norm_back([sums[0], sums[1]], value_ref, gain_ref, add_ref, *out_refs)

    weight = pl.BlockSpec((1, half, step), lambda p, n: (p, 0, part * steps + n))
    grad = pl.BlockSpec((1, half, step), lambda p, n: (p, 0, n))
    unit = pl.BlockSpec((1, rows, step), lambda p, n: (p, 0, n))
    whole = full((2, rows, half))
    grad_shape = jax.ShapeDtypeStruct((parts, half, ff), BF)
    wide = jax.ShapeDtypeStruct((2, rows, half), F32)
    outs = [wide] if finish is None else [wide, *back_shapes(rows, half)]
    return pl.pallas_call(
        kernel,
        name="mlp_backward",
        grid=(parts, steps),
        in_specs=[whole, whole, unit, weight, weight, weight, weight] + [full(extra.shape) for extra in extras],
        out_specs=[grad, grad] + [full(out.shape) for out in outs],
        out_shape=[grad_shape, grad_shape] + outs,
        scratch_shapes=[pltpu.VMEM((2, half, rows), BF), pltpu.VMEM((2, rows, half), F32)],
        compiler_params=params(),
        cost_estimate=cost(12 * rows * half * parts * ff),
    )(grads, rows_in, hidden, weight1.near, weight1.far, weight2.near, weight2.far, *extras)


def back_shapes(rows, half):
    return [jax.ShapeDtypeStruct((2, rows, half), BF), jax.ShapeDtypeStruct((2, 1, half), F32)]


def add_norm_back(incoming, value_ref, gain_ref, add_ref, out_ref, low_ref, d_gain_ref):
    back, gains = norm_back([value_ref[0], value_ref[1]], gain_ref, incoming)
    for side in range(2):
        total = add_ref[side] + back[side]
        out_ref[side] = total
        low_ref[side] = total.astype(BF)
        d_gain_ref[side] = gains[side]


def text_bias(lengths_ref, micro, words, strip, text_slots, axis):
    spot = lax.broadcasted_iota(jnp.int32, (1, words) if axis else (words, 1), axis)
    inner = spot % strip
    place = spot // strip * text_slots + inner
    live = (place < lengths_ref[micro, 0]) | (
        (place >= CLIP_LEN) & (place < CLIP_LEN + lengths_ref[micro, 1])
    )
    return jnp.where(live & (inner < text_slots), 0.0, MASKED)


def cross_forward(query, text_kv, lengths, text_slots):
    parts, micros, slots, lanes = query.shape
    zones, strip = text_kv.shape[1], text_kv.shape[3]
    words = zones * strip
    local = lanes // HP
    factor = HD ** (-0.5) * LOG2E

    def kernel(len_ref, q_ref, kv_ref, out_ref):
        bias = text_bias(len_ref, pl.program_id(1), words, strip, text_slots, 1)
        for h in range(local):
            cut = slice(h * HP, (h + 1) * HP)
            keys = kv_ref[0, :, 0, :, cut].reshape(words, HP)
            scores = dot_nt(q_ref[0, 0, :, cut], keys) + bias
            top = jnp.max(scores, -1, keepdims=True)
            raised = jnp.exp2((scores - top) * factor)
            total = jnp.sum(raised, -1, keepdims=True)
            values = kv_ref[0, :, 0, :, lanes + h * HP : lanes + (h + 1) * HP].reshape(words, HP)
            out_ref[0, 0, :, cut] = (dot_nn(raised.astype(BF), values) / total).astype(BF)

    spot = lambda p, m, c: (p, m, 0, 0)
    far = lambda p, m, c: (p, 0, m, 0, 0)
    return pl.pallas_call(
        kernel,
        name="cross_forward",
        grid_spec=pltpu.PrefetchScalarGridSpec(
            num_scalar_prefetch=1,
            grid=(parts, micros),
            in_specs=[
                pl.BlockSpec((1, 1, slots, lanes), spot),
                pl.BlockSpec((1, zones, 1, strip, 2 * lanes), far),
            ],
            out_specs=pl.BlockSpec((1, 1, slots, lanes), spot),
        ),
        out_shape=jax.ShapeDtypeStruct(query.shape, BF),
        compiler_params=params(),
        cost_estimate=cost(4 * parts * micros * slots * words * lanes),
    )(lengths, query, text_kv)


def cross_backward(query, text_kv, lengths, incoming, text_slots):
    parts, micros, slots, lanes = query.shape
    zones, strip = text_kv.shape[1], text_kv.shape[3]
    words = zones * strip
    local = lanes // HP
    scale = HD ** (-0.5)
    factor = scale * LOG2E

    def kernel(len_ref, q_ref, kv_ref, in_ref, dq_ref, dkv_ref):
        bias = text_bias(len_ref, pl.program_id(1), words, strip, text_slots, 0)
        for h in range(local):
            cut = slice(h * HP, (h + 1) * HP)
            far = slice(lanes + h * HP, lanes + (h + 1) * HP)
            rows = q_ref[0, 0, :, cut]
            keys = kv_ref[0, :, 0, :, cut].reshape(words, HP)
            values = kv_ref[0, :, 0, :, far].reshape(words, HP)
            grads = in_ref[0, 0, :, cut]
            scores = dot_nt(keys, rows) + bias
            top = jnp.max(scores, 0, keepdims=True)
            raised = jnp.exp2((scores - top) * factor)
            probs = raised * (1.0 / jnp.sum(raised, 0, keepdims=True))
            d_probs = dot_nt(values, grads)
            inner = jnp.sum(probs * d_probs, 0, keepdims=True)
            d_scores = (probs * (d_probs - inner)).astype(BF)
            shape = (zones, strip, HP)
            dkv_ref[0, :, 0, :, far] = dot_nn(probs.astype(BF), grads).astype(BF).reshape(shape)
            dkv_ref[0, :, 0, :, cut] = (dot_nn(d_scores, rows) * scale).astype(BF).reshape(shape)
            dq_ref[0, 0, :, cut] = (dot_tn(d_scores, keys) * scale).astype(BF)

    spot = lambda p, m, c: (p, m, 0, 0)
    far = lambda p, m, c: (p, 0, m, 0, 0)
    return pl.pallas_call(
        kernel,
        name="cross_backward",
        grid_spec=pltpu.PrefetchScalarGridSpec(
            num_scalar_prefetch=1,
            grid=(parts, micros),
            in_specs=[
                pl.BlockSpec((1, 1, slots, lanes), spot),
                pl.BlockSpec((1, zones, 1, strip, 2 * lanes), far),
                pl.BlockSpec((1, 1, slots, lanes), spot),
            ],
            out_specs=[
                pl.BlockSpec((1, 1, slots, lanes), spot),
                pl.BlockSpec((1, zones, 1, strip, 2 * lanes), far),
            ],
        ),
        out_shape=[
            jax.ShapeDtypeStruct(query.shape, BF),
            jax.ShapeDtypeStruct(text_kv.shape, BF),
        ],
        compiler_params=params(),
        cost_estimate=cost(10 * parts * micros * slots * words * lanes),
    )(lengths, query, text_kv, incoming)


def tie(*values):
    return lax.optimization_barrier(values)


class Cube:
    def __init__(self):
        self.size = lax.axis_size("dp")
        self.bits = self.size.bit_length() - 1
        self.outer = list(range(1, self.bits))
        self.rank = lax.axis_index("dp")
        self.masks = []
        for place in range(self.size):
            mask = place >> (self.bits - 1)
            for bit in self.outer:
                mask |= ((place >> (bit - 1)) & 1) << bit
            self.masks.append(mask)
        self.owners = self.rank ^ jnp.array(self.masks, jnp.int32)

    def swap(self, value, bit, axis="dp"):
        pairs = [(i, i ^ (1 << bit)) for i in range(lax.axis_size(axis))]
        return lax.ppermute(value, axis, pairs)

    def trade(self, value):
        blocks = {mask: value[mask] for mask in range(self.size)}
        for bit in range(self.bits):
            send = sorted(mask for mask in blocks if mask >> bit & 1)
            got = self.swap(jnp.stack([blocks[mask] for mask in send]), bit)
            for place, mask in enumerate(send):
                blocks[mask] = got[place]
        return jnp.stack([blocks[mask] for mask in range(self.size)])

    def spread(self, value):
        held = value[None]
        for bit in range(self.bits):
            held = jnp.concatenate([held, self.swap(held, bit)])
        return held

    def add(self, value, axis):
        for bit in range(lax.axis_size(axis).bit_length() - 1):
            value = value + self.swap(value, bit, axis)
        return value


class Gather:
    def __init__(self, cube, shard, flip, joined=False):
        self.cube = cube
        self.rows = shard.shape[1]
        self.masks = [[0]]
        self.pieces = [shard]
        self.todo = cube.outer[::-1] if flip else list(cube.outer)
        self.joined = joined

    def blocks(self, order):
        spots = {
            mask: (piece, index)
            for piece, masks in zip(self.pieces, self.masks)
            for index, mask in enumerate(masks)
        }
        return join_rows([spots[mask] for mask in order], self.rows)

    def move(self):
        bit = self.todo.pop(0)
        if self.joined and len(self.pieces) > 1:
            order = [mask for masks in self.masks for mask in masks]
            self.pieces, self.masks = [self.blocks(order)], [order]
        self.masks = self.masks + [[mask | (1 << bit) for mask in masks] for masks in self.masks]
        self.pieces = self.pieces + [self.cube.swap(piece, bit) for piece in self.pieces]

    def join(self):
        while self.todo:
            self.move()
        self.pieces = [self.blocks(self.cube.masks[: self.cube.size // 2])]

    def weight(self):
        near = self.pieces[0]
        return Lanes(near, self.cube.swap(near, 0))


class Scatter:
    def __init__(self, cube, near, other, flip, lanes=None, spot=0):
        self.cube = cube
        self.todo = list(cube.outer) if flip else cube.outer[::-1]
        self.rows = near.shape[1] // (cube.size // 2)
        self.places = list(range(cube.size // 2))
        self.near = near
        self.lanes = lanes or near.shape[2]
        self.spot = spot
        self.got = []
        self.pieces = [other]
        self.arriving = self.places

    def job(self, places):
        terms = [(self.near, places, self.spot)]
        for value, held, spot in self.got:
            terms.append((value, [held.index(place) for place in places], spot))
        return self.lanes, terms

    def absorb(self):
        self.got.append((self.pieces[0], self.arriving, 0 if self.got else self.spot))


def scatter(cube, terms, *shares):
    near, far = terms
    other = cube.swap(far, 0)
    return [Scatter(cube, near, other, flip, lanes, spot) for lanes, spot, flip in shares]


def pack(movers):
    jobs = []
    for mover in movers:
        mover.absorb()
        mover.bit = mover.todo.pop(0)
        weight = 1 << (mover.bit - 1)
        sent = [place for place in mover.places if place & weight]
        mover.places = [place for place in mover.places if not place & weight]
        mover.arriving = [place ^ weight for place in sent]
        jobs.append(mover.job(sent))
    for mover, value in zip(movers, sum_rows(jobs, movers[0].rows)):
        mover.pieces = [value]


def send(movers):
    for mover in movers:
        mover.pieces = [mover.cube.swap(mover.pieces[0], mover.bit)]


def results(movers):
    while movers[0].todo:
        pack(movers)
        send(movers)
    for mover in movers:
        mover.absorb()
    return sum_rows([mover.job([0]) for mover in movers], movers[0].rows)


def pin(value, *others):
    flat = []
    for other in others:
        flat += other.pieces if hasattr(other, "pieces") else [other]
    return tie(value, *flat)[0]


def bind(value, *movers):
    flat = [piece for mover in movers for piece in mover.pieces]
    held = tie(value, *flat)
    spot = 1
    for mover in movers:
        count = len(mover.pieces)
        mover.pieces = list(held[spot : spot + count])
        spot += count
    return held[0]


def hold(movers, *others):
    for mover in movers:
        mover.pieces = [pin(piece, *others) for piece in mover.pieces]


def on_device(
    tokens,
    skip_tokens,
    text,
    timestep,
    grid,
    text_len,
    w_skip,
    w_mod,
    w_qkv,
    w_out1,
    w_query2,
    w_text_kv,
    w_out2,
    w_fc1,
    w_fc2,
    gain_skip,
    gain_attn,
    gain_cross,
    gain_mlp,
    gain_query,
    gain_key,
    cotangent,
):
    micros, slots, width = tokens.shape
    parts = lax.axis_size("sp")
    zone = lax.axis_index("sp")
    cube = Cube()
    ranks = cube.size
    rows = micros * slots
    sequence = slots * parts
    local = H // parts
    lanes = local * HP + -local * HP % 128
    text_slots = text.shape[1]
    text_strip = -(-text_slots // 16) * 16
    features = text.shape[2]
    strip = width // ranks
    middle = width // 2
    kept = w_skip.shape[0]
    skip_lanes = -(-kept // 256) * 256
    skip_cut = skip_lanes // 2
    qkv_cut = (3 * lanes) // 256 * 128 + 128
    text_rows = w_text_kv.shape[0]

    def spread(shard, before=None):
        if before is not None:
            shard, before = tie(shard, before)
        return lax.all_gather(shard, "sp", axis=0, tiled=False)

    def fetch(value, cut, joined=False):
        return [Gather(cube, value[:, :, :cut], 0, joined), Gather(cube, value[:, :, cut:], 1, joined)]

    def advance(movers):
        for mover in movers:
            mover.move()

    def join(movers):
        for mover in movers:
            mover.join()

    def exchange(value):
        return lax.all_to_all(value, "sp", split_axis=0, concat_axis=0, tiled=True)

    skip_z = spread(jnp.pad(w_skip.T, ((0, 0), (0, skip_lanes - kept))))
    steps = cube.spread(timestep[:, 0])
    joined = side_by_side(tokens.reshape(rows, width), skip_tokens.reshape(rows, width), kept, skip_lanes)
    wide = grid[:, 0, 1]
    counts = grid[:, 0, 0] * wide
    cosine, sine = rope_tables(sequence, wide, lanes)
    skip_z, steps, joined, cosine, sine = tie(skip_z, steps, joined, cosine, sine)
    skip_m = fetch(skip_z, skip_cut)
    qkv_z = spread(pad_heads(w_qkv.reshape(strip, -1), local), skip_z)
    advance(skip_m)

    time_act = jax.nn.silu(time_embed(steps, width)).astype(BF).reshape(ranks * micros, parts, -1)
    time_part = lax.dynamic_index_in_dim(time_act, zone, 1, keepdims=False)
    shift = cube.add(jnp.dot(time_part, w_mod, preferred_element_type=F32), "sp")
    skip_m[0].pieces[1], shift = tie(skip_m[0].pieces[1], shift)
    while skip_m[0].todo:
        advance(skip_m)
    shift = cube.trade(shift.reshape(ranks, micros, strip))
    skip_m[0].pieces[-1], shift = tie(skip_m[0].pieces[-1], shift)
    shift = jnp.stack([shift[mask] for mask in cube.masks]).reshape(2, ranks // 2, micros, strip)
    shift = jnp.transpose(shift, (0, 2, 1, 3)).reshape(2, micros, middle)
    qkv_m = fetch(qkv_z, qkv_cut)
    hold(qkv_m, *skip_m)
    advance(qkv_m)
    cross_z = jnp.concatenate([pad_heads(side, local) for side in (w_out1.T, w_query2, w_out2.T)], 1)
    cross_z = spread(pin(cross_z, *skip_m))
    fc1_z = spread(pin(w_fc1, *skip_m))
    join(skip_m)
    skip_w = [mover.weight() for mover in skip_m]

    def shuffle(count):
        block = count // ranks
        place = jnp.arange(count, dtype=jnp.int32)
        source = cube.owners[place // block] * block + place % block
        return (place[:, None] == source[None, :]).astype(BF)

    turn = shuffle(width)
    text_turn = shuffle(features)
    gains = jnp.stack([gain_skip, gain_attn, gain_cross, gain_mlp])
    gains = gains.reshape(4, ranks, strip)[:, cube.owners].reshape(4, 2, 1, middle)
    g_skip, g_attn, g_cross, g_mlp = gains

    lengths = text_len[:, 0, :]
    place = zone * slots + jnp.arange(slots, dtype=jnp.int32)
    live = (place[None, :] < counts[:, None]).astype(F32).reshape(rows, 1)
    gain_q = pad_heads(jnp.tile(gain_query, local)[None, :], local)
    gain_k = pad_heads(jnp.tile(gain_key, local)[None, :], local)

    grad3 = jnp.stack(
        [
            jnp.dot(cotangent.reshape(rows, width), side, preferred_element_type=F32) * live
            for side in (turn[:, :middle], turn[:, middle:])
        ]
    )
    d_mlp = grad3.astype(BF)

    wide_shape = jax.ShapeDtypeStruct((2, rows, middle), F32)
    low_shape = jax.ShapeDtypeStruct((2, rows, middle), BF)
    gain_shape = jax.ShapeDtypeStruct((2, 1, middle), F32)

    def first_norms(sums, extra, out):
        g0_ref, g1_ref, shift_ref = extra
        base_ref, stream_ref, pre_ref = out
        unit, _ = norm_unit(sums)
        stream = [unit[side] * g0_ref[side] for side in range(2)]
        unit, _ = norm_unit(stream)
        for side in range(2):
            base_ref[side] = sums[side]
            stream_ref[side] = stream[side]
            for micro in range(micros):
                cut = slice(micro * slots, (micro + 1) * slots)
                pre = unit[side][cut] * g1_ref[side] + shift_ref[side, micro : micro + 1]
                pre_ref[side, cut] = pre.astype(BF)

    def next_norm(sums, extra, out):
        before_ref, gain_ref = extra
        after_ref, pre_ref = out
        stream = [before_ref[side] + sums[side] for side in range(2)]
        unit, _ = norm_unit(stream)
        for side in range(2):
            after_ref[side] = stream[side]
            pre_ref[side] = (unit[side] * gain_ref[side]).astype(BF)

    base, stream, pre_attn = to_features(
        joined, skip_w, [g_skip, g_attn, shift], [wide_shape, wide_shape, low_shape], first_norms
    )
    while qkv_m[0].todo:
        advance(qkv_m)
    after_qkv = [mover.pieces[-1] for mover in qkv_m]
    hold(qkv_m, pre_attn)
    join(qkv_m)
    fc2_z = spread(pin(w_fc2.T, *after_qkv))
    pre_attn, cross_z, fc1_z = tie(pre_attn, cross_z, fc1_z)
    cross_m = fetch(cross_z, 2 * lanes, True)
    hold(cross_m, *after_qkv)
    advance(cross_m)
    qkv_w = [mover.weight() for mover in qkv_m]
    projected = to_lanes(pre_attn, qkv_w)
    projected = bind(projected, *cross_m)
    projected, fc2_z = tie(projected, fc2_z)
    fc_m = [Gather(cube, fc1_z, 0, True), Gather(cube, fc2_z, 1, True)]
    advance(fc_m)
    raw = exchange(projected.reshape(parts, micros, slots, 3 * lanes))
    cross_m[0].pieces[0], d_mlp, turn, text_turn = tie(cross_m[0].pieces[0], d_mlp, turn, text_turn)
    arrived = fc_m[0].pieces + fc_m[1].pieces
    text_own = jnp.dot(text.reshape(-1, features), text_turn, preferred_element_type=F32).astype(BF)
    text_own = jnp.pad(
        text_own.reshape(micros, text_slots, features), ((0, 0), (0, text_strip - text_slots), (0, 0))
    ).reshape(micros * text_strip, features)
    text_z = jnp.pad(pad_heads(w_text_kv.reshape(text_rows, -1), local), ((0, max(0, strip - text_rows)), (0, 0)))
    while fc_m[0].todo:
        advance(fc_m)
    text_z = spread(pin(text_z, *arrived))
    text_all = spread(pin(text_own, *arrived))
    while cross_m[0].todo:
        advance(cross_m)
    join(cross_m)
    first_w, out2_w = [mover.weight() for mover in cross_m]
    out1_w, query2_w = (Lanes(first_w.near, first_w.far, lanes, index) for index in range(2))
    attended, turned_q, turned_k, norms = self_forward(raw, counts, cosine, sine, gain_q, gain_k)
    attended = bind(attended, *fc_m)
    attended, text_all, text_z, first_w.far, out2_w.far = tie(attended, text_all, text_z, first_w.far, out2_w.far)
    out1_w.far = query2_w.far = first_w.far
    text_m = Gather(cube, text_z[:, :text_rows], 0, True)
    text_m.move()
    attended = exchange(attended).reshape(parts, rows, lanes)
    join(fc_m)
    attended = bind(attended, text_m, *fc_m)
    while text_m.todo:
        text_m.move()
    text_all = text_all.reshape(-1, features)
    text_all = jnp.stack([text_all[:, : features // 2], text_all[:, features // 2 :]])
    stream1, pre_cross = to_features(
        attended, [out1_w], [stream, g_cross], [wide_shape, low_shape], next_norm
    )
    fc1_w, fc2_w = [mover.weight() for mover in fc_m]
    hold([text_m], pre_cross)
    text_m.join()
    text_w = text_m.weight()
    query2 = to_lanes(pre_cross, [query2_w]).reshape(parts, micros, slots, lanes)
    text_kv = to_lanes(text_all, [text_w]).reshape(parts, parts, micros, text_strip, 2 * lanes)
    crossed = cross_forward(query2, text_kv, lengths, text_slots).reshape(parts, rows, lanes)
    stream2, pre_mlp = to_features(
        crossed, [out2_w], [stream1, g_mlp], [wide_shape, low_shape], next_norm
    )
    hidden0, activ0, partial, fc2_n0, fc2_f0 = mlp_forward(pre_mlp, d_mlp, stream2, fc1_w, fc2_w, 0)
    hidden1, activ1, result, fc2_n1, fc2_f1 = mlp_forward(pre_mlp, d_mlp, partial, fc1_w, fc2_w, 1, live)
    share = fc2_n0.shape[2]
    fc2_s = scatter(cube, (fc2_n0, fc2_f0), (share, 0, 0)) + scatter(cube, (fc2_n1, fc2_f1), (share, 0, 1))

    def settle(values, before=None):
        value = values[0] if len(values) == 1 else jnp.concatenate(values, 2)
        if before is not None:
            value, before = tie(value, before)
        return lax.psum_scatter(value, "sp", scatter_dimension=0, tiled=False)

    fc1_n0, fc1_f0, partial = mlp_backward(d_mlp, pre_mlp, hidden0, fc1_w, fc2_w, 0, None)
    fc1_s = scatter(cube, (fc1_n0, fc1_f0), (share, 0, 0))
    pack(fc2_s)
    partial = bind(partial, *fc2_s)
    send(fc2_s)
    fc1_n1, fc1_f1, grad2, d_cross, d_gain_mlp = mlp_backward(
        d_mlp, pre_mlp, hidden1, fc1_w, fc2_w, 1, partial, [stream2, g_mlp, grad3]
    )
    fc1_s += scatter(cube, (fc1_n1, fc1_f1), (share, 0, 1))
    d_cross = bind(d_cross, *fc2_s)
    d_crossed = to_lanes(d_cross, [out2_w])
    pack(fc2_s)
    d_crossed = bind(d_crossed, *fc2_s)
    send(fc2_s)
    d_query2, d_text_kv = cross_backward(
        query2, text_kv, lengths, d_crossed.reshape(parts, micros, slots, lanes), text_slots
    )
    d_query2 = bind(d_query2, *fc2_s)
    d_query2 = d_query2.reshape(parts, rows, lanes)
    d_text_kv = d_text_kv.reshape(parts, -1, 2 * lanes)
    total_fc2 = results(fc2_s)
    term_fc2 = settle(total_fc2)

    def go_back(sums, extra, out):
        add_norm_back(sums, *extra, *out)

    grad1, d_attn, d_gain_cross = to_features(
        d_query2, [query2_w], [stream1, g_cross, grad2], [wide_shape, low_shape, gain_shape], go_back
    )
    d_attn = bind(d_attn, *fc1_s)
    pack(fc1_s)
    d_attn = bind(d_attn, *fc1_s)
    send(fc1_s)
    d_attended = to_lanes(d_attn, [out1_w])
    d_attended, d_text_kv, pre_cross = tie(d_attended, d_text_kv, pre_cross)
    d_heads = exchange(d_attended.reshape(parts, micros, slots, lanes))

    def words_back(sums, extra, out):
        size = micros * text_strip
        for zone in range(parts):
            for side in range(2):
                out[0][zone, side] = sums[side][zone * size : (zone + 1) * size].astype(BF)

    words_shape = jax.ShapeDtypeStruct((parts, 2, micros * text_strip, features // 2), BF)
    d_words = to_features(d_text_kv, [text_w], [], [words_shape], words_back)[0]
    text_t = list(terms_of([(text_all, d_text_kv, 2 * lanes, 0)]))
    cross_t = terms_of(
        [(d_attn, attended, lanes, 0), (pre_cross, d_query2, lanes, 0), (d_cross, crossed, lanes, 0)]
    )
    cross_t = list(cross_t)
    d_heads, d_words, text_t[1], cross_t[1] = tie(d_heads, d_words, text_t[1], cross_t[1])
    d_words = settle([d_words])
    text_s = scatter(cube, text_t, (lanes, 0, 0), (lanes, 1, 1))
    cross_s = scatter(cube, cross_t, (2 * lanes, 0, 0), (lanes, 2, 1))
    d_heads = bind(d_heads, *fc1_s)
    pack(fc1_s)
    d_heads = bind(d_heads, *fc1_s)
    send(fc1_s)
    d_raw, d_gain_q, d_gain_k = self_backward(
        raw, counts, cosine, sine, gain_q, gain_k, turned_q, turned_k, norms, d_heads
    )
    d_raw, term_fc2, d_words = tie(d_raw, term_fc2, d_words)
    d_raw = bind(d_raw, *fc1_s)
    d_projected = exchange(d_raw).reshape(parts, rows, 3 * lanes)
    other_s = cross_s + text_s
    total_fc1 = results(fc1_s)
    pack(cross_s)
    pack(text_s)
    send(other_s)
    d_projected = bind(d_projected, *other_s)
    term_fc1 = settle(total_fc1, d_projected)
    qkv_t = terms_of([(pre_attn, d_projected, 3 * lanes, 0)])
    qkv_s = scatter(cube, qkv_t, (2 * lanes, 0, 0), (lanes, 2, 1))
    pack(cross_s)
    pack(text_s)
    send(other_s)
    pack(qkv_s)
    d_projected = bind(d_projected, *qkv_s)
    send(qkv_s)

    def last_norms(sums, extra, out):
        stream_ref, g1_ref, base_ref, g0_ref, add_ref = extra
        low_ref, d_shift_ref, d_g1_ref, d_g0_ref = out
        back, gains1 = norm_back([stream_ref[0], stream_ref[1]], g1_ref, sums)
        total = [add_ref[side] + back[side] for side in range(2)]
        back, gains0 = norm_back([base_ref[0], base_ref[1]], g0_ref, total)
        for side in range(2):
            low_ref[side] = back[side].astype(BF)
            d_g1_ref[side] = gains1[side]
            d_g0_ref[side] = gains0[side]
            for micro in range(micros):
                part = sums[side][micro * slots : (micro + 1) * slots]
                d_shift_ref[side, micro : micro + 1] = jnp.sum(part, 0, keepdims=True)

    shift_shape = jax.ShapeDtypeStruct((2, micros, middle), F32)
    d_base, d_shift, d_gain_attn, d_gain_skip = to_features(
        d_projected,
        qkv_w,
        [stream, g_attn, base, g_skip, grad1],
        [low_shape, shift_shape, gain_shape, gain_shape],
        last_norms,
    )
    d_base = bind(d_base, *other_s)
    total_cross, total_text = list(results(cross_s)), list(results(text_s))
    d_base = bind(d_base, *qkv_s)
    d_base, total_cross[0], total_text[0] = tie(d_base, total_cross[0], total_text[0])
    term_cross, term_text = settle(total_cross), settle(total_text)
    skip_t = terms_of([(d_base, joined, skip_lanes, 0)])
    skip_s = scatter(cube, skip_t, (skip_cut, 0, 0), (skip_cut, 1, 1))
    pack(qkv_s)
    send(qkv_s)
    pack(skip_s)
    send(skip_s)
    total_qkv = list(results(qkv_s))
    total_qkv[0] = bind(total_qkv[0], *skip_s)
    total_skip = list(results(skip_s))
    total_skip[0], term_cross, term_text = tie(total_skip[0], term_cross, term_text)
    term_qkv = settle(total_qkv + total_skip)
    term_qkv, term_skip = term_qkv[:, : 3 * lanes], term_qkv[:, 3 * lanes :]
    d_joined = to_inputs(d_base, skip_w, kept)
    result = (
        jnp.dot(result[0], turn[:, :middle].T, preferred_element_type=F32)
        + jnp.dot(result[1], turn[:, middle:].T, preferred_element_type=F32)
    ).astype(BF)
    d_words = d_words.reshape(2, micros * text_strip, features // 2)
    d_words = jnp.dot(
        d_words[0], text_turn[:, : features // 2].T, preferred_element_type=F32
    ) + jnp.dot(d_words[1], text_turn[:, features // 2 :].T, preferred_element_type=F32)
    d_words = d_words.reshape(micros, text_strip, features)[:, :text_slots]

    d_shift = jnp.transpose(d_shift.reshape(2, micros, ranks // 2, strip), (0, 2, 1, 3))
    d_shift = d_shift.reshape(ranks, micros, strip)
    d_shift = jnp.stack([d_shift[cube.masks.index(mask)] for mask in range(ranks)])
    d_shift = cube.add(cube.trade(d_shift), "sp").reshape(ranks * micros, strip)
    term_mod = lax.dot_general(
        time_part.astype(F32), d_shift, (((0,), (0,)), ((), ())), precision=lax.Precision.HIGHEST
    )

    places = jnp.array([cube.masks.index(mask) for mask in range(ranks)], jnp.int32)
    places = places[jnp.arange(ranks, dtype=jnp.int32) ^ cube.rank]
    gains = jnp.stack([d_gain_skip, d_gain_attn, d_gain_cross, d_gain_mlp])
    gains = gains.reshape(4, ranks, strip)[:, places].reshape(-1)
    heads = jnp.stack([jnp.sum(d_gain_q, (0, 1)), jnp.sum(d_gain_k, (0, 1))])
    heads = jnp.sum(heads[:, : local * HP].reshape(2, local, HP)[:, :, :HD], 1)
    packed = jnp.concatenate([gains, heads.reshape(-1)])
    packed = cube.add(cube.add(packed, "sp"), "dp")
    gains = packed[: 4 * width].reshape(4, ranks * parts, -1)
    gains = lax.dynamic_index_in_dim(gains, cube.rank * parts + zone, 1, keepdims=False)
    heads = packed[4 * width :].reshape(2, HD)

    def whole(term, groups):
        return cut_heads(term.astype(F32), local).reshape(term.shape[0], groups, -1)

    return (
        result.reshape(tokens.shape),
        d_joined[0].reshape(tokens.shape),
        d_joined[1].reshape(tokens.shape),
        d_words.reshape(text.shape),
        term_skip.astype(F32)[:, :kept].T,
        term_mod,
        whole(term_qkv, 3),
        cut_heads(term_cross[:, :lanes].astype(F32), local).T,
        cut_heads(term_cross[:, lanes : 2 * lanes].astype(F32), local),
        whole(term_text, 2),
        cut_heads(term_cross[:, 2 * lanes :].astype(F32), local).T,
        term_fc1.astype(F32),
        term_fc2.astype(F32).T,
        gains[0],
        gains[1],
        gains[2],
        gains[3],
        heads[0],
        heads[1],
    )


def solution(mesh):
    rows = P(None, ("dp", "sp"), None)
    column = P("sp", "dp")
    row = P("dp", "sp")
    grouped = P("dp", None, "sp")
    in_specs = (
        (rows, rows, rows, P(None, "dp"), P(None, "dp", None), P(None, "dp", None))
        + (column, column, grouped, column, row, grouped, column, row, column)
        + (P(),) * 6
        + (rows,)
    )
    out_specs = (
        (rows, rows, rows, rows)
        + (column, column, grouped, column, row, grouped, column, row, column)
        + (P(("dp", "sp")),) * 4
        + (P(), P())
    )
    return jax.shard_map(
        on_device, mesh=mesh, in_specs=in_specs, out_specs=out_specs, check_vma=False
    )
```

```python
import math

import jax
import jax.numpy as jnp
from jax import lax
from jax.experimental import pallas as pl
from jax.experimental.pallas import tpu as pltpu
from jax.sharding import PartitionSpec as P

H = 16
HD = 88
HP = 96
CLIP_LEN = 77
ROWS = 256

EPS = 1e-06
MASKED = -1e30
LOG2E = 1.4426950408889634
BF = jnp.bfloat16
F32 = jnp.float32


def time_embed(step, width):
    half = width // 2
    rate = jnp.exp(-math.log(10000.0) * jnp.arange(half, dtype=F32) / half)
    angle = step.astype(F32)[..., None] * rate
    return jnp.concatenate([jnp.cos(angle), jnp.sin(angle)], -1)


def rope_tables(sequence, wide, lanes):
    place = jnp.arange(sequence, dtype=jnp.int32)[None, :, None]
    wide = wide[:, None, None]
    lane = jnp.arange(lanes, dtype=jnp.int32)[None, None, :] % HP
    pair = lane // 2
    quarter = HD // 4
    upper = pair < quarter
    rank = jnp.where(upper, pair, pair - quarter).astype(F32)
    rate = jnp.exp(-math.log(10000.0) * rank / quarter)
    angle = jnp.where(upper, place // wide, place % wide).astype(F32) * rate
    sine = jnp.sin(angle)
    return jnp.cos(angle), jnp.where(lane % 2 == 0, -sine, sine)


def pad_heads(packed, local):
    rows, lanes = packed.shape
    groups = packed.reshape(rows, lanes // (local * HD), local, HD)
    groups = jnp.pad(groups, ((0, 0), (0, 0), (0, 0), (0, HP - HD)))
    groups = groups.reshape(rows, -1, local * HP)
    return jnp.pad(groups, ((0, 0), (0, 0), (0, -local * HP % 128))).reshape(rows, -1)


def cut_heads(padded, local):
    rows = padded.shape[0]
    groups = padded.reshape(rows, -1, local * HP + -local * HP % 128)[:, :, : local * HP]
    return groups.reshape(rows, -1, local, HP)[..., :HD].reshape(rows, -1)


def head_masks(shape, local):
    lane = lax.broadcasted_iota(jnp.int32, shape, len(shape) - 1)
    inside = lane % HP < HD
    return [((lane // HP == h) & inside).astype(F32) for h in range(local)]


def head_mean(value, masks):
    total = None
    for mask in masks:
        term = (jnp.sum(value * mask, -1, keepdims=True) * (1.0 / HD)) * mask
        total = term if total is None else total + term
    return total


def head_unit(value, masks):
    centre = value - head_mean(value, masks)
    spread = None
    square = centre * centre
    for mask in masks:
        mean = jnp.sum(square * mask, -1, keepdims=True) * (1.0 / HD)
        term = lax.rsqrt(mean + EPS) * mask
        spread = term if spread is None else spread + term
    return centre * spread, spread


def turn_pairs(value):
    lanes = value.shape[-1]
    after = pltpu.roll(value, lanes - 1, 1)
    before = pltpu.roll(value, 1, 1)
    lane = lax.broadcasted_iota(jnp.int32, value.shape, 1)
    return jnp.where(lane % 2 == 0, after, before)


def dot_nt(left, right):
    return lax.dot_general(left, right, (((1,), (1,)), ((), ())), preferred_element_type=F32)


def dot_nn(left, right):
    return lax.dot_general(left, right, (((1,), (0,)), ((), ())), preferred_element_type=F32)


def dot_tn(left, right):
    return lax.dot_general(left, right, (((0,), (0,)), ((), ())), preferred_element_type=F32)


def self_forward(raw, counts, cosine, sine, gain_q, gain_k):
    parts, micros, slots, packed = raw.shape
    lanes = packed // 3
    local = lanes // HP
    sequence = parts * slots
    factor = HD ** (-0.5) * LOG2E

    def kernel(count_ref, raw_ref, cos_ref, sin_ref, gq_ref, gk_ref, out_ref, q_ref, k_ref, lse_ref):
        count = count_ref[pl.program_id(0)]
        blocks = (count + slots - 1) // slots
        out_ref[...] = jnp.zeros_like(out_ref)
        masks = head_masks((1, lanes), local)

        def prepare(part, carry):
            spot = pl.ds(pl.multiple_of(part * slots, slots), slots)
            cosine, sine = cos_ref[0, spot, :], sin_ref[0, spot, :]
            for index, gain_ref, dest in ((0, gq_ref, q_ref), (1, gk_ref, k_ref)):
                value = raw_ref[part, 0, :, index * lanes : (index + 1) * lanes].astype(F32)
                scaled = head_unit(value, masks)[0] * gain_ref[...]
                dest[0, spot, :] = (scaled * cosine + turn_pairs(scaled) * sine).astype(BF)
            return carry

        lax.fori_loop(0, parts, prepare, 0)
        column = lax.broadcasted_iota(jnp.int32, (1, sequence), 1)
        bias = jnp.where(column < count, 0.0, MASKED)
        for h in range(local):
            cut = slice(h * HP, (h + 1) * HP)
            keys = k_ref[0, :, cut]
            values = raw_ref[:, 0, :, 2 * lanes + h * HP : 2 * lanes + (h + 1) * HP].reshape(sequence, HP)

            def one_block(part, carry):
                spot = pl.ds(pl.multiple_of(part * slots, slots), slots)
                scores = dot_nt(q_ref[0, spot, cut], keys) + bias
                top = jnp.max(scores, -1, keepdims=True)
                raised = jnp.exp2((scores - top) * factor)
                total = jnp.sum(raised, -1, keepdims=True)
                result = dot_nn(raised.astype(BF), values) / total
                out_ref[part, 0, :, cut] = result.astype(BF)
                norm = jnp.broadcast_to(top * factor + jnp.log2(total), (slots, 128))
                lse_ref[0, h : h + 1, spot] = jnp.transpose(norm)[0:1, :]
                return carry

            lax.fori_loop(0, blocks, one_block, 0)

    whole = lambda m, c: (0, m, 0, 0)
    table = lambda m, c: (m, 0, 0)
    fixed = lambda m, c: (0, 0)
    return pl.pallas_call(
        kernel,
        name="self_forward",
        grid_spec=pltpu.PrefetchScalarGridSpec(
            num_scalar_prefetch=1,
            grid=(micros,),
            in_specs=[
                pl.BlockSpec((parts, 1, slots, packed), whole),
                pl.BlockSpec((1, sequence, lanes), table),
                pl.BlockSpec((1, sequence, lanes), table),
                pl.BlockSpec((1, lanes), fixed),
                pl.BlockSpec((1, lanes), fixed),
            ],
            out_specs=[
                pl.BlockSpec((parts, 1, slots, lanes), whole),
                pl.BlockSpec((1, sequence, lanes), table),
                pl.BlockSpec((1, sequence, lanes), table),
                pl.BlockSpec((1, local, sequence), table),
            ],
        ),
        out_shape=[
            jax.ShapeDtypeStruct((parts, micros, slots, lanes), BF),
            jax.ShapeDtypeStruct((micros, sequence, lanes), BF),
            jax.ShapeDtypeStruct((micros, sequence, lanes), BF),
            jax.ShapeDtypeStruct((micros, local, sequence), F32),
        ],
        compiler_params=params(),
        cost_estimate=cost(4 * micros * local * sequence * sequence * HP),
    )(counts, raw, cosine, sine, gain_q, gain_k)


def self_backward(raw, counts, cosine, sine, gain_q, gain_k, turned_q, turned_k, norms, incoming):
    parts, micros, slots, packed = raw.shape
    lanes = packed // 3
    local = lanes // HP
    sequence = parts * slots
    scale = HD ** (-0.5)
    factor = scale * LOG2E

    def kernel(
        count_ref,
        raw_ref,
        cos_ref,
        sin_ref,
        gq_ref,
        gk_ref,
        q_ref,
        k_ref,
        lse_ref,
        in_ref,
        out_ref,
        dgq_ref,
        dgk_ref,
        dq_s,
        dk_s,
        dv_s,
    ):
        count = count_ref[pl.program_id(0)]
        blocks = (count + slots - 1) // slots
        dq_s[...] = jnp.zeros_like(dq_s)
        dk_s[...] = jnp.zeros_like(dk_s)
        dv_s[...] = jnp.zeros_like(dv_s)
        row = lax.broadcasted_iota(jnp.int32, (sequence, 1), 0)
        bias = jnp.where(row < count, 0.0, MASKED)
        for h in range(local):
            cut = slice(h * HP, (h + 1) * HP)
            keys = k_ref[0, :, cut]
            values = raw_ref[:, 0, :, 2 * lanes + h * HP : 2 * lanes + (h + 1) * HP].reshape(sequence, HP)

            def one_block(part, carry):
                spot = pl.ds(pl.multiple_of(part * slots, slots), slots)
                rows = q_ref[0, spot, cut]
                grads = in_ref[part, 0, :, cut]
                norm = lse_ref[0, h : h + 1, spot]
                probs = jnp.exp2(dot_nt(keys, rows) * factor + bias - norm)
                d_probs = dot_nt(values, grads)
                inner = jnp.sum(probs * d_probs, 0, keepdims=True)
                d_scores = (probs * (d_probs - inner)).astype(BF)
                dv_s[:, cut] += dot_nn(probs.astype(BF), grads)
                dk_s[:, cut] += dot_nn(d_scores, rows)
                dq_s[spot, cut] = dot_tn(d_scores, keys)
                return carry

            lax.fori_loop(0, blocks, one_block, 0)
        masks = head_masks((1, lanes), local)

        def finish(part, carry):
            spot = pl.ds(pl.multiple_of(part * slots, slots), slots)
            cosine, sine = cos_ref[0, spot, :], sin_ref[0, spot, :]
            sums = []
            for index, gain_ref, source in ((0, gq_ref, dq_s), (1, gk_ref, dk_s)):
                grad = source[spot, :] * scale
                grad = grad * cosine - turn_pairs(grad) * sine
                value = raw_ref[part, 0, :, index * lanes : (index + 1) * lanes].astype(F32)
                unit, spread = head_unit(value, masks)
                leading = grad * gain_ref[...]
                back = leading - head_mean(leading, masks) - unit * head_mean(leading * unit, masks)
                out_ref[part, 0, :, index * lanes : (index + 1) * lanes] = (spread * back).astype(BF)
                sums.append(carry[index] + jnp.sum(grad * unit, 0, keepdims=True))
            out_ref[part, 0, :, 2 * lanes : 3 * lanes] = dv_s[spot, :].astype(BF)
            return tuple(sums)

        zero = jnp.zeros((1, lanes), F32)
        d_gains = lax.fori_loop(0, parts, finish, (zero, zero))
        dgq_ref[0] = d_gains[0]
        dgk_ref[0] = d_gains[1]

    whole = lambda m, c: (0, m, 0, 0)
    table = lambda m, c: (m, 0, 0)
    fixed = lambda m, c: (0, 0)
    return pl.pallas_call(
        kernel,
        name="self_backward",
        grid_spec=pltpu.PrefetchScalarGridSpec(
            num_scalar_prefetch=1,
            grid=(micros,),
            in_specs=[
                pl.BlockSpec((parts, 1, slots, packed), whole),
                pl.BlockSpec((1, sequence, lanes), table),
                pl.BlockSpec((1, sequence, lanes), table),
                pl.BlockSpec((1, lanes), fixed),
                pl.BlockSpec((1, lanes), fixed),
                pl.BlockSpec((1, sequence, lanes), table),
                pl.BlockSpec((1, sequence, lanes), table),
                pl.BlockSpec((1, local, sequence), table),
                pl.BlockSpec((parts, 1, slots, lanes), whole),
            ],
            out_specs=[
                pl.BlockSpec((parts, 1, slots, packed), whole),
                pl.BlockSpec((1, 1, lanes), table),
                pl.BlockSpec((1, 1, lanes), table),
            ],
            scratch_shapes=[pltpu.VMEM((sequence, lanes), F32) for index in range(3)],
        ),
        out_shape=[
            jax.ShapeDtypeStruct((parts, micros, slots, packed), BF),
            jax.ShapeDtypeStruct((micros, 1, lanes), F32),
            jax.ShapeDtypeStruct((micros, 1, lanes), F32),
        ],
        compiler_params=params(),
        cost_estimate=cost(10 * micros * local * sequence * sequence * HP),
    )(counts, raw, cosine, sine, gain_q, gain_k, turned_q, turned_k, norms, incoming)


def cost(flops):
    return pl.CostEstimate(flops=flops // 16, bytes_accessed=flops // 16000, transcendentals=0)


def full(shape):
    return pl.BlockSpec(shape, lambda *index: (0,) * len(shape))


def params(megabytes=60):
    return pltpu.CompilerParams(vmem_limit_bytes=megabytes << 20)


class Lanes:
    def __init__(self, near, far, block=None, index=0):
        self.near, self.far = near, far
        self.block = block or near.shape[2]
        self.index = index

    def spec(self):
        index = self.index
        return pl.BlockSpec((1, self.near.shape[1], self.block), lambda p, *rest: (p, 0, index))


def to_lanes(value, weights, dtype=BF, name="to_lanes"):
    rows = value.shape[1]
    parts, half, _ = weights[0].near.shape
    total = sum(weight.block for weight in weights)

    def kernel(x_ref, *refs):
        out_ref = refs[-1]
        at = 0
        for index, weight in enumerate(weights):
            result = dot_nn(x_ref[0], refs[2 * index][0]) + dot_nn(x_ref[1], refs[2 * index + 1][0])
            out_ref[0, :, at : at + weight.block] = result.astype(dtype)
            at += weight.block

    return pl.pallas_call(
        kernel,
        name=name,
        grid=(parts,),
        in_specs=[full(value.shape)] + [weight.spec() for weight in weights for side in range(2)],
        out_specs=pl.BlockSpec((1, rows, total), lambda p: (p, 0, 0)),
        out_shape=jax.ShapeDtypeStruct((parts, rows, total), dtype),
        compiler_params=params(),
        cost_estimate=cost(4 * rows * half * parts * total),
    )(value, *[side for weight in weights for side in (weight.near, weight.far)])


def to_inputs(value, weights, kept):
    rows = value.shape[1]
    parts, half, _ = weights[0].near.shape
    sides = parts // 2

    def kernel(x_ref, *refs):
        out_ref = refs[-1]
        for side in range(sides):

            @pl.when(pl.program_id(0) % sides == side)
            def _():
                at = 0
                for index, weight in enumerate(weights):
                    result = dot_nn(x_ref[0], refs[2 * index][0]) + dot_nn(
                        x_ref[1], refs[2 * index + 1][0]
                    )
                    take = min(weight.block, kept - at)
                    start = side * kept + at
                    out_ref[0, :, start : start + take] = result[:, :take]
                    at += take

    return pl.pallas_call(
        kernel,
        name="to_inputs",
        grid=(parts,),
        in_specs=[full(value.shape)] + [weight.spec() for weight in weights for side in range(2)],
        out_specs=pl.BlockSpec((1, rows, sides * kept), lambda p: (p // sides, 0, 0)),
        out_shape=jax.ShapeDtypeStruct((2, rows, sides * kept), F32),
        compiler_params=params(),
        cost_estimate=cost(4 * rows * half * parts * kept),
    )(value, *[side for weight in weights for side in (weight.near, weight.far)])


def to_features(value, weights, extras, outs, finish, name="to_features"):
    parts, rows, total = value.shape
    half = weights[0].near.shape[1]
    count = 2 * len(weights)

    def kernel(*refs):
        y_ref, weight_refs = refs[0], refs[1 : 1 + count]
        extra_refs = refs[1 + count : 1 + count + len(extras)]
        out_refs = refs[1 + count + len(extras) : -1]
        sums = refs[-1]

        @pl.when(pl.program_id(0) == 0)
        def _():
            sums[...] = jnp.zeros_like(sums)

        at = 0
        for index, weight in enumerate(weights):
            left = y_ref[0, :, at : at + weight.block]
            for side in range(2):
                sums[side] += dot_nt(left, weight_refs[2 * index + side][0])
            at += weight.block

        @pl.when(pl.program_id(0) == parts - 1)
        def _():
            finish([sums[0], sums[1]], extra_refs, out_refs)

    return pl.pallas_call(
        kernel,
        name=name,
        grid=(parts,),
        in_specs=[pl.BlockSpec((1, rows, total), lambda p: (p, 0, 0))]
        + [weight.spec() for weight in weights for side in range(2)]
        + [full(extra.shape) for extra in extras],
        out_specs=[full(out.shape) for out in outs],
        out_shape=outs,
        scratch_shapes=[pltpu.VMEM((2, rows, half), F32)],
        compiler_params=params(),
        cost_estimate=cost(4 * rows * half * parts * total),
    )(value, *[side for weight in weights for side in (weight.near, weight.far)], *extras)


def terms_of(pairs, name="terms_of"):
    half = pairs[0][0].shape[2]
    parts = pairs[0][1].shape[0]
    total = sum(pair[2] for pair in pairs)
    rows = [pair[0].shape[1] for pair in pairs]

    def kernel(*refs):
        count = len(pairs)
        lefts, rights = refs[:count], refs[count : 2 * count]
        near_ref, far_ref = refs[2 * count : 2 * count + 2]
        turned = refs[2 * count + 2 :]

        @pl.when(pl.program_id(0) == 0)
        def _():
            for left, flat in zip(lefts, turned):
                for side in range(2):
                    flat[side] = jnp.transpose(left[side])

        at = 0
        for pair, right, flat in zip(pairs, rights, turned):
            lanes = pair[2]
            near_ref[0, :, at : at + lanes] = dot_nn(flat[0], right[0]).astype(BF)
            far_ref[0, :, at : at + lanes] = dot_nn(flat[1], right[0]).astype(BF)
            at += lanes

    def right_spec(pair):
        return pl.BlockSpec((1, pair[1].shape[1], pair[2]), lambda p: (p, 0, pair[3]))

    out = jax.ShapeDtypeStruct((parts, half, total), BF)
    return pl.pallas_call(
        kernel,
        name=name,
        grid=(parts,),
        in_specs=[full(pair[0].shape) for pair in pairs] + [right_spec(pair) for pair in pairs],
        out_specs=[pl.BlockSpec((1, half, total), lambda p: (p, 0, 0))] * 2,
        out_shape=[out, out],
        scratch_shapes=[pltpu.VMEM((2, half, count), BF) for count in rows],
        compiler_params=params(),
        cost_estimate=cost(sum(4 * half * parts * pair[2] * count for pair, count in zip(pairs, rows))),
    )(*[pair[0] for pair in pairs], *[pair[1] for pair in pairs])


def norm_unit(halves):
    width = 2 * halves[0].shape[-1]
    mean = sum(jnp.sum(half, -1, keepdims=True) for half in halves) / width
    centre = [half - mean for half in halves]
    spread = sum(jnp.sum(half * half, -1, keepdims=True) for half in centre) / width
    scale = lax.rsqrt(spread + EPS)
    return [half * scale for half in centre], scale


def norm_back(halves, gain_ref, incoming):
    width = 2 * halves[0].shape[-1]
    unit, scale = norm_unit(halves)
    leading = [incoming[side] * gain_ref[side] for side in range(2)]
    mean = sum(jnp.sum(half, -1, keepdims=True) for half in leading) / width
    inner = sum(jnp.sum(leading[side] * unit[side], -1, keepdims=True) for side in range(2)) / width
    back = [scale * (leading[side] - mean - unit[side] * inner) for side in range(2)]
    gains = [jnp.sum(incoming[side] * unit[side], 0, keepdims=True) for side in range(2)]
    return back, gains


def join_rows(pieces, rows, name="join_rows"):
    parts, _, lanes = pieces[0][0].shape
    count = len(pieces)
    if rows % 16:
        return jnp.concatenate([array[:, block * rows : (block + 1) * rows] for array, block in pieces], 1)

    def kernel(*refs):
        for index in range(count):
            refs[-1][0, index * rows : (index + 1) * rows] = refs[index][0]

    def spec(block):
        return pl.BlockSpec((1, rows, lanes), lambda p: (p, block, 0))

    return pl.pallas_call(
        kernel,
        name=name,
        grid=(parts,),
        in_specs=[spec(block) for _, block in pieces],
        out_specs=pl.BlockSpec((1, count * rows, lanes), lambda p: (p, 0, 0)),
        out_shape=jax.ShapeDtypeStruct((parts, count * rows, lanes), BF),
        compiler_params=params(),
        cost_estimate=cost(parts * count * rows * lanes),
    )(*[array for array, _ in pieces])


def sum_rows(jobs, rows, name="sum_rows"):
    parts = jobs[0][1][0][0].shape[0]
    if rows % 16:
        results = []
        for lanes, terms in jobs:
            value = 0.0
            for array, blocks, spot in terms:
                split = array[:, :, spot * lanes : (spot + 1) * lanes].reshape(parts, -1, rows, lanes)
                value = value + jnp.stack([split[:, block] for block in blocks], 1).astype(F32)
            results.append(value.astype(BF).reshape(parts, -1, lanes))
        return results
    spots = [
        (array, blocks[index], spot, lanes)
        for lanes, terms in jobs
        for index in range(len(terms[0][1]))
        for array, blocks, spot in terms
    ]

    def kernel(*refs):
        at = 0
        for order, (_, terms) in enumerate(jobs):
            out_ref = refs[len(spots) + order]
            for index in range(len(terms[0][1])):
                value = refs[at][0].astype(F32)
                for offset in range(1, len(terms)):
                    value = value + refs[at + offset][0].astype(F32)
                out_ref[0, index * rows : (index + 1) * rows] = value.astype(BF)
                at += len(terms)

    def spec(block, spot, lanes):
        return pl.BlockSpec((1, rows, lanes), lambda p: (p, block, spot))

    shapes = [(len(terms[0][1]) * rows, lanes) for lanes, terms in jobs]
    return pl.pallas_call(
        kernel,
        name=name,
        grid=(parts,),
        in_specs=[spec(*rest) for _, *rest in spots],
        out_specs=[pl.BlockSpec((1, *shape), lambda p: (p, 0, 0)) for shape in shapes],
        out_shape=[jax.ShapeDtypeStruct((parts, *shape), BF) for shape in shapes],
        compiler_params=params(),
        cost_estimate=cost(sum(parts * size * lanes for size, lanes in shapes)),
    )(*[array for array, *_ in spots])


def side_by_side(left, right, kept, lanes):
    rows, width = left.shape
    count = width // kept

    def kernel(left_ref, right_ref, out_ref):
        for index, ref in enumerate((left_ref, right_ref)):
            for side in range(count):
                spot = count * index + side
                out_ref[spot, :, :kept] = ref[:, side * kept : (side + 1) * kept]
                if lanes > kept:
                    out_ref[spot, :, kept:] = jnp.zeros((rows, lanes - kept), BF)

    return pl.pallas_call(
        kernel,
        name="side_by_side",
        out_shape=jax.ShapeDtypeStruct((2 * count, rows, lanes), BF),
        compiler_params=params(),
        cost_estimate=cost(4 * rows * lanes),
    )(left, right)


def mlp_forward(rows_in, grads, start, weight1, weight2, part, live=None):
    _, rows, half = rows_in.shape
    parts, _, lanes = weight1.near.shape
    ff = lanes // 2
    step = 768 if ff % 768 == 0 else ff
    steps = ff // step
    extras = [] if live is None else [live]

    def kernel(x_ref, g_ref, s_ref, n1_ref, f1_ref, n2_ref, f2_ref, *refs):
        hid_ref, act_ref, out_ref, dn2_ref, df2_ref, turned, sums = refs[len(extras) :]
        first = (pl.program_id(0) == 0) & (pl.program_id(1) == 0)
        last = (pl.program_id(0) == parts - 1) & (pl.program_id(1) == steps - 1)

        @pl.when(first)
        def _():
            for side in range(2):
                turned[side] = jnp.transpose(g_ref[side])
            sums[...] = s_ref[...]

        hidden = dot_nn(x_ref[0], n1_ref[0]) + dot_nn(x_ref[1], f1_ref[0])
        hid_ref[0] = hidden
        activ = jax.nn.gelu(hidden, approximate=True).astype(BF)
        act_ref[0] = activ
        sums[0] += dot_nt(activ, n2_ref[0])
        sums[1] += dot_nt(activ, f2_ref[0])
        dn2_ref[0] = dot_nn(turned[0], activ).astype(BF)
        df2_ref[0] = dot_nn(turned[1], activ).astype(BF)

        @pl.when(last)
        def _():
            if live is None:
                out_ref[...] = sums[...]
            else:
                out_ref[...] = (sums[...] * refs[0][...]).astype(BF)

    weight = pl.BlockSpec((1, half, step), lambda p, n: (p, 0, part * steps + n))
    grad = pl.BlockSpec((1, half, step), lambda p, n: (p, 0, n))
    unit = pl.BlockSpec((1, rows, step), lambda p, n: (p, 0, n))
    whole = full((2, rows, half))
    grad_shape = jax.ShapeDtypeStruct((parts, half, ff), BF)
    return pl.pallas_call(
        kernel,
        name="mlp_forward",
        grid=(parts, steps),
        in_specs=[whole, whole, whole, weight, weight, weight, weight] + [full(extra.shape) for extra in extras],
        out_specs=[unit, unit, whole, grad, grad],
        out_shape=[
            jax.ShapeDtypeStruct((parts, rows, ff), F32),
            jax.ShapeDtypeStruct((parts, rows, ff), BF),
            jax.ShapeDtypeStruct((2, rows, half), F32 if live is None else BF),
            grad_shape,
            grad_shape,
        ],
        scratch_shapes=[pltpu.VMEM((2, half, rows), BF), pltpu.VMEM((2, rows, half), F32)],
        compiler_params=params(),
        cost_estimate=cost(12 * rows * half * parts * ff),
    )(rows_in, grads, start, weight1.near, weight1.far, weight2.near, weight2.far, *extras)


def gelu_slope(value):
    root = math.sqrt(2.0 / math.pi)
    square = value * value
    curve = jnp.tanh(root * value * (1.0 + 0.044715 * square))
    return 0.5 * (1.0 + curve) + 0.5 * value * (1.0 - curve * curve) * root * (
        1.0 + 3.0 * 0.044715 * square
    )


def mlp_backward(grads, rows_in, hidden, weight1, weight2, part, start, finish=None):
    _, rows, half = rows_in.shape
    parts, _, lanes = weight1.near.shape
    ff = lanes // 2
    step = 768 if ff % 768 == 0 else ff
    steps = ff // step
    extras = list(finish or []) + ([] if start is None else [start])

    def kernel(g_ref, x_ref, hid_ref, n1_ref, f1_ref, n2_ref, f2_ref, *refs):
        extra_refs, refs = refs[: len(extras)], refs[len(extras) :]
        dn1_ref, df1_ref = refs[:2]
        out_refs = refs[2:-2]
        turned, sums = refs[-2:]
        first = (pl.program_id(0) == 0) & (pl.program_id(1) == 0)
        last = (pl.program_id(0) == parts - 1) & (pl.program_id(1) == steps - 1)

        @pl.when(first)
        def _():
            for side in range(2):
                turned[side] = jnp.transpose(x_ref[side])
            sums[...] = jnp.zeros_like(sums) if start is None else extra_refs[-1][...]

        d_activ = dot_nn(g_ref[0], n2_ref[0]) + dot_nn(g_ref[1], f2_ref[0])
        d_hidden = (d_activ * gelu_slope(hid_ref[0])).astype(BF)
        dn1_ref[0] = dot_nn(turned[0], d_hidden).astype(BF)
        df1_ref[0] = dot_nn(turned[1], d_hidden).astype(BF)
        sums[0] += dot_nt(d_hidden, n1_ref[0])
        sums[1] += dot_nt(d_hidden, f1_ref[0])

        @pl.when(last)
        def _():
            if finish is None:
                out_refs[0][...] = sums[...]
            else:
                value_ref, gain_ref, add_ref = extra_refs[:3]
                add_norm_back([sums[0], sums[1]], value_ref, gain_ref, add_ref, *out_refs)

    weight = pl.BlockSpec((1, half, step), lambda p, n: (p, 0, part * steps + n))
    grad = pl.BlockSpec((1, half, step), lambda p, n: (p, 0, n))
    unit = pl.BlockSpec((1, rows, step), lambda p, n: (p, 0, n))
    whole = full((2, rows, half))
    grad_shape = jax.ShapeDtypeStruct((parts, half, ff), BF)
    wide = jax.ShapeDtypeStruct((2, rows, half), F32)
    outs = [wide] if finish is None else [wide, *back_shapes(rows, half)]
    return pl.pallas_call(
        kernel,
        name="mlp_backward",
        grid=(parts, steps),
        in_specs=[whole, whole, unit, weight, weight, weight, weight] + [full(extra.shape) for extra in extras],
        out_specs=[grad, grad] + [full(out.shape) for out in outs],
        out_shape=[grad_shape, grad_shape] + outs,
        scratch_shapes=[pltpu.VMEM((2, half, rows), BF), pltpu.VMEM((2, rows, half), F32)],
        compiler_params=params(),
        cost_estimate=cost(12 * rows * half * parts * ff),
    )(grads, rows_in, hidden, weight1.near, weight1.far, weight2.near, weight2.far, *extras)


def back_shapes(rows, half):
    return [jax.ShapeDtypeStruct((2, rows, half), BF), jax.ShapeDtypeStruct((2, 1, half), F32)]


def add_norm_back(incoming, value_ref, gain_ref, add_ref, out_ref, low_ref, d_gain_ref):
    back, gains = norm_back([value_ref[0], value_ref[1]], gain_ref, incoming)
    for side in range(2):
        total = add_ref[side] + back[side]
        out_ref[side] = total
        low_ref[side] = total.astype(BF)
        d_gain_ref[side] = gains[side]


def text_bias(lengths_ref, micro, words, strip, text_slots, axis):
    spot = lax.broadcasted_iota(jnp.int32, (1, words) if axis else (words, 1), axis)
    inner = spot % strip
    place = spot // strip * text_slots + inner
    live = (place < lengths_ref[micro, 0]) | (
        (place >= CLIP_LEN) & (place < CLIP_LEN + lengths_ref[micro, 1])
    )
    return jnp.where(live & (inner < text_slots), 0.0, MASKED)


def cross_forward(query, text_kv, lengths, text_slots):
    parts, micros, slots, lanes = query.shape
    zones, strip = text_kv.shape[1], text_kv.shape[3]
    words = zones * strip
    local = lanes // HP
    factor = HD ** (-0.5) * LOG2E

    def kernel(len_ref, q_ref, kv_ref, out_ref):
        bias = text_bias(len_ref, pl.program_id(1), words, strip, text_slots, 1)
        for h in range(local):
            cut = slice(h * HP, (h + 1) * HP)
            keys = kv_ref[0, :, 0, :, cut].reshape(words, HP)
            scores = dot_nt(q_ref[0, 0, :, cut], keys) + bias
            top = jnp.max(scores, -1, keepdims=True)
            raised = jnp.exp2((scores - top) * factor)
            total = jnp.sum(raised, -1, keepdims=True)
            values = kv_ref[0, :, 0, :, lanes + h * HP : lanes + (h + 1) * HP].reshape(words, HP)
            out_ref[0, 0, :, cut] = (dot_nn(raised.astype(BF), values) / total).astype(BF)

    spot = lambda p, m, c: (p, m, 0, 0)
    far = lambda p, m, c: (p, 0, m, 0, 0)
    return pl.pallas_call(
        kernel,
        name="cross_forward",
        grid_spec=pltpu.PrefetchScalarGridSpec(
            num_scalar_prefetch=1,
            grid=(parts, micros),
            in_specs=[
                pl.BlockSpec((1, 1, slots, lanes), spot),
                pl.BlockSpec((1, zones, 1, strip, 2 * lanes), far),
            ],
            out_specs=pl.BlockSpec((1, 1, slots, lanes), spot),
        ),
        out_shape=jax.ShapeDtypeStruct(query.shape, BF),
        compiler_params=params(),
        cost_estimate=cost(4 * parts * micros * slots * words * lanes),
    )(lengths, query, text_kv)


def cross_backward(query, text_kv, lengths, incoming, text_slots):
    parts, micros, slots, lanes = query.shape
    zones, strip = text_kv.shape[1], text_kv.shape[3]
    words = zones * strip
    local = lanes // HP
    scale = HD ** (-0.5)
    factor = scale * LOG2E

    def kernel(len_ref, q_ref, kv_ref, in_ref, dq_ref, dkv_ref):
        bias = text_bias(len_ref, pl.program_id(1), words, strip, text_slots, 0)
        for h in range(local):
            cut = slice(h * HP, (h + 1) * HP)
            far = slice(lanes + h * HP, lanes + (h + 1) * HP)
            rows = q_ref[0, 0, :, cut]
            keys = kv_ref[0, :, 0, :, cut].reshape(words, HP)
            values = kv_ref[0, :, 0, :, far].reshape(words, HP)
            grads = in_ref[0, 0, :, cut]
            scores = dot_nt(keys, rows) + bias
            top = jnp.max(scores, 0, keepdims=True)
            raised = jnp.exp2((scores - top) * factor)
            probs = raised * (1.0 / jnp.sum(raised, 0, keepdims=True))
            d_probs = dot_nt(values, grads)
            inner = jnp.sum(probs * d_probs, 0, keepdims=True)
            d_scores = (probs * (d_probs - inner)).astype(BF)
            shape = (zones, strip, HP)
            dkv_ref[0, :, 0, :, far] = dot_nn(probs.astype(BF), grads).astype(BF).reshape(shape)
            dkv_ref[0, :, 0, :, cut] = (dot_nn(d_scores, rows) * scale).astype(BF).reshape(shape)
            dq_ref[0, 0, :, cut] = (dot_tn(d_scores, keys) * scale).astype(BF)

    spot = lambda p, m, c: (p, m, 0, 0)
    far = lambda p, m, c: (p, 0, m, 0, 0)
    return pl.pallas_call(
        kernel,
        name="cross_backward",
        grid_spec=pltpu.PrefetchScalarGridSpec(
            num_scalar_prefetch=1,
            grid=(parts, micros),
            in_specs=[
                pl.BlockSpec((1, 1, slots, lanes), spot),
                pl.BlockSpec((1, zones, 1, strip, 2 * lanes), far),
                pl.BlockSpec((1, 1, slots, lanes), spot),
            ],
            out_specs=[
                pl.BlockSpec((1, 1, slots, lanes), spot),
                pl.BlockSpec((1, zones, 1, strip, 2 * lanes), far),
            ],
        ),
        out_shape=[
            jax.ShapeDtypeStruct(query.shape, BF),
            jax.ShapeDtypeStruct(text_kv.shape, BF),
        ],
        compiler_params=params(),
        cost_estimate=cost(10 * parts * micros * slots * words * lanes),
    )(lengths, query, text_kv, incoming)


def tie(*values):
    return lax.optimization_barrier(values)


class Cube:
    def __init__(self):
        self.size = lax.axis_size("dp")
        self.bits = self.size.bit_length() - 1
        self.outer = list(range(1, self.bits))
        self.rank = lax.axis_index("dp")
        self.masks = []
        for place in range(self.size):
            mask = place >> (self.bits - 1)
            for bit in self.outer:
                mask |= ((place >> (bit - 1)) & 1) << bit
            self.masks.append(mask)
        self.owners = self.rank ^ jnp.array(self.masks, jnp.int32)

    def swap(self, value, bit, axis="dp"):
        pairs = [(i, i ^ (1 << bit)) for i in range(lax.axis_size(axis))]
        return lax.ppermute(value, axis, pairs)

    def trade(self, value):
        blocks = {mask: value[mask] for mask in range(self.size)}
        for bit in range(self.bits):
            send = sorted(mask for mask in blocks if mask >> bit & 1)
            got = self.swap(jnp.stack([blocks[mask] for mask in send]), bit)
            for place, mask in enumerate(send):
                blocks[mask] = got[place]
        return jnp.stack([blocks[mask] for mask in range(self.size)])

    def spread(self, value):
        held = value[None]
        for bit in range(self.bits):
            held = jnp.concatenate([held, self.swap(held, bit)])
        return held

    def add(self, value, axis):
        for bit in range(lax.axis_size(axis).bit_length() - 1):
            value = value + self.swap(value, bit, axis)
        return value


class Gather:
    def __init__(self, cube, shard, flip, joined=False):
        self.cube = cube
        self.rows = shard.shape[1]
        self.masks = [[0]]
        self.pieces = [shard]
        self.todo = cube.outer[::-1] if flip else list(cube.outer)
        self.joined = joined

    def blocks(self, order):
        spots = {
            mask: (piece, index)
            for piece, masks in zip(self.pieces, self.masks)
            for index, mask in enumerate(masks)
        }
        return join_rows([spots[mask] for mask in order], self.rows)

    def move(self):
        bit = self.todo.pop(0)
        if self.joined and len(self.pieces) > 1:
            order = [mask for masks in self.masks for mask in masks]
            self.pieces, self.masks = [self.blocks(order)], [order]
        self.masks = self.masks + [[mask | (1 << bit) for mask in masks] for masks in self.masks]
        self.pieces = self.pieces + [self.cube.swap(piece, bit) for piece in self.pieces]

    def join(self):
        while self.todo:
            self.move()
        self.pieces = [self.blocks(self.cube.masks[: self.cube.size // 2])]

    def weight(self):
        near = self.pieces[0]
        return Lanes(near, self.cube.swap(near, 0))


class Scatter:
    def __init__(self, cube, near, other, flip, lanes=None, spot=0):
        self.cube = cube
        self.todo = list(cube.outer) if flip else cube.outer[::-1]
        self.rows = near.shape[1] // (cube.size // 2)
        self.places = list(range(cube.size // 2))
        self.near = near
        self.lanes = lanes or near.shape[2]
        self.spot = spot
        self.got = []
        self.pieces = [other]
        self.arriving = self.places

    def job(self, places):
        terms = [(self.near, places, self.spot)]
        for value, held, spot in self.got:
            terms.append((value, [held.index(place) for place in places], spot))
        return self.lanes, terms

    def absorb(self):
        self.got.append((self.pieces[0], self.arriving, 0 if self.got else self.spot))


def scatter(cube, terms, *shares):
    near, far = terms
    other = cube.swap(far, 0)
    return [Scatter(cube, near, other, flip, lanes, spot) for lanes, spot, flip in shares]


def pack(movers):
    jobs = []
    for mover in movers:
        mover.absorb()
        mover.bit = mover.todo.pop(0)
        weight = 1 << (mover.bit - 1)
        sent = [place for place in mover.places if place & weight]
        mover.places = [place for place in mover.places if not place & weight]
        mover.arriving = [place ^ weight for place in sent]
        jobs.append(mover.job(sent))
    for mover, value in zip(movers, sum_rows(jobs, movers[0].rows)):
        mover.pieces = [value]


def send(movers):
    for mover in movers:
        mover.pieces = [mover.cube.swap(mover.pieces[0], mover.bit)]


def results(movers):
    while movers[0].todo:
        pack(movers)
        send(movers)
    for mover in movers:
        mover.absorb()
    return sum_rows([mover.job([0]) for mover in movers], movers[0].rows)


def pin(value, *others):
    flat = []
    for other in others:
        flat += other.pieces if hasattr(other, "pieces") else [other]
    return tie(value, *flat)[0]


def bind(value, *movers):
    flat = [piece for mover in movers for piece in mover.pieces]
    held = tie(value, *flat)
    spot = 1
    for mover in movers:
        count = len(mover.pieces)
        mover.pieces = list(held[spot : spot + count])
        spot += count
    return held[0]


def hold(movers, *others):
    for mover in movers:
        mover.pieces = [pin(piece, *others) for piece in mover.pieces]


def on_device(
    tokens,
    skip_tokens,
    text,
    timestep,
    grid,
    text_len,
    w_skip,
    w_mod,
    w_qkv,
    w_out1,
    w_query2,
    w_text_kv,
    w_out2,
    w_fc1,
    w_fc2,
    gain_skip,
    gain_attn,
    gain_cross,
    gain_mlp,
    gain_query,
    gain_key,
    cotangent,
):
    micros, slots, width = tokens.shape
    parts = lax.axis_size("sp")
    zone = lax.axis_index("sp")
    cube = Cube()
    ranks = cube.size
    rows = micros * slots
    sequence = slots * parts
    local = H // parts
    lanes = local * HP + -local * HP % 128
    text_slots = text.shape[1]
    text_strip = -(-text_slots // 16) * 16
    features = text.shape[2]
    strip = width // ranks
    middle = width // 2
    kept = w_skip.shape[0]
    skip_lanes = -(-kept // 256) * 256
    skip_cut = skip_lanes // 2
    qkv_cut = (3 * lanes) // 256 * 128 + 128
    text_rows = w_text_kv.shape[0]

    def spread(shard, before=None):
        if before is not None:
            shard, before = tie(shard, before)
        return lax.all_gather(shard, "sp", axis=0, tiled=False)

    def fetch(value, cut, joined=False):
        return [Gather(cube, value[:, :, :cut], 0, joined), Gather(cube, value[:, :, cut:], 1, joined)]

    def advance(movers):
        for mover in movers:
            mover.move()

    def join(movers):
        for mover in movers:
            mover.join()

    def exchange(value):
        return lax.all_to_all(value, "sp", split_axis=0, concat_axis=0, tiled=True)

    skip_z = spread(jnp.pad(w_skip.T, ((0, 0), (0, skip_lanes - kept))))
    steps = cube.spread(timestep[:, 0])
    joined = side_by_side(tokens.reshape(rows, width), skip_tokens.reshape(rows, width), kept, skip_lanes)
    wide = grid[:, 0, 1]
    counts = grid[:, 0, 0] * wide
    cosine, sine = rope_tables(sequence, wide, lanes)
    skip_z, steps, joined, cosine, sine = tie(skip_z, steps, joined, cosine, sine)
    skip_m = fetch(skip_z, skip_cut)
    qkv_z = spread(pad_heads(w_qkv.reshape(strip, -1), local), skip_z)
    advance(skip_m)

    time_act = jax.nn.silu(time_embed(steps, width)).astype(BF).reshape(ranks * micros, parts, -1)
    time_part = lax.dynamic_index_in_dim(time_act, zone, 1, keepdims=False)
    shift = cube.add(jnp.dot(time_part, w_mod, preferred_element_type=F32), "sp")
    skip_m[0].pieces[1], shift = tie(skip_m[0].pieces[1], shift)
    while skip_m[0].todo:
        advance(skip_m)
    shift = cube.trade(shift.reshape(ranks, micros, strip))
    skip_m[0].pieces[-1], shift = tie(skip_m[0].pieces[-1], shift)
    shift = jnp.stack([shift[mask] for mask in cube.masks]).reshape(2, ranks // 2, micros, strip)
    shift = jnp.transpose(shift, (0, 2, 1, 3)).reshape(2, micros, middle)
    qkv_m = fetch(qkv_z, qkv_cut)
    hold(qkv_m, *skip_m)
    advance(qkv_m)
    cross_z = jnp.concatenate([pad_heads(side, local) for side in (w_out1.T, w_query2, w_out2.T)], 1)
    cross_z = spread(pin(cross_z, *skip_m))
    fc1_z = spread(pin(w_fc1, *skip_m))
    join(skip_m)
    skip_w = [mover.weight() for mover in skip_m]

    def shuffle(count):
        block = count // ranks
        place = jnp.arange(count, dtype=jnp.int32)
        source = cube.owners[place // block] * block + place % block
        return (place[:, None] == source[None, :]).astype(BF)

    turn = shuffle(width)
    text_turn = shuffle(features)
    gains = jnp.stack([gain_skip, gain_attn, gain_cross, gain_mlp])
    gains = gains.reshape(4, ranks, strip)[:, cube.owners].reshape(4, 2, 1, middle)
    g_skip, g_attn, g_cross, g_mlp = gains

    lengths = text_len[:, 0, :]
    place = zone * slots + jnp.arange(slots, dtype=jnp.int32)
    live = (place[None, :] < counts[:, None]).astype(F32).reshape(rows, 1)
    gain_q = pad_heads(jnp.tile(gain_query, local)[None, :], local)
    gain_k = pad_heads(jnp.tile(gain_key, local)[None, :], local)

    grad3 = jnp.stack(
        [
            jnp.dot(cotangent.reshape(rows, width), side, preferred_element_type=F32) * live
            for side in (turn[:, :middle], turn[:, middle:])
        ]
    )
    d_mlp = grad3.astype(BF)

    wide_shape = jax.ShapeDtypeStruct((2, rows, middle), F32)
    low_shape = jax.ShapeDtypeStruct((2, rows, middle), BF)
    gain_shape = jax.ShapeDtypeStruct((2, 1, middle), F32)

    def first_norms(sums, extra, out):
        g0_ref, g1_ref, shift_ref = extra
        base_ref, stream_ref, pre_ref = out
        unit, _ = norm_unit(sums)
        stream = [unit[side] * g0_ref[side] for side in range(2)]
        unit, _ = norm_unit(stream)
        for side in range(2):
            base_ref[side] = sums[side]
            stream_ref[side] = stream[side]
            for micro in range(micros):
                cut = slice(micro * slots, (micro + 1) * slots)
                pre = unit[side][cut] * g1_ref[side] + shift_ref[side, micro : micro + 1]
                pre_ref[side, cut] = pre.astype(BF)

    def next_norm(sums, extra, out):
        before_ref, gain_ref = extra
        after_ref, pre_ref = out
        stream = [before_ref[side] + sums[side] for side in range(2)]
        unit, _ = norm_unit(stream)
        for side in range(2):
            after_ref[side] = stream[side]
            pre_ref[side] = (unit[side] * gain_ref[side]).astype(BF)

    base, stream, pre_attn = to_features(
        joined, skip_w, [g_skip, g_attn, shift], [wide_shape, wide_shape, low_shape], first_norms
    )
    while qkv_m[0].todo:
        advance(qkv_m)
    after_qkv = [mover.pieces[-1] for mover in qkv_m]
    hold(qkv_m, pre_attn)
    join(qkv_m)
    fc2_z = spread(pin(w_fc2.T, *after_qkv))
    pre_attn, cross_z, fc1_z = tie(pre_attn, cross_z, fc1_z)
    cross_m = fetch(cross_z, 2 * lanes, True)
    hold(cross_m, *after_qkv)
    advance(cross_m)
    qkv_w = [mover.weight() for mover in qkv_m]
    projected = to_lanes(pre_attn, qkv_w)
    projected = bind(projected, *cross_m)
    projected, fc2_z = tie(projected, fc2_z)
    while cross_m[0].todo:
        advance(cross_m)
    fc_m = [Gather(cube, fc1_z, 0, True), Gather(cube, fc2_z, 1, True)]
    hold(fc_m, cross_m[0].pieces[-1], cross_m[1].pieces[-1])
    advance(fc_m)
    raw = exchange(projected.reshape(parts, micros, slots, 3 * lanes))
    arrived = [mover.pieces[-1] for mover in cross_m]
    text_own = jnp.dot(text.reshape(-1, features), text_turn, preferred_element_type=F32).astype(BF)
    text_own = jnp.pad(
        text_own.reshape(micros, text_slots, features), ((0, 0), (0, text_strip - text_slots), (0, 0))
    ).reshape(micros * text_strip, features)
    text_z = jnp.pad(pad_heads(w_text_kv.reshape(text_rows, -1), local), ((0, max(0, strip - text_rows)), (0, 0)))
    while fc_m[0].todo:
        advance(fc_m)
    text_z = spread(pin(text_z, *arrived))
    text_all = spread(pin(text_own, *arrived))
    fc_m[0].pieces[0], d_mlp, turn, text_turn = tie(fc_m[0].pieces[0], d_mlp, turn, text_turn)
    join(cross_m)
    first_w, out2_w = [mover.weight() for mover in cross_m]
    out1_w, query2_w = (Lanes(first_w.near, first_w.far, lanes, index) for index in range(2))
    attended, turned_q, turned_k, norms = self_forward(raw, counts, cosine, sine, gain_q, gain_k)
    attended, text_all, text_z, first_w.far, out2_w.far = tie(attended, text_all, text_z, first_w.far, out2_w.far)
    out1_w.far = query2_w.far = first_w.far
    text_m = Gather(cube, text_z[:, :text_rows], 0, True)
    text_m.move()
    attended = exchange(attended).reshape(parts, rows, lanes)
    attended = bind(attended, text_m, *fc_m)
    while text_m.todo:
        text_m.move()
    join(fc_m)
    text_all = text_all.reshape(-1, features)
    text_all = jnp.stack([text_all[:, : features // 2], text_all[:, features // 2 :]])
    stream1, pre_cross = to_features(
        attended, [out1_w], [stream, g_cross], [wide_shape, low_shape], next_norm
    )
    fc1_w, fc2_w = [mover.weight() for mover in fc_m]
    hold([text_m], pre_cross)
    text_m.join()
    text_w = text_m.weight()
    query2 = to_lanes(pre_cross, [query2_w]).reshape(parts, micros, slots, lanes)
    text_kv = to_lanes(text_all, [text_w]).reshape(parts, parts, micros, text_strip, 2 * lanes)
    crossed = cross_forward(query2, text_kv, lengths, text_slots).reshape(parts, rows, lanes)
    stream2, pre_mlp = to_features(
        crossed, [out2_w], [stream1, g_mlp], [wide_shape, low_shape], next_norm
    )
    hidden0, activ0, partial, fc2_n0, fc2_f0 = mlp_forward(pre_mlp, d_mlp, stream2, fc1_w, fc2_w, 0)
    hidden1, activ1, result, fc2_n1, fc2_f1 = mlp_forward(pre_mlp, d_mlp, partial, fc1_w, fc2_w, 1, live)
    share = fc2_n0.shape[2]
    fc2_s = scatter(cube, (fc2_n0, fc2_f0), (share, 0, 0)) + scatter(cube, (fc2_n1, fc2_f1), (share, 0, 1))

    def settle(values, before=None):
        value = values[0] if len(values) == 1 else jnp.concatenate(values, 2)
        if before is not None:
            value, before = tie(value, before)
        return lax.psum_scatter(value, "sp", scatter_dimension=0, tiled=False)

    fc1_n0, fc1_f0, partial = mlp_backward(d_mlp, pre_mlp, hidden0, fc1_w, fc2_w, 0, None)
    fc1_s = scatter(cube, (fc1_n0, fc1_f0), (share, 0, 0))
    pack(fc2_s)
    partial = bind(partial, *fc2_s)
    send(fc2_s)
    fc1_n1, fc1_f1, grad2, d_cross, d_gain_mlp = mlp_backward(
        d_mlp, pre_mlp, hidden1, fc1_w, fc2_w, 1, partial, [stream2, g_mlp, grad3]
    )
    fc1_s += scatter(cube, (fc1_n1, fc1_f1), (share, 0, 1))
    d_cross = bind(d_cross, *fc2_s)
    d_crossed = to_lanes(d_cross, [out2_w])
    pack(fc2_s)
    d_crossed = bind(d_crossed, *fc2_s)
    send(fc2_s)
    d_query2, d_text_kv = cross_backward(
        query2, text_kv, lengths, d_crossed.reshape(parts, micros, slots, lanes), text_slots
    )
    d_query2 = bind(d_query2, *fc2_s)
    d_query2 = d_query2.reshape(parts, rows, lanes)
    d_text_kv = d_text_kv.reshape(parts, -1, 2 * lanes)
    total_fc2 = results(fc2_s)
    term_fc2 = settle(total_fc2)

    def go_back(sums, extra, out):
        add_norm_back(sums, *extra, *out)

    grad1, d_attn, d_gain_cross = to_features(
        d_query2, [query2_w], [stream1, g_cross, grad2], [wide_shape, low_shape, gain_shape], go_back
    )
    d_attn = bind(d_attn, *fc1_s)
    pack(fc1_s)
    d_attn = bind(d_attn, *fc1_s)
    send(fc1_s)
    d_attended = to_lanes(d_attn, [out1_w])
    d_attended, d_text_kv, pre_cross = tie(d_attended, d_text_kv, pre_cross)
    d_heads = exchange(d_attended.reshape(parts, micros, slots, lanes))

    def words_back(sums, extra, out):
        size = micros * text_strip
        for zone in range(parts):
            for side in range(2):
                out[0][zone, side] = sums[side][zone * size : (zone + 1) * size].astype(BF)

    words_shape = jax.ShapeDtypeStruct((parts, 2, micros * text_strip, features // 2), BF)
    d_words = to_features(d_text_kv, [text_w], [], [words_shape], words_back)[0]
    text_t = list(terms_of([(text_all, d_text_kv, 2 * lanes, 0)]))
    cross_t = terms_of(
        [(d_attn, attended, lanes, 0), (pre_cross, d_query2, lanes, 0), (d_cross, crossed, lanes, 0)]
    )
    cross_t = list(cross_t)
    d_heads, d_words, text_t[1], cross_t[1] = tie(d_heads, d_words, text_t[1], cross_t[1])
    d_words = settle([d_words])
    text_s = scatter(cube, text_t, (2 * lanes, 0, 1))
    cross_s = scatter(cube, cross_t, (2 * lanes, 0, 0), (lanes, 2, 1))
    d_heads = bind(d_heads, *fc1_s)
    pack(fc1_s)
    d_heads = bind(d_heads, *fc1_s)
    send(fc1_s)
    d_raw, d_gain_q, d_gain_k = self_backward(
        raw, counts, cosine, sine, gain_q, gain_k, turned_q, turned_k, norms, d_heads
    )
    d_raw, term_fc2, d_words = tie(d_raw, term_fc2, d_words)
    d_raw = bind(d_raw, *fc1_s)
    d_projected = exchange(d_raw).reshape(parts, rows, 3 * lanes)
    other_s = cross_s + text_s
    total_fc1 = results(fc1_s)
    pack(cross_s)
    pack(text_s)
    send(other_s)
    d_projected = bind(d_projected, *other_s)
    term_fc1 = settle(total_fc1, d_projected)
    qkv_t = terms_of([(pre_attn, d_projected, 3 * lanes, 0)])
    qkv_s = scatter(cube, qkv_t, (2 * lanes, 0, 0), (lanes, 2, 1))
    pack(cross_s)
    pack(text_s)
    send(other_s)
    pack(qkv_s)
    d_projected = bind(d_projected, *qkv_s)
    send(qkv_s)

    def last_norms(sums, extra, out):
        stream_ref, g1_ref, base_ref, g0_ref, add_ref = extra
        low_ref, d_shift_ref, d_g1_ref, d_g0_ref = out
        back, gains1 = norm_back([stream_ref[0], stream_ref[1]], g1_ref, sums)
        total = [add_ref[side] + back[side] for side in range(2)]
        back, gains0 = norm_back([base_ref[0], base_ref[1]], g0_ref, total)
        for side in range(2):
            low_ref[side] = back[side].astype(BF)
            d_g1_ref[side] = gains1[side]
            d_g0_ref[side] = gains0[side]
            for micro in range(micros):
                part = sums[side][micro * slots : (micro + 1) * slots]
                d_shift_ref[side, micro : micro + 1] = jnp.sum(part, 0, keepdims=True)

    shift_shape = jax.ShapeDtypeStruct((2, micros, middle), F32)
    d_base, d_shift, d_gain_attn, d_gain_skip = to_features(
        d_projected,
        qkv_w,
        [stream, g_attn, base, g_skip, grad1],
        [low_shape, shift_shape, gain_shape, gain_shape],
        last_norms,
    )
    d_base = bind(d_base, *other_s)
    skip_t = terms_of([(d_base, joined, skip_lanes, 0)])
    skip_s = scatter(cube, skip_t, (skip_cut, 0, 0), (skip_cut, 1, 1))
    pack(skip_s)
    pack(qkv_s)
    skip_s[0].pieces[0] = bind(skip_s[0].pieces[0], *qkv_s)
    send(qkv_s)
    send(skip_s)
    term_cross, term_text = settle(results(cross_s)), settle(results(text_s))
    total_qkv = results(qkv_s)
    last = settle(list(total_qkv) + list(results(skip_s)))
    term_qkv, term_skip = last[:, : 3 * lanes], last[:, 3 * lanes :]
    d_joined = to_inputs(d_base, skip_w, kept)
    result = (
        jnp.dot(result[0], turn[:, :middle].T, preferred_element_type=F32)
        + jnp.dot(result[1], turn[:, middle:].T, preferred_element_type=F32)
    ).astype(BF)
    d_words = d_words.reshape(2, micros * text_strip, features // 2)
    d_words = jnp.dot(
        d_words[0], text_turn[:, : features // 2].T, preferred_element_type=F32
    ) + jnp.dot(d_words[1], text_turn[:, features // 2 :].T, preferred_element_type=F32)
    d_words = d_words.reshape(micros, text_strip, features)[:, :text_slots]

    d_shift = jnp.transpose(d_shift.reshape(2, micros, ranks // 2, strip), (0, 2, 1, 3))
    d_shift = d_shift.reshape(ranks, micros, strip)
    d_shift = jnp.stack([d_shift[cube.masks.index(mask)] for mask in range(ranks)])
    d_shift = cube.add(cube.trade(d_shift), "sp").reshape(ranks * micros, strip)
    term_mod = lax.dot_general(
        time_part.astype(F32), d_shift, (((0,), (0,)), ((), ())), precision=lax.Precision.HIGHEST
    )

    places = jnp.array([cube.masks.index(mask) for mask in range(ranks)], jnp.int32)
    places = places[jnp.arange(ranks, dtype=jnp.int32) ^ cube.rank]
    gains = jnp.stack([d_gain_skip, d_gain_attn, d_gain_cross, d_gain_mlp])
    gains = gains.reshape(4, ranks, strip)[:, places].reshape(-1)
    heads = jnp.stack([jnp.sum(d_gain_q, (0, 1)), jnp.sum(d_gain_k, (0, 1))])
    heads = jnp.sum(heads[:, : local * HP].reshape(2, local, HP)[:, :, :HD], 1)
    packed = jnp.concatenate([gains, heads.reshape(-1)])
    packed = cube.add(cube.add(packed, "sp"), "dp")
    gains = packed[: 4 * width].reshape(4, ranks * parts, -1)
    gains = lax.dynamic_index_in_dim(gains, cube.rank * parts + zone, 1, keepdims=False)
    heads = packed[4 * width :].reshape(2, HD)

    def whole(term, groups):
        return cut_heads(term.astype(F32), local).reshape(term.shape[0], groups, -1)

    return (
        result.reshape(tokens.shape),
        d_joined[0].reshape(tokens.shape),
        d_joined[1].reshape(tokens.shape),
        d_words.reshape(text.shape),
        term_skip.astype(F32)[:, :kept].T,
        term_mod,
        whole(term_qkv, 3),
        cut_heads(term_cross[:, :lanes].astype(F32), local).T,
        cut_heads(term_cross[:, lanes : 2 * lanes].astype(F32), local),
        whole(term_text, 2),
        cut_heads(term_cross[:, 2 * lanes :].astype(F32), local).T,
        term_fc1.astype(F32),
        term_fc2.astype(F32).T,
        gains[0],
        gains[1],
        gains[2],
        gains[3],
        heads[0],
        heads[1],
    )


def solution(mesh):
    rows = P(None, ("dp", "sp"), None)
    column = P("sp", "dp")
    row = P("dp", "sp")
    grouped = P("dp", None, "sp")
    in_specs = (
        (rows, rows, rows, P(None, "dp"), P(None, "dp", None), P(None, "dp", None))
        + (column, column, grouped, column, row, grouped, column, row, column)
        + (P(),) * 6
        + (rows,)
    )
    out_specs = (
        (rows, rows, rows, rows)
        + (column, column, grouped, column, row, grouped, column, row, column)
        + (P(("dp", "sp")),) * 4
        + (P(), P())
    )
    return jax.shard_map(
        on_device, mesh=mesh, in_specs=in_specs, out_specs=out_specs, check_vma=False
    )
```

```python
import math

import jax
import jax.numpy as jnp
from jax import lax
from jax.experimental import pallas as pl
from jax.experimental.pallas import tpu as pltpu
from jax.sharding import PartitionSpec as P

H = 16
HD = 88
HP = 96
CLIP_LEN = 77
ROWS = 256

EPS = 1e-06
MASKED = -1e30
LOG2E = 1.4426950408889634
BF = jnp.bfloat16
F32 = jnp.float32


def time_embed(step, width):
    half = width // 2
    rate = jnp.exp(-math.log(10000.0) * jnp.arange(half, dtype=F32) / half)
    angle = step.astype(F32)[..., None] * rate
    return jnp.concatenate([jnp.cos(angle), jnp.sin(angle)], -1)


def rope_tables(sequence, wide, lanes):
    place = jnp.arange(sequence, dtype=jnp.int32)[None, :, None]
    wide = wide[:, None, None]
    lane = jnp.arange(lanes, dtype=jnp.int32)[None, None, :] % HP
    pair = lane // 2
    quarter = HD // 4
    upper = pair < quarter
    rank = jnp.where(upper, pair, pair - quarter).astype(F32)
    rate = jnp.exp(-math.log(10000.0) * rank / quarter)
    angle = jnp.where(upper, place // wide, place % wide).astype(F32) * rate
    sine = jnp.sin(angle)
    return jnp.cos(angle), jnp.where(lane % 2 == 0, -sine, sine)


def pad_heads(packed, local):
    rows, lanes = packed.shape
    groups = packed.reshape(rows, lanes // (local * HD), local, HD)
    groups = jnp.pad(groups, ((0, 0), (0, 0), (0, 0), (0, HP - HD)))
    groups = groups.reshape(rows, -1, local * HP)
    return jnp.pad(groups, ((0, 0), (0, 0), (0, -local * HP % 128))).reshape(rows, -1)


def cut_heads(padded, local):
    rows = padded.shape[0]
    groups = padded.reshape(rows, -1, local * HP + -local * HP % 128)[:, :, : local * HP]
    return groups.reshape(rows, -1, local, HP)[..., :HD].reshape(rows, -1)


def head_masks(shape, local):
    lane = lax.broadcasted_iota(jnp.int32, shape, len(shape) - 1)
    inside = lane % HP < HD
    return [((lane // HP == h) & inside).astype(F32) for h in range(local)]


def head_mean(value, masks):
    total = None
    for mask in masks:
        term = (jnp.sum(value * mask, -1, keepdims=True) * (1.0 / HD)) * mask
        total = term if total is None else total + term
    return total


def head_unit(value, masks):
    centre = value - head_mean(value, masks)
    spread = None
    square = centre * centre
    for mask in masks:
        mean = jnp.sum(square * mask, -1, keepdims=True) * (1.0 / HD)
        term = lax.rsqrt(mean + EPS) * mask
        spread = term if spread is None else spread + term
    return centre * spread, spread


def turn_pairs(value):
    lanes = value.shape[-1]
    after = pltpu.roll(value, lanes - 1, 1)
    before = pltpu.roll(value, 1, 1)
    lane = lax.broadcasted_iota(jnp.int32, value.shape, 1)
    return jnp.where(lane % 2 == 0, after, before)


def dot_nt(left, right):
    return lax.dot_general(left, right, (((1,), (1,)), ((), ())), preferred_element_type=F32)


def dot_nn(left, right):
    return lax.dot_general(left, right, (((1,), (0,)), ((), ())), preferred_element_type=F32)


def dot_tn(left, right):
    return lax.dot_general(left, right, (((0,), (0,)), ((), ())), preferred_element_type=F32)


def self_forward(raw, counts, cosine, sine, gain_q, gain_k):
    parts, micros, slots, packed = raw.shape
    lanes = packed // 3
    local = lanes // HP
    sequence = parts * slots
    factor = HD ** (-0.5) * LOG2E

    def kernel(count_ref, raw_ref, cos_ref, sin_ref, gq_ref, gk_ref, out_ref, q_ref, k_ref, lse_ref):
        count = count_ref[pl.program_id(0)]
        blocks = (count + slots - 1) // slots
        out_ref[...] = jnp.zeros_like(out_ref)
        masks = head_masks((1, lanes), local)

        def prepare(part, carry):
            spot = pl.ds(pl.multiple_of(part * slots, slots), slots)
            cosine, sine = cos_ref[0, spot, :], sin_ref[0, spot, :]
            for index, gain_ref, dest in ((0, gq_ref, q_ref), (1, gk_ref, k_ref)):
                value = raw_ref[part, 0, :, index * lanes : (index + 1) * lanes].astype(F32)
                scaled = head_unit(value, masks)[0] * gain_ref[...]
                dest[0, spot, :] = (scaled * cosine + turn_pairs(scaled) * sine).astype(BF)
            return carry

        lax.fori_loop(0, parts, prepare, 0)
        column = lax.broadcasted_iota(jnp.int32, (1, sequence), 1)
        bias = jnp.where(column < count, 0.0, MASKED)
        for h in range(local):
            cut = slice(h * HP, (h + 1) * HP)
            keys = k_ref[0, :, cut]
            values = raw_ref[:, 0, :, 2 * lanes + h * HP : 2 * lanes + (h + 1) * HP].reshape(sequence, HP)

            def one_block(part, carry):
                spot = pl.ds(pl.multiple_of(part * slots, slots), slots)
                scores = dot_nt(q_ref[0, spot, cut], keys) + bias
                top = jnp.max(scores, -1, keepdims=True)
                raised = jnp.exp2((scores - top) * factor)
                total = jnp.sum(raised, -1, keepdims=True)
                result = dot_nn(raised.astype(BF), values) / total
                out_ref[part, 0, :, cut] = result.astype(BF)
                norm = jnp.broadcast_to(top * factor + jnp.log2(total), (slots, 128))
                lse_ref[0, h : h + 1, spot] = jnp.transpose(norm)[0:1, :]
                return carry

            lax.fori_loop(0, blocks, one_block, 0)

    whole = lambda m, c: (0, m, 0, 0)
    table = lambda m, c: (m, 0, 0)
    fixed = lambda m, c: (0, 0)
    return pl.pallas_call(
        kernel,
        name="self_forward",
        grid_spec=pltpu.PrefetchScalarGridSpec(
            num_scalar_prefetch=1,
            grid=(micros,),
            in_specs=[
                pl.BlockSpec((parts, 1, slots, packed), whole),
                pl.BlockSpec((1, sequence, lanes), table),
                pl.BlockSpec((1, sequence, lanes), table),
                pl.BlockSpec((1, lanes), fixed),
                pl.BlockSpec((1, lanes), fixed),
            ],
            out_specs=[
                pl.BlockSpec((parts, 1, slots, lanes), whole),
                pl.BlockSpec((1, sequence, lanes), table),
                pl.BlockSpec((1, sequence, lanes), table),
                pl.BlockSpec((1, local, sequence), table),
            ],
        ),
        out_shape=[
            jax.ShapeDtypeStruct((parts, micros, slots, lanes), BF),
            jax.ShapeDtypeStruct((micros, sequence, lanes), BF),
            jax.ShapeDtypeStruct((micros, sequence, lanes), BF),
            jax.ShapeDtypeStruct((micros, local, sequence), F32),
        ],
        compiler_params=params(),
        cost_estimate=cost(4 * micros * local * sequence * sequence * HP),
    )(counts, raw, cosine, sine, gain_q, gain_k)


def self_backward(raw, counts, cosine, sine, gain_q, gain_k, turned_q, turned_k, norms, incoming):
    parts, micros, slots, packed = raw.shape
    lanes = packed // 3
    local = lanes // HP
    sequence = parts * slots
    scale = HD ** (-0.5)
    factor = scale * LOG2E

    def kernel(
        count_ref,
        raw_ref,
        cos_ref,
        sin_ref,
        gq_ref,
        gk_ref,
        q_ref,
        k_ref,
        lse_ref,
        in_ref,
        out_ref,
        dgq_ref,
        dgk_ref,
        dq_s,
        dk_s,
        dv_s,
    ):
        count = count_ref[pl.program_id(0)]
        blocks = (count + slots - 1) // slots
        dq_s[...] = jnp.zeros_like(dq_s)
        dk_s[...] = jnp.zeros_like(dk_s)
        dv_s[...] = jnp.zeros_like(dv_s)
        row = lax.broadcasted_iota(jnp.int32, (sequence, 1), 0)
        bias = jnp.where(row < count, 0.0, MASKED)
        for h in range(local):
            cut = slice(h * HP, (h + 1) * HP)
            keys = k_ref[0, :, cut]
            values = raw_ref[:, 0, :, 2 * lanes + h * HP : 2 * lanes + (h + 1) * HP].reshape(sequence, HP)

            def one_block(part, carry):
                spot = pl.ds(pl.multiple_of(part * slots, slots), slots)
                rows = q_ref[0, spot, cut]
                grads = in_ref[part, 0, :, cut]
                norm = lse_ref[0, h : h + 1, spot]
                probs = jnp.exp2(dot_nt(keys, rows) * factor + bias - norm)
                d_probs = dot_nt(values, grads)
                inner = jnp.sum(probs * d_probs, 0, keepdims=True)
                d_scores = (probs * (d_probs - inner)).astype(BF)
                dv_s[:, cut] += dot_nn(probs.astype(BF), grads)
                dk_s[:, cut] += dot_nn(d_scores, rows)
                dq_s[spot, cut] = dot_tn(d_scores, keys)
                return carry

            lax.fori_loop(0, blocks, one_block, 0)
        masks = head_masks((1, lanes), local)

        def finish(part, carry):
            spot = pl.ds(pl.multiple_of(part * slots, slots), slots)
            cosine, sine = cos_ref[0, spot, :], sin_ref[0, spot, :]
            sums = []
            for index, gain_ref, source in ((0, gq_ref, dq_s), (1, gk_ref, dk_s)):
                grad = source[spot, :] * scale
                grad = grad * cosine - turn_pairs(grad) * sine
                value = raw_ref[part, 0, :, index * lanes : (index + 1) * lanes].astype(F32)
                unit, spread = head_unit(value, masks)
                leading = grad * gain_ref[...]
                back = leading - head_mean(leading, masks) - unit * head_mean(leading * unit, masks)
                out_ref[part, 0, :, index * lanes : (index + 1) * lanes] = (spread * back).astype(BF)
                sums.append(carry[index] + jnp.sum(grad * unit, 0, keepdims=True))
            out_ref[part, 0, :, 2 * lanes : 3 * lanes] = dv_s[spot, :].astype(BF)
            return tuple(sums)

        zero = jnp.zeros((1, lanes), F32)
        d_gains = lax.fori_loop(0, parts, finish, (zero, zero))
        dgq_ref[0] = d_gains[0]
        dgk_ref[0] = d_gains[1]

    whole = lambda m, c: (0, m, 0, 0)
    table = lambda m, c: (m, 0, 0)
    fixed = lambda m, c: (0, 0)
    return pl.pallas_call(
        kernel,
        name="self_backward",
        grid_spec=pltpu.PrefetchScalarGridSpec(
            num_scalar_prefetch=1,
            grid=(micros,),
            in_specs=[
                pl.BlockSpec((parts, 1, slots, packed), whole),
                pl.BlockSpec((1, sequence, lanes), table),
                pl.BlockSpec((1, sequence, lanes), table),
                pl.BlockSpec((1, lanes), fixed),
                pl.BlockSpec((1, lanes), fixed),
                pl.BlockSpec((1, sequence, lanes), table),
                pl.BlockSpec((1, sequence, lanes), table),
                pl.BlockSpec((1, local, sequence), table),
                pl.BlockSpec((parts, 1, slots, lanes), whole),
            ],
            out_specs=[
                pl.BlockSpec((parts, 1, slots, packed), whole),
                pl.BlockSpec((1, 1, lanes), table),
                pl.BlockSpec((1, 1, lanes), table),
            ],
            scratch_shapes=[pltpu.VMEM((sequence, lanes), F32) for index in range(3)],
        ),
        out_shape=[
            jax.ShapeDtypeStruct((parts, micros, slots, packed), BF),
            jax.ShapeDtypeStruct((micros, 1, lanes), F32),
            jax.ShapeDtypeStruct((micros, 1, lanes), F32),
        ],
        compiler_params=params(),
        cost_estimate=cost(10 * micros * local * sequence * sequence * HP),
    )(counts, raw, cosine, sine, gain_q, gain_k, turned_q, turned_k, norms, incoming)


def cost(flops):
    return pl.CostEstimate(flops=flops // 16, bytes_accessed=flops // 16000, transcendentals=0)


def full(shape):
    return pl.BlockSpec(shape, lambda *index: (0,) * len(shape))


def params(megabytes=60):
    return pltpu.CompilerParams(vmem_limit_bytes=megabytes << 20)


class Lanes:
    def __init__(self, near, far, block=None, index=0):
        self.near, self.far = near, far
        self.block = block or near.shape[2]
        self.index = index

    def spec(self):
        index = self.index
        return pl.BlockSpec((1, self.near.shape[1], self.block), lambda p, *rest: (p, 0, index))


def to_lanes(value, weights, dtype=BF, name="to_lanes"):
    rows = value.shape[1]
    parts, half, _ = weights[0].near.shape
    total = sum(weight.block for weight in weights)

    def kernel(x_ref, *refs):
        out_ref = refs[-1]
        at = 0
        for index, weight in enumerate(weights):
            result = dot_nn(x_ref[0], refs[2 * index][0]) + dot_nn(x_ref[1], refs[2 * index + 1][0])
            out_ref[0, :, at : at + weight.block] = result.astype(dtype)
            at += weight.block

    return pl.pallas_call(
        kernel,
        name=name,
        grid=(parts,),
        in_specs=[full(value.shape)] + [weight.spec() for weight in weights for side in range(2)],
        out_specs=pl.BlockSpec((1, rows, total), lambda p: (p, 0, 0)),
        out_shape=jax.ShapeDtypeStruct((parts, rows, total), dtype),
        compiler_params=params(),
        cost_estimate=cost(4 * rows * half * parts * total),
    )(value, *[side for weight in weights for side in (weight.near, weight.far)])


def to_inputs(value, weights, kept):
    rows = value.shape[1]
    parts, half, _ = weights[0].near.shape
    sides = parts // 2

    def kernel(x_ref, *refs):
        out_ref = refs[-1]
        for side in range(sides):

            @pl.when(pl.program_id(0) % sides == side)
            def _():
                at = 0
                for index, weight in enumerate(weights):
                    result = dot_nn(x_ref[0], refs[2 * index][0]) + dot_nn(
                        x_ref[1], refs[2 * index + 1][0]
                    )
                    take = min(weight.block, kept - at)
                    start = side * kept + at
                    out_ref[0, :, start : start + take] = result[:, :take]
                    at += take

    return pl.pallas_call(
        kernel,
        name="to_inputs",
        grid=(parts,),
        in_specs=[full(value.shape)] + [weight.spec() for weight in weights for side in range(2)],
        out_specs=pl.BlockSpec((1, rows, sides * kept), lambda p: (p // sides, 0, 0)),
        out_shape=jax.ShapeDtypeStruct((2, rows, sides * kept), F32),
        compiler_params=params(),
        cost_estimate=cost(4 * rows * half * parts * kept),
    )(value, *[side for weight in weights for side in (weight.near, weight.far)])


def to_features(value, weights, extras, outs, finish, name="to_features"):
    parts, rows, total = value.shape
    half = weights[0].near.shape[1]
    count = 2 * len(weights)

    def kernel(*refs):
        y_ref, weight_refs = refs[0], refs[1 : 1 + count]
        extra_refs = refs[1 + count : 1 + count + len(extras)]
        out_refs = refs[1 + count + len(extras) : -1]
        sums = refs[-1]

        @pl.when(pl.program_id(0) == 0)
        def _():
            sums[...] = jnp.zeros_like(sums)

        at = 0
        for index, weight in enumerate(weights):
            left = y_ref[0, :, at : at + weight.block]
            for side in range(2):
                sums[side] += dot_nt(left, weight_refs[2 * index + side][0])
            at += weight.block

        @pl.when(pl.program_id(0) == parts - 1)
        def _():
            finish([sums[0], sums[1]], extra_refs, out_refs)

    return pl.pallas_call(
        kernel,
        name=name,
        grid=(parts,),
        in_specs=[pl.BlockSpec((1, rows, total), lambda p: (p, 0, 0))]
        + [weight.spec() for weight in weights for side in range(2)]
        + [full(extra.shape) for extra in extras],
        out_specs=[full(out.shape) for out in outs],
        out_shape=outs,
        scratch_shapes=[pltpu.VMEM((2, rows, half), F32)],
        compiler_params=params(),
        cost_estimate=cost(4 * rows * half * parts * total),
    )(value, *[side for weight in weights for side in (weight.near, weight.far)], *extras)


def terms_of(pairs, name="terms_of"):
    half = pairs[0][0].shape[2]
    parts = pairs[0][1].shape[0]
    total = sum(pair[2] for pair in pairs)
    rows = [pair[0].shape[1] for pair in pairs]

    def kernel(*refs):
        count = len(pairs)
        lefts, rights = refs[:count], refs[count : 2 * count]
        near_ref, far_ref = refs[2 * count : 2 * count + 2]
        turned = refs[2 * count + 2 :]

        @pl.when(pl.program_id(0) == 0)
        def _():
            for left, flat in zip(lefts, turned):
                for side in range(2):
                    flat[side] = jnp.transpose(left[side])

        at = 0
        for pair, right, flat in zip(pairs, rights, turned):
            lanes = pair[2]
            near_ref[0, :, at : at + lanes] = dot_nn(flat[0], right[0]).astype(BF)
            far_ref[0, :, at : at + lanes] = dot_nn(flat[1], right[0]).astype(BF)
            at += lanes

    def right_spec(pair):
        return pl.BlockSpec((1, pair[1].shape[1], pair[2]), lambda p: (p, 0, pair[3]))

    out = jax.ShapeDtypeStruct((parts, half, total), BF)
    return pl.pallas_call(
        kernel,
        name=name,
        grid=(parts,),
        in_specs=[full(pair[0].shape) for pair in pairs] + [right_spec(pair) for pair in pairs],
        out_specs=[pl.BlockSpec((1, half, total), lambda p: (p, 0, 0))] * 2,
        out_shape=[out, out],
        scratch_shapes=[pltpu.VMEM((2, half, count), BF) for count in rows],
        compiler_params=params(),
        cost_estimate=cost(sum(4 * half * parts * pair[2] * count for pair, count in zip(pairs, rows))),
    )(*[pair[0] for pair in pairs], *[pair[1] for pair in pairs])


def norm_unit(halves):
    width = 2 * halves[0].shape[-1]
    mean = sum(jnp.sum(half, -1, keepdims=True) for half in halves) / width
    centre = [half - mean for half in halves]
    spread = sum(jnp.sum(half * half, -1, keepdims=True) for half in centre) / width
    scale = lax.rsqrt(spread + EPS)
    return [half * scale for half in centre], scale


def norm_back(halves, gain_ref, incoming):
    width = 2 * halves[0].shape[-1]
    unit, scale = norm_unit(halves)
    leading = [incoming[side] * gain_ref[side] for side in range(2)]
    mean = sum(jnp.sum(half, -1, keepdims=True) for half in leading) / width
    inner = sum(jnp.sum(leading[side] * unit[side], -1, keepdims=True) for side in range(2)) / width
    back = [scale * (leading[side] - mean - unit[side] * inner) for side in range(2)]
    gains = [jnp.sum(incoming[side] * unit[side], 0, keepdims=True) for side in range(2)]
    return back, gains


def join_rows(pieces, rows, name="join_rows"):
    parts, _, lanes = pieces[0][0].shape
    count = len(pieces)
    if rows % 16:
        return jnp.concatenate([array[:, block * rows : (block + 1) * rows] for array, block in pieces], 1)

    def kernel(*refs):
        for index in range(count):
            refs[-1][0, index * rows : (index + 1) * rows] = refs[index][0]

    def spec(block):
        return pl.BlockSpec((1, rows, lanes), lambda p: (p, block, 0))

    return pl.pallas_call(
        kernel,
        name=name,
        grid=(parts,),
        in_specs=[spec(block) for _, block in pieces],
        out_specs=pl.BlockSpec((1, count * rows, lanes), lambda p: (p, 0, 0)),
        out_shape=jax.ShapeDtypeStruct((parts, count * rows, lanes), BF),
        compiler_params=params(),
        cost_estimate=cost(parts * count * rows * lanes),
    )(*[array for array, _ in pieces])


def sum_rows(jobs, rows, name="sum_rows"):
    parts = jobs[0][1][0][0].shape[0]
    if rows % 16:
        results = []
        for lanes, terms in jobs:
            value = 0.0
            for array, blocks, spot in terms:
                split = array[:, :, spot * lanes : (spot + 1) * lanes].reshape(parts, -1, rows, lanes)
                value = value + jnp.stack([split[:, block] for block in blocks], 1).astype(F32)
            results.append(value.astype(BF).reshape(parts, -1, lanes))
        return results
    spots = [
        (array, blocks[index], spot, lanes)
        for lanes, terms in jobs
        for index in range(len(terms[0][1]))
        for array, blocks, spot in terms
    ]

    def kernel(*refs):
        at = 0
        for order, (_, terms) in enumerate(jobs):
            out_ref = refs[len(spots) + order]
            for index in range(len(terms[0][1])):
                value = refs[at][0].astype(F32)
                for offset in range(1, len(terms)):
                    value = value + refs[at + offset][0].astype(F32)
                out_ref[0, index * rows : (index + 1) * rows] = value.astype(BF)
                at += len(terms)

    def spec(block, spot, lanes):
        return pl.BlockSpec((1, rows, lanes), lambda p: (p, block, spot))

    shapes = [(len(terms[0][1]) * rows, lanes) for lanes, terms in jobs]
    return pl.pallas_call(
        kernel,
        name=name,
        grid=(parts,),
        in_specs=[spec(*rest) for _, *rest in spots],
        out_specs=[pl.BlockSpec((1, *shape), lambda p: (p, 0, 0)) for shape in shapes],
        out_shape=[jax.ShapeDtypeStruct((parts, *shape), BF) for shape in shapes],
        compiler_params=params(),
        cost_estimate=cost(sum(parts * size * lanes for size, lanes in shapes)),
    )(*[array for array, *_ in spots])


def side_by_side(left, right, kept, lanes):
    rows, width = left.shape
    count = width // kept

    def kernel(left_ref, right_ref, out_ref):
        for index, ref in enumerate((left_ref, right_ref)):
            for side in range(count):
                spot = count * index + side
                out_ref[spot, :, :kept] = ref[:, side * kept : (side + 1) * kept]
                if lanes > kept:
                    out_ref[spot, :, kept:] = jnp.zeros((rows, lanes - kept), BF)

    return pl.pallas_call(
        kernel,
        name="side_by_side",
        out_shape=jax.ShapeDtypeStruct((2 * count, rows, lanes), BF),
        compiler_params=params(),
        cost_estimate=cost(4 * rows * lanes),
    )(left, right)


def mlp_forward(rows_in, grads, start, weight1, weight2, part, live=None):
    _, rows, half = rows_in.shape
    parts, _, lanes = weight1.near.shape
    ff = lanes // 2
    step = 768 if ff % 768 == 0 else ff
    steps = ff // step
    extras = [] if live is None else [live]

    def kernel(x_ref, g_ref, s_ref, n1_ref, f1_ref, n2_ref, f2_ref, *refs):
        hid_ref, act_ref, out_ref, dn2_ref, df2_ref, turned, sums = refs[len(extras) :]
        first = (pl.program_id(0) == 0) & (pl.program_id(1) == 0)
        last = (pl.program_id(0) == parts - 1) & (pl.program_id(1) == steps - 1)

        @pl.when(first)
        def _():
            for side in range(2):
                turned[side] = jnp.transpose(g_ref[side])
            sums[...] = s_ref[...]

        hidden = dot_nn(x_ref[0], n1_ref[0]) + dot_nn(x_ref[1], f1_ref[0])
        hid_ref[0] = hidden
        activ = jax.nn.gelu(hidden, approximate=True).astype(BF)
        act_ref[0] = activ
        sums[0] += dot_nt(activ, n2_ref[0])
        sums[1] += dot_nt(activ, f2_ref[0])
        dn2_ref[0] = dot_nn(turned[0], activ).astype(BF)
        df2_ref[0] = dot_nn(turned[1], activ).astype(BF)

        @pl.when(last)
        def _():
            if live is None:
                out_ref[...] = sums[...]
            else:
                out_ref[...] = (sums[...] * refs[0][...]).astype(BF)

    weight = pl.BlockSpec((1, half, step), lambda p, n: (p, 0, part * steps + n))
    grad = pl.BlockSpec((1, half, step), lambda p, n: (p, 0, n))
    unit = pl.BlockSpec((1, rows, step), lambda p, n: (p, 0, n))
    whole = full((2, rows, half))
    grad_shape = jax.ShapeDtypeStruct((parts, half, ff), BF)
    return pl.pallas_call(
        kernel,
        name="mlp_forward",
        grid=(parts, steps),
        in_specs=[whole, whole, whole, weight, weight, weight, weight] + [full(extra.shape) for extra in extras],
        out_specs=[unit, unit, whole, grad, grad],
        out_shape=[
            jax.ShapeDtypeStruct((parts, rows, ff), F32),
            jax.ShapeDtypeStruct((parts, rows, ff), BF),
            jax.ShapeDtypeStruct((2, rows, half), F32 if live is None else BF),
            grad_shape,
            grad_shape,
        ],
        scratch_shapes=[pltpu.VMEM((2, half, rows), BF), pltpu.VMEM((2, rows, half), F32)],
        compiler_params=params(),
        cost_estimate=cost(12 * rows * half * parts * ff),
    )(rows_in, grads, start, weight1.near, weight1.far, weight2.near, weight2.far, *extras)


def gelu_slope(value):
    root = math.sqrt(2.0 / math.pi)
    square = value * value
    curve = jnp.tanh(root * value * (1.0 + 0.044715 * square))
    return 0.5 * (1.0 + curve) + 0.5 * value * (1.0 - curve * curve) * root * (
        1.0 + 3.0 * 0.044715 * square
    )


def mlp_backward(grads, rows_in, hidden, weight1, weight2, part, start, finish=None):
    _, rows, half = rows_in.shape
    parts, _, lanes = weight1.near.shape
    ff = lanes // 2
    step = 768 if ff % 768 == 0 else ff
    steps = ff // step
    extras = list(finish or []) + ([] if start is None else [start])

    def kernel(g_ref, x_ref, hid_ref, n1_ref, f1_ref, n2_ref, f2_ref, *refs):
        extra_refs, refs = refs[: len(extras)], refs[len(extras) :]
        dn1_ref, df1_ref = refs[:2]
        out_refs = refs[2:-2]
        turned, sums = refs[-2:]
        first = (pl.program_id(0) == 0) & (pl.program_id(1) == 0)
        last = (pl.program_id(0) == parts - 1) & (pl.program_id(1) == steps - 1)

        @pl.when(first)
        def _():
            for side in range(2):
                turned[side] = jnp.transpose(x_ref[side])
            sums[...] = jnp.zeros_like(sums) if start is None else extra_refs[-1][...]

        d_activ = dot_nn(g_ref[0], n2_ref[0]) + dot_nn(g_ref[1], f2_ref[0])
        d_hidden = (d_activ * gelu_slope(hid_ref[0])).astype(BF)
        dn1_ref[0] = dot_nn(turned[0], d_hidden).astype(BF)
        df1_ref[0] = dot_nn(turned[1], d_hidden).astype(BF)
        sums[0] += dot_nt(d_hidden, n1_ref[0])
        sums[1] += dot_nt(d_hidden, f1_ref[0])

        @pl.when(last)
        def _():
            if finish is None:
                out_refs[0][...] = sums[...]
            else:
                value_ref, gain_ref, add_ref = extra_refs[:3]
                add_norm_back([sums[0], sums[1]], value_ref, gain_ref, add_ref, *out_refs)

    weight = pl.BlockSpec((1, half, step), lambda p, n: (p, 0, part * steps + n))
    grad = pl.BlockSpec((1, half, step), lambda p, n: (p, 0, n))
    unit = pl.BlockSpec((1, rows, step), lambda p, n: (p, 0, n))
    whole = full((2, rows, half))
    grad_shape = jax.ShapeDtypeStruct((parts, half, ff), BF)
    wide = jax.ShapeDtypeStruct((2, rows, half), F32)
    outs = [wide] if finish is None else [wide, *back_shapes(rows, half)]
    return pl.pallas_call(
        kernel,
        name="mlp_backward",
        grid=(parts, steps),
        in_specs=[whole, whole, unit, weight, weight, weight, weight] + [full(extra.shape) for extra in extras],
        out_specs=[grad, grad] + [full(out.shape) for out in outs],
        out_shape=[grad_shape, grad_shape] + outs,
        scratch_shapes=[pltpu.VMEM((2, half, rows), BF), pltpu.VMEM((2, rows, half), F32)],
        compiler_params=params(),
        cost_estimate=cost(12 * rows * half * parts * ff),
    )(grads, rows_in, hidden, weight1.near, weight1.far, weight2.near, weight2.far, *extras)


def back_shapes(rows, half):
    return [jax.ShapeDtypeStruct((2, rows, half), BF), jax.ShapeDtypeStruct((2, 1, half), F32)]


def add_norm_back(incoming, value_ref, gain_ref, add_ref, out_ref, low_ref, d_gain_ref):
    back, gains = norm_back([value_ref[0], value_ref[1]], gain_ref, incoming)
    for side in range(2):
        total = add_ref[side] + back[side]
        out_ref[side] = total
        low_ref[side] = total.astype(BF)
        d_gain_ref[side] = gains[side]


def text_bias(lengths_ref, micro, words, strip, text_slots, axis):
    spot = lax.broadcasted_iota(jnp.int32, (1, words) if axis else (words, 1), axis)
    inner = spot % strip
    place = spot // strip * text_slots + inner
    live = (place < lengths_ref[micro, 0]) | (
        (place >= CLIP_LEN) & (place < CLIP_LEN + lengths_ref[micro, 1])
    )
    return jnp.where(live & (inner < text_slots), 0.0, MASKED)


def cross_forward(query, text_kv, lengths, text_slots):
    parts, micros, slots, lanes = query.shape
    zones, strip = text_kv.shape[1], text_kv.shape[3]
    words = zones * strip
    local = lanes // HP
    factor = HD ** (-0.5) * LOG2E

    def kernel(len_ref, q_ref, kv_ref, out_ref):
        bias = text_bias(len_ref, pl.program_id(1), words, strip, text_slots, 1)
        for h in range(local):
            cut = slice(h * HP, (h + 1) * HP)
            keys = kv_ref[0, :, 0, :, cut].reshape(words, HP)
            scores = dot_nt(q_ref[0, 0, :, cut], keys) + bias
            top = jnp.max(scores, -1, keepdims=True)
            raised = jnp.exp2((scores - top) * factor)
            total = jnp.sum(raised, -1, keepdims=True)
            values = kv_ref[0, :, 0, :, lanes + h * HP : lanes + (h + 1) * HP].reshape(words, HP)
            out_ref[0, 0, :, cut] = (dot_nn(raised.astype(BF), values) / total).astype(BF)

    spot = lambda p, m, c: (p, m, 0, 0)
    far = lambda p, m, c: (p, 0, m, 0, 0)
    return pl.pallas_call(
        kernel,
        name="cross_forward",
        grid_spec=pltpu.PrefetchScalarGridSpec(
            num_scalar_prefetch=1,
            grid=(parts, micros),
            in_specs=[
                pl.BlockSpec((1, 1, slots, lanes), spot),
                pl.BlockSpec((1, zones, 1, strip, 2 * lanes), far),
            ],
            out_specs=pl.BlockSpec((1, 1, slots, lanes), spot),
        ),
        out_shape=jax.ShapeDtypeStruct(query.shape, BF),
        compiler_params=params(),
        cost_estimate=cost(4 * parts * micros * slots * words * lanes),
    )(lengths, query, text_kv)


def cross_backward(query, text_kv, lengths, incoming, text_slots):
    parts, micros, slots, lanes = query.shape
    zones, strip = text_kv.shape[1], text_kv.shape[3]
    words = zones * strip
    local = lanes // HP
    scale = HD ** (-0.5)
    factor = scale * LOG2E

    def kernel(len_ref, q_ref, kv_ref, in_ref, dq_ref, dkv_ref):
        bias = text_bias(len_ref, pl.program_id(1), words, strip, text_slots, 0)
        for h in range(local):
            cut = slice(h * HP, (h + 1) * HP)
            far = slice(lanes + h * HP, lanes + (h + 1) * HP)
            rows = q_ref[0, 0, :, cut]
            keys = kv_ref[0, :, 0, :, cut].reshape(words, HP)
            values = kv_ref[0, :, 0, :, far].reshape(words, HP)
            grads = in_ref[0, 0, :, cut]
            scores = dot_nt(keys, rows) + bias
            top = jnp.max(scores, 0, keepdims=True)
            raised = jnp.exp2((scores - top) * factor)
            probs = raised * (1.0 / jnp.sum(raised, 0, keepdims=True))
            d_probs = dot_nt(values, grads)
            inner = jnp.sum(probs * d_probs, 0, keepdims=True)
            d_scores = (probs * (d_probs - inner)).astype(BF)
            shape = (zones, strip, HP)
            dkv_ref[0, :, 0, :, far] = dot_nn(probs.astype(BF), grads).astype(BF).reshape(shape)
            dkv_ref[0, :, 0, :, cut] = (dot_nn(d_scores, rows) * scale).astype(BF).reshape(shape)
            dq_ref[0, 0, :, cut] = (dot_tn(d_scores, keys) * scale).astype(BF)

    spot = lambda p, m, c: (p, m, 0, 0)
    far = lambda p, m, c: (p, 0, m, 0, 0)
    return pl.pallas_call(
        kernel,
        name="cross_backward",
        grid_spec=pltpu.PrefetchScalarGridSpec(
            num_scalar_prefetch=1,
            grid=(parts, micros),
            in_specs=[
                pl.BlockSpec((1, 1, slots, lanes), spot),
                pl.BlockSpec((1, zones, 1, strip, 2 * lanes), far),
                pl.BlockSpec((1, 1, slots, lanes), spot),
            ],
            out_specs=[
                pl.BlockSpec((1, 1, slots, lanes), spot),
                pl.BlockSpec((1, zones, 1, strip, 2 * lanes), far),
            ],
        ),
        out_shape=[
            jax.ShapeDtypeStruct(query.shape, BF),
            jax.ShapeDtypeStruct(text_kv.shape, BF),
        ],
        compiler_params=params(),
        cost_estimate=cost(10 * parts * micros * slots * words * lanes),
    )(lengths, query, text_kv, incoming)


def tie(*values):
    return lax.optimization_barrier(values)


class Cube:
    def __init__(self):
        self.size = lax.axis_size("dp")
        self.bits = self.size.bit_length() - 1
        self.outer = list(range(1, self.bits))
        self.rank = lax.axis_index("dp")
        self.masks = []
        for place in range(self.size):
            mask = place >> (self.bits - 1)
            for bit in self.outer:
                mask |= ((place >> (bit - 1)) & 1) << bit
            self.masks.append(mask)
        self.owners = self.rank ^ jnp.array(self.masks, jnp.int32)

    def swap(self, value, bit, axis="dp"):
        pairs = [(i, i ^ (1 << bit)) for i in range(lax.axis_size(axis))]
        return lax.ppermute(value, axis, pairs)

    def trade(self, value):
        blocks = {mask: value[mask] for mask in range(self.size)}
        for bit in range(self.bits):
            send = sorted(mask for mask in blocks if mask >> bit & 1)
            got = self.swap(jnp.stack([blocks[mask] for mask in send]), bit)
            for place, mask in enumerate(send):
                blocks[mask] = got[place]
        return jnp.stack([blocks[mask] for mask in range(self.size)])

    def spread(self, value):
        held = value[None]
        for bit in range(self.bits):
            held = jnp.concatenate([held, self.swap(held, bit)])
        return held

    def add(self, value, axis):
        for bit in range(lax.axis_size(axis).bit_length() - 1):
            value = value + self.swap(value, bit, axis)
        return value


class Gather:
    def __init__(self, cube, shard, flip, joined=False):
        self.cube = cube
        self.rows = shard.shape[1]
        self.masks = [[0]]
        self.pieces = [shard]
        self.todo = cube.outer[::-1] if flip else list(cube.outer)
        self.joined = joined

    def blocks(self, order):
        spots = {
            mask: (piece, index)
            for piece, masks in zip(self.pieces, self.masks)
            for index, mask in enumerate(masks)
        }
        return join_rows([spots[mask] for mask in order], self.rows)

    def move(self):
        bit = self.todo.pop(0)
        if self.joined and len(self.pieces) > 1:
            order = [mask for masks in self.masks for mask in masks]
            self.pieces, self.masks = [self.blocks(order)], [order]
        self.masks = self.masks + [[mask | (1 << bit) for mask in masks] for masks in self.masks]
        self.pieces = self.pieces + [self.cube.swap(piece, bit) for piece in self.pieces]

    def join(self):
        while self.todo:
            self.move()
        self.pieces = [self.blocks(self.cube.masks[: self.cube.size // 2])]

    def weight(self):
        near = self.pieces[0]
        return Lanes(near, self.cube.swap(near, 0))


class Scatter:
    def __init__(self, cube, near, other, flip, lanes=None, spot=0):
        self.cube = cube
        self.todo = list(cube.outer) if flip else cube.outer[::-1]
        self.rows = near.shape[1] // (cube.size // 2)
        self.places = list(range(cube.size // 2))
        self.near = near
        self.lanes = lanes or near.shape[2]
        self.spot = spot
        self.got = []
        self.pieces = [other]
        self.arriving = self.places

    def job(self, places):
        terms = [(self.near, places, self.spot)]
        for value, held, spot in self.got:
            terms.append((value, [held.index(place) for place in places], spot))
        return self.lanes, terms

    def absorb(self):
        self.got.append((self.pieces[0], self.arriving, 0 if self.got else self.spot))


def scatter(cube, terms, *shares):
    near, far = terms
    other = cube.swap(far, 0)
    return [Scatter(cube, near, other, flip, lanes, spot) for lanes, spot, flip in shares]


def pack(movers):
    jobs = []
    for mover in movers:
        mover.absorb()
        mover.bit = mover.todo.pop(0)
        weight = 1 << (mover.bit - 1)
        sent = [place for place in mover.places if place & weight]
        mover.places = [place for place in mover.places if not place & weight]
        mover.arriving = [place ^ weight for place in sent]
        jobs.append(mover.job(sent))
    for mover, value in zip(movers, sum_rows(jobs, movers[0].rows)):
        mover.pieces = [value]


def send(movers):
    for mover in movers:
        mover.pieces = [mover.cube.swap(mover.pieces[0], mover.bit)]


def results(movers):
    while movers[0].todo:
        pack(movers)
        send(movers)
    for mover in movers:
        mover.absorb()
    return sum_rows([mover.job([0]) for mover in movers], movers[0].rows)


def pin(value, *others):
    flat = []
    for other in others:
        flat += other.pieces if hasattr(other, "pieces") else [other]
    return tie(value, *flat)[0]


def bind(value, *movers):
    flat = [piece for mover in movers for piece in mover.pieces]
    held = tie(value, *flat)
    spot = 1
    for mover in movers:
        count = len(mover.pieces)
        mover.pieces = list(held[spot : spot + count])
        spot += count
    return held[0]


def hold(movers, *others):
    for mover in movers:
        mover.pieces = [pin(piece, *others) for piece in mover.pieces]


def on_device(
    tokens,
    skip_tokens,
    text,
    timestep,
    grid,
    text_len,
    w_skip,
    w_mod,
    w_qkv,
    w_out1,
    w_query2,
    w_text_kv,
    w_out2,
    w_fc1,
    w_fc2,
    gain_skip,
    gain_attn,
    gain_cross,
    gain_mlp,
    gain_query,
    gain_key,
    cotangent,
):
    micros, slots, width = tokens.shape
    parts = lax.axis_size("sp")
    zone = lax.axis_index("sp")
    cube = Cube()
    ranks = cube.size
    rows = micros * slots
    sequence = slots * parts
    local = H // parts
    lanes = local * HP + -local * HP % 128
    text_slots = text.shape[1]
    text_strip = -(-text_slots // 16) * 16
    features = text.shape[2]
    strip = width // ranks
    middle = width // 2
    kept = w_skip.shape[0]
    skip_lanes = -(-kept // 256) * 256
    skip_cut = skip_lanes // 2
    qkv_cut = (3 * lanes) // 256 * 128 + 128
    text_rows = w_text_kv.shape[0]

    def spread(shard, before=None):
        if before is not None:
            shard, before = tie(shard, before)
        return lax.all_gather(shard, "sp", axis=0, tiled=False)

    def fetch(value, cut, joined=False):
        return [Gather(cube, value[:, :, :cut], 0, joined), Gather(cube, value[:, :, cut:], 1, joined)]

    def advance(movers):
        for mover in movers:
            mover.move()

    def join(movers):
        for mover in movers:
            mover.join()

    def exchange(value):
        return lax.all_to_all(value, "sp", split_axis=0, concat_axis=0, tiled=True)

    skip_z = spread(jnp.pad(w_skip.T, ((0, 0), (0, skip_lanes - kept))))
    steps = cube.spread(timestep[:, 0])
    joined = side_by_side(tokens.reshape(rows, width), skip_tokens.reshape(rows, width), kept, skip_lanes)
    wide = grid[:, 0, 1]
    counts = grid[:, 0, 0] * wide
    cosine, sine = rope_tables(sequence, wide, lanes)
    skip_z, steps, joined, cosine, sine = tie(skip_z, steps, joined, cosine, sine)
    skip_m = fetch(skip_z, skip_cut)
    qkv_z = spread(pad_heads(w_qkv.reshape(strip, -1), local), skip_z)
    advance(skip_m)

    time_act = jax.nn.silu(time_embed(steps, width)).astype(BF).reshape(ranks * micros, parts, -1)
    time_part = lax.dynamic_index_in_dim(time_act, zone, 1, keepdims=False)
    shift = cube.add(jnp.dot(time_part, w_mod, preferred_element_type=F32), "sp")
    skip_m[0].pieces[1], shift = tie(skip_m[0].pieces[1], shift)
    while skip_m[0].todo:
        advance(skip_m)
    shift = cube.trade(shift.reshape(ranks, micros, strip))
    skip_m[0].pieces[-1], shift = tie(skip_m[0].pieces[-1], shift)
    shift = jnp.stack([shift[mask] for mask in cube.masks]).reshape(2, ranks // 2, micros, strip)
    shift = jnp.transpose(shift, (0, 2, 1, 3)).reshape(2, micros, middle)
    qkv_m = fetch(qkv_z, qkv_cut)
    hold(qkv_m, *skip_m)
    advance(qkv_m)
    cross_z = jnp.concatenate([pad_heads(side, local) for side in (w_out1.T, w_query2, w_out2.T)], 1)
    cross_z = spread(pin(cross_z, *skip_m))
    text_z = jnp.pad(pad_heads(w_text_kv.reshape(text_rows, -1), local), ((0, max(0, strip - text_rows)), (0, 0)))
    text_z = spread(pin(text_z, *skip_m))
    fc1_z = spread(pin(w_fc1, *qkv_m))
    join(skip_m)
    skip_w = [mover.weight() for mover in skip_m]

    def shuffle(count):
        block = count // ranks
        place = jnp.arange(count, dtype=jnp.int32)
        source = cube.owners[place // block] * block + place % block
        return (place[:, None] == source[None, :]).astype(BF)

    turn = shuffle(width)
    text_turn = shuffle(features)
    gains = jnp.stack([gain_skip, gain_attn, gain_cross, gain_mlp])
    gains = gains.reshape(4, ranks, strip)[:, cube.owners].reshape(4, 2, 1, middle)
    g_skip, g_attn, g_cross, g_mlp = gains

    lengths = text_len[:, 0, :]
    place = zone * slots + jnp.arange(slots, dtype=jnp.int32)
    live = (place[None, :] < counts[:, None]).astype(F32).reshape(rows, 1)
    gain_q = pad_heads(jnp.tile(gain_query, local)[None, :], local)
    gain_k = pad_heads(jnp.tile(gain_key, local)[None, :], local)

    grad3 = jnp.stack(
        [
            jnp.dot(cotangent.reshape(rows, width), side, preferred_element_type=F32) * live
            for side in (turn[:, :middle], turn[:, middle:])
        ]
    )
    d_mlp = grad3.astype(BF)

    wide_shape = jax.ShapeDtypeStruct((2, rows, middle), F32)
    low_shape = jax.ShapeDtypeStruct((2, rows, middle), BF)
    gain_shape = jax.ShapeDtypeStruct((2, 1, middle), F32)

    def first_norms(sums, extra, out):
        g0_ref, g1_ref, shift_ref = extra
        base_ref, stream_ref, pre_ref = out
        unit, _ = norm_unit(sums)
        stream = [unit[side] * g0_ref[side] for side in range(2)]
        unit, _ = norm_unit(stream)
        for side in range(2):
            base_ref[side] = sums[side]
            stream_ref[side] = stream[side]
            for micro in range(micros):
                cut = slice(micro * slots, (micro + 1) * slots)
                pre = unit[side][cut] * g1_ref[side] + shift_ref[side, micro : micro + 1]
                pre_ref[side, cut] = pre.astype(BF)

    def next_norm(sums, extra, out):
        before_ref, gain_ref = extra
        after_ref, pre_ref = out
        stream = [before_ref[side] + sums[side] for side in range(2)]
        unit, _ = norm_unit(stream)
        for side in range(2):
            after_ref[side] = stream[side]
            pre_ref[side] = (unit[side] * gain_ref[side]).astype(BF)

    base, stream, pre_attn = to_features(
        joined, skip_w, [g_skip, g_attn, shift], [wide_shape, wide_shape, low_shape], first_norms
    )
    while qkv_m[0].todo:
        advance(qkv_m)
    after_qkv = [mover.pieces[-1] for mover in qkv_m]
    hold(qkv_m, pre_attn)
    join(qkv_m)
    fc2_z = spread(pin(w_fc2.T, *after_qkv))
    pre_attn, cross_z, text_z = tie(pre_attn, cross_z, text_z)
    text_m = Gather(cube, text_z[:, :text_rows], 0, True)
    hold([text_m], *after_qkv)
    text_m.move()
    cross_m = fetch(cross_z, 2 * lanes, True)
    hold(cross_m, *after_qkv)
    advance(cross_m)
    qkv_w = [mover.weight() for mover in qkv_m]
    projected = to_lanes(pre_attn, qkv_w)
    projected = bind(projected, text_m, *cross_m)
    projected, fc1_z = tie(projected, fc1_z)
    while cross_m[0].todo:
        advance(cross_m + [text_m])
    fc_m = [Gather(cube, fc1_z, 0, True), Gather(cube, fc2_z, 1, True)]
    arrived = [mover.pieces[-1] for mover in cross_m + [text_m]]
    hold(fc_m, *arrived)
    advance(fc_m)
    raw = exchange(projected.reshape(parts, micros, slots, 3 * lanes))
    text_own = jnp.dot(text.reshape(-1, features), text_turn, preferred_element_type=F32).astype(BF)
    text_own = jnp.pad(
        text_own.reshape(micros, text_slots, features), ((0, 0), (0, text_strip - text_slots), (0, 0))
    ).reshape(micros * text_strip, features)
    while fc_m[0].todo:
        advance(fc_m)
    text_all = spread(pin(text_own, *arrived))
    fc_m[0].pieces[0], d_mlp, turn, text_turn = tie(fc_m[0].pieces[0], d_mlp, turn, text_turn)
    join(cross_m + [text_m])
    first_w, out2_w = [mover.weight() for mover in cross_m]
    text_w = text_m.weight()
    out1_w, query2_w = (Lanes(first_w.near, first_w.far, lanes, index) for index in range(2))
    attended, turned_q, turned_k, norms = self_forward(raw, counts, cosine, sine, gain_q, gain_k)
    attended, first_w.far, out2_w.far, text_w.far = tie(attended, first_w.far, out2_w.far, text_w.far)
    out1_w.far = query2_w.far = first_w.far
    attended = exchange(attended).reshape(parts, rows, lanes)
    text_all = text_all.reshape(-1, features)
    text_all = jnp.stack([text_all[:, : features // 2], text_all[:, features // 2 :]])
    text_kv = to_lanes(text_all, [text_w]).reshape(parts, parts, micros, text_strip, 2 * lanes)
    attended, text_kv = tie(attended, text_kv)
    stream1, pre_cross = to_features(
        attended, [out1_w], [stream, g_cross], [wide_shape, low_shape], next_norm
    )
    hold(fc_m, pre_cross)
    join(fc_m)
    fc1_w, fc2_w = [mover.weight() for mover in fc_m]
    query2 = to_lanes(pre_cross, [query2_w]).reshape(parts, micros, slots, lanes)
    crossed = cross_forward(query2, text_kv, lengths, text_slots).reshape(parts, rows, lanes)
    stream2, pre_mlp = to_features(
        crossed, [out2_w], [stream1, g_mlp], [wide_shape, low_shape], next_norm
    )
    hidden0, activ0, partial, fc2_n0, fc2_f0 = mlp_forward(pre_mlp, d_mlp, stream2, fc1_w, fc2_w, 0)
    hidden1, activ1, result, fc2_n1, fc2_f1 = mlp_forward(pre_mlp, d_mlp, partial, fc1_w, fc2_w, 1, live)
    share = fc2_n0.shape[2]
    fc2_s = scatter(cube, (fc2_n0, fc2_f0), (share, 0, 0)) + scatter(cube, (fc2_n1, fc2_f1), (share, 0, 1))

    def settle(values, before=None):
        value = values[0] if len(values) == 1 else jnp.concatenate(values, 2)
        if before is not None:
            value, before = tie(value, before)
        return lax.psum_scatter(value, "sp", scatter_dimension=0, tiled=False)

    fc1_n0, fc1_f0, partial = mlp_backward(d_mlp, pre_mlp, hidden0, fc1_w, fc2_w, 0, None)
    fc1_s = scatter(cube, (fc1_n0, fc1_f0), (share, 0, 0))
    pack(fc2_s)
    partial = bind(partial, *fc2_s)
    send(fc2_s)
    fc1_n1, fc1_f1, grad2, d_cross, d_gain_mlp = mlp_backward(
        d_mlp, pre_mlp, hidden1, fc1_w, fc2_w, 1, partial, [stream2, g_mlp, grad3]
    )
    fc1_s += scatter(cube, (fc1_n1, fc1_f1), (share, 0, 1))
    d_cross = bind(d_cross, *fc2_s)
    d_crossed = to_lanes(d_cross, [out2_w])
    pack(fc2_s)
    d_crossed = bind(d_crossed, *fc2_s)
    send(fc2_s)
    d_query2, d_text_kv = cross_backward(
        query2, text_kv, lengths, d_crossed.reshape(parts, micros, slots, lanes), text_slots
    )
    d_query2 = bind(d_query2, *fc2_s)
    d_query2 = d_query2.reshape(parts, rows, lanes)
    d_text_kv = d_text_kv.reshape(parts, -1, 2 * lanes)
    total_fc2 = results(fc2_s)
    term_fc2 = settle(total_fc2)

    def go_back(sums, extra, out):
        add_norm_back(sums, *extra, *out)

    grad1, d_attn, d_gain_cross = to_features(
        d_query2, [query2_w], [stream1, g_cross, grad2], [wide_shape, low_shape, gain_shape], go_back
    )
    d_attn = bind(d_attn, *fc1_s)
    pack(fc1_s)
    d_attn = bind(d_attn, *fc1_s)
    send(fc1_s)
    d_attended = to_lanes(d_attn, [out1_w])
    d_attended, d_text_kv, pre_cross = tie(d_attended, d_text_kv, pre_cross)
    d_heads = exchange(d_attended.reshape(parts, micros, slots, lanes))

    def words_back(sums, extra, out):
        size = micros * text_strip
        for zone in range(parts):
            for side in range(2):
                out[0][zone, side] = sums[side][zone * size : (zone + 1) * size].astype(BF)

    words_shape = jax.ShapeDtypeStruct((parts, 2, micros * text_strip, features // 2), BF)
    d_words = to_features(d_text_kv, [text_w], [], [words_shape], words_back)[0]
    text_t = list(terms_of([(text_all, d_text_kv, 2 * lanes, 0)]))
    cross_t = terms_of(
        [(d_attn, attended, lanes, 0), (pre_cross, d_query2, lanes, 0), (d_cross, crossed, lanes, 0)]
    )
    cross_t = list(cross_t)
    d_heads, d_words, text_t[1], cross_t[1] = tie(d_heads, d_words, text_t[1], cross_t[1])
    d_words = settle([d_words])
    text_s = scatter(cube, text_t, (2 * lanes, 0, 1))
    cross_s = scatter(cube, cross_t, (2 * lanes, 0, 0), (lanes, 2, 1))
    d_heads = bind(d_heads, *fc1_s)
    pack(fc1_s)
    d_heads = bind(d_heads, *fc1_s)
    send(fc1_s)
    d_raw, d_gain_q, d_gain_k = self_backward(
        raw, counts, cosine, sine, gain_q, gain_k, turned_q, turned_k, norms, d_heads
    )
    d_raw, term_fc2, d_words = tie(d_raw, term_fc2, d_words)
    d_raw = bind(d_raw, *fc1_s)
    d_projected = exchange(d_raw).reshape(parts, rows, 3 * lanes)
    other_s = cross_s + text_s
    total_fc1 = results(fc1_s)
    pack(cross_s)
    pack(text_s)
    send(other_s)
    d_projected = bind(d_projected, *other_s)
    term_fc1 = settle(total_fc1, d_projected)
    qkv_t = terms_of([(pre_attn, d_projected, 3 * lanes, 0)])
    qkv_s = scatter(cube, qkv_t, (2 * lanes, 0, 0), (lanes, 2, 1))
    pack(cross_s)
    pack(text_s)
    send(other_s)
    pack(qkv_s)
    d_projected = bind(d_projected, *qkv_s)
    send(qkv_s)

    def last_norms(sums, extra, out):
        stream_ref, g1_ref, base_ref, g0_ref, add_ref = extra
        low_ref, d_shift_ref, d_g1_ref, d_g0_ref = out
        back, gains1 = norm_back([stream_ref[0], stream_ref[1]], g1_ref, sums)
        total = [add_ref[side] + back[side] for side in range(2)]
        back, gains0 = norm_back([base_ref[0], base_ref[1]], g0_ref, total)
        for side in range(2):
            low_ref[side] = back[side].astype(BF)
            d_g1_ref[side] = gains1[side]
            d_g0_ref[side] = gains0[side]
            for micro in range(micros):
                part = sums[side][micro * slots : (micro + 1) * slots]
                d_shift_ref[side, micro : micro + 1] = jnp.sum(part, 0, keepdims=True)

    shift_shape = jax.ShapeDtypeStruct((2, micros, middle), F32)
    d_base, d_shift, d_gain_attn, d_gain_skip = to_features(
        d_projected,
        qkv_w,
        [stream, g_attn, base, g_skip, grad1],
        [low_shape, shift_shape, gain_shape, gain_shape],
        last_norms,
    )
    d_base = bind(d_base, *other_s)
    total_cross, total_text = list(results(cross_s)), list(results(text_s))
    d_base = bind(d_base, *qkv_s)
    d_base, total_cross[0], total_text[0] = tie(d_base, total_cross[0], total_text[0])
    term_cross, term_text = settle(total_cross), settle(total_text)
    skip_t = terms_of([(d_base, joined, skip_lanes, 0)])
    skip_s = scatter(cube, skip_t, (skip_cut, 0, 0), (skip_cut, 1, 1))
    pack(qkv_s)
    send(qkv_s)
    pack(skip_s)
    send(skip_s)
    total_qkv = list(results(qkv_s))
    total_qkv[0] = bind(total_qkv[0], *skip_s)
    last = settle(total_qkv + list(results(skip_s)))
    term_qkv, term_skip = last[:, : 3 * lanes], last[:, 3 * lanes :]
    d_joined = to_inputs(d_base, skip_w, kept)
    result = (
        jnp.dot(result[0], turn[:, :middle].T, preferred_element_type=F32)
        + jnp.dot(result[1], turn[:, middle:].T, preferred_element_type=F32)
    ).astype(BF)
    d_words = d_words.reshape(2, micros * text_strip, features // 2)
    d_words = jnp.dot(
        d_words[0], text_turn[:, : features // 2].T, preferred_element_type=F32
    ) + jnp.dot(d_words[1], text_turn[:, features // 2 :].T, preferred_element_type=F32)
    d_words = d_words.reshape(micros, text_strip, features)[:, :text_slots]

    d_shift = jnp.transpose(d_shift.reshape(2, micros, ranks // 2, strip), (0, 2, 1, 3))
    d_shift = d_shift.reshape(ranks, micros, strip)
    d_shift = jnp.stack([d_shift[cube.masks.index(mask)] for mask in range(ranks)])
    d_shift = cube.add(cube.trade(d_shift), "sp").reshape(ranks * micros, strip)
    term_mod = lax.dot_general(
        time_part.astype(F32), d_shift, (((0,), (0,)), ((), ())), precision=lax.Precision.HIGHEST
    )

    places = jnp.array([cube.masks.index(mask) for mask in range(ranks)], jnp.int32)
    places = places[jnp.arange(ranks, dtype=jnp.int32) ^ cube.rank]
    gains = jnp.stack([d_gain_skip, d_gain_attn, d_gain_cross, d_gain_mlp])
    gains = gains.reshape(4, ranks, strip)[:, places].reshape(-1)
    heads = jnp.stack([jnp.sum(d_gain_q, (0, 1)), jnp.sum(d_gain_k, (0, 1))])
    heads = jnp.sum(heads[:, : local * HP].reshape(2, local, HP)[:, :, :HD], 1)
    packed = jnp.concatenate([gains, heads.reshape(-1)])
    packed = cube.add(cube.add(packed, "sp"), "dp")
    gains = packed[: 4 * width].reshape(4, ranks * parts, -1)
    gains = lax.dynamic_index_in_dim(gains, cube.rank * parts + zone, 1, keepdims=False)
    heads = packed[4 * width :].reshape(2, HD)

    def whole(term, groups):
        return cut_heads(term.astype(F32), local).reshape(term.shape[0], groups, -1)

    return (
        result.reshape(tokens.shape),
        d_joined[0].reshape(tokens.shape),
        d_joined[1].reshape(tokens.shape),
        d_words.reshape(text.shape),
        term_skip.astype(F32)[:, :kept].T,
        term_mod,
        whole(term_qkv, 3),
        cut_heads(term_cross[:, :lanes].astype(F32), local).T,
        cut_heads(term_cross[:, lanes : 2 * lanes].astype(F32), local),
        whole(term_text, 2),
        cut_heads(term_cross[:, 2 * lanes :].astype(F32), local).T,
        term_fc1.astype(F32),
        term_fc2.astype(F32).T,
        gains[0],
        gains[1],
        gains[2],
        gains[3],
        heads[0],
        heads[1],
    )


def solution(mesh):
    rows = P(None, ("dp", "sp"), None)
    column = P("sp", "dp")
    row = P("dp", "sp")
    grouped = P("dp", None, "sp")
    in_specs = (
        (rows, rows, rows, P(None, "dp"), P(None, "dp", None), P(None, "dp", None))
        + (column, column, grouped, column, row, grouped, column, row, column)
        + (P(),) * 6
        + (rows,)
    )
    out_specs = (
        (rows, rows, rows, rows)
        + (column, column, grouped, column, row, grouped, column, row, column)
        + (P(("dp", "sp")),) * 4
        + (P(), P())
    )
    return jax.shard_map(
        on_device, mesh=mesh, in_specs=in_specs, out_specs=out_specs, check_vma=False
    )
```

```python
import math

import jax
import jax.numpy as jnp
from jax import lax
from jax.experimental import pallas as pl
from jax.experimental.pallas import tpu as pltpu
from jax.sharding import PartitionSpec as P

H = 16
HD = 88
HP = 96
CLIP_LEN = 77
ROWS = 256

EPS = 1e-06
MASKED = -1e30
LOG2E = 1.4426950408889634
BF = jnp.bfloat16
F32 = jnp.float32


def time_embed(step, width):
    half = width // 2
    rate = jnp.exp(-math.log(10000.0) * jnp.arange(half, dtype=F32) / half)
    angle = step.astype(F32)[..., None] * rate
    return jnp.concatenate([jnp.cos(angle), jnp.sin(angle)], -1)


def rope_tables(sequence, wide, lanes):
    place = jnp.arange(sequence, dtype=jnp.int32)[None, :, None]
    wide = wide[:, None, None]
    lane = jnp.arange(lanes, dtype=jnp.int32)[None, None, :] % HP
    pair = lane // 2
    quarter = HD // 4
    upper = pair < quarter
    rank = jnp.where(upper, pair, pair - quarter).astype(F32)
    rate = jnp.exp(-math.log(10000.0) * rank / quarter)
    angle = jnp.where(upper, place // wide, place % wide).astype(F32) * rate
    sine = jnp.sin(angle)
    return jnp.cos(angle), jnp.where(lane % 2 == 0, -sine, sine)


def pad_heads(packed, local):
    rows, lanes = packed.shape
    groups = packed.reshape(rows, lanes // (local * HD), local, HD)
    groups = jnp.pad(groups, ((0, 0), (0, 0), (0, 0), (0, HP - HD)))
    groups = groups.reshape(rows, -1, local * HP)
    return jnp.pad(groups, ((0, 0), (0, 0), (0, -local * HP % 128))).reshape(rows, -1)


def cut_heads(padded, local):
    rows = padded.shape[0]
    groups = padded.reshape(rows, -1, local * HP + -local * HP % 128)[:, :, : local * HP]
    return groups.reshape(rows, -1, local, HP)[..., :HD].reshape(rows, -1)


def head_masks(shape, local):
    lane = lax.broadcasted_iota(jnp.int32, shape, len(shape) - 1)
    inside = lane % HP < HD
    return [((lane // HP == h) & inside).astype(F32) for h in range(local)]


def head_mean(value, masks):
    total = None
    for mask in masks:
        term = (jnp.sum(value * mask, -1, keepdims=True) * (1.0 / HD)) * mask
        total = term if total is None else total + term
    return total


def head_unit(value, masks):
    centre = value - head_mean(value, masks)
    spread = None
    square = centre * centre
    for mask in masks:
        mean = jnp.sum(square * mask, -1, keepdims=True) * (1.0 / HD)
        term = lax.rsqrt(mean + EPS) * mask
        spread = term if spread is None else spread + term
    return centre * spread, spread


def turn_pairs(value):
    lanes = value.shape[-1]
    after = pltpu.roll(value, lanes - 1, 1)
    before = pltpu.roll(value, 1, 1)
    lane = lax.broadcasted_iota(jnp.int32, value.shape, 1)
    return jnp.where(lane % 2 == 0, after, before)


def dot_nt(left, right):
    return lax.dot_general(left, right, (((1,), (1,)), ((), ())), preferred_element_type=F32)


def dot_nn(left, right):
    return lax.dot_general(left, right, (((1,), (0,)), ((), ())), preferred_element_type=F32)


def dot_tn(left, right):
    return lax.dot_general(left, right, (((0,), (0,)), ((), ())), preferred_element_type=F32)


def self_forward(raw, counts, cosine, sine, gain_q, gain_k):
    parts, micros, slots, packed = raw.shape
    lanes = packed // 3
    local = lanes // HP
    sequence = parts * slots
    factor = HD ** (-0.5) * LOG2E

    def kernel(count_ref, raw_ref, cos_ref, sin_ref, gq_ref, gk_ref, out_ref, q_ref, k_ref, lse_ref):
        count = count_ref[pl.program_id(0)]
        blocks = (count + slots - 1) // slots
        out_ref[...] = jnp.zeros_like(out_ref)
        masks = head_masks((1, lanes), local)

        def prepare(part, carry):
            spot = pl.ds(pl.multiple_of(part * slots, slots), slots)
            cosine, sine = cos_ref[0, spot, :], sin_ref[0, spot, :]
            for index, gain_ref, dest in ((0, gq_ref, q_ref), (1, gk_ref, k_ref)):
                value = raw_ref[part, 0, :, index * lanes : (index + 1) * lanes].astype(F32)
                scaled = head_unit(value, masks)[0] * gain_ref[...]
                dest[0, spot, :] = (scaled * cosine + turn_pairs(scaled) * sine).astype(BF)
            return carry

        lax.fori_loop(0, parts, prepare, 0)
        column = lax.broadcasted_iota(jnp.int32, (1, sequence), 1)
        bias = jnp.where(column < count, 0.0, MASKED)
        for h in range(local):
            cut = slice(h * HP, (h + 1) * HP)
            keys = k_ref[0, :, cut]
            values = raw_ref[:, 0, :, 2 * lanes + h * HP : 2 * lanes + (h + 1) * HP].reshape(sequence, HP)

            def one_block(part, carry):
                spot = pl.ds(pl.multiple_of(part * slots, slots), slots)
                scores = dot_nt(q_ref[0, spot, cut], keys) + bias
                top = jnp.max(scores, -1, keepdims=True)
                raised = jnp.exp2((scores - top) * factor)
                total = jnp.sum(raised, -1, keepdims=True)
                result = dot_nn(raised.astype(BF), values) / total
                out_ref[part, 0, :, cut] = result.astype(BF)
                norm = jnp.broadcast_to(top * factor + jnp.log2(total), (slots, 128))
                lse_ref[0, h : h + 1, spot] = jnp.transpose(norm)[0:1, :]
                return carry

            lax.fori_loop(0, blocks, one_block, 0)

    whole = lambda m, c: (0, m, 0, 0)
    table = lambda m, c: (m, 0, 0)
    fixed = lambda m, c: (0, 0)
    return pl.pallas_call(
        kernel,
        name="self_forward",
        grid_spec=pltpu.PrefetchScalarGridSpec(
            num_scalar_prefetch=1,
            grid=(micros,),
            in_specs=[
                pl.BlockSpec((parts, 1, slots, packed), whole),
                pl.BlockSpec((1, sequence, lanes), table),
                pl.BlockSpec((1, sequence, lanes), table),
                pl.BlockSpec((1, lanes), fixed),
                pl.BlockSpec((1, lanes), fixed),
            ],
            out_specs=[
                pl.BlockSpec((parts, 1, slots, lanes), whole),
                pl.BlockSpec((1, sequence, lanes), table),
                pl.BlockSpec((1, sequence, lanes), table),
                pl.BlockSpec((1, local, sequence), table),
            ],
        ),
        out_shape=[
            jax.ShapeDtypeStruct((parts, micros, slots, lanes), BF),
            jax.ShapeDtypeStruct((micros, sequence, lanes), BF),
            jax.ShapeDtypeStruct((micros, sequence, lanes), BF),
            jax.ShapeDtypeStruct((micros, local, sequence), F32),
        ],
        compiler_params=params(),
        cost_estimate=cost(4 * micros * local * sequence * sequence * HP),
    )(counts, raw, cosine, sine, gain_q, gain_k)


def self_backward(raw, counts, cosine, sine, gain_q, gain_k, turned_q, turned_k, norms, incoming):
    parts, micros, slots, packed = raw.shape
    lanes = packed // 3
    local = lanes // HP
    sequence = parts * slots
    scale = HD ** (-0.5)
    factor = scale * LOG2E

    def kernel(
        count_ref,
        raw_ref,
        cos_ref,
        sin_ref,
        gq_ref,
        gk_ref,
        q_ref,
        k_ref,
        lse_ref,
        in_ref,
        out_ref,
        dgq_ref,
        dgk_ref,
        dq_s,
        dk_s,
        dv_s,
    ):
        count = count_ref[pl.program_id(0)]
        blocks = (count + slots - 1) // slots
        dq_s[...] = jnp.zeros_like(dq_s)
        dk_s[...] = jnp.zeros_like(dk_s)
        dv_s[...] = jnp.zeros_like(dv_s)
        row = lax.broadcasted_iota(jnp.int32, (sequence, 1), 0)
        bias = jnp.where(row < count, 0.0, MASKED)
        for h in range(local):
            cut = slice(h * HP, (h + 1) * HP)
            keys = k_ref[0, :, cut]
            values = raw_ref[:, 0, :, 2 * lanes + h * HP : 2 * lanes + (h + 1) * HP].reshape(sequence, HP)

            def one_block(part, carry):
                spot = pl.ds(pl.multiple_of(part * slots, slots), slots)
                rows = q_ref[0, spot, cut]
                grads = in_ref[part, 0, :, cut]
                norm = lse_ref[0, h : h + 1, spot]
                probs = jnp.exp2(dot_nt(keys, rows) * factor + bias - norm)
                d_probs = dot_nt(values, grads)
                inner = jnp.sum(probs * d_probs, 0, keepdims=True)
                d_scores = (probs * (d_probs - inner)).astype(BF)
                dv_s[:, cut] += dot_nn(probs.astype(BF), grads)
                dk_s[:, cut] += dot_nn(d_scores, rows)
                dq_s[spot, cut] = dot_tn(d_scores, keys)
                return carry

            lax.fori_loop(0, blocks, one_block, 0)
        masks = head_masks((1, lanes), local)

        def finish(part, carry):
            spot = pl.ds(pl.multiple_of(part * slots, slots), slots)
            cosine, sine = cos_ref[0, spot, :], sin_ref[0, spot, :]
            sums = []
            for index, gain_ref, source in ((0, gq_ref, dq_s), (1, gk_ref, dk_s)):
                grad = source[spot, :] * scale
                grad = grad * cosine - turn_pairs(grad) * sine
                value = raw_ref[part, 0, :, index * lanes : (index + 1) * lanes].astype(F32)
                unit, spread = head_unit(value, masks)
                leading = grad * gain_ref[...]
                back = leading - head_mean(leading, masks) - unit * head_mean(leading * unit, masks)
                out_ref[part, 0, :, index * lanes : (index + 1) * lanes] = (spread * back).astype(BF)
                sums.append(carry[index] + jnp.sum(grad * unit, 0, keepdims=True))
            out_ref[part, 0, :, 2 * lanes : 3 * lanes] = dv_s[spot, :].astype(BF)
            return tuple(sums)

        zero = jnp.zeros((1, lanes), F32)
        d_gains = lax.fori_loop(0, parts, finish, (zero, zero))
        dgq_ref[0] = d_gains[0]
        dgk_ref[0] = d_gains[1]

    whole = lambda m, c: (0, m, 0, 0)
    table = lambda m, c: (m, 0, 0)
    fixed = lambda m, c: (0, 0)
    return pl.pallas_call(
        kernel,
        name="self_backward",
        grid_spec=pltpu.PrefetchScalarGridSpec(
            num_scalar_prefetch=1,
            grid=(micros,),
            in_specs=[
                pl.BlockSpec((parts, 1, slots, packed), whole),
                pl.BlockSpec((1, sequence, lanes), table),
                pl.BlockSpec((1, sequence, lanes), table),
                pl.BlockSpec((1, lanes), fixed),
                pl.BlockSpec((1, lanes), fixed),
                pl.BlockSpec((1, sequence, lanes), table),
                pl.BlockSpec((1, sequence, lanes), table),
                pl.BlockSpec((1, local, sequence), table),
                pl.BlockSpec((parts, 1, slots, lanes), whole),
            ],
            out_specs=[
                pl.BlockSpec((parts, 1, slots, packed), whole),
                pl.BlockSpec((1, 1, lanes), table),
                pl.BlockSpec((1, 1, lanes), table),
            ],
            scratch_shapes=[pltpu.VMEM((sequence, lanes), F32) for index in range(3)],
        ),
        out_shape=[
            jax.ShapeDtypeStruct((parts, micros, slots, packed), BF),
            jax.ShapeDtypeStruct((micros, 1, lanes), F32),
            jax.ShapeDtypeStruct((micros, 1, lanes), F32),
        ],
        compiler_params=params(),
        cost_estimate=cost(10 * micros * local * sequence * sequence * HP),
    )(counts, raw, cosine, sine, gain_q, gain_k, turned_q, turned_k, norms, incoming)


def cost(flops):
    return pl.CostEstimate(flops=flops // 16, bytes_accessed=flops // 16000, transcendentals=0)


def full(shape):
    return pl.BlockSpec(shape, lambda *index: (0,) * len(shape))


def params(megabytes=60):
    return pltpu.CompilerParams(vmem_limit_bytes=megabytes << 20)


class Lanes:
    def __init__(self, near, far, block=None, index=0):
        self.near, self.far = near, far
        self.block = block or near.shape[2]
        self.index = index

    def spec(self):
        index = self.index
        return pl.BlockSpec((1, self.near.shape[1], self.block), lambda p, *rest: (p, 0, index))


def to_lanes(value, weights, dtype=BF, name="to_lanes"):
    rows = value.shape[1]
    parts, half, _ = weights[0].near.shape
    total = sum(weight.block for weight in weights)

    def kernel(x_ref, *refs):
        out_ref = refs[-1]
        at = 0
        for index, weight in enumerate(weights):
            result = dot_nn(x_ref[0], refs[2 * index][0]) + dot_nn(x_ref[1], refs[2 * index + 1][0])
            out_ref[0, :, at : at + weight.block] = result.astype(dtype)
            at += weight.block

    return pl.pallas_call(
        kernel,
        name=name,
        grid=(parts,),
        in_specs=[full(value.shape)] + [weight.spec() for weight in weights for side in range(2)],
        out_specs=pl.BlockSpec((1, rows, total), lambda p: (p, 0, 0)),
        out_shape=jax.ShapeDtypeStruct((parts, rows, total), dtype),
        compiler_params=params(),
        cost_estimate=cost(4 * rows * half * parts * total),
    )(value, *[side for weight in weights for side in (weight.near, weight.far)])


def to_inputs(value, weights, kept):
    rows = value.shape[1]
    parts, half, _ = weights[0].near.shape
    sides = parts // 2

    def kernel(x_ref, *refs):
        out_ref = refs[-1]
        for side in range(sides):

            @pl.when(pl.program_id(0) % sides == side)
            def _():
                at = 0
                for index, weight in enumerate(weights):
                    result = dot_nn(x_ref[0], refs[2 * index][0]) + dot_nn(
                        x_ref[1], refs[2 * index + 1][0]
                    )
                    take = min(weight.block, kept - at)
                    start = side * kept + at
                    out_ref[0, :, start : start + take] = result[:, :take]
                    at += take

    return pl.pallas_call(
        kernel,
        name="to_inputs",
        grid=(parts,),
        in_specs=[full(value.shape)] + [weight.spec() for weight in weights for side in range(2)],
        out_specs=pl.BlockSpec((1, rows, sides * kept), lambda p: (p // sides, 0, 0)),
        out_shape=jax.ShapeDtypeStruct((2, rows, sides * kept), F32),
        compiler_params=params(),
        cost_estimate=cost(4 * rows * half * parts * kept),
    )(value, *[side for weight in weights for side in (weight.near, weight.far)])


def to_features(value, weights, extras, outs, finish, name="to_features"):
    parts, rows, total = value.shape
    half = weights[0].near.shape[1]
    count = 2 * len(weights)

    def kernel(*refs):
        y_ref, weight_refs = refs[0], refs[1 : 1 + count]
        extra_refs = refs[1 + count : 1 + count + len(extras)]
        out_refs = refs[1 + count + len(extras) : -1]
        sums = refs[-1]

        @pl.when(pl.program_id(0) == 0)
        def _():
            sums[...] = jnp.zeros_like(sums)

        at = 0
        for index, weight in enumerate(weights):
            left = y_ref[0, :, at : at + weight.block]
            for side in range(2):
                sums[side] += dot_nt(left, weight_refs[2 * index + side][0])
            at += weight.block

        @pl.when(pl.program_id(0) == parts - 1)
        def _():
            finish([sums[0], sums[1]], extra_refs, out_refs)

    return pl.pallas_call(
        kernel,
        name=name,
        grid=(parts,),
        in_specs=[pl.BlockSpec((1, rows, total), lambda p: (p, 0, 0))]
        + [weight.spec() for weight in weights for side in range(2)]
        + [full(extra.shape) for extra in extras],
        out_specs=[full(out.shape) for out in outs],
        out_shape=outs,
        scratch_shapes=[pltpu.VMEM((2, rows, half), F32)],
        compiler_params=params(),
        cost_estimate=cost(4 * rows * half * parts * total),
    )(value, *[side for weight in weights for side in (weight.near, weight.far)], *extras)


def terms_of(pairs, name="terms_of"):
    half = pairs[0][0].shape[2]
    parts = pairs[0][1].shape[0]
    total = sum(pair[2] for pair in pairs)
    rows = [pair[0].shape[1] for pair in pairs]

    def kernel(*refs):
        count = len(pairs)
        lefts, rights = refs[:count], refs[count : 2 * count]
        near_ref, far_ref = refs[2 * count : 2 * count + 2]
        turned = refs[2 * count + 2 :]

        @pl.when(pl.program_id(0) == 0)
        def _():
            for left, flat in zip(lefts, turned):
                for side in range(2):
                    flat[side] = jnp.transpose(left[side])

        at = 0
        for pair, right, flat in zip(pairs, rights, turned):
            lanes = pair[2]
            near_ref[0, :, at : at + lanes] = dot_nn(flat[0], right[0]).astype(BF)
            far_ref[0, :, at : at + lanes] = dot_nn(flat[1], right[0]).astype(BF)
            at += lanes

    def right_spec(pair):
        return pl.BlockSpec((1, pair[1].shape[1], pair[2]), lambda p: (p, 0, pair[3]))

    out = jax.ShapeDtypeStruct((parts, half, total), BF)
    return pl.pallas_call(
        kernel,
        name=name,
        grid=(parts,),
        in_specs=[full(pair[0].shape) for pair in pairs] + [right_spec(pair) for pair in pairs],
        out_specs=[pl.BlockSpec((1, half, total), lambda p: (p, 0, 0))] * 2,
        out_shape=[out, out],
        scratch_shapes=[pltpu.VMEM((2, half, count), BF) for count in rows],
        compiler_params=params(),
        cost_estimate=cost(sum(4 * half * parts * pair[2] * count for pair, count in zip(pairs, rows))),
    )(*[pair[0] for pair in pairs], *[pair[1] for pair in pairs])


def norm_unit(halves):
    width = 2 * halves[0].shape[-1]
    mean = sum(jnp.sum(half, -1, keepdims=True) for half in halves) / width
    centre = [half - mean for half in halves]
    spread = sum(jnp.sum(half * half, -1, keepdims=True) for half in centre) / width
    scale = lax.rsqrt(spread + EPS)
    return [half * scale for half in centre], scale


def norm_back(halves, gain_ref, incoming):
    width = 2 * halves[0].shape[-1]
    unit, scale = norm_unit(halves)
    leading = [incoming[side] * gain_ref[side] for side in range(2)]
    mean = sum(jnp.sum(half, -1, keepdims=True) for half in leading) / width
    inner = sum(jnp.sum(leading[side] * unit[side], -1, keepdims=True) for side in range(2)) / width
    back = [scale * (leading[side] - mean - unit[side] * inner) for side in range(2)]
    gains = [jnp.sum(incoming[side] * unit[side], 0, keepdims=True) for side in range(2)]
    return back, gains


def join_rows(pieces, rows, name="join_rows"):
    parts, _, lanes = pieces[0][0].shape
    count = len(pieces)
    if rows % 16:
        return jnp.concatenate([array[:, block * rows : (block + 1) * rows] for array, block in pieces], 1)

    def kernel(*refs):
        for index in range(count):
            refs[-1][0, index * rows : (index + 1) * rows] = refs[index][0]

    def spec(block):
        return pl.BlockSpec((1, rows, lanes), lambda p: (p, block, 0))

    return pl.pallas_call(
        kernel,
        name=name,
        grid=(parts,),
        in_specs=[spec(block) for _, block in pieces],
        out_specs=pl.BlockSpec((1, count * rows, lanes), lambda p: (p, 0, 0)),
        out_shape=jax.ShapeDtypeStruct((parts, count * rows, lanes), BF),
        compiler_params=params(),
        cost_estimate=cost(parts * count * rows * lanes),
    )(*[array for array, _ in pieces])


def sum_rows(jobs, rows, name="sum_rows"):
    parts = jobs[0][1][0][0].shape[0]
    if rows % 16:
        results = []
        for lanes, terms in jobs:
            value = 0.0
            for array, blocks, spot in terms:
                split = array[:, :, spot * lanes : (spot + 1) * lanes].reshape(parts, -1, rows, lanes)
                value = value + jnp.stack([split[:, block] for block in blocks], 1).astype(F32)
            results.append(value.astype(BF).reshape(parts, -1, lanes))
        return results
    spots = [
        (array, blocks[index], spot, lanes)
        for lanes, terms in jobs
        for index in range(len(terms[0][1]))
        for array, blocks, spot in terms
    ]

    def kernel(*refs):
        at = 0
        for order, (_, terms) in enumerate(jobs):
            out_ref = refs[len(spots) + order]
            for index in range(len(terms[0][1])):
                value = refs[at][0].astype(F32)
                for offset in range(1, len(terms)):
                    value = value + refs[at + offset][0].astype(F32)
                out_ref[0, index * rows : (index + 1) * rows] = value.astype(BF)
                at += len(terms)

    def spec(block, spot, lanes):
        return pl.BlockSpec((1, rows, lanes), lambda p: (p, block, spot))

    shapes = [(len(terms[0][1]) * rows, lanes) for lanes, terms in jobs]
    return pl.pallas_call(
        kernel,
        name=name,
        grid=(parts,),
        in_specs=[spec(*rest) for _, *rest in spots],
        out_specs=[pl.BlockSpec((1, *shape), lambda p: (p, 0, 0)) for shape in shapes],
        out_shape=[jax.ShapeDtypeStruct((parts, *shape), BF) for shape in shapes],
        compiler_params=params(),
        cost_estimate=cost(sum(parts * size * lanes for size, lanes in shapes)),
    )(*[array for array, *_ in spots])


def side_by_side(left, right, kept, lanes):
    rows, width = left.shape
    count = width // kept

    def kernel(left_ref, right_ref, out_ref):
        for index, ref in enumerate((left_ref, right_ref)):
            for side in range(count):
                spot = count * index + side
                out_ref[spot, :, :kept] = ref[:, side * kept : (side + 1) * kept]
                if lanes > kept:
                    out_ref[spot, :, kept:] = jnp.zeros((rows, lanes - kept), BF)

    return pl.pallas_call(
        kernel,
        name="side_by_side",
        out_shape=jax.ShapeDtypeStruct((2 * count, rows, lanes), BF),
        compiler_params=params(),
        cost_estimate=cost(4 * rows * lanes),
    )(left, right)


def mlp_forward(rows_in, grads, start, weight1, weight2, part, live=None):
    _, rows, half = rows_in.shape
    parts, _, lanes = weight1.near.shape
    ff = lanes // 2
    step = 768 if ff % 768 == 0 else ff
    steps = ff // step
    extras = [] if live is None else [live]

    def kernel(x_ref, g_ref, s_ref, n1_ref, f1_ref, n2_ref, f2_ref, *refs):
        hid_ref, act_ref, out_ref, dn2_ref, df2_ref, turned, sums = refs[len(extras) :]
        first = (pl.program_id(0) == 0) & (pl.program_id(1) == 0)
        last = (pl.program_id(0) == parts - 1) & (pl.program_id(1) == steps - 1)

        @pl.when(first)
        def _():
            for side in range(2):
                turned[side] = jnp.transpose(g_ref[side])
            sums[...] = s_ref[...]

        hidden = dot_nn(x_ref[0], n1_ref[0]) + dot_nn(x_ref[1], f1_ref[0])
        hid_ref[0] = hidden
        activ = jax.nn.gelu(hidden, approximate=True).astype(BF)
        act_ref[0] = activ
        sums[0] += dot_nt(activ, n2_ref[0])
        sums[1] += dot_nt(activ, f2_ref[0])
        dn2_ref[0] = dot_nn(turned[0], activ).astype(BF)
        df2_ref[0] = dot_nn(turned[1], activ).astype(BF)

        @pl.when(last)
        def _():
            if live is None:
                out_ref[...] = sums[...]
            else:
                out_ref[...] = (sums[...] * refs[0][...]).astype(BF)

    weight = pl.BlockSpec((1, half, step), lambda p, n: (p, 0, part * steps + n))
    grad = pl.BlockSpec((1, half, step), lambda p, n: (p, 0, n))
    unit = pl.BlockSpec((1, rows, step), lambda p, n: (p, 0, n))
    whole = full((2, rows, half))
    grad_shape = jax.ShapeDtypeStruct((parts, half, ff), BF)
    return pl.pallas_call(
        kernel,
        name="mlp_forward",
        grid=(parts, steps),
        in_specs=[whole, whole, whole, weight, weight, weight, weight] + [full(extra.shape) for extra in extras],
        out_specs=[unit, unit, whole, grad, grad],
        out_shape=[
            jax.ShapeDtypeStruct((parts, rows, ff), F32),
            jax.ShapeDtypeStruct((parts, rows, ff), BF),
            jax.ShapeDtypeStruct((2, rows, half), F32 if live is None else BF),
            grad_shape,
            grad_shape,
        ],
        scratch_shapes=[pltpu.VMEM((2, half, rows), BF), pltpu.VMEM((2, rows, half), F32)],
        compiler_params=params(),
        cost_estimate=cost(12 * rows * half * parts * ff),
    )(rows_in, grads, start, weight1.near, weight1.far, weight2.near, weight2.far, *extras)


def gelu_slope(value):
    root = math.sqrt(2.0 / math.pi)
    square = value * value
    curve = jnp.tanh(root * value * (1.0 + 0.044715 * square))
    return 0.5 * (1.0 + curve) + 0.5 * value * (1.0 - curve * curve) * root * (
        1.0 + 3.0 * 0.044715 * square
    )


def mlp_backward(grads, rows_in, hidden, weight1, weight2, part, start, finish=None):
    _, rows, half = rows_in.shape
    parts, _, lanes = weight1.near.shape
    ff = lanes // 2
    step = 768 if ff % 768 == 0 else ff
    steps = ff // step
    extras = list(finish or []) + ([] if start is None else [start])

    def kernel(g_ref, x_ref, hid_ref, n1_ref, f1_ref, n2_ref, f2_ref, *refs):
        extra_refs, refs = refs[: len(extras)], refs[len(extras) :]
        dn1_ref, df1_ref = refs[:2]
        out_refs = refs[2:-2]
        turned, sums = refs[-2:]
        first = (pl.program_id(0) == 0) & (pl.program_id(1) == 0)
        last = (pl.program_id(0) == parts - 1) & (pl.program_id(1) == steps - 1)

        @pl.when(first)
        def _():
            for side in range(2):
                turned[side] = jnp.transpose(x_ref[side])
            sums[...] = jnp.zeros_like(sums) if start is None else extra_refs[-1][...]

        d_activ = dot_nn(g_ref[0], n2_ref[0]) + dot_nn(g_ref[1], f2_ref[0])
        d_hidden = (d_activ * gelu_slope(hid_ref[0])).astype(BF)
        dn1_ref[0] = dot_nn(turned[0], d_hidden).astype(BF)
        df1_ref[0] = dot_nn(turned[1], d_hidden).astype(BF)
        sums[0] += dot_nt(d_hidden, n1_ref[0])
        sums[1] += dot_nt(d_hidden, f1_ref[0])

        @pl.when(last)
        def _():
            if finish is None:
                out_refs[0][...] = sums[...]
            else:
                value_ref, gain_ref, add_ref = extra_refs[:3]
                add_norm_back([sums[0], sums[1]], value_ref, gain_ref, add_ref, *out_refs)

    weight = pl.BlockSpec((1, half, step), lambda p, n: (p, 0, part * steps + n))
    grad = pl.BlockSpec((1, half, step), lambda p, n: (p, 0, n))
    unit = pl.BlockSpec((1, rows, step), lambda p, n: (p, 0, n))
    whole = full((2, rows, half))
    grad_shape = jax.ShapeDtypeStruct((parts, half, ff), BF)
    wide = jax.ShapeDtypeStruct((2, rows, half), F32)
    outs = [wide] if finish is None else [wide, *back_shapes(rows, half)]
    return pl.pallas_call(
        kernel,
        name="mlp_backward",
        grid=(parts, steps),
        in_specs=[whole, whole, unit, weight, weight, weight, weight] + [full(extra.shape) for extra in extras],
        out_specs=[grad, grad] + [full(out.shape) for out in outs],
        out_shape=[grad_shape, grad_shape] + outs,
        scratch_shapes=[pltpu.VMEM((2, half, rows), BF), pltpu.VMEM((2, rows, half), F32)],
        compiler_params=params(),
        cost_estimate=cost(12 * rows * half * parts * ff),
    )(grads, rows_in, hidden, weight1.near, weight1.far, weight2.near, weight2.far, *extras)


def back_shapes(rows, half):
    return [jax.ShapeDtypeStruct((2, rows, half), BF), jax.ShapeDtypeStruct((2, 1, half), F32)]


def add_norm_back(incoming, value_ref, gain_ref, add_ref, out_ref, low_ref, d_gain_ref):
    back, gains = norm_back([value_ref[0], value_ref[1]], gain_ref, incoming)
    for side in range(2):
        total = add_ref[side] + back[side]
        out_ref[side] = total
        low_ref[side] = total.astype(BF)
        d_gain_ref[side] = gains[side]


def text_bias(lengths_ref, micro, words, strip, text_slots, axis):
    spot = lax.broadcasted_iota(jnp.int32, (1, words) if axis else (words, 1), axis)
    inner = spot % strip
    place = spot // strip * text_slots + inner
    live = (place < lengths_ref[micro, 0]) | (
        (place >= CLIP_LEN) & (place < CLIP_LEN + lengths_ref[micro, 1])
    )
    return jnp.where(live & (inner < text_slots), 0.0, MASKED)


def cross_forward(query, text_kv, lengths, text_slots):
    parts, micros, slots, lanes = query.shape
    zones, strip = text_kv.shape[1], text_kv.shape[3]
    words = zones * strip
    local = lanes // HP
    factor = HD ** (-0.5) * LOG2E

    def kernel(len_ref, q_ref, kv_ref, out_ref):
        bias = text_bias(len_ref, pl.program_id(1), words, strip, text_slots, 1)
        for h in range(local):
            cut = slice(h * HP, (h + 1) * HP)
            keys = kv_ref[0, :, 0, :, cut].reshape(words, HP)
            scores = dot_nt(q_ref[0, 0, :, cut], keys) + bias
            top = jnp.max(scores, -1, keepdims=True)
            raised = jnp.exp2((scores - top) * factor)
            total = jnp.sum(raised, -1, keepdims=True)
            values = kv_ref[0, :, 0, :, lanes + h * HP : lanes + (h + 1) * HP].reshape(words, HP)
            out_ref[0, 0, :, cut] = (dot_nn(raised.astype(BF), values) / total).astype(BF)

    spot = lambda p, m, c: (p, m, 0, 0)
    far = lambda p, m, c: (p, 0, m, 0, 0)
    return pl.pallas_call(
        kernel,
        name="cross_forward",
        grid_spec=pltpu.PrefetchScalarGridSpec(
            num_scalar_prefetch=1,
            grid=(parts, micros),
            in_specs=[
                pl.BlockSpec((1, 1, slots, lanes), spot),
                pl.BlockSpec((1, zones, 1, strip, 2 * lanes), far),
            ],
            out_specs=pl.BlockSpec((1, 1, slots, lanes), spot),
        ),
        out_shape=jax.ShapeDtypeStruct(query.shape, BF),
        compiler_params=params(),
        cost_estimate=cost(4 * parts * micros * slots * words * lanes),
    )(lengths, query, text_kv)


def cross_backward(query, text_kv, lengths, incoming, text_slots):
    parts, micros, slots, lanes = query.shape
    zones, strip = text_kv.shape[1], text_kv.shape[3]
    words = zones * strip
    local = lanes // HP
    scale = HD ** (-0.5)
    factor = scale * LOG2E

    def kernel(len_ref, q_ref, kv_ref, in_ref, dq_ref, dkv_ref):
        bias = text_bias(len_ref, pl.program_id(1), words, strip, text_slots, 0)
        for h in range(local):
            cut = slice(h * HP, (h + 1) * HP)
            far = slice(lanes + h * HP, lanes + (h + 1) * HP)
            rows = q_ref[0, 0, :, cut]
            keys = kv_ref[0, :, 0, :, cut].reshape(words, HP)
            values = kv_ref[0, :, 0, :, far].reshape(words, HP)
            grads = in_ref[0, 0, :, cut]
            scores = dot_nt(keys, rows) + bias
            top = jnp.max(scores, 0, keepdims=True)
            raised = jnp.exp2((scores - top) * factor)
            probs = raised * (1.0 / jnp.sum(raised, 0, keepdims=True))
            d_probs = dot_nt(values, grads)
            inner = jnp.sum(probs * d_probs, 0, keepdims=True)
            d_scores = (probs * (d_probs - inner)).astype(BF)
            shape = (zones, strip, HP)
            dkv_ref[0, :, 0, :, far] = dot_nn(probs.astype(BF), grads).astype(BF).reshape(shape)
            dkv_ref[0, :, 0, :, cut] = (dot_nn(d_scores, rows) * scale).astype(BF).reshape(shape)
            dq_ref[0, 0, :, cut] = (dot_tn(d_scores, keys) * scale).astype(BF)

    spot = lambda p, m, c: (p, m, 0, 0)
    far = lambda p, m, c: (p, 0, m, 0, 0)
    return pl.pallas_call(
        kernel,
        name="cross_backward",
        grid_spec=pltpu.PrefetchScalarGridSpec(
            num_scalar_prefetch=1,
            grid=(parts, micros),
            in_specs=[
                pl.BlockSpec((1, 1, slots, lanes), spot),
                pl.BlockSpec((1, zones, 1, strip, 2 * lanes), far),
                pl.BlockSpec((1, 1, slots, lanes), spot),
            ],
            out_specs=[
                pl.BlockSpec((1, 1, slots, lanes), spot),
                pl.BlockSpec((1, zones, 1, strip, 2 * lanes), far),
            ],
        ),
        out_shape=[
            jax.ShapeDtypeStruct(query.shape, BF),
            jax.ShapeDtypeStruct(text_kv.shape, BF),
        ],
        compiler_params=params(),
        cost_estimate=cost(10 * parts * micros * slots * words * lanes),
    )(lengths, query, text_kv, incoming)


def tie(*values):
    return lax.optimization_barrier(values)


class Cube:
    def __init__(self):
        self.size = lax.axis_size("dp")
        self.bits = self.size.bit_length() - 1
        self.outer = list(range(1, self.bits))
        self.rank = lax.axis_index("dp")
        self.masks = []
        for place in range(self.size):
            mask = place >> (self.bits - 1)
            for bit in self.outer:
                mask |= ((place >> (bit - 1)) & 1) << bit
            self.masks.append(mask)
        self.owners = self.rank ^ jnp.array(self.masks, jnp.int32)

    def swap(self, value, bit, axis="dp"):
        pairs = [(i, i ^ (1 << bit)) for i in range(lax.axis_size(axis))]
        return lax.ppermute(value, axis, pairs)

    def trade(self, value):
        blocks = {mask: value[mask] for mask in range(self.size)}
        for bit in range(self.bits):
            send = sorted(mask for mask in blocks if mask >> bit & 1)
            got = self.swap(jnp.stack([blocks[mask] for mask in send]), bit)
            for place, mask in enumerate(send):
                blocks[mask] = got[place]
        return jnp.stack([blocks[mask] for mask in range(self.size)])

    def spread(self, value):
        held = value[None]
        for bit in range(self.bits):
            held = jnp.concatenate([held, self.swap(held, bit)])
        return held

    def add(self, value, axis):
        for bit in range(lax.axis_size(axis).bit_length() - 1):
            value = value + self.swap(value, bit, axis)
        return value


class Gather:
    def __init__(self, cube, shard, flip, joined=False):
        self.cube = cube
        self.rows = shard.shape[1]
        self.masks = [[0]]
        self.pieces = [shard]
        self.todo = cube.outer[::-1] if flip else list(cube.outer)
        self.joined = joined

    def blocks(self, order):
        spots = {
            mask: (piece, index)
            for piece, masks in zip(self.pieces, self.masks)
            for index, mask in enumerate(masks)
        }
        return join_rows([spots[mask] for mask in order], self.rows)

    def move(self):
        bit = self.todo.pop(0)
        if self.joined and len(self.pieces) > 1:
            order = [mask for masks in self.masks for mask in masks]
            self.pieces, self.masks = [self.blocks(order)], [order]
        self.masks = self.masks + [[mask | (1 << bit) for mask in masks] for masks in self.masks]
        self.pieces = self.pieces + [self.cube.swap(piece, bit) for piece in self.pieces]

    def join(self):
        while self.todo:
            self.move()
        self.pieces = [self.blocks(self.cube.masks[: self.cube.size // 2])]

    def weight(self):
        near = self.pieces[0]
        return Lanes(near, self.cube.swap(near, 0))


class Scatter:
    def __init__(self, cube, near, other, flip, lanes=None, spot=0):
        self.cube = cube
        self.todo = list(cube.outer) if flip else cube.outer[::-1]
        self.rows = near.shape[1] // (cube.size // 2)
        self.places = list(range(cube.size // 2))
        self.near = near
        self.lanes = lanes or near.shape[2]
        self.spot = spot
        self.got = []
        self.pieces = [other]
        self.arriving = self.places

    def job(self, places):
        terms = [(self.near, places, self.spot)]
        for value, held, spot in self.got:
            terms.append((value, [held.index(place) for place in places], spot))
        return self.lanes, terms

    def absorb(self):
        self.got.append((self.pieces[0], self.arriving, 0 if self.got else self.spot))


def scatter(cube, terms, *shares):
    near, far = terms
    other = cube.swap(far, 0)
    return [Scatter(cube, near, other, flip, lanes, spot) for lanes, spot, flip in shares]


def pack(movers):
    jobs = []
    for mover in movers:
        mover.absorb()
        mover.bit = mover.todo.pop(0)
        weight = 1 << (mover.bit - 1)
        sent = [place for place in mover.places if place & weight]
        mover.places = [place for place in mover.places if not place & weight]
        mover.arriving = [place ^ weight for place in sent]
        jobs.append(mover.job(sent))
    for mover, value in zip(movers, sum_rows(jobs, movers[0].rows)):
        mover.pieces = [value]


def send(movers):
    for mover in movers:
        mover.pieces = [mover.cube.swap(mover.pieces[0], mover.bit)]


def results(movers):
    while movers[0].todo:
        pack(movers)
        send(movers)
    for mover in movers:
        mover.absorb()
    return sum_rows([mover.job([0]) for mover in movers], movers[0].rows)


def pin(value, *others):
    flat = []
    for other in others:
        flat += other.pieces if hasattr(other, "pieces") else [other]
    return tie(value, *flat)[0]


def bind(value, *movers):
    flat = [piece for mover in movers for piece in mover.pieces]
    held = tie(value, *flat)
    spot = 1
    for mover in movers:
        count = len(mover.pieces)
        mover.pieces = list(held[spot : spot + count])
        spot += count
    return held[0]


def hold(movers, *others):
    for mover in movers:
        mover.pieces = [pin(piece, *others) for piece in mover.pieces]


def on_device(
    tokens,
    skip_tokens,
    text,
    timestep,
    grid,
    text_len,
    w_skip,
    w_mod,
    w_qkv,
    w_out1,
    w_query2,
    w_text_kv,
    w_out2,
    w_fc1,
    w_fc2,
    gain_skip,
    gain_attn,
    gain_cross,
    gain_mlp,
    gain_query,
    gain_key,
    cotangent,
):
    micros, slots, width = tokens.shape
    parts = lax.axis_size("sp")
    zone = lax.axis_index("sp")
    cube = Cube()
    ranks = cube.size
    rows = micros * slots
    sequence = slots * parts
    local = H // parts
    lanes = local * HP + -local * HP % 128
    text_slots = text.shape[1]
    text_strip = -(-text_slots // 16) * 16
    features = text.shape[2]
    strip = width // ranks
    middle = width // 2
    kept = w_skip.shape[0]
    skip_lanes = -(-kept // 256) * 256
    skip_cut = skip_lanes // 2
    qkv_cut = (3 * lanes) // 256 * 128 + 128
    text_rows = w_text_kv.shape[0]

    def spread(shard, before=None):
        if before is not None:
            shard, before = tie(shard, before)
        return lax.all_gather(shard, "sp", axis=0, tiled=False)

    def fetch(value, cut, joined=False):
        return [Gather(cube, value[:, :, :cut], 0, joined), Gather(cube, value[:, :, cut:], 1, joined)]

    def advance(movers):
        for mover in movers:
            mover.move()

    def join(movers):
        for mover in movers:
            mover.join()

    def exchange(value):
        return lax.all_to_all(value, "sp", split_axis=0, concat_axis=0, tiled=True)

    skip_z = spread(jnp.pad(w_skip.T, ((0, 0), (0, skip_lanes - kept))))
    steps = cube.spread(timestep[:, 0])
    joined = side_by_side(tokens.reshape(rows, width), skip_tokens.reshape(rows, width), kept, skip_lanes)
    wide = grid[:, 0, 1]
    counts = grid[:, 0, 0] * wide
    cosine, sine = rope_tables(sequence, wide, lanes)
    skip_z, steps, joined, cosine, sine = tie(skip_z, steps, joined, cosine, sine)
    skip_m = fetch(skip_z, skip_cut)
    qkv_z = spread(pad_heads(w_qkv.reshape(strip, -1), local), skip_z)
    advance(skip_m)

    time_act = jax.nn.silu(time_embed(steps, width)).astype(BF).reshape(ranks * micros, parts, -1)
    time_part = lax.dynamic_index_in_dim(time_act, zone, 1, keepdims=False)
    shift = cube.add(jnp.dot(time_part, w_mod, preferred_element_type=F32), "sp")
    skip_m[0].pieces[1], shift = tie(skip_m[0].pieces[1], shift)
    while skip_m[0].todo:
        advance(skip_m)
    shift = cube.trade(shift.reshape(ranks, micros, strip))
    skip_m[0].pieces[-1], shift = tie(skip_m[0].pieces[-1], shift)
    shift = jnp.stack([shift[mask] for mask in cube.masks]).reshape(2, ranks // 2, micros, strip)
    shift = jnp.transpose(shift, (0, 2, 1, 3)).reshape(2, micros, middle)
    qkv_m = fetch(qkv_z, qkv_cut)
    hold(qkv_m, *skip_m)
    advance(qkv_m)
    cross_z = jnp.concatenate([pad_heads(side, local) for side in (w_out1.T, w_query2, w_out2.T)], 1)
    cross_z = spread(pin(cross_z, *skip_m))
    fc1_z = spread(pin(w_fc1, *skip_m))
    join(skip_m)
    skip_w = [mover.weight() for mover in skip_m]

    def shuffle(count):
        block = count // ranks
        place = jnp.arange(count, dtype=jnp.int32)
        source = cube.owners[place // block] * block + place % block
        return (place[:, None] == source[None, :]).astype(BF)

    turn = shuffle(width)
    text_turn = shuffle(features)
    gains = jnp.stack([gain_skip, gain_attn, gain_cross, gain_mlp])
    gains = gains.reshape(4, ranks, strip)[:, cube.owners].reshape(4, 2, 1, middle)
    g_skip, g_attn, g_cross, g_mlp = gains

    lengths = text_len[:, 0, :]
    place = zone * slots + jnp.arange(slots, dtype=jnp.int32)
    live = (place[None, :] < counts[:, None]).astype(F32).reshape(rows, 1)
    gain_q = pad_heads(jnp.tile(gain_query, local)[None, :], local)
    gain_k = pad_heads(jnp.tile(gain_key, local)[None, :], local)

    grad3 = jnp.stack(
        [
            jnp.dot(cotangent.reshape(rows, width), side, preferred_element_type=F32) * live
            for side in (turn[:, :middle], turn[:, middle:])
        ]
    )
    d_mlp = grad3.astype(BF)

    wide_shape = jax.ShapeDtypeStruct((2, rows, middle), F32)
    low_shape = jax.ShapeDtypeStruct((2, rows, middle), BF)
    gain_shape = jax.ShapeDtypeStruct((2, 1, middle), F32)

    def first_norms(sums, extra, out):
        g0_ref, g1_ref, shift_ref = extra
        base_ref, stream_ref, pre_ref = out
        unit, _ = norm_unit(sums)
        stream = [unit[side] * g0_ref[side] for side in range(2)]
        unit, _ = norm_unit(stream)
        for side in range(2):
            base_ref[side] = sums[side]
            stream_ref[side] = stream[side]
            for micro in range(micros):
                cut = slice(micro * slots, (micro + 1) * slots)
                pre = unit[side][cut] * g1_ref[side] + shift_ref[side, micro : micro + 1]
                pre_ref[side, cut] = pre.astype(BF)

    def next_norm(sums, extra, out):
        before_ref, gain_ref = extra
        after_ref, pre_ref = out
        stream = [before_ref[side] + sums[side] for side in range(2)]
        unit, _ = norm_unit(stream)
        for side in range(2):
            after_ref[side] = stream[side]
            pre_ref[side] = (unit[side] * gain_ref[side]).astype(BF)

    base, stream, pre_attn = to_features(
        joined, skip_w, [g_skip, g_attn, shift], [wide_shape, wide_shape, low_shape], first_norms
    )
    while qkv_m[0].todo:
        advance(qkv_m)
    after_qkv = [mover.pieces[-1] for mover in qkv_m]
    hold(qkv_m, pre_attn)
    join(qkv_m)
    fc2_z = spread(pin(w_fc2.T, *after_qkv))
    pre_attn, cross_z, fc1_z = tie(pre_attn, cross_z, fc1_z)
    cross_m = fetch(cross_z, 2 * lanes, True)
    hold(cross_m, *after_qkv)
    advance(cross_m)
    qkv_w = [mover.weight() for mover in qkv_m]
    projected = to_lanes(pre_attn, qkv_w)
    projected = bind(projected, *cross_m)
    text_z = jnp.pad(pad_heads(w_text_kv.reshape(text_rows, -1), local), ((0, max(0, strip - text_rows)), (0, 0)))
    projected, fc2_z, text_z = tie(projected, fc2_z, text_z)
    text_z = spread(text_z)
    while cross_m[0].todo:
        advance(cross_m)
    fc_m = [Gather(cube, fc1_z, 0, True), Gather(cube, fc2_z, 1, True)]
    hold(fc_m, cross_m[0].pieces[-1], cross_m[1].pieces[-1])
    advance(fc_m)
    raw = exchange(projected.reshape(parts, micros, slots, 3 * lanes))
    arrived = [mover.pieces[-1] for mover in cross_m]
    text_m = Gather(cube, text_z[:, :text_rows], 0, True)
    hold([text_m], *arrived)
    while text_m.todo:
        text_m.move()
    text_own = jnp.dot(text.reshape(-1, features), text_turn, preferred_element_type=F32).astype(BF)
    text_own = jnp.pad(
        text_own.reshape(micros, text_slots, features), ((0, 0), (0, text_strip - text_slots), (0, 0))
    ).reshape(micros * text_strip, features)
    while fc_m[0].todo:
        advance(fc_m)
    text_all = spread(pin(text_own, *arrived))
    fc_m[0].pieces[0], d_mlp, turn, text_turn = tie(fc_m[0].pieces[0], d_mlp, turn, text_turn)
    join(cross_m + [text_m])
    first_w, out2_w = [mover.weight() for mover in cross_m]
    text_w = text_m.weight()
    out1_w, query2_w = (Lanes(first_w.near, first_w.far, lanes, index) for index in range(2))
    attended, turned_q, turned_k, norms = self_forward(raw, counts, cosine, sine, gain_q, gain_k)
    attended, first_w.far, out2_w.far, text_w.far = tie(attended, first_w.far, out2_w.far, text_w.far)
    out1_w.far = query2_w.far = first_w.far
    attended = exchange(attended).reshape(parts, rows, lanes)
    text_all = text_all.reshape(-1, features)
    text_all = jnp.stack([text_all[:, : features // 2], text_all[:, features // 2 :]])
    text_kv = to_lanes(text_all, [text_w]).reshape(parts, parts, micros, text_strip, 2 * lanes)
    attended, text_kv = tie(attended, text_kv)
    stream1, pre_cross = to_features(
        attended, [out1_w], [stream, g_cross], [wide_shape, low_shape], next_norm
    )
    hold(fc_m, pre_cross)
    join(fc_m)
    fc1_w, fc2_w = [mover.weight() for mover in fc_m]
    query2 = to_lanes(pre_cross, [query2_w]).reshape(parts, micros, slots, lanes)
    crossed = cross_forward(query2, text_kv, lengths, text_slots).reshape(parts, rows, lanes)
    stream2, pre_mlp = to_features(
        crossed, [out2_w], [stream1, g_mlp], [wide_shape, low_shape], next_norm
    )
    hidden0, activ0, partial, fc2_n0, fc2_f0 = mlp_forward(pre_mlp, d_mlp, stream2, fc1_w, fc2_w, 0)
    hidden1, activ1, result, fc2_n1, fc2_f1 = mlp_forward(pre_mlp, d_mlp, partial, fc1_w, fc2_w, 1, live)
    share = fc2_n0.shape[2]
    fc2_s = scatter(cube, (fc2_n0, fc2_f0), (share, 0, 0)) + scatter(cube, (fc2_n1, fc2_f1), (share, 0, 1))

    def settle(values, before=None):
        value = values[0] if len(values) == 1 else jnp.concatenate(values, 2)
        if before is not None:
            value, before = tie(value, before)
        return lax.psum_scatter(value, "sp", scatter_dimension=0, tiled=False)

    fc1_n0, fc1_f0, partial = mlp_backward(d_mlp, pre_mlp, hidden0, fc1_w, fc2_w, 0, None)
    fc1_s = scatter(cube, (fc1_n0, fc1_f0), (share, 0, 0))
    pack(fc2_s)
    partial = bind(partial, *fc2_s)
    send(fc2_s)
    fc1_n1, fc1_f1, grad2, d_cross, d_gain_mlp = mlp_backward(
        d_mlp, pre_mlp, hidden1, fc1_w, fc2_w, 1, partial, [stream2, g_mlp, grad3]
    )
    fc1_s += scatter(cube, (fc1_n1, fc1_f1), (share, 0, 1))
    d_cross = bind(d_cross, *fc2_s)
    d_crossed = to_lanes(d_cross, [out2_w])
    pack(fc2_s)
    d_crossed = bind(d_crossed, *fc2_s)
    send(fc2_s)
    d_query2, d_text_kv = cross_backward(
        query2, text_kv, lengths, d_crossed.reshape(parts, micros, slots, lanes), text_slots
    )
    d_query2 = bind(d_query2, *fc2_s)
    d_query2 = d_query2.reshape(parts, rows, lanes)
    d_text_kv = d_text_kv.reshape(parts, -1, 2 * lanes)
    total_fc2 = results(fc2_s)
    term_fc2 = settle(total_fc2)

    def go_back(sums, extra, out):
        add_norm_back(sums, *extra, *out)

    grad1, d_attn, d_gain_cross = to_features(
        d_query2, [query2_w], [stream1, g_cross, grad2], [wide_shape, low_shape, gain_shape], go_back
    )
    d_attn = bind(d_attn, *fc1_s)
    pack(fc1_s)
    d_attn = bind(d_attn, *fc1_s)
    send(fc1_s)
    d_attended = to_lanes(d_attn, [out1_w])
    d_attended, d_text_kv, pre_cross = tie(d_attended, d_text_kv, pre_cross)
    d_heads = exchange(d_attended.reshape(parts, micros, slots, lanes))

    def words_back(sums, extra, out):
        size = micros * text_strip
        for zone in range(parts):
            for side in range(2):
                out[0][zone, side] = sums[side][zone * size : (zone + 1) * size].astype(BF)

    words_shape = jax.ShapeDtypeStruct((parts, 2, micros * text_strip, features // 2), BF)
    d_words = to_features(d_text_kv, [text_w], [], [words_shape], words_back)[0]
    text_t = list(terms_of([(text_all, d_text_kv, 2 * lanes, 0)]))
    cross_t = terms_of(
        [(d_attn, attended, lanes, 0), (pre_cross, d_query2, lanes, 0), (d_cross, crossed, lanes, 0)]
    )
    cross_t = list(cross_t)
    d_heads, d_words, text_t[1], cross_t[1] = tie(d_heads, d_words, text_t[1], cross_t[1])
    d_words = settle([d_words])
    text_s = scatter(cube, text_t, (2 * lanes, 0, 1))
    cross_s = scatter(cube, cross_t, (2 * lanes, 0, 0), (lanes, 2, 1))
    d_heads = bind(d_heads, *fc1_s)
    pack(fc1_s)
    d_heads = bind(d_heads, *fc1_s)
    send(fc1_s)
    d_raw, d_gain_q, d_gain_k = self_backward(
        raw, counts, cosine, sine, gain_q, gain_k, turned_q, turned_k, norms, d_heads
    )
    d_raw, term_fc2, d_words = tie(d_raw, term_fc2, d_words)
    d_raw = bind(d_raw, *fc1_s)
    d_projected = exchange(d_raw).reshape(parts, rows, 3 * lanes)
    other_s = cross_s + text_s
    total_fc1 = results(fc1_s)
    pack(cross_s)
    pack(text_s)
    send(other_s)
    d_projected = bind(d_projected, *other_s)
    term_fc1 = settle(total_fc1, d_projected)
    qkv_t = terms_of([(pre_attn, d_projected, 3 * lanes, 0)])
    qkv_s = scatter(cube, qkv_t, (2 * lanes, 0, 0), (lanes, 2, 1))
    pack(cross_s)
    pack(text_s)
    send(other_s)
    pack(qkv_s)
    d_projected = bind(d_projected, *qkv_s)
    send(qkv_s)

    def last_norms(sums, extra, out):
        stream_ref, g1_ref, base_ref, g0_ref, add_ref = extra
        low_ref, d_shift_ref, d_g1_ref, d_g0_ref = out
        back, gains1 = norm_back([stream_ref[0], stream_ref[1]], g1_ref, sums)
        total = [add_ref[side] + back[side] for side in range(2)]
        back, gains0 = norm_back([base_ref[0], base_ref[1]], g0_ref, total)
        for side in range(2):
            low_ref[side] = back[side].astype(BF)
            d_g1_ref[side] = gains1[side]
            d_g0_ref[side] = gains0[side]
            for micro in range(micros):
                part = sums[side][micro * slots : (micro + 1) * slots]
                d_shift_ref[side, micro : micro + 1] = jnp.sum(part, 0, keepdims=True)

    shift_shape = jax.ShapeDtypeStruct((2, micros, middle), F32)
    d_base, d_shift, d_gain_attn, d_gain_skip = to_features(
        d_projected,
        qkv_w,
        [stream, g_attn, base, g_skip, grad1],
        [low_shape, shift_shape, gain_shape, gain_shape],
        last_norms,
    )
    d_base = bind(d_base, *other_s)
    skip_t = terms_of([(d_base, joined, skip_lanes, 0)])
    skip_s = scatter(cube, skip_t, (skip_cut, 0, 0), (skip_cut, 1, 1))
    pack(skip_s)
    pack(qkv_s)
    skip_s[0].pieces[0] = bind(skip_s[0].pieces[0], *qkv_s)
    send(qkv_s)
    send(skip_s)
    term_cross, term_text = settle(results(cross_s)), settle(results(text_s))
    total_qkv = results(qkv_s)
    last = settle(list(total_qkv) + list(results(skip_s)))
    term_qkv, term_skip = last[:, : 3 * lanes], last[:, 3 * lanes :]
    d_joined = to_inputs(d_base, skip_w, kept)
    result = (
        jnp.dot(result[0], turn[:, :middle].T, preferred_element_type=F32)
        + jnp.dot(result[1], turn[:, middle:].T, preferred_element_type=F32)
    ).astype(BF)
    d_words = d_words.reshape(2, micros * text_strip, features // 2)
    d_words = jnp.dot(
        d_words[0], text_turn[:, : features // 2].T, preferred_element_type=F32
    ) + jnp.dot(d_words[1], text_turn[:, features // 2 :].T, preferred_element_type=F32)
    d_words = d_words.reshape(micros, text_strip, features)[:, :text_slots]

    d_shift = jnp.transpose(d_shift.reshape(2, micros, ranks // 2, strip), (0, 2, 1, 3))
    d_shift = d_shift.reshape(ranks, micros, strip)
    d_shift = jnp.stack([d_shift[cube.masks.index(mask)] for mask in range(ranks)])
    d_shift = cube.add(cube.trade(d_shift), "sp").reshape(ranks * micros, strip)
    term_mod = lax.dot_general(
        time_part.astype(F32), d_shift, (((0,), (0,)), ((), ())), precision=lax.Precision.HIGHEST
    )

    places = jnp.array([cube.masks.index(mask) for mask in range(ranks)], jnp.int32)
    places = places[jnp.arange(ranks, dtype=jnp.int32) ^ cube.rank]
    gains = jnp.stack([d_gain_skip, d_gain_attn, d_gain_cross, d_gain_mlp])
    gains = gains.reshape(4, ranks, strip)[:, places].reshape(-1)
    heads = jnp.stack([jnp.sum(d_gain_q, (0, 1)), jnp.sum(d_gain_k, (0, 1))])
    heads = jnp.sum(heads[:, : local * HP].reshape(2, local, HP)[:, :, :HD], 1)
    packed = jnp.concatenate([gains, heads.reshape(-1)])
    packed = cube.add(cube.add(packed, "sp"), "dp")
    gains = packed[: 4 * width].reshape(4, ranks * parts, -1)
    gains = lax.dynamic_index_in_dim(gains, cube.rank * parts + zone, 1, keepdims=False)
    heads = packed[4 * width :].reshape(2, HD)

    def whole(term, groups):
        return cut_heads(term.astype(F32), local).reshape(term.shape[0], groups, -1)

    return (
        result.reshape(tokens.shape),
        d_joined[0].reshape(tokens.shape),
        d_joined[1].reshape(tokens.shape),
        d_words.reshape(text.shape),
        term_skip.astype(F32)[:, :kept].T,
        term_mod,
        whole(term_qkv, 3),
        cut_heads(term_cross[:, :lanes].astype(F32), local).T,
        cut_heads(term_cross[:, lanes : 2 * lanes].astype(F32), local),
        whole(term_text, 2),
        cut_heads(term_cross[:, 2 * lanes :].astype(F32), local).T,
        term_fc1.astype(F32),
        term_fc2.astype(F32).T,
        gains[0],
        gains[1],
        gains[2],
        gains[3],
        heads[0],
        heads[1],
    )


def solution(mesh):
    rows = P(None, ("dp", "sp"), None)
    column = P("sp", "dp")
    row = P("dp", "sp")
    grouped = P("dp", None, "sp")
    in_specs = (
        (rows, rows, rows, P(None, "dp"), P(None, "dp", None), P(None, "dp", None))
        + (column, column, grouped, column, row, grouped, column, row, column)
        + (P(),) * 6
        + (rows,)
    )
    out_specs = (
        (rows, rows, rows, rows)
        + (column, column, grouped, column, row, grouped, column, row, column)
        + (P(("dp", "sp")),) * 4
        + (P(), P())
    )
    return jax.shard_map(
        on_device, mesh=mesh, in_specs=in_specs, out_specs=out_specs, check_vma=False
    )
```
